32 devices in a mesh: clip: 8 (over z, y), ha: 2 (over core), wa: 2 (over x).
Axes of the slice: x: 2, y: 2, z: 4, core: 2. Of those that a mesh axis runs over, the one named last changes fastest.
Arguments:
- slow_input: bfloat16 [32, 12, 14, 14, 1024], P('clip', None, 'ha', 'wa'), may hold values from -6 to 6
- fast_input: bfloat16 [32, 48, 14, 14, 128], P('clip', None, 'ha', 'wa'), may hold values from -6 to 6
- frame_counts: int32 [32], replicated, may hold values from 4 to 12, as said below
- lateral_weight: bfloat16 [5, 128, 256], replicated, may hold values from -0.25 to 0.25
- slow_a_weight: bfloat16 [3, 1280, 256], replicated, may hold values from -0.09375 to 0.09375
- slow_b_weight: bfloat16 [3, 3, 256, 256], replicated, may hold values from -0.125 to 0.125
- slow_c_weight: bfloat16 [256, 1024], replicated, may hold values from -0.375 to 0.375
- slow_proj_weight: bfloat16 [1280, 1024], replicated, may hold values from -0.15625 to 0.15625
- fast_a_weight: bfloat16 [3, 128, 32], replicated, may hold values from -0.3125 to 0.3125
- fast_b_weight: bfloat16 [3, 3, 32, 32], replicated, may hold values from -0.375 to 0.375
- fast_c_weight: bfloat16 [32, 128], replicated, may hold values from -1 to 1
- slow_gain: float32 [2560], replicated, may hold values from 0.1 to 1.9
- slow_shift: float32 [2560], replicated, may hold values from -3 to 3
- fast_gain: float32 [192], replicated, may hold values from 0.1 to 1.9
- fast_shift: float32 [192], replicated, may hold values from -3 to 3
- slow_cotangent: bfloat16 [32, 12, 14, 14, 1024], P('clip', None, 'ha', 'wa'), may hold values from -6 to 6
- fast_cotangent: bfloat16 [32, 48, 14, 14, 128], P('clip', None, 'ha', 'wa'), may hold values from -6 to 6
Outputs:
- slow_output: bfloat16 [32, 12, 14, 14, 1024], P('clip', None, 'ha', 'wa')
- fast_output: bfloat16 [32, 48, 14, 14, 128], P('clip', None, 'ha', 'wa')
- slow_input_grad: bfloat16 [32, 12, 14, 14, 1024], P('clip', None, 'ha', 'wa')
- fast_input_grad: bfloat16 [32, 48, 14, 14, 128], P('clip', None, 'ha', 'wa')
- lateral_weight_grad: float32 [5, 128, 256], replicated
- slow_a_weight_grad: float32 [3, 1280, 256], replicated
- slow_b_weight_grad: float32 [3, 3, 256, 256], replicated
- slow_c_weight_grad: float32 [256, 1024], replicated
- slow_proj_weight_grad: float32 [1280, 1024], replicated
- fast_a_weight_grad: float32 [3, 128, 32], replicated
- fast_b_weight_grad: float32 [3, 3, 32, 32], replicated
- fast_c_weight_grad: float32 [32, 128], replicated
- slow_gain_grad: float32 [2560], replicated
- slow_shift_grad: float32 [2560], replicated
- fast_gain_grad: float32 [192], replicated
- fast_shift_grad: float32 [192], replicated
The draws below stay inside these ranges and needn't reach their ends.
Inputs may be any that keep to these rules, and one draw needn't show every extreme that they name: `frame_counts`: some clip has exactly 12 real frames and some exactly 4.
All inputs are finite; a program needn't handle non-finite values.
Results may differ from the reference program's by a relative error of at most 0.0088.
Values may be sent and summed in bfloat16 or wider, within the bound.
A program may use at most 256 MiB of HBM per device.

```python
import jax
import jax.numpy as jnp
from jax import lax

TS = 12
ALPHA = 4
H = 14
W = 14
C_IN = 1024
C_LAT = 256
C_MID = 256
C_FAST = 128
C_FMID = 32
TF = 48
LEN_MIN = 4
CLIPS = 32


def clip_field(key, extent):
    clip_count = extent[0]
    rising = 0.5 * 3.0 ** (jnp.arange(clip_count, dtype=jnp.float32) / max(clip_count - 1, 1))
    rising = rising.reshape((clip_count,) + (1,) * (len(extent) - 1))
    values = jnp.clip(jax.random.normal(key, extent, jnp.float32), -4.0, 4.0)
    return (values * rising).astype(jnp.bfloat16)


def draw_slow_input(key, part):
    return clip_field(jax.random.fold_in(key, 11), (CLIPS, TS, H, W, C_IN))


def draw_fast_input(key, part):
    return clip_field(jax.random.fold_in(key, 13), (CLIPS, TF, H, W, C_FAST))


def draw_frame_counts(key, part):
    counted = jax.random.randint(jax.random.fold_in(key, 17), (CLIPS,), LEN_MIN, TS + 1)
    places = jax.random.permutation(jax.random.fold_in(key, 19), CLIPS)
    counted = counted.at[places[0]].set(TS).at[places[1]].set(LEN_MIN)
    return counted.astype(jnp.int32)


def shard_levels(key, shape, split, smallest, top_value):
    def one(axis_at, shards_of):
        heights = jax.random.uniform(jax.random.fold_in(jax.random.fold_in(key, 6), axis_at), (shards_of,), jnp.float32, smallest / len(split), top_value / len(split))
        return jnp.repeat(jnp.exp(heights), shape[axis_at] // shards_of).reshape((-1,) + (1,) * (len(shape) - axis_at - 1))

    gain = one(*split[0])
    for cut in split[1:]:
        gain = gain * one(*cut)
    return gain


def noise(key, dims, scale, limit, split=(), kind=jnp.bfloat16):
    factor_of = shard_levels(key, dims, split, -0.22, 0.18) if split else 1.0
    entries = jax.random.normal(key, dims, jnp.float32) * scale * factor_of
    return jnp.minimum(jnp.maximum(entries, -limit), limit).astype(kind)


def setup_inputs(seed: int = 0) -> dict:
    splits = jax.random.split(jax.random.key(seed), 18)
    slow_input = draw_slow_input(jax.random.fold_in(splits[17], 71), 0)
    fast_input = draw_fast_input(jax.random.fold_in(splits[17], 71), 0)
    frame_counts = draw_frame_counts(jax.random.fold_in(splits[17], 71), 0)
    lateral_weight = noise(splits[3], (5, C_FAST, C_LAT), (5 * C_FAST) ** -0.5, 0.25)
    slow_a_weight = noise(splits[4], (3, C_IN + C_LAT, C_MID), (3 * (C_IN + C_LAT)) ** -0.5, 0.09375)
    slow_b_weight = noise(splits[5], (3, 3, C_MID, C_MID), (9 * C_MID) ** -0.5, 0.125)
    slow_c_weight = noise(splits[6], (C_MID, C_IN), C_MID ** -0.5, 0.375)
    slow_proj_weight = noise(splits[7], (C_IN + C_LAT, C_IN), (C_IN + C_LAT) ** -0.5, 0.15625)
    fast_a_weight = noise(splits[8], (3, C_FAST, C_FMID), (3 * C_FAST) ** -0.5, 0.3125)
    fast_b_weight = noise(splits[9], (3, 3, C_FMID, C_FMID), (9 * C_FMID) ** -0.5, 0.375)
    fast_c_weight = noise(splits[10], (C_FMID, C_FAST), C_FMID ** -0.5, 1.0)
    slow_gain = jnp.clip(1.0 + 0.18 * jax.random.normal(splits[11], (2 * C_MID + 2 * C_IN,), jnp.float32), 0.1, 1.9)
    slow_shift = noise(splits[12], (2 * C_MID + 2 * C_IN,), 0.5, 3.0, (), jnp.float32)
    fast_gain = jnp.clip(1.0 + 0.18 * jax.random.normal(splits[13], (2 * C_FMID + C_FAST,), jnp.float32), 0.1, 1.9)
    fast_shift = noise(splits[14], (2 * C_FMID + C_FAST,), 0.5, 3.0, (), jnp.float32)
    slow_cotangent = noise(splits[15], (CLIPS, TS, H, W, C_IN), 1.0, 6.0, ((0, 8), (2, 2), (3, 2)))
    fast_cotangent = noise(splits[16], (CLIPS, TF, H, W, C_FAST), 1.0, 6.0, ((0, 8), (2, 2), (3, 2)))
    return dict(slow_input=slow_input, fast_input=fast_input, frame_counts=frame_counts, lateral_weight=lateral_weight, slow_a_weight=slow_a_weight, slow_b_weight=slow_b_weight, slow_c_weight=slow_c_weight, slow_proj_weight=slow_proj_weight, fast_a_weight=fast_a_weight, fast_b_weight=fast_b_weight, fast_c_weight=fast_c_weight, slow_gain=slow_gain, slow_shift=slow_shift, fast_gain=fast_gain, fast_shift=fast_shift, slow_cotangent=slow_cotangent, fast_cotangent=fast_cotangent)


@jax.custom_vjp
def low(v):
    return lax.optimization_barrier(v.astype(jnp.bfloat16)).astype(jnp.float32)

@jax.custom_vjp
def low_back(v):
    return v

def low_keep(v):
    return (low(v), None)

def low_pass(kept, grad):
    return (grad,)

def back_keep(v):
    return (v, None)

def back_low(kept, grad):
    return (low(grad),)
low.defvjp(low_keep, low_pass)
low_back.defvjp(back_keep, back_low)
eps_norm = 1e-05
highest = lax.Precision.HIGHEST

def product(values, weight):
    return jnp.einsum('cthwi,io->cthwo', values, weight, precision=highest)

def conv_time(values, weight):
    frames = values.shape[1]
    padded = jnp.pad(values, ((0, 0), (1, 1), (0, 0), (0, 0), (0, 0)))
    return sum((product(padded[:, k:k + frames], weight[k]) for k in range(3)))

def conv_space(values, weight):
    height = values.shape[2]
    width = values.shape[3]
    padded = jnp.pad(values, ((0, 0), (0, 0), (1, 1), (1, 1), (0, 0)))
    return sum((product(padded[:, :, i:i + height, j:j + width], weight[i, j]) for i in range(3) for j in range(3)))

def conv_lateral(values, weight):
    padded = jnp.pad(values, ((0, 0), (2, 2), (0, 0), (0, 0), (0, 0)))
    return sum((product(padded[:, k:k + ALPHA * TS:ALPHA], weight[k]) for k in range(5)))

def normalize(values, gains, shifts, frame_mask, counted):
    means = lax.optimization_barrier(jnp.sum(frame_mask * values, axis=(0, 1, 2, 3))) / counted
    spread = lax.optimization_barrier(jnp.sum(frame_mask * (values - means) ** 2, axis=(0, 1, 2, 3))) / counted
    return gains * (values - means) * lax.rsqrt(spread + eps_norm) + shifts

def reference(slow_input, fast_input, frame_counts, lateral_weight, slow_a_weight, slow_b_weight, slow_c_weight, slow_proj_weight, fast_a_weight, fast_b_weight, fast_c_weight, slow_gain, slow_shift, fast_gain, fast_shift, slow_cotangent, fast_cotangent):
    slow_mask = (jnp.arange(TS)[None, :] < frame_counts[:, None]).astype(jnp.float32)[:, :, None, None, None]
    fast_mask = (jnp.arange(TF)[None, :] < ALPHA * frame_counts[:, None]).astype(jnp.float32)[:, :, None, None, None]
    slow_total = jnp.sum(frame_counts).astype(jnp.float32) * (H * W)
    fast_total = slow_total * ALPHA
    slow_bounds = [0, C_MID, 2 * C_MID, 2 * C_MID + C_IN, 2 * C_MID + 2 * C_IN]
    fast_bounds = [0, C_FMID, 2 * C_FMID, 2 * C_FMID + C_FAST]

    def forward(slow_in, fast_in, lat_w, sa_w, sb_w, sc_w, sp_w, fa_w, fb_w, fc_w, s_gain, s_shift, f_gain, f_shift):

        def slow_norm(values, index):
            return normalize(values, s_gain[slow_bounds[index]:slow_bounds[index + 1]], s_shift[slow_bounds[index]:slow_bounds[index + 1]], slow_mask, slow_total)

        def fast_norm(values, index):
            return normalize(values, f_gain[fast_bounds[index]:fast_bounds[index + 1]], f_shift[fast_bounds[index]:fast_bounds[index + 1]], fast_mask, fast_total)
        slow_zero = slow_in * slow_mask
        fast_zero = fast_in * fast_mask
        lateral = low(low_back(conv_lateral(fast_zero, lat_w)))
        joined = jnp.concatenate([slow_zero, lateral], axis=-1)
        slow_first = low(jax.nn.silu(slow_norm(low_back(conv_time(joined, sa_w)), 0)) * slow_mask)
        slow_second = low(jax.nn.silu(slow_norm(low_back(conv_space(slow_first, sb_w)), 1)) * slow_mask)
        slow_pre = slow_norm(low_back(product(slow_second, sc_w)), 2) + slow_norm(low_back(product(joined, sp_w)), 3)
        slow_out = jax.nn.silu(slow_pre) * slow_mask
        fast_first = low(jax.nn.silu(fast_norm(low_back(conv_time(fast_zero, fa_w)), 0)) * fast_mask)
        fast_second = low(jax.nn.silu(fast_norm(low_back(conv_space(fast_first, fb_w)), 1)) * fast_mask)
        fast_pre = fast_norm(low_back(product(fast_second, fc_w)), 2) + fast_zero
        fast_out = jax.nn.silu(fast_pre) * fast_mask
        return (slow_out, fast_out)
    primals = tuple((v.astype(jnp.float32) for v in (slow_input, fast_input, lateral_weight, slow_a_weight, slow_b_weight, slow_c_weight, slow_proj_weight, fast_a_weight, fast_b_weight, fast_c_weight, slow_gain, slow_shift, fast_gain, fast_shift)))
    outputs, pullback = jax.vjp(forward, *primals)
    grads = pullback((slow_cotangent.astype(jnp.float32), fast_cotangent.astype(jnp.float32)))
    return (outputs[0].astype(jnp.bfloat16), outputs[1].astype(jnp.bfloat16), grads[0].astype(jnp.bfloat16), grads[1].astype(jnp.bfloat16), grads[2], grads[3], grads[4], grads[5], grads[6], grads[7], grads[8], grads[9], grads[10], grads[11], grads[12], grads[13])
```

```python
import functools

import jax
import jax.numpy as jnp
from jax import lax
from jax.experimental import pallas as pl
from jax.experimental.pallas import tpu as pltpu
from jax.sharding import PartitionSpec as P

ALPHA = 4
H = 14
W = 14
C_IN = 1024
C_LAT = 256
C_MID = 256
C_FAST = 128
C_FMID = 32
C_JOIN = C_IN + C_LAT
MIX = C_MID + ALPHA * C_FMID
WIDE_FAST = ALPHA * C_FAST

eps_norm = 1e-05
f32 = jnp.float32
bf16 = jnp.bfloat16
MESH = pl.DeviceIdType.MESH
MIB = 1 << 20


def dot(a, b):
    return lax.dot_general(a, b, (((1,), (0,)), ((), ())), preferred_element_type=f32)


def dot_nt(a, b):
    return lax.dot_general(a, b, (((1,), (1,)), ((), ())), preferred_element_type=f32)


def dot_tn(a, b):
    return lax.dot_general(a, b, (((0,), (0,)), ((), ())), preferred_element_type=f32)


def sigmoid(v):
    return 0.5 + 0.5 * jnp.tanh(0.5 * v)


def later(y, clips):
    return jnp.concatenate([jnp.zeros_like(y[:, :clips]), y[:, : y.shape[1] - clips]], axis=1)


def sooner(y, clips):
    return jnp.concatenate([y[:, clips:], jnp.zeros_like(y[:, :clips])], axis=1)


def rows_sum(v):
    return jnp.sum(jnp.sum(v, axis=0), axis=0, keepdims=True)


def phase_sum(v):
    out = v
    for k in range(1, ALPHA):
        out = out + pltpu.roll(v, k * C_FMID, 1)
    return out


def block_sum(v):
    return sum(v[:, p * C_FAST : (p + 1) * C_FAST] for p in range(ALPHA))


def spread(mask, width):
    return jnp.tile(mask, (1, width // 128))


def frames_matrix(wfa_ref, out_ref, ends_ref):
    out_ref[...] = jnp.zeros_like(out_ref)
    ends_ref[...] = jnp.zeros_like(ends_ref)
    for p in range(ALPHA):
        for s in range(max(p - 1, 0), min(p + 2, ALPHA)):
            out_ref[p * C_FMID : (p + 1) * C_FMID, s * C_FAST : (s + 1) * C_FAST] = wfa_ref[s - p + 1]
    ends_ref[0, 0:C_FMID] = wfa_ref[0]
    ends_ref[1, 3 * C_FMID :] = wfa_ref[2]


def expand_matrix(wfc_ref, out_ref):
    out_ref[...] = jnp.zeros_like(out_ref)
    for p in range(ALPHA):
        out_ref[p * C_FMID : (p + 1) * C_FMID, p * C_FAST : (p + 1) * C_FAST] = wfc_ref[...]


def first_convs(clips, xs, xf, m, perm, wl, wa, wp, wfa, x_out, f_out, z_out, zp_out, st, base_out,
                taps, ends, base, one, two):
    h = pl.program_id(0)
    cols = xs.shape[1]
    slab = m.shape[0]
    rows = cols * slab

    @pl.when(h == 0)
    def _():
        frames_matrix(wfa, taps, ends)

    mask_in = spread(m[...], C_IN).astype(bf16)
    for w in range(cols):
        x_out[w, :, :C_IN] = xs[:, w].reshape(slab, C_IN) * mask_in
        phases = dot(perm[...], xf[:, w].reshape(ALPHA * slab, C_FAST)).astype(bf16)
        for p in range(ALPHA):
            f_out[w, :, p * C_FAST : (p + 1) * C_FAST] = phases[p * slab : (p + 1) * slab]
    fast = f_out[...].reshape(rows, WIDE_FAST)
    lat = dot(fast[:, : 3 * C_FAST], wl[2:5].reshape(3 * C_FAST, C_LAT)).reshape(cols, slab, C_LAT)
    back = dot(fast[:, 2 * C_FAST :], wl[0:2].reshape(2 * C_FAST, C_LAT)).reshape(cols, slab, C_LAT)
    x_out[:, :, C_IN:] = (lat + later(back, clips)).astype(bf16)
    joined = x_out[...].reshape(rows, C_JOIN)
    za = dot(joined, wa[1]).reshape(cols, slab, C_MID)
    za = za + later(dot(joined, wa[0]).reshape(cols, slab, C_MID), clips)
    za = za + sooner(dot(joined, wa[2]).reshape(cols, slab, C_MID), clips)
    fa = dot_nt(fast, taps[...]).reshape(cols, slab, 128)
    fa = fa + later(dot_nt(fast[:, 3 * C_FAST :], ends[0]).reshape(cols, slab, 128), clips)
    fa = fa + sooner(dot_nt(fast[:, :C_FAST], ends[1]).reshape(cols, slab, 128), clips)
    zp = dot(joined, wp[...]).reshape(cols, slab, C_IN)
    z_out[:, :, :C_MID] = za
    z_out[:, :, C_MID:] = fa
    parts = ((0, za), (C_MID, fa), (MIX, zp))
    here = cols * jnp.sum(m[...], axis=0, keepdims=True)

    @pl.when(h == 0)
    def _():
        for at, z in parts:
            width = z.shape[-1]
            mean = rows_sum(z * spread(m[...], width)) / spread(here, width)
            if at == C_MID:
                mean = phase_sum(mean) * 0.25
            base[:, at : at + width] = mean
        one[...] = jnp.zeros_like(one)
        two[...] = jnp.zeros_like(two)

    for at, z in parts:
        width = z.shape[-1]
        off = z - base[:, at : at + width]
        if at == MIX:
            zp_out[...] = off.astype(bf16)
        off = off * spread(m[...], width)
        one[:, at : at + width] += rows_sum(off)
        two[:, at : at + width] += rows_sum(off * off)

    @pl.when(h == pl.num_programs(0) - 1)
    def _():
        count = pl.num_programs(0) * here
        base_out[...] = base[:, MIX:]
        finish_moments(st, base[...], one[...], two[...], count, ((0, C_MID, 0), (C_MID, 128, 1), (MIX, C_IN, 0)))


def finish_moments(st, base, one, two, count, parts):
    for at, width, fast in parts:
        s1 = one[:, at : at + width]
        s2 = two[:, at : at + width]
        if fast:
            s1 = phase_sum(s1) * 0.25
            s2 = phase_sum(s2) * 0.25
        n = spread(count.astype(f32), width)
        s1 = s1 / n
        st[0:1, at : at + width] = base[:, at : at + width] + s1
        st[1:2, at : at + width] = s2 / n - s1 * s1


def affine(moments, gain, shift, at, width):
    mean = moments[0:1, at : at + width]
    scale = lax.rsqrt(moments[1:2, at : at + width] + eps_norm)
    return mean, scale, gain[...], shift[...]


def space_convs(place, z1, row, col, corner, mom, gain, shift, m, wb, wfb, a_out, z_out, st, one, two):
    ha, wa = place[0], place[1]
    high, cols, slab, _ = z1.shape
    rows = cols * slab
    mean, scale, g, b = affine(mom, gain, shift, 0, MIX)
    mult = scale * g
    mask = spread(m[...], MIX)

    def act(z):
        v = (z - mean) * mult + b
        return (v * sigmoid(v) * mask).astype(bf16)

    far = high + 1
    a_out[far * ha] = jnp.zeros((cols + 2, slab, MIX), bf16)
    a_out[:, far * wa] = jnp.zeros((high + 2, slab, MIX), bf16)
    a_out[far * (1 - ha), 1 : 1 + cols] = act(row[...])
    a_out[1 : 1 + high, far * (1 - wa)] = act(col[...])
    a_out[far * (1 - ha), far * (1 - wa)] = act(corner[...])

    def fill(h, carry):
        a_out[h + 1, 1 : 1 + cols] = act(z1[h])
        return carry

    lax.fori_loop(0, high, fill, 0)

    def line(h, carry):
        slow = jnp.zeros((rows, C_MID), f32)
        fast = jnp.zeros((rows, 128), f32)
        for i in range(3):
            for j in range(3):
                v = a_out[h + i, j : j + cols].reshape(rows, MIX)
                slow = slow + dot(v[:, :C_MID], wb[i, j])
                fast = fast + dot(v[:, C_MID:], wfb[3 * i + j])
        z_out[h, :, :, :C_MID] = slow.reshape(cols, slab, C_MID)
        z_out[h, :, :, C_MID:] = fast.reshape(cols, slab, 128)
        return carry

    lax.fori_loop(0, high, line, 0)
    here = cols * jnp.sum(m[...], axis=0, keepdims=True)
    base = rows_sum(z_out[0] * mask) / spread(here, MIX)
    base = jnp.concatenate([base[:, :C_MID], phase_sum(base[:, C_MID:]) * 0.25], axis=1)
    one[...] = jnp.zeros_like(one)
    two[...] = jnp.zeros_like(two)

    def gather(h, carry):
        off = (z_out[h] - base) * mask
        one[...] += rows_sum(off)
        two[...] += rows_sum(off * off)
        return carry

    lax.fori_loop(0, high, gather, 0)
    finish_moments(st, base, one[...], two[...], high * here, ((0, C_MID, 0), (C_MID, 128, 1)))


def expand_moments(z2, mom, gain, shift, m, wc, wfc, a_out, st, big, base, one, two):
    h = pl.program_id(0)
    cols, slab, _ = z2.shape
    rows = cols * slab

    @pl.when(h == 0)
    def _():
        expand_matrix(wfc, big)

    mean, scale, g, b = affine(mom, gain, shift, 0, MIX)
    v = (z2[...] - mean) * (scale * g) + b
    a_out[...] = (v * sigmoid(v) * spread(m[...], MIX)).astype(bf16)
    a2 = a_out[...].reshape(rows, MIX)
    zc = dot(a2[:, :C_MID], wc[...]).reshape(cols, slab, C_IN)
    fc = dot(a2[:, C_MID:], big[...]).reshape(cols, slab, WIDE_FAST)
    here = cols * jnp.sum(m[...], axis=0, keepdims=True)

    @pl.when(h == 0)
    def _():
        base[:, :C_IN] = rows_sum(zc * spread(m[...], C_IN)) / spread(here, C_IN)
        base[:, C_IN:] = block_sum(rows_sum(fc * spread(m[...], WIDE_FAST))) / (4.0 * here)
        one[...] = jnp.zeros_like(one)
        two[...] = jnp.zeros_like(two)

    off = (zc - base[:, :C_IN]) * spread(m[...], C_IN)
    one[:, :C_IN] += rows_sum(off)
    two[:, :C_IN] += rows_sum(off * off)
    off = (fc - jnp.tile(base[:, C_IN:], (1, ALPHA))) * spread(m[...], WIDE_FAST)
    one[:, C_IN:] += block_sum(rows_sum(off)) * 0.25
    two[:, C_IN:] += block_sum(rows_sum(off * off)) * 0.25

    @pl.when(h == pl.num_programs(0) - 1)
    def _():
        count = pl.num_programs(0) * here
        finish_moments(st, base[...], one[...], two[...], count, ((0, C_IN + C_FAST, 0),))


def outputs(a2, zp, base, mom1, mom3, sgain, sshift, fgain, fshift, cot, fcot, fast_in, m, perm, wc, wfc,
            so, fo, gs, gf, sums, big):
    h = pl.program_id(0)
    cols, slab, _ = a2.shape

    @pl.when(h == 0)
    def _():
        expand_matrix(wfc, big)
        sums[...] = jnp.zeros_like(sums)

    mask = spread(m[...], C_IN)
    mean_c = mom3[0:1, :C_IN]
    scale_c = lax.rsqrt(mom3[1:2, :C_IN] + eps_norm)
    mean_p = mom1[0:1, MIX:] - base[...]
    scale_p = lax.rsqrt(mom1[1:2, MIX:] + eps_norm)
    mean_f = jnp.tile(mom3[0:1, C_IN:], (1, ALPHA))
    scale_f = jnp.tile(lax.rsqrt(mom3[1:2, C_IN:] + eps_norm), (1, ALPHA))
    gain_c, gain_p = sgain[:, :C_IN], sgain[:, C_IN:]
    shift_cp = sshift[:, :C_IN] + sshift[:, C_IN:]
    gain_f = jnp.tile(fgain[...], (1, ALPHA))
    shift_f = jnp.tile(fshift[...], (1, ALPHA))

    def tile_sum(v):
        return jnp.sum(v.reshape(slab // 8, 8, v.shape[-1]), axis=0)

    totals = [jnp.zeros((8, C_IN), f32)] * 3 + [jnp.zeros((8, WIDE_FAST), f32)] * 2
    for w in range(cols):
        zc = (dot(a2[w, :, :C_MID], wc[...]) - mean_c) * scale_c
        zq = (zp[w].astype(f32) - mean_p) * scale_p
        ps = gain_c * zc + gain_p * zq + shift_cp
        sig = sigmoid(ps)
        so[:, w] = (ps * sig * mask).astype(bf16).reshape(slab // cot.shape[2], cot.shape[2], C_IN)
        back = cot[:, w].reshape(slab, C_IN).astype(f32) * (sig * (1.0 + ps * (1.0 - sig)) * mask)
        gs[w] = back
        totals[0] += tile_sum(back)
        totals[1] += tile_sum(back * zc)
        totals[2] += tile_sum(back * zq)
        fc = (dot(a2[w, :, C_MID:], big[...]) - mean_f) * scale_f
        pf = gain_f * fc + shift_f + fast_in[w].astype(f32)
        sig = sigmoid(pf)
        res = (pf * sig).astype(bf16)
        stacked = jnp.concatenate([res[:, p * C_FAST : (p + 1) * C_FAST] for p in range(ALPHA)], axis=0)
        fo[:, w] = dot_tn(perm[...], stacked).astype(bf16).reshape(fo.shape[0], slab, C_FAST)
        phases = dot(perm[...], fcot[:, w].reshape(ALPHA * slab, C_FAST))
        wide = jnp.concatenate([phases[p * slab : (p + 1) * slab] for p in range(ALPHA)], axis=1)
        fback = wide * (sig * (1.0 + pf * (1.0 - sig)))
        gf[w] = fback
        totals[3] += tile_sum(fback)
        totals[4] += tile_sum(fback * fc)
    for k in range(3):
        sums[:, k * C_IN : (k + 1) * C_IN] += jnp.sum(totals[k], axis=0, keepdims=True)
    for k in range(2):
        at = 3 * C_IN + k * C_FAST
        sums[:, at : at + C_FAST] += block_sum(jnp.sum(totals[3 + k], axis=0, keepdims=True))


def expand_back(gs, gf, a2, zp, base, z2, mom1, mom2, mom3, tot, inv, sgain, fgain, gain2, shift2, m, wc, wfc,
                dzc_out, dzp_out, dfc_out, q_out, sums, big):
    h = pl.program_id(0)
    cols, slab, _ = a2.shape
    rows = cols * slab

    @pl.when(h == 0)
    def _():
        expand_matrix(wfc, big)
        sums[...] = jnp.zeros_like(sums)

    mask = spread(m[...], C_IN)
    inv_s = spread(inv[...], C_IN)
    inv_f = 0.25 * inv[...]
    mean_c = mom3[0:1, :C_IN]
    scale_c = lax.rsqrt(mom3[1:2, :C_IN] + eps_norm)
    mean_p = mom1[0:1, MIX:] - base[...]
    scale_p = lax.rsqrt(mom1[1:2, MIX:] + eps_norm)
    mean_f = jnp.tile(mom3[0:1, C_IN:], (1, ALPHA))
    scale_f = jnp.tile(lax.rsqrt(mom3[1:2, C_IN:] + eps_norm), (1, ALPHA))
    mult_c = sgain[:, :C_IN] * scale_c
    mult_p = sgain[:, C_IN:] * scale_p
    mult_f = jnp.tile(fgain[...], (1, ALPHA)) * scale_f
    first_s = tot[:, :C_IN] * inv_s
    second_c = tot[:, C_IN : 2 * C_IN] * inv_s
    second_p = tot[:, 2 * C_IN : 3 * C_IN] * inv_s
    first_f = jnp.tile(tot[:, 3 * C_IN : 3 * C_IN + C_FAST] * inv_f, (1, ALPHA))
    second_f = jnp.tile(tot[:, 3 * C_IN + C_FAST :] * inv_f, (1, ALPHA))
    mask_f = spread(m[...], WIDE_FAST)
    for w in range(cols):
        zc = (dot(a2[w, :, :C_MID], wc[...]) - mean_c) * scale_c
        zq = (zp[w].astype(f32) - mean_p) * scale_p
        g = gs[w].astype(f32)
        dzc_out[w] = (mult_c * (g - mask * (first_s + zc * second_c))).astype(bf16)
        dzp_out[w] = (mult_p * (g - mask * (first_s + zq * second_p))).astype(bf16)
        fc = (dot(a2[w, :, C_MID:], big[...]) - mean_f) * scale_f
        dfc_out[w] = (mult_f * (gf[w].astype(f32) - mask_f * (first_f + fc * second_f))).astype(bf16)
    da = dot_nt(dzc_out[...].reshape(rows, C_IN), wc[...]).reshape(cols, slab, C_MID)
    df = dot_nt(dfc_out[...].reshape(rows, WIDE_FAST), big[...]).reshape(cols, slab, 128)
    grads = jnp.concatenate([da, df], axis=2)
    slope_back(grads, z2[...], mom2, gain2, shift2, m, q_out, sums)


def slope_back(grads, z, mom, gain, shift, m, q_out, sums):
    mean, scale, g, b = affine(mom, gain, shift, 0, MIX)
    zhat = (z - mean) * scale
    v = g * zhat + b
    sig = sigmoid(v)
    q = grads * (sig * (1.0 + v * (1.0 - sig)) * spread(m[...], MIX))
    q_out[...] = q
    for k, s in enumerate((rows_sum(q), rows_sum(q * zhat))):
        at = k * MIX
        sums[:, at : at + C_MID] += s[:, :C_MID]
        sums[:, at + C_MID : at + MIX] += phase_sum(s[:, C_MID:])


def expand_weights(x, a2, dzp, dzc, dfc, wp_out, wc_out, wfc_out):
    i = pl.program_id(0)
    n, slab, _ = x.shape
    rows = n * slab
    wp_out[...] = dot_tn(x[...].reshape(rows, C_MID), dzp[...].reshape(rows, C_IN))

    @pl.when(i == pl.num_programs(0) - 1)
    def _():
        a = a2[...].reshape(rows, MIX)
        wc_out[...] = dot_tn(a[:, :C_MID], dzc[...].reshape(rows, C_IN))
        wide = dot_tn(a[:, C_MID:], dfc[...].reshape(rows, WIDE_FAST))
        wfc_out[...] = sum(
            wide[p * C_FMID : (p + 1) * C_FMID, p * C_FAST : (p + 1) * C_FAST] for p in range(ALPHA)
        )


def norm_terms(mom, gain, tot, inv):
    mean = mom[0:1, :MIX]
    scale = lax.rsqrt(mom[1:2, :MIX] + eps_norm)
    share = jnp.concatenate([spread(inv[...], C_MID), 0.25 * inv[...]], axis=1)
    return mean, scale, gain[...] * scale, tot[:, :MIX] * share, tot[:, MIX:] * share


def space_back(place, q2, z2, qrow, qcol, qcorner, zrow, zcol, zcorner, a1, z1, mom1, mom2, tot, inv, gain1, shift1,
               gain2, m, wb, wfb, q_out, sums, wb_out, wfb_out, wide, keep, keep_f):
    ha, wa = place[0], place[1]
    high, cols, slab, _ = z1.shape
    rows = cols * slab
    mean, scale, mult, first, second = norm_terms(mom2, gain2, tot, inv)
    mask = spread(m[...], MIX)

    def grad(q, z):
        return (mult * (q - mask * (first + (z - mean) * scale * second))).astype(bf16)

    far = high + 1
    wide[far * ha] = jnp.zeros((cols + 2, slab, MIX), bf16)
    wide[:, far * wa] = jnp.zeros((high + 2, slab, MIX), bf16)
    wide[far * (1 - ha), 1 : 1 + cols] = grad(qrow[...], zrow[...])
    wide[1 : 1 + high, far * (1 - wa)] = grad(qcol[...], zcol[...])
    wide[far * (1 - ha), far * (1 - wa)] = grad(qcorner[...], zcorner[...])

    def fill(h, carry):
        wide[h + 1, 1 : 1 + cols] = grad(q2[h], z2[h])
        return carry

    lax.fori_loop(0, high, fill, 0)
    sums[...] = jnp.zeros_like(sums)
    keep[...] = jnp.zeros_like(keep)
    keep_f[...] = jnp.zeros_like(keep_f)

    def line(h, carry):
        slow = jnp.zeros((rows, C_MID), f32)
        fast = jnp.zeros((rows, 128), f32)
        for i in range(3):
            for j in range(3):
                v = wide[h + 2 - i, 2 - j : 2 - j + cols].reshape(rows, MIX)
                slow = slow + dot_nt(v[:, :C_MID], wb[i, j])
                fast = fast + dot_nt(v[:, C_MID:], wfb[3 * i + j])
        grads = jnp.concatenate([slow, fast], axis=1).reshape(cols, slab, MIX)
        slope_back(grads, z1[h], mom1, gain1, shift1, m, q_out.at[h], sums)
        d = wide[h + 1, 1 : 1 + cols].reshape(rows, MIX)
        for i in range(3):
            for j in range(3):
                v = a1[h + i, j : j + cols].reshape(rows, MIX)
                keep[i, j] += dot_tn(v[:, :C_MID], d[:, :C_MID])
                keep_f[3 * i + j] += dot_tn(v[:, C_MID:], d[:, C_MID:])
        return carry

    lax.fori_loop(0, high, line, 0)
    wb_out[...] = keep[...]
    for k in range(9):
        wfb_out[k] = sum(
            keep_f[k, p * C_FMID : (p + 1) * C_FMID, p * C_FMID : (p + 1) * C_FMID] for p in range(ALPHA)
        )


def first_back(clips, q1, z1, mom1, tot, inv, gain1, m, perm, dzp, gf, wl, wa, wp, wfa, sx, fx, da_out, dl_out, df_out,
               taps, ends):
    h = pl.program_id(0)
    cols, slab, _ = q1.shape
    rows = cols * slab

    @pl.when(h == 0)
    def _():
        frames_matrix(wfa, taps, ends)

    mean, scale, mult, first, second = norm_terms(mom1, gain1, tot, inv)
    zhat = (z1[...] - mean) * scale
    dz = mult * (q1[...] - spread(m[...], MIX) * (first + zhat * second))
    up, down = sooner(dz, clips), later(dz, clips)
    for k, v in enumerate((up, dz, down)):
        da_out[:, :, k * C_MID : (k + 1) * C_MID] = v[:, :, :C_MID].astype(bf16)
        df_out[:, :, k * 128 : (k + 1) * 128] = v[:, :, C_MID:].astype(bf16)
    dj = dot_nt(dzp[...].reshape(rows, C_IN), wp[...])
    for k in range(3):
        dj = dj + dot_nt(da_out[:, :, k * C_MID : (k + 1) * C_MID].reshape(rows, C_MID), wa[k])
    mask = spread(m[...], C_IN)
    dj = dj.reshape(cols, slab, C_JOIN)
    for w in range(cols):
        sx[:, w] = (dj[w, :, :C_IN] * mask).astype(bf16).reshape(slab // clips, clips, C_IN)
    dlat = dj[:, :, C_IN:].astype(bf16).astype(f32)
    dl_out[:, :, :C_LAT] = dlat.astype(bf16)
    dl_out[:, :, C_LAT:] = sooner(dlat, clips).astype(bf16)
    df = df_out[...].reshape(rows, 3 * 128)
    dl = dl_out[...].reshape(rows, 2 * C_LAT)
    total = gf[...].reshape(rows, WIDE_FAST).astype(f32) + dot(df[:, 128:256], taps[...])
    head = dot_nt(dl[:, :C_LAT], wl[2:5].reshape(3 * C_FAST, C_LAT))
    tail = dot_nt(dl[:, C_LAT:], wl[0:2].reshape(2 * C_FAST, C_LAT))
    blocks = [total[:, p * C_FAST : (p + 1) * C_FAST] for p in range(ALPHA)]
    for p in range(3):
        blocks[p] = blocks[p] + head[:, p * C_FAST : (p + 1) * C_FAST]
    for p in range(2):
        blocks[2 + p] = blocks[2 + p] + tail[:, p * C_FAST : (p + 1) * C_FAST]
    blocks[3] = blocks[3] + dot(df[:, :128], ends[0])
    blocks[0] = blocks[0] + dot(df[:, 256:], ends[1])
    blocks = [v.astype(bf16) for v in blocks]
    for w in range(cols):
        stacked = jnp.concatenate([v[w * slab : (w + 1) * slab] for v in blocks], axis=0)
        fx[:, w] = dot_tn(perm[...], stacked).astype(bf16).reshape(clips, slab, C_FAST)


def first_weights(x, f, da, dl, df, wa_out, wl_out, wfa_out):
    i = pl.program_id(0)
    n, slab, _ = x.shape
    rows = n * slab
    for k in range(3):
        wa_out[k] = dot_tn(x[...].reshape(rows, C_MID), da[:, :, k * C_MID : (k + 1) * C_MID].reshape(rows, C_MID))

    @pl.when(i == pl.num_programs(0) - 1)
    def _():
        fast = f[...].reshape(rows, WIDE_FAST)
        d = dl[...].reshape(rows, 2 * C_LAT)
        wl_out[2:5] = dot_tn(fast[:, : 3 * C_FAST], d[:, :C_LAT]).reshape(3, C_FAST, C_LAT)
        wl_out[0:2] = dot_tn(fast[:, 2 * C_FAST :], d[:, C_LAT:]).reshape(2, C_FAST, C_LAT)
        g = df[...].reshape(rows, 3 * 128)
        mid = dot_tn(g[:, 128:256], fast)
        sums = [jnp.zeros((C_FMID, C_FAST), f32) for _ in range(3)]
        for p in range(ALPHA):
            for s in range(max(p - 1, 0), min(p + 2, ALPHA)):
                sums[s - p + 1] += mid[p * C_FMID : (p + 1) * C_FMID, s * C_FAST : (s + 1) * C_FAST]
        sums[0] += dot_tn(g[:, :128], fast[:, 3 * C_FAST :])[:C_FMID]
        sums[2] += dot_tn(g[:, 256:], fast[:, :C_FAST])[3 * C_FMID :]
        for k in range(3):
            wfa_out[k] = sums[k]


def exchange(n_clip, moments, edges, *refs):
    refs = list(refs)
    part, weight = refs.pop(0), refs.pop(0)
    source = refs.pop(0) if edges else None
    out = refs.pop(0)
    rims = [refs.pop(0) for _ in range(3)] if edges else None
    near, mid, far, near_send, near_recv, far_send, far_recv = refs[:7]
    refs = refs[7:]
    clip, ha, wa = lax.axis_index("clip"), lax.axis_index("ha"), lax.axis_index("wa")
    me = 2 * ha + wa
    peers = [(1 - ha, wa), (ha, 1 - wa), (1 - ha, 1 - wa)]
    if edges:
        line, side, packs, lands, local_sem, rim_send, rim_recv = refs
        high, cols = source.shape[0], source.shape[1]
        first = pltpu.make_async_copy(source.at[(high - 1) * (1 - ha)], line, local_sem.at[0])
        second = pltpu.make_async_copy(source.at[:, (cols - 1) * (1 - wa)], side, local_sem.at[1])
        first.start()
        second.start()
    barrier = pltpu.get_barrier_semaphore()
    for a, b in peers:
        pl.semaphore_signal(barrier, inc=1, device_id=(clip, a, b), device_id_type=MESH)
    for d in range(1, n_clip):
        other = lax.rem(clip + d, n_clip)
        pl.semaphore_signal(barrier, inc=1, device_id=(other, ha, wa), device_id_type=MESH)
    pl.semaphore_wait(barrier, 3 + n_clip - 1)
    copies = []
    for k, (a, b) in enumerate(peers):
        copy = pltpu.make_async_remote_copy(
            src_ref=part, dst_ref=near.at[me], send_sem=near_send.at[k], recv_sem=near_recv.at[me],
            device_id=(clip, a, b), device_id_type=MESH,
        )
        copy.start()
        copies.append(copy)
    if edges:
        first.wait()
        second.wait()
        centre = part[0:1, :MIX] if moments else jnp.zeros((1, MIX), f32)
        packs[0, : cols] = (line[...] - centre).astype(bf16)
        packs[1, : high] = (side[...] - centre).astype(bf16)
        packs[2, 0] = packs[0, (cols - 1) * (1 - wa)]
        for k, (a, b) in enumerate(peers):
            size = 1 if k == 2 else cols
            copy = pltpu.make_async_remote_copy(
                src_ref=packs.at[k, pl.ds(0, size)], dst_ref=lands.at[k, pl.ds(0, size)],
                send_sem=rim_send.at[k], recv_sem=rim_recv.at[k], device_id=(clip, a, b), device_id_type=MESH,
            )
            copy.start()
            copies.append(copy)
    near[me] = part[...]
    for a, b in peers:
        other = 2 * a + b
        pltpu.make_async_remote_copy(
            src_ref=part, dst_ref=near.at[other], send_sem=near_send.at[0], recv_sem=near_recv.at[other],
            device_id=(clip, a, b), device_id_type=MESH,
        ).wait_recv()
    if moments:
        mean = (near[0, 0:1] + near[1, 0:1] + near[2, 0:1] + near[3, 0:1]) * 0.25
        var = sum(near[k, 1:2] + (near[k, 0:1] - mean) ** 2 for k in range(4)) * 0.25
        mid[0:1] = mean
        mid[1:2] = var
    else:
        mid[...] = near[0] + near[1] + near[2] + near[3]
    for d in range(1, n_clip):
        other = lax.rem(clip + d, n_clip)
        copy = pltpu.make_async_remote_copy(
            src_ref=mid, dst_ref=far.at[clip], send_sem=far_send.at[d], recv_sem=far_recv.at[clip],
            device_id=(other, ha, wa), device_id_type=MESH,
        )
        copy.start()
        copies.append(copy)
    far[clip] = mid[...]
    for d in range(1, n_clip):
        other = lax.rem(clip + d, n_clip)
        pltpu.make_async_remote_copy(
            src_ref=mid, dst_ref=far.at[other], send_sem=far_send.at[0], recv_sem=far_recv.at[other],
            device_id=(other, ha, wa), device_id_type=MESH,
        ).wait_recv()
    width = out.shape[1]
    if moments:
        mean = sum(far[k, 0:1] * spread(weight[k], width) for k in range(n_clip))
        var = sum((far[k, 1:2] + (far[k, 0:1] - mean) ** 2) * spread(weight[k], width) for k in range(n_clip))
        out[0:1] = mean
        out[1:2] = var
    else:
        out[...] = sum(far[k] for k in range(n_clip))
    if edges:
        for k, (a, b) in enumerate(peers):
            size = 1 if k == 2 else cols
            pltpu.make_async_remote_copy(
                src_ref=packs.at[k, pl.ds(0, size)], dst_ref=lands.at[k, pl.ds(0, size)],
                send_sem=rim_send.at[k], recv_sem=rim_recv.at[k], device_id=(clip, a, b), device_id_type=MESH,
            ).wait_recv()
            centre = near[2 * a + b, 0:1, :MIX] if moments else jnp.zeros((1, MIX), f32)
            land = lands[k, 0].astype(f32) if k == 2 else lands[k, 0:cols].astype(f32)
            rims[k][...] = land + centre
    for copy in copies:
        copy.wait_send()


def vmem_spec():
    return pl.BlockSpec(memory_space=pltpu.VMEM)


def run_exchange(ident, n_clip, part, weight, moments, source=None):
    edges = source is not None
    count, width = part.shape
    out_shape = [jax.ShapeDtypeStruct((count, width), f32)]
    ins = [part, weight]
    in_specs = [vmem_spec(), vmem_spec()]
    scratch = [
        pltpu.VMEM((4, count, width), f32),
        pltpu.VMEM((count, width), f32),
        pltpu.VMEM((n_clip, count, width), f32),
        pltpu.SemaphoreType.DMA((3,)),
        pltpu.SemaphoreType.DMA((4,)),
        pltpu.SemaphoreType.DMA((n_clip,)),
        pltpu.SemaphoreType.DMA((n_clip,)),
    ]
    if edges:
        high, cols, slab, _ = source.shape
        ins.append(source)
        in_specs.append(pl.BlockSpec(memory_space=pl.ANY))
        out_shape += [
            jax.ShapeDtypeStruct((cols, slab, MIX), f32),
            jax.ShapeDtypeStruct((high, slab, MIX), f32),
            jax.ShapeDtypeStruct((slab, MIX), f32),
        ]
        scratch += [
            pltpu.VMEM((cols, slab, MIX), f32),
            pltpu.VMEM((high, slab, MIX), f32),
            pltpu.VMEM((3, cols, slab, MIX), bf16),
            pltpu.VMEM((3, cols, slab, MIX), bf16),
            pltpu.SemaphoreType.DMA((2,)),
            pltpu.SemaphoreType.DMA((3,)),
            pltpu.SemaphoreType.DMA((3,)),
        ]
    return pl.pallas_call(
        functools.partial(exchange, n_clip, moments, edges),
        out_shape=tuple(out_shape),
        in_specs=in_specs,
        out_specs=tuple(vmem_spec() for _ in out_shape),
        scratch_shapes=scratch,
        compiler_params=pltpu.CompilerParams(
            collective_id=ident, has_side_effects=True, vmem_limit_bytes=16 * MIB
        ),
        name=f"exchange{ident}",
    )(*ins)


def whole(shape):
    return pl.BlockSpec(shape, lambda h: (0,) * len(shape))


def per_line(shape):
    return pl.BlockSpec((None,) + tuple(shape), lambda h: (h,) + (0,) * len(shape))


def params(limit):
    return pltpu.CompilerParams(vmem_limit_bytes=limit * MIB)


def shaped(shape, kind):
    return jax.ShapeDtypeStruct(shape, kind)


def on_device(
    slow_input,
    fast_input,
    frame_counts,
    lateral_weight,
    slow_a_weight,
    slow_b_weight,
    slow_c_weight,
    slow_proj_weight,
    fast_a_weight,
    fast_b_weight,
    fast_c_weight,
    slow_gain,
    slow_shift,
    fast_gain,
    fast_shift,
    slow_cotangent,
    fast_cotangent,
):
    n_clip = lax.axis_size("clip")
    clips, frames, high, cols, _ = slow_input.shape
    slab = clips * frames
    own = lax.dynamic_slice_in_dim(frame_counts, lax.axis_index("clip") * clips, clips)
    row_t = jnp.arange(slab) // clips
    row_c = jnp.arange(slab) % clips
    real = row_t < own[row_c]
    m = jnp.broadcast_to(real.astype(f32)[:, None], (slab, 128))
    col_c = jnp.arange(ALPHA * slab) // (ALPHA * frames)
    col_f = jnp.arange(ALPHA * slab) % (ALPHA * frames)
    want_f = (ALPHA * row_t[None, :] + jnp.arange(ALPHA)[:, None]).reshape(-1)
    want_c = jnp.tile(row_c, ALPHA)
    perm = (
        (want_f[:, None] == col_f[None, :]) & (want_c[:, None] == col_c[None, :]) & jnp.tile(real, ALPHA)[:, None]
    ).astype(bf16)
    real_total = jnp.sum(frame_counts).astype(f32)
    weight = jnp.broadcast_to(
        (jnp.sum(frame_counts.reshape(n_clip, clips), axis=1).astype(f32) / real_total)[:, None, None], (n_clip, 1, 128)
    )
    inv = jnp.full((1, 128), 1.0, f32) / (real_total * (H * W))
    place = jnp.stack([lax.axis_index("ha"), lax.axis_index("wa")]).astype(jnp.int32)

    def mixed(slow, fast, k):
        lo = fast[k * C_FMID : (k + 1) * C_FMID]
        return jnp.concatenate([slow[k * C_MID : (k + 1) * C_MID], jnp.tile(lo, ALPHA)])[None]

    gain1, shift1 = mixed(slow_gain, fast_gain, 0), mixed(slow_shift, fast_shift, 0)
    gain2, shift2 = mixed(slow_gain, fast_gain, 1), mixed(slow_shift, fast_shift, 1)
    sgain, sshift = slow_gain[None, 2 * C_MID :], slow_shift[None, 2 * C_MID :]
    fgain, fshift = fast_gain[None, 2 * C_FMID :], fast_shift[None, 2 * C_FMID :]
    wfa = fast_a_weight.transpose(0, 2, 1)
    eye = jnp.eye(ALPHA, dtype=bf16)
    wfb = (eye[None, :, None, :, None] * fast_b_weight.reshape(9, 1, C_FMID, 1, C_FMID)).reshape(9, 128, 128)

    xs = slow_input.transpose(1, 2, 3, 0, 4)
    xf = fast_input.transpose(0, 2, 3, 1, 4)
    cot = slow_cotangent.transpose(1, 2, 3, 0, 4)
    fcot = fast_cotangent.transpose(0, 2, 3, 1, 4)
    slow_block = pl.BlockSpec((frames, None, cols, clips, C_IN), lambda h: (0, h, 0, 0, 0))
    fast_block = pl.BlockSpec((clips, None, cols, ALPHA * frames, C_FAST), lambda h: (0, h, 0, 0, 0))

    def lines(c, kind):
        return shaped((high, cols, slab, c), kind)

    m_spec = whole((slab, 128))
    perm_spec = whole((ALPHA * slab, ALPHA * slab))
    L1 = MIX + C_IN
    x, f, z1, zp, st1, base = pl.pallas_call(
        functools.partial(first_convs, clips),
        grid=(high,),
        in_specs=[
            slow_block, fast_block, m_spec, perm_spec, whole((5, C_FAST, C_LAT)), whole((3, C_JOIN, C_MID)),
            whole((C_JOIN, C_IN)), whole((3, C_FMID, C_FAST)),
        ],
        out_specs=(
            per_line((cols, slab, C_JOIN)), per_line((cols, slab, WIDE_FAST)), per_line((cols, slab, MIX)),
            per_line((cols, slab, C_IN)), whole((2, L1)), whole((1, C_IN)),
        ),
        out_shape=(
            lines(C_JOIN, bf16), lines(WIDE_FAST, bf16), lines(MIX, f32), lines(C_IN, bf16), shaped((2, L1), f32),
            shaped((1, C_IN), f32),
        ),
        scratch_shapes=[
            pltpu.VMEM((128, WIDE_FAST), bf16), pltpu.VMEM((2, 128, C_FAST), bf16), pltpu.VMEM((1, L1), f32),
            pltpu.VMEM((1, L1), f32), pltpu.VMEM((1, L1), f32),
        ],
        compiler_params=params(40),
        name="first_convs",
    )(xs, xf, m, perm, lateral_weight, slow_a_weight, slow_proj_weight, wfa)

    mom1, row1, col1, corner1 = run_exchange(1, n_clip, st1, weight, True, z1)
    smem = pl.BlockSpec(memory_space=pltpu.SMEM)
    vm = vmem_spec()
    a1, z2, st2 = pl.pallas_call(
        space_convs,
        in_specs=[smem] + [vm] * 10,
        out_specs=(vm, vm, vm),
        out_shape=(
            shaped((high + 2, cols + 2, slab, MIX), bf16), lines(MIX, f32), shaped((2, MIX), f32),
        ),
        scratch_shapes=[pltpu.VMEM((1, MIX), f32), pltpu.VMEM((1, MIX), f32)],
        compiler_params=params(32),
        name="space_convs",
    )(place, z1, row1, col1, corner1, mom1, gain1, shift1, m, slow_b_weight, wfb)
    mom2, zrow, zcol, zcorner = run_exchange(2, n_clip, st2, weight, True, z2)

    L3 = C_IN + C_FAST
    a2, st3 = pl.pallas_call(
        expand_moments,
        grid=(high,),
        in_specs=[
            per_line((cols, slab, MIX)), whole((2, MIX)), whole((1, MIX)), whole((1, MIX)), m_spec, whole((C_MID, C_IN)),
            whole((C_FMID, C_FAST)),
        ],
        out_specs=(per_line((cols, slab, MIX)), whole((2, L3))),
        out_shape=(lines(MIX, bf16), shaped((2, L3), f32)),
        scratch_shapes=[pltpu.VMEM((128, WIDE_FAST), bf16)] + [pltpu.VMEM((1, L3), f32)] * 3,
        compiler_params=params(24),
        name="expand_moments",
    )(z2, mom2, gain2, shift2, m, slow_c_weight, fast_c_weight)
    (mom3,) = run_exchange(3, n_clip, st3, weight, True)

    L4 = 3 * C_IN + 2 * C_FAST
    so, fo, gs, gf, part4 = pl.pallas_call(
        outputs,
        grid=(high,),
        in_specs=[
            per_line((cols, slab, MIX)), per_line((cols, slab, C_IN)), whole((1, C_IN)), whole((2, L1)), whole((2, L3)),
            whole((1, 2 * C_IN)), whole((1, 2 * C_IN)), whole((1, C_FAST)), whole((1, C_FAST)), slow_block, fast_block,
            per_line((cols, slab, WIDE_FAST)), m_spec, perm_spec, whole((C_MID, C_IN)), whole((C_FMID, C_FAST)),
        ],
        out_specs=(
            slow_block, fast_block, per_line((cols, slab, C_IN)), per_line((cols, slab, WIDE_FAST)), whole((1, L4)),
        ),
        out_shape=(
            shaped(xs.shape, bf16), shaped(xf.shape, bf16), lines(C_IN, f32), lines(WIDE_FAST, f32),
            shaped((1, L4), f32),
        ),
        scratch_shapes=[pltpu.VMEM((128, WIDE_FAST), bf16)],
        compiler_params=params(32),
        name="outputs",
    )(a2, zp, base, mom1, mom3, sgain, sshift, fgain, fshift, cot, fcot, f, m, perm, slow_c_weight, fast_c_weight)
    (tot4,) = run_exchange(4, n_clip, part4, weight, False)

    dzc, dzp, dfc, q2, part5 = pl.pallas_call(
        expand_back,
        grid=(high,),
        in_specs=[
            per_line((cols, slab, C_IN)), per_line((cols, slab, WIDE_FAST)), per_line((cols, slab, MIX)),
            per_line((cols, slab, C_IN)), whole((1, C_IN)), per_line((cols, slab, MIX)), whole((2, L1)), whole((2, MIX)),
            whole((2, L3)), whole((1, L4)), whole((1, 128)), whole((1, 2 * C_IN)), whole((1, C_FAST)), whole((1, MIX)),
            whole((1, MIX)), m_spec, whole((C_MID, C_IN)), whole((C_FMID, C_FAST)),
        ],
        out_specs=(
            per_line((cols, slab, C_IN)), per_line((cols, slab, C_IN)), per_line((cols, slab, WIDE_FAST)),
            per_line((cols, slab, MIX)), whole((1, 2 * MIX)),
        ),
        out_shape=(
            lines(C_IN, bf16), lines(C_IN, bf16), lines(WIDE_FAST, bf16), lines(MIX, f32), shaped((1, 2 * MIX), f32),
        ),
        scratch_shapes=[pltpu.VMEM((128, WIDE_FAST), bf16)],
        compiler_params=params(32),
        name="expand_back",
    )(gs, gf, a2, zp, base, z2, mom1, mom2, mom3, tot4, inv, sgain, fgain, gain2, shift2, m, slow_c_weight, fast_c_weight)
    tot5, qrow, qcol, qcorner = run_exchange(5, n_clip, part5, weight, False, q2)

    n = high * cols

    def flat(v):
        return v.reshape((n,) + v.shape[2:])

    dwp, dwc, dwfc = pl.pallas_call(
        expand_weights,
        grid=(C_JOIN // C_MID,),
        in_specs=[
            pl.BlockSpec((n, slab, C_MID), lambda i: (0, 0, i)), whole((n, slab, MIX)), whole((n, slab, C_IN)),
            whole((n, slab, C_IN)), whole((n, slab, WIDE_FAST)),
        ],
        out_specs=(
            pl.BlockSpec((C_MID, C_IN), lambda i: (i, 0)), whole((C_MID, C_IN)), whole((C_FMID, C_FAST)),
        ),
        out_shape=(shaped((C_JOIN, C_IN), f32), shaped((C_MID, C_IN), f32), shaped((C_FMID, C_FAST), f32)),
        compiler_params=params(56),
        name="expand_weights",
    )(flat(x), flat(a2), flat(dzp), flat(dzc), flat(dfc))

    q1, part6, dwb, dwfb = pl.pallas_call(
        space_back,
        in_specs=[smem] + [vm] * 20,
        out_specs=(vm, vm, vm, vm),
        out_shape=(
            lines(MIX, f32), shaped((1, 2 * MIX), f32), shaped((3, 3, C_MID, C_MID), f32),
            shaped((9, C_FMID, C_FMID), f32),
        ),
        scratch_shapes=[
            pltpu.VMEM((high + 2, cols + 2, slab, MIX), bf16), pltpu.VMEM((3, 3, C_MID, C_MID), f32),
            pltpu.VMEM((9, 128, 128), f32),
        ],
        compiler_params=params(48),
        name="space_back",
    )(
        place, q2, z2, qrow, qcol, qcorner, zrow, zcol, zcorner, a1, z1, mom1, mom2, tot5, inv, gain1, shift1, gain2, m,
        slow_b_weight, wfb,
    )
    (tot6,) = run_exchange(6, n_clip, part6, weight, False)

    sx, fx, da, dl, df = pl.pallas_call(
        functools.partial(first_back, clips),
        grid=(high,),
        in_specs=[
            per_line((cols, slab, MIX)), per_line((cols, slab, MIX)), whole((2, L1)), whole((1, 2 * MIX)),
            whole((1, 128)), whole((1, MIX)), m_spec, perm_spec, per_line((cols, slab, C_IN)),
            per_line((cols, slab, WIDE_FAST)), whole((5, C_FAST, C_LAT)), whole((3, C_JOIN, C_MID)),
            whole((C_JOIN, C_IN)), whole((3, C_FMID, C_FAST)),
        ],
        out_specs=(
            slow_block, fast_block, per_line((cols, slab, 3 * C_MID)), per_line((cols, slab, 2 * C_LAT)),
            per_line((cols, slab, 3 * 128)),
        ),
        out_shape=(
            shaped(xs.shape, bf16), shaped(xf.shape, bf16), lines(3 * C_MID, bf16), lines(2 * C_LAT, bf16),
            lines(3 * 128, bf16),
        ),
        scratch_shapes=[pltpu.VMEM((128, WIDE_FAST), bf16), pltpu.VMEM((2, 128, C_FAST), bf16)],
        compiler_params=params(40),
        name="first_back",
    )(q1, z1, mom1, tot6, inv, gain1, m, perm, dzp, gf, lateral_weight, slow_a_weight, slow_proj_weight, wfa)

    dwa, dwl, dwfa = pl.pallas_call(
        first_weights,
        grid=(C_JOIN // C_MID,),
        in_specs=[
            pl.BlockSpec((n, slab, C_MID), lambda i: (0, 0, i)), whole((n, slab, WIDE_FAST)),
            whole((n, slab, 3 * C_MID)), whole((n, slab, 2 * C_LAT)), whole((n, slab, 3 * 128)),
        ],
        out_specs=(
            pl.BlockSpec((3, C_MID, C_MID), lambda i: (0, i, 0)), whole((5, C_FAST, C_LAT)), whole((3, C_FMID, C_FAST)),
        ),
        out_shape=(
            shaped((3, C_JOIN, C_MID), f32), shaped((5, C_FAST, C_LAT), f32), shaped((3, C_FMID, C_FAST), f32),
        ),
        compiler_params=params(48),
        name="first_weights",
    )(flat(x), flat(f), flat(da), flat(dl), flat(df))

    axes = ("clip", "ha", "wa")
    dwp, dwc, dwb, dwa, dwl = [
        v.astype(f32) for v in lax.psum(tuple(v.astype(bf16) for v in (dwp, dwc, dwb, dwa, dwl)), axes)
    ]
    dwfc, dwfb, dwfa = lax.psum((dwfc, dwfb, dwfa), axes)

    def joined_sums(k):
        first = [tot6[0, k * MIX : (k + 1) * MIX], tot5[0, k * MIX : (k + 1) * MIX]]
        last = tot4[0, :C_IN] if k == 0 else tot4[0, C_IN : 2 * C_IN]
        proj = tot4[0, :C_IN] if k == 0 else tot4[0, 2 * C_IN : 3 * C_IN]
        at = 3 * C_IN + k * C_FAST
        slow = jnp.concatenate([first[0][:C_MID], first[1][:C_MID], last, proj])
        lo = C_MID + C_FMID
        fast = jnp.concatenate([first[0][C_MID:lo], first[1][C_MID:lo], tot4[0, at : at + C_FAST]])
        return slow, fast

    slow_shift_grad, fast_shift_grad = joined_sums(0)
    slow_gain_grad, fast_gain_grad = joined_sums(1)
    return (
        so.transpose(3, 0, 1, 2, 4),
        fo.transpose(0, 3, 1, 2, 4),
        sx.transpose(3, 0, 1, 2, 4),
        fx.transpose(0, 3, 1, 2, 4),
        dwl,
        dwa,
        dwb,
        dwc,
        dwp,
        dwfa.transpose(0, 2, 1),
        dwfb.reshape(3, 3, C_FMID, C_FMID),
        dwfc,
        slow_gain_grad,
        slow_shift_grad,
        fast_gain_grad,
        fast_shift_grad,
    )


def solution(mesh):
    tiles = P("clip", None, "ha", "wa", None)
    return jax.shard_map(
        on_device,
        mesh=mesh,
        in_specs=(tiles, tiles) + (P(),) * 13 + (tiles, tiles),
        out_specs=(tiles,) * 4 + (P(),) * 12,
        check_vma=False,
    )
```

```python
import functools

import jax
import jax.numpy as jnp
from jax import lax
from jax.experimental import pallas as pl
from jax.experimental.pallas import tpu as pltpu
from jax.sharding import PartitionSpec as P

ALPHA = 4
H = 14
W = 14
C_IN = 1024
C_LAT = 256
C_MID = 256
C_FAST = 128
C_FMID = 32
C_JOIN = C_IN + C_LAT
MIX = C_MID + ALPHA * C_FMID
WIDE_FAST = ALPHA * C_FAST

eps_norm = 1e-05
f32 = jnp.float32
bf16 = jnp.bfloat16
MESH = pl.DeviceIdType.MESH
MIB = 1 << 20


def dot(a, b):
    return lax.dot_general(a, b, (((1,), (0,)), ((), ())), preferred_element_type=f32)


def dot_nt(a, b):
    return lax.dot_general(a, b, (((1,), (1,)), ((), ())), preferred_element_type=f32)


def dot_tn(a, b):
    return lax.dot_general(a, b, (((0,), (0,)), ((), ())), preferred_element_type=f32)


def sigmoid(v):
    return 0.5 + 0.5 * jnp.tanh(0.5 * v)


def later(y, clips):
    return jnp.concatenate([jnp.zeros_like(y[:, :clips]), y[:, : y.shape[1] - clips]], axis=1)


def sooner(y, clips):
    return jnp.concatenate([y[:, clips:], jnp.zeros_like(y[:, :clips])], axis=1)


def rows_sum(v):
    return jnp.sum(jnp.sum(v, axis=0), axis=0, keepdims=True)


def phase_sum(v):
    out = v
    for k in range(1, ALPHA):
        out = out + pltpu.roll(v, k * C_FMID, 1)
    return out


def block_sum(v):
    return sum(v[:, p * C_FAST : (p + 1) * C_FAST] for p in range(ALPHA))


def spread(mask, width):
    return jnp.tile(mask, (1, width // 128))


def frames_matrix(wfa_ref, out_ref, ends_ref):
    out_ref[...] = jnp.zeros_like(out_ref)
    ends_ref[...] = jnp.zeros_like(ends_ref)
    for p in range(ALPHA):
        for s in range(max(p - 1, 0), min(p + 2, ALPHA)):
            out_ref[p * C_FMID : (p + 1) * C_FMID, s * C_FAST : (s + 1) * C_FAST] = wfa_ref[s - p + 1]
    ends_ref[0, 0:C_FMID] = wfa_ref[0]
    ends_ref[1, 3 * C_FMID :] = wfa_ref[2]


def expand_matrix(wfc_ref, out_ref):
    out_ref[...] = jnp.zeros_like(out_ref)
    for p in range(ALPHA):
        out_ref[p * C_FMID : (p + 1) * C_FMID, p * C_FAST : (p + 1) * C_FAST] = wfc_ref[...]


def first_convs(clips, xs, xf, m, perm, wl, wa, wp, wfa, x_out, f_out, z_out, zp_out, st, base_out,
                taps, ends, base, one, two):
    h = pl.program_id(0)
    cols = xs.shape[1]
    slab = m.shape[0]
    rows = cols * slab

    @pl.when(h == 0)
    def _():
        frames_matrix(wfa, taps, ends)

    mask_in = spread(m[...], C_IN).astype(bf16)
    for w in range(cols):
        x_out[w, :, :C_IN] = xs[:, w].reshape(slab, C_IN) * mask_in
        phases = dot(perm[...], xf[:, w].reshape(ALPHA * slab, C_FAST)).astype(bf16)
        for p in range(ALPHA):
            f_out[w, :, p * C_FAST : (p + 1) * C_FAST] = phases[p * slab : (p + 1) * slab]
    fast = f_out[...].reshape(rows, WIDE_FAST)
    lat = dot(fast[:, : 3 * C_FAST], wl[2:5].reshape(3 * C_FAST, C_LAT)).reshape(cols, slab, C_LAT)
    back = dot(fast[:, 2 * C_FAST :], wl[0:2].reshape(2 * C_FAST, C_LAT)).reshape(cols, slab, C_LAT)
    x_out[:, :, C_IN:] = (lat + later(back, clips)).astype(bf16)
    joined = x_out[...].reshape(rows, C_JOIN)
    za = dot(joined, wa[1]).reshape(cols, slab, C_MID)
    za = za + later(dot(joined, wa[0]).reshape(cols, slab, C_MID), clips)
    za = za + sooner(dot(joined, wa[2]).reshape(cols, slab, C_MID), clips)
    fa = dot_nt(fast, taps[...]).reshape(cols, slab, 128)
    fa = fa + later(dot_nt(fast[:, 3 * C_FAST :], ends[0]).reshape(cols, slab, 128), clips)
    fa = fa + sooner(dot_nt(fast[:, :C_FAST], ends[1]).reshape(cols, slab, 128), clips)
    zp = dot(joined, wp[...]).reshape(cols, slab, C_IN)
    z_out[:, :, :C_MID] = za
    z_out[:, :, C_MID:] = fa
    parts = ((0, za), (C_MID, fa), (MIX, zp))
    here = cols * jnp.sum(m[...], axis=0, keepdims=True)

    @pl.when(h == 0)
    def _():
        for at, z in parts:
            width = z.shape[-1]
            mean = rows_sum(z * spread(m[...], width)) / spread(here, width)
            if at == C_MID:
                mean = phase_sum(mean) * 0.25
            base[:, at : at + width] = mean
        one[...] = jnp.zeros_like(one)
        two[...] = jnp.zeros_like(two)

    for at, z in parts:
        width = z.shape[-1]
        off = z - base[:, at : at + width]
        if at == MIX:
            zp_out[...] = off.astype(bf16)
        off = off * spread(m[...], width)
        one[:, at : at + width] += rows_sum(off)
        two[:, at : at + width] += rows_sum(off * off)

    @pl.when(h == pl.num_programs(0) - 1)
    def _():
        count = pl.num_programs(0) * here
        base_out[...] = base[:, MIX:]
        finish_moments(st, base[...], one[...], two[...], count, ((0, C_MID, 0), (C_MID, 128, 1), (MIX, C_IN, 0)))


def finish_moments(st, base, one, two, count, parts):
    for at, width, fast in parts:
        s1 = one[:, at : at + width]
        s2 = two[:, at : at + width]
        if fast:
            s1 = phase_sum(s1) * 0.25
            s2 = phase_sum(s2) * 0.25
        n = spread(count.astype(f32), width)
        s1 = s1 / n
        st[0:1, at : at + width] = base[:, at : at + width] + s1
        st[1:2, at : at + width] = s2 / n - s1 * s1


def affine(moments, gain, shift, at, width):
    mean = moments[0:1, at : at + width]
    scale = lax.rsqrt(moments[1:2, at : at + width] + eps_norm)
    return mean, scale, gain[...], shift[...]


def space_convs(place, z1, row, col, corner, mom, gain, shift, m, wb, wfb, a_out, z_out, st, one, two):
    ha, wa = place[0], place[1]
    high, cols, slab, _ = z1.shape
    rows = cols * slab
    mean, scale, g, b = affine(mom, gain, shift, 0, MIX)
    mult = scale * g
    mask = spread(m[...], MIX)

    def act(z):
        v = (z - mean) * mult + b
        return (v * sigmoid(v) * mask).astype(bf16)

    far = high + 1
    a_out[far * ha] = jnp.zeros((cols + 2, slab, MIX), bf16)
    a_out[:, far * wa] = jnp.zeros((high + 2, slab, MIX), bf16)
    a_out[far * (1 - ha), 1 : 1 + cols] = act(row[...])
    a_out[1 : 1 + high, far * (1 - wa)] = act(col[...])
    a_out[far * (1 - ha), far * (1 - wa)] = act(corner[...])

    def fill(h, carry):
        a_out[h + 1, 1 : 1 + cols] = act(z1[h])
        return carry

    lax.fori_loop(0, high, fill, 0)

    def line(h, carry):
        slow = jnp.zeros((rows, C_MID), f32)
        fast = jnp.zeros((rows, 128), f32)
        for i in range(3):
            for j in range(3):
                v = a_out[h + i, j : j + cols].reshape(rows, MIX)
                slow = slow + dot(v[:, :C_MID], wb[i, j])
                fast = fast + dot(v[:, C_MID:], wfb[3 * i + j])
        z_out[h, :, :, :C_MID] = slow.reshape(cols, slab, C_MID)
        z_out[h, :, :, C_MID:] = fast.reshape(cols, slab, 128)
        return carry

    lax.fori_loop(0, high, line, 0)
    here = cols * jnp.sum(m[...], axis=0, keepdims=True)
    base = rows_sum(z_out[0] * mask) / spread(here, MIX)
    base = jnp.concatenate([base[:, :C_MID], phase_sum(base[:, C_MID:]) * 0.25], axis=1)
    one[...] = jnp.zeros_like(one)
    two[...] = jnp.zeros_like(two)

    def gather(h, carry):
        off = (z_out[h] - base) * mask
        one[...] += rows_sum(off)
        two[...] += rows_sum(off * off)
        return carry

    lax.fori_loop(0, high, gather, 0)
    finish_moments(st, base, one[...], two[...], high * here, ((0, C_MID, 0), (C_MID, 128, 1)))


def expand_moments(z2, mom, gain, shift, m, wc, wfc, a_out, st, big, base, one, two):
    h = pl.program_id(0)
    cols, slab, _ = z2.shape
    rows = cols * slab

    @pl.when(h == 0)
    def _():
        expand_matrix(wfc, big)

    mean, scale, g, b = affine(mom, gain, shift, 0, MIX)
    v = (z2[...] - mean) * (scale * g) + b
    a_out[...] = (v * sigmoid(v) * spread(m[...], MIX)).astype(bf16)
    a2 = a_out[...].reshape(rows, MIX)
    zc = dot(a2[:, :C_MID], wc[...]).reshape(cols, slab, C_IN)
    fc = dot(a2[:, C_MID:], big[...]).reshape(cols, slab, WIDE_FAST)
    here = cols * jnp.sum(m[...], axis=0, keepdims=True)

    @pl.when(h == 0)
    def _():
        base[:, :C_IN] = rows_sum(zc * spread(m[...], C_IN)) / spread(here, C_IN)
        base[:, C_IN:] = block_sum(rows_sum(fc * spread(m[...], WIDE_FAST))) / (4.0 * here)
        one[...] = jnp.zeros_like(one)
        two[...] = jnp.zeros_like(two)

    off = (zc - base[:, :C_IN]) * spread(m[...], C_IN)
    one[:, :C_IN] += rows_sum(off)
    two[:, :C_IN] += rows_sum(off * off)
    off = (fc - jnp.tile(base[:, C_IN:], (1, ALPHA))) * spread(m[...], WIDE_FAST)
    one[:, C_IN:] += block_sum(rows_sum(off)) * 0.25
    two[:, C_IN:] += block_sum(rows_sum(off * off)) * 0.25

    @pl.when(h == pl.num_programs(0) - 1)
    def _():
        count = pl.num_programs(0) * here
        finish_moments(st, base[...], one[...], two[...], count, ((0, C_IN + C_FAST, 0),))


def outputs(a2, zp, base, mom1, mom3, sgain, sshift, fgain, fshift, cot, fcot, fast_in, m, perm, wc, wfc,
            so, fo, gs, gf, sums, big):
    h = pl.program_id(0)
    cols, slab, _ = a2.shape

    @pl.when(h == 0)
    def _():
        expand_matrix(wfc, big)
        sums[...] = jnp.zeros_like(sums)

    mask = spread(m[...], C_IN)
    mean_c = mom3[0:1, :C_IN]
    scale_c = lax.rsqrt(mom3[1:2, :C_IN] + eps_norm)
    mean_p = mom1[0:1, MIX:] - base[...]
    scale_p = lax.rsqrt(mom1[1:2, MIX:] + eps_norm)
    mean_f = jnp.tile(mom3[0:1, C_IN:], (1, ALPHA))
    scale_f = jnp.tile(lax.rsqrt(mom3[1:2, C_IN:] + eps_norm), (1, ALPHA))
    gain_c, gain_p = sgain[:, :C_IN], sgain[:, C_IN:]
    shift_cp = sshift[:, :C_IN] + sshift[:, C_IN:]
    gain_f = jnp.tile(fgain[...], (1, ALPHA))
    shift_f = jnp.tile(fshift[...], (1, ALPHA))

    def tile_sum(v):
        return jnp.sum(v.reshape(slab // 8, 8, v.shape[-1]), axis=0)

    totals = [jnp.zeros((8, C_IN), f32)] * 3 + [jnp.zeros((8, WIDE_FAST), f32)] * 2
    for w in range(cols):
        zc = (dot(a2[w, :, :C_MID], wc[...]) - mean_c) * scale_c
        zq = (zp[w].astype(f32) - mean_p) * scale_p
        ps = gain_c * zc + gain_p * zq + shift_cp
        sig = sigmoid(ps)
        so[:, w] = (ps * sig * mask).astype(bf16).reshape(slab // cot.shape[2], cot.shape[2], C_IN)
        back = cot[:, w].reshape(slab, C_IN).astype(f32) * (sig * (1.0 + ps * (1.0 - sig)) * mask)
        gs[w] = back
        totals[0] += tile_sum(back)
        totals[1] += tile_sum(back * zc)
        totals[2] += tile_sum(back * zq)
        fc = (dot(a2[w, :, C_MID:], big[...]) - mean_f) * scale_f
        pf = gain_f * fc + shift_f + fast_in[w].astype(f32)
        sig = sigmoid(pf)
        res = (pf * sig).astype(bf16)
        stacked = jnp.concatenate([res[:, p * C_FAST : (p + 1) * C_FAST] for p in range(ALPHA)], axis=0)
        fo[:, w] = dot_tn(perm[...], stacked).astype(bf16).reshape(fo.shape[0], slab, C_FAST)
        phases = dot(perm[...], fcot[:, w].reshape(ALPHA * slab, C_FAST))
        wide = jnp.concatenate([phases[p * slab : (p + 1) * slab] for p in range(ALPHA)], axis=1)
        fback = wide * (sig * (1.0 + pf * (1.0 - sig)))
        gf[w] = fback
        totals[3] += tile_sum(fback)
        totals[4] += tile_sum(fback * fc)
    for k in range(3):
        sums[:, k * C_IN : (k + 1) * C_IN] += jnp.sum(totals[k], axis=0, keepdims=True)
    for k in range(2):
        at = 3 * C_IN + k * C_FAST
        sums[:, at : at + C_FAST] += block_sum(jnp.sum(totals[3 + k], axis=0, keepdims=True))


def expand_back(gs, gf, a2, zp, base, z2, mom1, mom2, mom3, tot, inv, sgain, fgain, gain2, shift2, m, wc, wfc,
                dzc_out, dzp_out, dfc_out, q_out, sums, big):
    h = pl.program_id(0)
    cols, slab, _ = a2.shape
    rows = cols * slab

    @pl.when(h == 0)
    def _():
        expand_matrix(wfc, big)
        sums[...] = jnp.zeros_like(sums)

    mask = spread(m[...], C_IN)
    inv_s = spread(inv[...], C_IN)
    inv_f = 0.25 * inv[...]
    mean_c = mom3[0:1, :C_IN]
    scale_c = lax.rsqrt(mom3[1:2, :C_IN] + eps_norm)
    mean_p = mom1[0:1, MIX:] - base[...]
    scale_p = lax.rsqrt(mom1[1:2, MIX:] + eps_norm)
    mean_f = jnp.tile(mom3[0:1, C_IN:], (1, ALPHA))
    scale_f = jnp.tile(lax.rsqrt(mom3[1:2, C_IN:] + eps_norm), (1, ALPHA))
    mult_c = sgain[:, :C_IN] * scale_c
    mult_p = sgain[:, C_IN:] * scale_p
    mult_f = jnp.tile(fgain[...], (1, ALPHA)) * scale_f
    first_s = tot[:, :C_IN] * inv_s
    second_c = tot[:, C_IN : 2 * C_IN] * inv_s
    second_p = tot[:, 2 * C_IN : 3 * C_IN] * inv_s
    first_f = jnp.tile(tot[:, 3 * C_IN : 3 * C_IN + C_FAST] * inv_f, (1, ALPHA))
    second_f = jnp.tile(tot[:, 3 * C_IN + C_FAST :] * inv_f, (1, ALPHA))
    mask_f = spread(m[...], WIDE_FAST)
    for w in range(cols):
        zc = (dot(a2[w, :, :C_MID], wc[...]) - mean_c) * scale_c
        zq = (zp[w].astype(f32) - mean_p) * scale_p
        g = gs[w].astype(f32)
        dzc_out[w] = (mult_c * (g - mask * (first_s + zc * second_c))).astype(bf16)
        dzp_out[w] = (mult_p * (g - mask * (first_s + zq * second_p))).astype(bf16)
        fc = (dot(a2[w, :, C_MID:], big[...]) - mean_f) * scale_f
        dfc_out[w] = (mult_f * (gf[w].astype(f32) - mask_f * (first_f + fc * second_f))).astype(bf16)
    da = dot_nt(dzc_out[...].reshape(rows, C_IN), wc[...]).reshape(cols, slab, C_MID)
    df = dot_nt(dfc_out[...].reshape(rows, WIDE_FAST), big[...]).reshape(cols, slab, 128)
    grads = jnp.concatenate([da, df], axis=2)
    slope_back(grads, z2[...], mom2, gain2, shift2, m, q_out, sums)


def slope_back(grads, z, mom, gain, shift, m, q_out, sums):
    mean, scale, g, b = affine(mom, gain, shift, 0, MIX)
    zhat = (z - mean) * scale
    v = g * zhat + b
    sig = sigmoid(v)
    q = grads * (sig * (1.0 + v * (1.0 - sig)) * spread(m[...], MIX))
    q_out[...] = q
    for k, s in enumerate((rows_sum(q), rows_sum(q * zhat))):
        at = k * MIX
        sums[:, at : at + C_MID] += s[:, :C_MID]
        sums[:, at + C_MID : at + MIX] += phase_sum(s[:, C_MID:])


def expand_weights(x, a2, dzp, dzc, dfc, wp_out, wc_out, wfc_out):
    i = pl.program_id(0)
    n, slab, _ = x.shape
    rows = n * slab
    wp_out[...] = dot_tn(x[...].reshape(rows, C_MID), dzp[...].reshape(rows, C_IN)).astype(bf16)

    @pl.when(i == pl.num_programs(0) - 1)
    def _():
        a = a2[...].reshape(rows, MIX)
        wc_out[...] = dot_tn(a[:, :C_MID], dzc[...].reshape(rows, C_IN)).astype(bf16)
        wide = dot_tn(a[:, C_MID:], dfc[...].reshape(rows, WIDE_FAST))
        wfc_out[...] = sum(
            wide[p * C_FMID : (p + 1) * C_FMID, p * C_FAST : (p + 1) * C_FAST] for p in range(ALPHA)
        )


def norm_terms(mom, gain, tot, inv):
    mean = mom[0:1, :MIX]
    scale = lax.rsqrt(mom[1:2, :MIX] + eps_norm)
    share = jnp.concatenate([spread(inv[...], C_MID), 0.25 * inv[...]], axis=1)
    return mean, scale, gain[...] * scale, tot[:, :MIX] * share, tot[:, MIX:] * share


def space_back(place, q2, z2, qrow, qcol, qcorner, zrow, zcol, zcorner, a1, z1, mom1, mom2, tot, inv, gain1, shift1,
               gain2, m, wb, wfb, q_out, sums, wb_out, wfb_out, wide, keep, keep_f):
    ha, wa = place[0], place[1]
    high, cols, slab, _ = z1.shape
    rows = cols * slab
    mean, scale, mult, first, second = norm_terms(mom2, gain2, tot, inv)
    mask = spread(m[...], MIX)

    def grad(q, z):
        return (mult * (q - mask * (first + (z - mean) * scale * second))).astype(bf16)

    far = high + 1
    wide[far * ha] = jnp.zeros((cols + 2, slab, MIX), bf16)
    wide[:, far * wa] = jnp.zeros((high + 2, slab, MIX), bf16)
    wide[far * (1 - ha), 1 : 1 + cols] = grad(qrow[...], zrow[...])
    wide[1 : 1 + high, far * (1 - wa)] = grad(qcol[...], zcol[...])
    wide[far * (1 - ha), far * (1 - wa)] = grad(qcorner[...], zcorner[...])

    def fill(h, carry):
        wide[h + 1, 1 : 1 + cols] = grad(q2[h], z2[h])
        return carry

    lax.fori_loop(0, high, fill, 0)
    sums[...] = jnp.zeros_like(sums)
    keep[...] = jnp.zeros_like(keep)
    keep_f[...] = jnp.zeros_like(keep_f)

    def line(h, carry):
        slow = jnp.zeros((rows, C_MID), f32)
        fast = jnp.zeros((rows, 128), f32)
        for i in range(3):
            for j in range(3):
                v = wide[h + 2 - i, 2 - j : 2 - j + cols].reshape(rows, MIX)
                slow = slow + dot_nt(v[:, :C_MID], wb[i, j])
                fast = fast + dot_nt(v[:, C_MID:], wfb[3 * i + j])
        grads = jnp.concatenate([slow, fast], axis=1).reshape(cols, slab, MIX)
        slope_back(grads, z1[h], mom1, gain1, shift1, m, q_out.at[h], sums)
        d = wide[h + 1, 1 : 1 + cols].reshape(rows, MIX)
        for i in range(3):
            for j in range(3):
                v = a1[h + i, j : j + cols].reshape(rows, MIX)
                keep[i, j] += dot_tn(v[:, :C_MID], d[:, :C_MID])
                keep_f[3 * i + j] += dot_tn(v[:, C_MID:], d[:, C_MID:])
        return carry

    lax.fori_loop(0, high, line, 0)
    wb_out[...] = keep[...].astype(bf16)
    for k in range(9):
        wfb_out[k] = sum(
            keep_f[k, p * C_FMID : (p + 1) * C_FMID, p * C_FMID : (p + 1) * C_FMID] for p in range(ALPHA)
        )


def first_back(clips, q1, z1, mom1, tot, inv, gain1, m, perm, dzp, gf, wl, wa, wp, wfa, sx, fx, da_out, dl_out, df_out,
               taps, ends):
    h = pl.program_id(0)
    cols, slab, _ = q1.shape
    rows = cols * slab

    @pl.when(h == 0)
    def _():
        frames_matrix(wfa, taps, ends)

    mean, scale, mult, first, second = norm_terms(mom1, gain1, tot, inv)
    zhat = (z1[...] - mean) * scale
    dz = mult * (q1[...] - spread(m[...], MIX) * (first + zhat * second))
    up, down = sooner(dz, clips), later(dz, clips)
    for k, v in enumerate((up, dz, down)):
        da_out[:, :, k * C_MID : (k + 1) * C_MID] = v[:, :, :C_MID].astype(bf16)
        df_out[:, :, k * 128 : (k + 1) * 128] = v[:, :, C_MID:].astype(bf16)
    dj = dot_nt(dzp[...].reshape(rows, C_IN), wp[...])
    for k in range(3):
        dj = dj + dot_nt(da_out[:, :, k * C_MID : (k + 1) * C_MID].reshape(rows, C_MID), wa[k])
    mask = spread(m[...], C_IN)
    dj = dj.reshape(cols, slab, C_JOIN)
    for w in range(cols):
        sx[:, w] = (dj[w, :, :C_IN] * mask).astype(bf16).reshape(slab // clips, clips, C_IN)
    dlat = dj[:, :, C_IN:].astype(bf16).astype(f32)
    dl_out[:, :, :C_LAT] = dlat.astype(bf16)
    dl_out[:, :, C_LAT:] = sooner(dlat, clips).astype(bf16)
    df = df_out[...].reshape(rows, 3 * 128)
    dl = dl_out[...].reshape(rows, 2 * C_LAT)
    total = gf[...].reshape(rows, WIDE_FAST).astype(f32) + dot(df[:, 128:256], taps[...])
    head = dot_nt(dl[:, :C_LAT], wl[2:5].reshape(3 * C_FAST, C_LAT))
    tail = dot_nt(dl[:, C_LAT:], wl[0:2].reshape(2 * C_FAST, C_LAT))
    blocks = [total[:, p * C_FAST : (p + 1) * C_FAST] for p in range(ALPHA)]
    for p in range(3):
        blocks[p] = blocks[p] + head[:, p * C_FAST : (p + 1) * C_FAST]
    for p in range(2):
        blocks[2 + p] = blocks[2 + p] + tail[:, p * C_FAST : (p + 1) * C_FAST]
    blocks[3] = blocks[3] + dot(df[:, :128], ends[0])
    blocks[0] = blocks[0] + dot(df[:, 256:], ends[1])
    blocks = [v.astype(bf16) for v in blocks]
    for w in range(cols):
        stacked = jnp.concatenate([v[w * slab : (w + 1) * slab] for v in blocks], axis=0)
        fx[:, w] = dot_tn(perm[...], stacked).astype(bf16).reshape(clips, slab, C_FAST)


def first_weights(x, f, da, dl, df, dwfc, dwfb, wa_out, wl_out, small_out):
    i = pl.program_id(0)
    n, slab, _ = x.shape
    rows = n * slab
    for k in range(3):
        wa_out[k] = dot_tn(x[...].reshape(rows, C_MID), da[:, :, k * C_MID : (k + 1) * C_MID].reshape(rows, C_MID)).astype(bf16)

    @pl.when(i == pl.num_programs(0) - 1)
    def _():
        fast = f[...].reshape(rows, WIDE_FAST)
        d = dl[...].reshape(rows, 2 * C_LAT)
        wl_out[2:5] = dot_tn(fast[:, : 3 * C_FAST], d[:, :C_LAT]).reshape(3, C_FAST, C_LAT).astype(bf16)
        wl_out[0:2] = dot_tn(fast[:, 2 * C_FAST :], d[:, C_LAT:]).reshape(2, C_FAST, C_LAT).astype(bf16)
        g = df[...].reshape(rows, 3 * 128)
        mid = dot_tn(g[:, 128:256], fast)
        sums = [jnp.zeros((C_FMID, C_FAST), f32) for _ in range(3)]
        for p in range(ALPHA):
            for s in range(max(p - 1, 0), min(p + 2, ALPHA)):
                sums[s - p + 1] += mid[p * C_FMID : (p + 1) * C_FMID, s * C_FAST : (s + 1) * C_FAST]
        sums[0] += dot_tn(g[:, :128], fast[:, 3 * C_FAST :])[:C_FMID]
        sums[2] += dot_tn(g[:, 256:], fast[:, :C_FAST])[3 * C_FMID :]
        small_out[...] = jnp.zeros_like(small_out)
        for k in range(3):
            small_out[k * C_FMID : (k + 1) * C_FMID] = sums[k].astype(bf16)
        small_out[3 * C_FMID : 4 * C_FMID] = dwfc[...].astype(bf16)
        for k in range(9):
            at = (4 + k) * C_FMID
            small_out[at : at + C_FMID, :C_FMID] = dwfb[k].astype(bf16)


def exchange(n_clip, moments, edges, *refs):
    refs = list(refs)
    part, weight = refs.pop(0), refs.pop(0)
    source = refs.pop(0) if edges else None
    out = refs.pop(0)
    rims = [refs.pop(0) for _ in range(3)] if edges else None
    near, mid, far, near_send, near_recv, far_send, far_recv = refs[:7]
    refs = refs[7:]
    clip, ha, wa = lax.axis_index("clip"), lax.axis_index("ha"), lax.axis_index("wa")
    me = 2 * ha + wa
    peers = [(1 - ha, wa), (ha, 1 - wa), (1 - ha, 1 - wa)]
    if edges:
        line, side, packs, lands, local_sem, rim_send, rim_recv = refs
        high, cols = source.shape[0], source.shape[1]
        first = pltpu.make_async_copy(source.at[(high - 1) * (1 - ha)], line, local_sem.at[0])
        second = pltpu.make_async_copy(source.at[:, (cols - 1) * (1 - wa)], side, local_sem.at[1])
        first.start()
        second.start()
    barrier = pltpu.get_barrier_semaphore()
    for a, b in peers:
        pl.semaphore_signal(barrier, inc=1, device_id=(clip, a, b), device_id_type=MESH)
    for d in range(1, n_clip):
        other = lax.rem(clip + d, n_clip)
        pl.semaphore_signal(barrier, inc=1, device_id=(other, ha, wa), device_id_type=MESH)
    pl.semaphore_wait(barrier, 3 + n_clip - 1)
    copies = []
    for k, (a, b) in enumerate(peers):
        copy = pltpu.make_async_remote_copy(
            src_ref=part, dst_ref=near.at[me], send_sem=near_send.at[k], recv_sem=near_recv.at[me],
            device_id=(clip, a, b), device_id_type=MESH,
        )
        copy.start()
        copies.append(copy)
    if edges:
        first.wait()
        second.wait()
        centre = part[0:1, :MIX] if moments else jnp.zeros((1, MIX), f32)
        packs[0, : cols] = (line[...] - centre).astype(bf16)
        packs[1, : high] = (side[...] - centre).astype(bf16)
        packs[2, 0] = packs[0, (cols - 1) * (1 - wa)]
        for k, (a, b) in enumerate(peers):
            size = 1 if k == 2 else cols
            copy = pltpu.make_async_remote_copy(
                src_ref=packs.at[k, pl.ds(0, size)], dst_ref=lands.at[k, pl.ds(0, size)],
                send_sem=rim_send.at[k], recv_sem=rim_recv.at[k], device_id=(clip, a, b), device_id_type=MESH,
            )
            copy.start()
            copies.append(copy)
    near[me] = part[...]
    for a, b in peers:
        other = 2 * a + b
        pltpu.make_async_remote_copy(
            src_ref=part, dst_ref=near.at[other], send_sem=near_send.at[0], recv_sem=near_recv.at[other],
            device_id=(clip, a, b), device_id_type=MESH,
        ).wait_recv()
    if moments:
        mean = (near[0, 0:1] + near[1, 0:1] + near[2, 0:1] + near[3, 0:1]) * 0.25
        var = sum(near[k, 1:2] + (near[k, 0:1] - mean) ** 2 for k in range(4)) * 0.25
        mid[0:1] = mean
        mid[1:2] = var
    else:
        mid[...] = near[0] + near[1] + near[2] + near[3]
    for d in range(1, n_clip):
        other = lax.rem(clip + d, n_clip)
        copy = pltpu.make_async_remote_copy(
            src_ref=mid, dst_ref=far.at[clip], send_sem=far_send.at[d], recv_sem=far_recv.at[clip],
            device_id=(other, ha, wa), device_id_type=MESH,
        )
        copy.start()
        copies.append(copy)
    far[clip] = mid[...]
    for d in range(1, n_clip):
        other = lax.rem(clip + d, n_clip)
        pltpu.make_async_remote_copy(
            src_ref=mid, dst_ref=far.at[other], send_sem=far_send.at[0], recv_sem=far_recv.at[other],
            device_id=(other, ha, wa), device_id_type=MESH,
        ).wait_recv()
    width = out.shape[1]
    if moments:
        mean = sum(far[k, 0:1] * spread(weight[k], width) for k in range(n_clip))
        var = sum((far[k, 1:2] + (far[k, 0:1] - mean) ** 2) * spread(weight[k], width) for k in range(n_clip))
        out[0:1] = mean
        out[1:2] = var
    else:
        out[...] = sum(far[k] for k in range(n_clip))
    if edges:
        for k, (a, b) in enumerate(peers):
            size = 1 if k == 2 else cols
            pltpu.make_async_remote_copy(
                src_ref=packs.at[k, pl.ds(0, size)], dst_ref=lands.at[k, pl.ds(0, size)],
                send_sem=rim_send.at[k], recv_sem=rim_recv.at[k], device_id=(clip, a, b), device_id_type=MESH,
            ).wait_recv()
            centre = near[2 * a + b, 0:1, :MIX] if moments else jnp.zeros((1, MIX), f32)
            land = lands[k, 0].astype(f32) if k == 2 else lands[k, 0:cols].astype(f32)
            rims[k][...] = land + centre
    for copy in copies:
        copy.wait_send()


UNIT = 512


def bit_of(axis, power):
    return lax.rem(lax.axis_index(axis) // (1 << power), 2)


def partner_of(axis, power, bit):
    where = {name: lax.axis_index(name) for name in ("clip", "ha", "wa")}
    where[axis] = where[axis] + (1 - 2 * bit) * (1 << power)
    return (where["clip"], where["ha"], where["wa"])


def stage_orders(n_clip, sets):
    rest = [("wa", 0)] + [("clip", b) for b in range(n_clip.bit_length() - 1)]
    turn, last = rest[:3], rest[3:]
    return [[("ha", 0)] + turn[s % len(turn) :] + turn[: s % len(turn)] + last for s in range(sets)]


def chunk_of(rows):
    best = 16
    for k in range(16, min(rows, 256) + 1, 16):
        if rows % k == 0:
            best = k
    return best


def land_plan(n_clip, sizes):
    stages = len(stage_orders(n_clip, 1)[0])
    starts, total = [], 0
    for size in sizes:
        starts.append(total)
        for _ in range(stages):
            size = size // 2 if size % 32 == 0 else size
            total += size
    return starts, total


def reduce_sets(n_clip, starts, sizes, mine, land, done, rs_send, rs_recv, ag_send, ag_recv):
    orders = stage_orders(n_clip, len(starts))
    stages = len(orders[0])
    low = [jnp.int32(v) for v in starts]
    size = list(sizes)
    at = land_plan(n_clip, sizes)[0]
    trail = [[] for _ in starts]
    sent = []

    def rows(ref, begin, count):
        return ref.at[pl.ds(pl.multiple_of(begin, 16), count)]

    def send(s, k):
        axis, power = orders[s][k]
        bit = bit_of(axis, power)
        halve = size[s] % 32 == 0
        count = size[s] // 2 if halve else size[s]
        begin = low[s] + (1 - bit) * count if halve else low[s]
        copy = pltpu.make_async_remote_copy(
            src_ref=rows(mine, begin, count), dst_ref=rows(land, at[s], count),
            send_sem=rs_send.at[s, k], recv_sem=rs_recv.at[s, k],
            device_id=partner_of(axis, power, bit), device_id_type=MESH,
        )
        copy.start()
        trail[s].append((copy, low[s], count, halve, axis, power, bit, at[s]))
        if halve:
            low[s] = low[s] + bit * count
            size[s] = count
        at[s] += count

    def gather(s, k):
        copy, _, count, halve, axis, power, bit, begin = trail[s][k]
        copy.wait_recv()
        if not halve:
            copy.wait_send()
        step = chunk_of(count)

        def add(i, carry):
            own = pl.ds(pl.multiple_of(low[s] + i * step, 16), step)
            came = pl.ds(pl.multiple_of(begin + i * step, 16), step)
            mine[own, :] = (mine[own, :].astype(f32) + land[came, :].astype(f32)).astype(bf16)
            return carry

        lax.fori_loop(0, count // step, add, 0)
        if halve:
            sent.append(copy)

    for s in range(len(starts)):
        send(s, 0)
    for k in range(stages):
        for s in range(len(starts)):
            gather(s, k)
            if k + 1 < stages:
                send(s, k + 1)
    for copy in sent:
        copy.wait_send()

    for s in range(len(starts)):
        step = chunk_of(size[s])

        def keep(i, carry):
            own = pl.ds(pl.multiple_of(low[s] + i * step, 16), step)
            done[own, :] = mine[own, :]
            return carry

        lax.fori_loop(0, size[s] // step, keep, 0)

    copies = []
    pending = [None] * len(starts)

    def spread_out(s, k):
        _, before, count, halve, axis, power, bit, _ = trail[s][k]
        if not halve:
            return
        copy = pltpu.make_async_remote_copy(
            src_ref=rows(done, low[s], count), dst_ref=rows(done, low[s], count),
            send_sem=ag_send.at[s, k], recv_sem=ag_recv.at[s, k],
            device_id=partner_of(axis, power, bit), device_id_type=MESH,
        )
        copy.start()
        other = before + (1 - bit) * count
        pending[s] = pltpu.make_async_remote_copy(
            src_ref=rows(done, other, count), dst_ref=rows(done, other, count),
            send_sem=ag_send.at[s, k], recv_sem=ag_recv.at[s, k],
            device_id=partner_of(axis, power, bit), device_id_type=MESH,
        )
        low[s] = before
        copies.append(copy)

    for s in range(len(starts)):
        spread_out(s, stages - 1)
    for k in range(stages - 1, -1, -1):
        for s in range(len(starts)):
            if pending[s] is not None:
                pending[s].wait_recv()
                pending[s] = None
            if k > 0:
                spread_out(s, k - 1)
    for copy in copies:
        copy.wait_send()


def greet(n_clip):
    barrier = pltpu.get_barrier_semaphore()
    stages = stage_orders(n_clip, 1)[0]
    for axis, power in stages:
        bit = bit_of(axis, power)
        pl.semaphore_signal(barrier, inc=1, device_id=partner_of(axis, power, bit), device_id_type=MESH)
    pl.semaphore_wait(barrier, len(stages))


def weight_pieces(dws_rows):
    pieces = []
    row = 0
    for which, count in ((0, C_JOIN), (1, C_MID)):
        for b in range(C_IN // 256):
            pieces.append((row, count, which, (slice(None), slice(b * 256, (b + 1) * 256))))
            row += count
    for i in range(3):
        for j in range(3):
            pieces.append((row, C_MID, 2, (i, j)))
            row += C_MID
    for k in range(3):
        pieces.append((row, C_JOIN, 3, (k,)))
        row += C_JOIN
    for k in range(5):
        pieces.append((row, C_FAST, 4, (k,)))
        row += C_FAST
    return pieces, row


def reduce_weights(n_clip, starts, sizes, dwp, dwc, dwb, dwa, dwl, dws, done,
                   mine, land, rs_send, rs_recv, ag_send, ag_recv):
    sources = (dwp, dwc, dwb, dwa, dwl)
    pieces, row = weight_pieces(dws.shape[0])
    for begin, count, which, at in pieces:
        mine[begin : begin + count, :] = sources[which].at[at][...]
    half = dws.shape[0] // 2
    mine[row : row + half, :128] = dws[:half]
    mine[row : row + half, 128:] = dws[half:]
    end = row + half
    if end < mine.shape[0]:
        mine[end:, :] = jnp.zeros((mine.shape[0] - end, 256), bf16)
    greet(n_clip)
    reduce_sets(n_clip, starts, sizes, mine, land, done, rs_send, rs_recv, ag_send, ag_recv)


def unpack_weights(done, wp_out, wc_out, wb_out, wa_out, wl_out, ws_out):
    targets = (wp_out, wc_out, wb_out, wa_out, wl_out)
    pieces, row = weight_pieces(ws_out.shape[0])
    for begin, count, which, at in pieces:
        targets[which].at[at][...] = done[begin : begin + count, :].astype(f32)
    half = ws_out.shape[0] // 2
    ws_out[:half] = done[row : row + half, :128].astype(f32)
    ws_out[half:] = done[row : row + half, 128:].astype(f32)


def vmem_spec():
    return pl.BlockSpec(memory_space=pltpu.VMEM)


def shaped(shape, kind):
    return jax.ShapeDtypeStruct(shape, kind)


def run_reduce(ident, n_clip, arrays):
    total = sum(v.size for v in arrays) // 256
    units = -(-total // UNIT)
    share = [-(-units // 3), -(-(units - units // 3) // 2), units // 3]
    share[1] = units - share[0] - share[2]
    sizes = [v * UNIT for v in share]
    starts = [0, sizes[0], sizes[0] + sizes[1]]
    rows = units * UNIT
    land_rows = land_plan(n_clip, sizes)[1]
    stages = len(stage_orders(n_clip, 1)[0])
    sems = [pltpu.SemaphoreType.DMA((3, stages))] * 4
    vm = vmem_spec()
    done = pl.pallas_call(
        functools.partial(reduce_weights, n_clip, starts, sizes),
        in_specs=[vm] * len(arrays),
        out_specs=vm,
        out_shape=shaped((rows, 256), bf16),
        scratch_shapes=[pltpu.VMEM((v, 256), bf16) for v in (rows, land_rows)] + sems,
        compiler_params=pltpu.CompilerParams(
            collective_id=ident, has_side_effects=True, vmem_limit_bytes=60 * MIB
        ),
        name=f"reduce{ident}",
    )(*arrays)
    return pl.pallas_call(
        unpack_weights,
        in_specs=[vm],
        out_specs=(vm,) * len(arrays),
        out_shape=tuple(shaped(v.shape, f32) for v in arrays),
        compiler_params=params(60),
        name="unpack_weights",
    )(done)


def run_exchange(ident, n_clip, part, weight, moments, source=None):
    edges = source is not None
    count, width = part.shape
    out_shape = [jax.ShapeDtypeStruct((count, width), f32)]
    ins = [part, weight]
    in_specs = [vmem_spec(), vmem_spec()]
    scratch = [
        pltpu.VMEM((4, count, width), f32),
        pltpu.VMEM((count, width), f32),
        pltpu.VMEM((n_clip, count, width), f32),
        pltpu.SemaphoreType.DMA((3,)),
        pltpu.SemaphoreType.DMA((4,)),
        pltpu.SemaphoreType.DMA((n_clip,)),
        pltpu.SemaphoreType.DMA((n_clip,)),
    ]
    if edges:
        high, cols, slab, _ = source.shape
        ins.append(source)
        in_specs.append(pl.BlockSpec(memory_space=pl.ANY))
        out_shape += [
            jax.ShapeDtypeStruct((cols, slab, MIX), f32),
            jax.ShapeDtypeStruct((high, slab, MIX), f32),
            jax.ShapeDtypeStruct((slab, MIX), f32),
        ]
        scratch += [
            pltpu.VMEM((cols, slab, MIX), f32),
            pltpu.VMEM((high, slab, MIX), f32),
            pltpu.VMEM((3, cols, slab, MIX), bf16),
            pltpu.VMEM((3, cols, slab, MIX), bf16),
            pltpu.SemaphoreType.DMA((2,)),
            pltpu.SemaphoreType.DMA((3,)),
            pltpu.SemaphoreType.DMA((3,)),
        ]
    return pl.pallas_call(
        functools.partial(exchange, n_clip, moments, edges),
        out_shape=tuple(out_shape),
        in_specs=in_specs,
        out_specs=tuple(vmem_spec() for _ in out_shape),
        scratch_shapes=scratch,
        compiler_params=pltpu.CompilerParams(
            collective_id=ident, has_side_effects=True, vmem_limit_bytes=60 * MIB
        ),
        name=f"exchange{ident}",
    )(*ins)


def whole(shape):
    return pl.BlockSpec(shape, lambda h: (0,) * len(shape))


def per_line(shape):
    return pl.BlockSpec((None,) + tuple(shape), lambda h: (h,) + (0,) * len(shape))


def params(limit):
    return pltpu.CompilerParams(vmem_limit_bytes=60 * MIB)


def on_device(
    slow_input,
    fast_input,
    frame_counts,
    lateral_weight,
    slow_a_weight,
    slow_b_weight,
    slow_c_weight,
    slow_proj_weight,
    fast_a_weight,
    fast_b_weight,
    fast_c_weight,
    slow_gain,
    slow_shift,
    fast_gain,
    fast_shift,
    slow_cotangent,
    fast_cotangent,
):
    n_clip = lax.axis_size("clip")
    clips, frames, high, cols, _ = slow_input.shape
    slab = clips * frames
    own = lax.dynamic_slice_in_dim(frame_counts, lax.axis_index("clip") * clips, clips)
    row_t = jnp.arange(slab) // clips
    row_c = jnp.arange(slab) % clips
    real = row_t < own[row_c]
    m = jnp.broadcast_to(real.astype(f32)[:, None], (slab, 128))
    col_c = jnp.arange(ALPHA * slab) // (ALPHA * frames)
    col_f = jnp.arange(ALPHA * slab) % (ALPHA * frames)
    want_f = (ALPHA * row_t[None, :] + jnp.arange(ALPHA)[:, None]).reshape(-1)
    want_c = jnp.tile(row_c, ALPHA)
    perm = (
        (want_f[:, None] == col_f[None, :]) & (want_c[:, None] == col_c[None, :]) & jnp.tile(real, ALPHA)[:, None]
    ).astype(bf16)
    real_total = jnp.sum(frame_counts).astype(f32)
    weight = jnp.broadcast_to(
        (jnp.sum(frame_counts.reshape(n_clip, clips), axis=1).astype(f32) / real_total)[:, None, None], (n_clip, 1, 128)
    )
    inv = jnp.full((1, 128), 1.0, f32) / (real_total * (H * W))
    place = jnp.stack([lax.axis_index("ha"), lax.axis_index("wa")]).astype(jnp.int32)

    def mixed(slow, fast, k):
        lo = fast[k * C_FMID : (k + 1) * C_FMID]
        return jnp.concatenate([slow[k * C_MID : (k + 1) * C_MID], jnp.tile(lo, ALPHA)])[None]

    gain1, shift1 = mixed(slow_gain, fast_gain, 0), mixed(slow_shift, fast_shift, 0)
    gain2, shift2 = mixed(slow_gain, fast_gain, 1), mixed(slow_shift, fast_shift, 1)
    sgain, sshift = slow_gain[None, 2 * C_MID :], slow_shift[None, 2 * C_MID :]
    fgain, fshift = fast_gain[None, 2 * C_FMID :], fast_shift[None, 2 * C_FMID :]
    wfa = fast_a_weight.transpose(0, 2, 1)
    eye = jnp.eye(ALPHA, dtype=bf16)
    wfb = (eye[None, :, None, :, None] * fast_b_weight.reshape(9, 1, C_FMID, 1, C_FMID)).reshape(9, 128, 128)

    xs = slow_input.transpose(1, 2, 3, 0, 4)
    xf = fast_input.transpose(0, 2, 3, 1, 4)
    cot = slow_cotangent.transpose(1, 2, 3, 0, 4)
    fcot = fast_cotangent.transpose(0, 2, 3, 1, 4)
    slow_block = pl.BlockSpec((frames, None, cols, clips, C_IN), lambda h: (0, h, 0, 0, 0))
    fast_block = pl.BlockSpec((clips, None, cols, ALPHA * frames, C_FAST), lambda h: (0, h, 0, 0, 0))

    def lines(c, kind):
        return shaped((high, cols, slab, c), kind)

    m_spec = whole((slab, 128))
    perm_spec = whole((ALPHA * slab, ALPHA * slab))
    L1 = MIX + C_IN
    x, f, z1, zp, st1, base = pl.pallas_call(
        functools.partial(first_convs, clips),
        grid=(high,),
        in_specs=[
            slow_block, fast_block, m_spec, perm_spec, whole((5, C_FAST, C_LAT)), whole((3, C_JOIN, C_MID)),
            whole((C_JOIN, C_IN)), whole((3, C_FMID, C_FAST)),
        ],
        out_specs=(
            per_line((cols, slab, C_JOIN)), per_line((cols, slab, WIDE_FAST)), per_line((cols, slab, MIX)),
            per_line((cols, slab, C_IN)), whole((2, L1)), whole((1, C_IN)),
        ),
        out_shape=(
            lines(C_JOIN, bf16), lines(WIDE_FAST, bf16), lines(MIX, f32), lines(C_IN, bf16), shaped((2, L1), f32),
            shaped((1, C_IN), f32),
        ),
        scratch_shapes=[
            pltpu.VMEM((128, WIDE_FAST), bf16), pltpu.VMEM((2, 128, C_FAST), bf16), pltpu.VMEM((1, L1), f32),
            pltpu.VMEM((1, L1), f32), pltpu.VMEM((1, L1), f32),
        ],
        compiler_params=params(40),
        name="first_convs",
    )(xs, xf, m, perm, lateral_weight, slow_a_weight, slow_proj_weight, wfa)

    mom1, row1, col1, corner1 = run_exchange(1, n_clip, st1, weight, True, z1)
    smem = pl.BlockSpec(memory_space=pltpu.SMEM)
    vm = vmem_spec()
    a1, z2, st2 = pl.pallas_call(
        space_convs,
        in_specs=[smem] + [vm] * 10,
        out_specs=(vm, vm, vm),
        out_shape=(
            shaped((high + 2, cols + 2, slab, MIX), bf16), lines(MIX, f32), shaped((2, MIX), f32),
        ),
        scratch_shapes=[pltpu.VMEM((1, MIX), f32), pltpu.VMEM((1, MIX), f32)],
        compiler_params=params(32),
        name="space_convs",
    )(place, z1, row1, col1, corner1, mom1, gain1, shift1, m, slow_b_weight, wfb)
    mom2, zrow, zcol, zcorner = run_exchange(2, n_clip, st2, weight, True, z2)

    L3 = C_IN + C_FAST
    a2, st3 = pl.pallas_call(
        expand_moments,
        grid=(high,),
        in_specs=[
            per_line((cols, slab, MIX)), whole((2, MIX)), whole((1, MIX)), whole((1, MIX)), m_spec, whole((C_MID, C_IN)),
            whole((C_FMID, C_FAST)),
        ],
        out_specs=(per_line((cols, slab, MIX)), whole((2, L3))),
        out_shape=(lines(MIX, bf16), shaped((2, L3), f32)),
        scratch_shapes=[pltpu.VMEM((128, WIDE_FAST), bf16)] + [pltpu.VMEM((1, L3), f32)] * 3,
        compiler_params=params(24),
        name="expand_moments",
    )(z2, mom2, gain2, shift2, m, slow_c_weight, fast_c_weight)
    (mom3,) = run_exchange(3, n_clip, st3, weight, True)

    L4 = 3 * C_IN + 2 * C_FAST
    so, fo, gs, gf, part4 = pl.pallas_call(
        outputs,
        grid=(high,),
        in_specs=[
            per_line((cols, slab, MIX)), per_line((cols, slab, C_IN)), whole((1, C_IN)), whole((2, L1)), whole((2, L3)),
            whole((1, 2 * C_IN)), whole((1, 2 * C_IN)), whole((1, C_FAST)), whole((1, C_FAST)), slow_block, fast_block,
            per_line((cols, slab, WIDE_FAST)), m_spec, perm_spec, whole((C_MID, C_IN)), whole((C_FMID, C_FAST)),
        ],
        out_specs=(
            slow_block, fast_block, per_line((cols, slab, C_IN)), per_line((cols, slab, WIDE_FAST)), whole((1, L4)),
        ),
        out_shape=(
            shaped(xs.shape, bf16), shaped(xf.shape, bf16), lines(C_IN, f32), lines(WIDE_FAST, f32),
            shaped((1, L4), f32),
        ),
        scratch_shapes=[pltpu.VMEM((128, WIDE_FAST), bf16)],
        compiler_params=params(32),
        name="outputs",
    )(a2, zp, base, mom1, mom3, sgain, sshift, fgain, fshift, cot, fcot, f, m, perm, slow_c_weight, fast_c_weight)
    (tot4,) = run_exchange(4, n_clip, part4, weight, False)

    dzc, dzp, dfc, q2, part5 = pl.pallas_call(
        expand_back,
        grid=(high,),
        in_specs=[
            per_line((cols, slab, C_IN)), per_line((cols, slab, WIDE_FAST)), per_line((cols, slab, MIX)),
            per_line((cols, slab, C_IN)), whole((1, C_IN)), per_line((cols, slab, MIX)), whole((2, L1)), whole((2, MIX)),
            whole((2, L3)), whole((1, L4)), whole((1, 128)), whole((1, 2 * C_IN)), whole((1, C_FAST)), whole((1, MIX)),
            whole((1, MIX)), m_spec, whole((C_MID, C_IN)), whole((C_FMID, C_FAST)),
        ],
        out_specs=(
            per_line((cols, slab, C_IN)), per_line((cols, slab, C_IN)), per_line((cols, slab, WIDE_FAST)),
            per_line((cols, slab, MIX)), whole((1, 2 * MIX)),
        ),
        out_shape=(
            lines(C_IN, bf16), lines(C_IN, bf16), lines(WIDE_FAST, bf16), lines(MIX, f32), shaped((1, 2 * MIX), f32),
        ),
        scratch_shapes=[pltpu.VMEM((128, WIDE_FAST), bf16)],
        compiler_params=params(32),
        name="expand_back",
    )(gs, gf, a2, zp, base, z2, mom1, mom2, mom3, tot4, inv, sgain, fgain, gain2, shift2, m, slow_c_weight, fast_c_weight)
    tot5, qrow, qcol, qcorner = run_exchange(5, n_clip, part5, weight, False, q2)

    n = high * cols

    def flat(v):
        return v.reshape((n,) + v.shape[2:])

    dwp, dwc, dwfc = pl.pallas_call(
        expand_weights,
        grid=(C_JOIN // C_MID,),
        in_specs=[
            pl.BlockSpec((n, slab, C_MID), lambda i: (0, 0, i)), whole((n, slab, MIX)), whole((n, slab, C_IN)),
            whole((n, slab, C_IN)), whole((n, slab, WIDE_FAST)),
        ],
        out_specs=(
            pl.BlockSpec((C_MID, C_IN), lambda i: (i, 0)), whole((C_MID, C_IN)), whole((C_FMID, C_FAST)),
        ),
        out_shape=(shaped((C_JOIN, C_IN), bf16), shaped((C_MID, C_IN), bf16), shaped((C_FMID, C_FAST), f32)),
        compiler_params=params(56),
        name="expand_weights",
    )(flat(x), flat(a2), flat(dzp), flat(dzc), flat(dfc))

    q1, part6, dwb, dwfb = pl.pallas_call(
        space_back,
        in_specs=[smem] + [vm] * 20,
        out_specs=(vm, vm, vm, vm),
        out_shape=(
            lines(MIX, f32), shaped((1, 2 * MIX), f32), shaped((3, 3, C_MID, C_MID), bf16),
            shaped((9, C_FMID, C_FMID), f32),
        ),
        scratch_shapes=[
            pltpu.VMEM((high + 2, cols + 2, slab, MIX), bf16), pltpu.VMEM((3, 3, C_MID, C_MID), f32),
            pltpu.VMEM((9, 128, 128), f32),
        ],
        compiler_params=params(48),
        name="space_back",
    )(
        place, q2, z2, qrow, qcol, qcorner, zrow, zcol, zcorner, a1, z1, mom1, mom2, tot5, inv, gain1, shift1, gain2, m,
        slow_b_weight, wfb,
    )
    (tot6,) = run_exchange(6, n_clip, part6, weight, False)

    sx, fx, da, dl, df = pl.pallas_call(
        functools.partial(first_back, clips),
        grid=(high,),
        in_specs=[
            per_line((cols, slab, MIX)), per_line((cols, slab, MIX)), whole((2, L1)), whole((1, 2 * MIX)),
            whole((1, 128)), whole((1, MIX)), m_spec, perm_spec, per_line((cols, slab, C_IN)),
            per_line((cols, slab, WIDE_FAST)), whole((5, C_FAST, C_LAT)), whole((3, C_JOIN, C_MID)),
            whole((C_JOIN, C_IN)), whole((3, C_FMID, C_FAST)),
        ],
        out_specs=(
            slow_block, fast_block, per_line((cols, slab, 3 * C_MID)), per_line((cols, slab, 2 * C_LAT)),
            per_line((cols, slab, 3 * 128)),
        ),
        out_shape=(
            shaped(xs.shape, bf16), shaped(xf.shape, bf16), lines(3 * C_MID, bf16), lines(2 * C_LAT, bf16),
            lines(3 * 128, bf16),
        ),
        scratch_shapes=[pltpu.VMEM((128, WIDE_FAST), bf16), pltpu.VMEM((2, 128, C_FAST), bf16)],
        compiler_params=params(40),
        name="first_back",
    )(q1, z1, mom1, tot6, inv, gain1, m, perm, dzp, gf, lateral_weight, slow_a_weight, slow_proj_weight, wfa)

    dwa, dwl, dws = pl.pallas_call(
        first_weights,
        grid=(C_JOIN // C_MID,),
        in_specs=[
            pl.BlockSpec((n, slab, C_MID), lambda i: (0, 0, i)), whole((n, slab, WIDE_FAST)),
            whole((n, slab, 3 * C_MID)), whole((n, slab, 2 * C_LAT)), whole((n, slab, 3 * 128)),
            whole((C_FMID, C_FAST)), whole((9, C_FMID, C_FMID)),
        ],
        out_specs=(
            pl.BlockSpec((3, C_MID, C_MID), lambda i: (0, i, 0)), whole((5, C_FAST, C_LAT)), whole((512, C_FAST)),
        ),
        out_shape=(
            shaped((3, C_JOIN, C_MID), bf16), shaped((5, C_FAST, C_LAT), bf16), shaped((512, C_FAST), bf16),
        ),
        compiler_params=params(48),
        name="first_weights",
    )(flat(x), flat(f), flat(da), flat(dl), flat(df), dwfc, dwfb)

    dwp, dwc, dwb, dwa, dwl, dws = run_reduce(7, n_clip, (dwp, dwc, dwb, dwa, dwl, dws))
    dwfa = dws[: 3 * C_FMID].reshape(3, C_FMID, C_FAST)
    dwfc = dws[3 * C_FMID : 4 * C_FMID]
    dwfb = dws[4 * C_FMID : 13 * C_FMID, :C_FMID]

    def joined_sums(k):
        first = [tot6[0, k * MIX : (k + 1) * MIX], tot5[0, k * MIX : (k + 1) * MIX]]
        last = tot4[0, :C_IN] if k == 0 else tot4[0, C_IN : 2 * C_IN]
        proj = tot4[0, :C_IN] if k == 0 else tot4[0, 2 * C_IN : 3 * C_IN]
        at = 3 * C_IN + k * C_FAST
        slow = jnp.concatenate([first[0][:C_MID], first[1][:C_MID], last, proj])
        lo = C_MID + C_FMID
        fast = jnp.concatenate([first[0][C_MID:lo], first[1][C_MID:lo], tot4[0, at : at + C_FAST]])
        return slow, fast

    slow_shift_grad, fast_shift_grad = joined_sums(0)
    slow_gain_grad, fast_gain_grad = joined_sums(1)
    return (
        so.transpose(3, 0, 1, 2, 4),
        fo.transpose(0, 3, 1, 2, 4),
        sx.transpose(3, 0, 1, 2, 4),
        fx.transpose(0, 3, 1, 2, 4),
        dwl,
        dwa,
        dwb,
        dwc,
        dwp,
        dwfa.transpose(0, 2, 1),
        dwfb.reshape(3, 3, C_FMID, C_FMID),
        dwfc,
        slow_gain_grad,
        slow_shift_grad,
        fast_gain_grad,
        fast_shift_grad,
    )


def solution(mesh):
    tiles = P("clip", None, "ha", "wa", None)
    return jax.shard_map(
        on_device,
        mesh=mesh,
        in_specs=(tiles, tiles) + (P(),) * 13 + (tiles, tiles),
        out_specs=(tiles,) * 4 + (P(),) * 12,
        check_vma=False,
    )
```

```python
import functools

import jax
import jax.numpy as jnp
from jax import lax
from jax.experimental import pallas as pl
from jax.experimental.pallas import tpu as pltpu
from jax.sharding import PartitionSpec as P

ALPHA = 4
H = 14
W = 14
C_IN = 1024
C_LAT = 256
C_MID = 256
C_FAST = 128
C_FMID = 32
C_JOIN = C_IN + C_LAT
MIX = C_MID + ALPHA * C_FMID
WIDE_FAST = ALPHA * C_FAST

eps_norm = 1e-05
f32 = jnp.float32
bf16 = jnp.bfloat16
MESH = pl.DeviceIdType.MESH
MIB = 1 << 20


def dot(a, b):
    return lax.dot_general(a, b, (((1,), (0,)), ((), ())), preferred_element_type=f32)


def dot_nt(a, b):
    return lax.dot_general(a, b, (((1,), (1,)), ((), ())), preferred_element_type=f32)


def dot_tn(a, b):
    return lax.dot_general(a, b, (((0,), (0,)), ((), ())), preferred_element_type=f32)


def sigmoid(v):
    return 0.5 + 0.5 * jnp.tanh(0.5 * v)


def later(y, clips):
    return jnp.concatenate([jnp.zeros_like(y[:, :clips]), y[:, : y.shape[1] - clips]], axis=1)


def sooner(y, clips):
    return jnp.concatenate([y[:, clips:], jnp.zeros_like(y[:, :clips])], axis=1)


def rows_sum(v):
    return jnp.sum(jnp.sum(v, axis=0), axis=0, keepdims=True)


def phase_sum(v):
    out = v
    for k in range(1, ALPHA):
        out = out + pltpu.roll(v, k * C_FMID, 1)
    return out


def block_sum(v):
    return sum(v[:, p * C_FAST : (p + 1) * C_FAST] for p in range(ALPHA))


def spread(mask, width):
    return jnp.tile(mask, (1, width // 128))


def frames_matrix(wfa_ref, out_ref, ends_ref):
    out_ref[...] = jnp.zeros_like(out_ref)
    ends_ref[...] = jnp.zeros_like(ends_ref)
    for p in range(ALPHA):
        for s in range(max(p - 1, 0), min(p + 2, ALPHA)):
            out_ref[p * C_FMID : (p + 1) * C_FMID, s * C_FAST : (s + 1) * C_FAST] = wfa_ref[s - p + 1]
    ends_ref[0, 0:C_FMID] = wfa_ref[0]
    ends_ref[1, 3 * C_FMID :] = wfa_ref[2]


def expand_matrix(wfc_ref, out_ref):
    out_ref[...] = jnp.zeros_like(out_ref)
    for p in range(ALPHA):
        out_ref[p * C_FMID : (p + 1) * C_FMID, p * C_FAST : (p + 1) * C_FAST] = wfc_ref[...]


class Exchange:
    def __init__(self, n_clip, moments, refs, rim_refs=None):
        self.n = n_clip
        self.moments = moments
        self.part, self.near, self.mid, self.far, self.near_send, self.near_recv, self.far_send, self.far_recv = refs
        self.clip, self.ha, self.wa = lax.axis_index("clip"), lax.axis_index("ha"), lax.axis_index("wa")
        self.me = 2 * self.ha + self.wa
        self.peers = [(1 - self.ha, self.wa), (self.ha, 1 - self.wa), (1 - self.ha, 1 - self.wa)]
        self.others = [lax.rem(self.clip + d, n_clip) for d in range(1, n_clip)]
        if rim_refs is not None:
            self.packs, self.lands, self.rim_send, self.rim_recv = rim_refs

    def signal(self):
        barrier = pltpu.get_barrier_semaphore()
        for a, b in self.peers:
            pl.semaphore_signal(barrier, inc=1, device_id=(self.clip, a, b), device_id_type=MESH)
        for other in self.others:
            pl.semaphore_signal(barrier, inc=1, device_id=(other, self.ha, self.wa), device_id_type=MESH)

    def meet(self):
        pl.semaphore_wait(pltpu.get_barrier_semaphore(), 3 + self.n - 1)

    def near_copy(self, k, slot):
        a, b = self.peers[k]
        return pltpu.make_async_remote_copy(
            src_ref=self.part, dst_ref=self.near.at[slot], send_sem=self.near_send.at[k],
            recv_sem=self.near_recv.at[slot], device_id=(self.clip, a, b), device_id_type=MESH,
        )

    def far_copy(self, d, slot):
        return pltpu.make_async_remote_copy(
            src_ref=self.mid, dst_ref=self.far.at[slot], send_sem=self.far_send.at[d],
            recv_sem=self.far_recv.at[slot], device_id=(self.others[d], self.ha, self.wa), device_id_type=MESH,
        )

    def rim_copy(self, k):
        a, b = self.peers[k]
        size = 1 if k == 2 else self.packs.shape[1]
        return pltpu.make_async_remote_copy(
            src_ref=self.packs.at[k, pl.ds(0, size)], dst_ref=self.lands.at[k, pl.ds(0, size)],
            send_sem=self.rim_send.at[k], recv_sem=self.rim_recv.at[k], device_id=(self.clip, a, b),
            device_id_type=MESH,
        )

    def send_near(self):
        for k in range(3):
            self.near_copy(k, self.me).start()
        self.near[self.me] = self.part[...]

    def send_rims(self, line, side):
        count = self.packs.shape[1]
        centre = self.part[0:1, :MIX] if self.moments else jnp.zeros((1, MIX), f32)
        self.packs[0] = (line[...] - centre).astype(bf16)
        self.packs[1] = (side[...] - centre).astype(bf16)
        self.packs[2, 0] = self.packs[0, (count - 1) * (1 - self.wa)]
        for k in range(3):
            self.rim_copy(k).start()

    def send_far(self):
        for k, (a, b) in enumerate(self.peers):
            self.near_copy(k, 2 * a + b).wait_recv()
        near = self.near
        if self.moments:
            mean = (near[0, 0:1] + near[1, 0:1] + near[2, 0:1] + near[3, 0:1]) * 0.25
            self.mid[0:1] = mean
            self.mid[1:2] = sum(near[k, 1:2] + (near[k, 0:1] - mean) ** 2 for k in range(4)) * 0.25
        else:
            self.mid[...] = near[0] + near[1] + near[2] + near[3]
        for d in range(self.n - 1):
            self.far_copy(d, self.clip).start()
        self.far[self.clip] = self.mid[...]

    def finish(self, out, weight):
        for d, other in enumerate(self.others):
            self.far_copy(d, other).wait_recv()
        width = out.shape[1]
        far = self.far
        if self.moments:
            mean = sum(far[k, 0:1] * spread(weight[k], width) for k in range(self.n))
            out[0:1] = mean
            out[1:2] = sum((far[k, 1:2] + (far[k, 0:1] - mean) ** 2) * spread(weight[k], width) for k in range(self.n))
        else:
            out[...] = sum(far[k] for k in range(self.n))
        for k in range(3):
            self.near_copy(k, self.me).wait_send()
        for d in range(self.n - 1):
            self.far_copy(d, self.clip).wait_send()

    def finish_rims(self, rims):
        for k, (a, b) in enumerate(self.peers):
            self.rim_copy(k).wait_recv()
            centre = self.near[2 * a + b, 0:1, :MIX] if self.moments else jnp.zeros((1, MIX), f32)
            land = self.lands[k, 0] if k == 2 else self.lands[k]
            rims[k][...] = land.astype(f32) + centre
        for k in range(3):
            self.rim_copy(k).wait_send()


def exchange_scratch(n_clip, count, width):
    return [
        pltpu.VMEM((count, width), f32),
        pltpu.VMEM((4, count, width), f32),
        pltpu.VMEM((count, width), f32),
        pltpu.VMEM((n_clip, count, width), f32),
        pltpu.SemaphoreType.DMA((3,)),
        pltpu.SemaphoreType.DMA((4,)),
        pltpu.SemaphoreType.DMA((n_clip,)),
        pltpu.SemaphoreType.DMA((n_clip,)),
    ]


def rim_scratch(side, slab):
    return [
        pltpu.VMEM((3, side, slab, MIX), bf16),
        pltpu.VMEM((3, side, slab, MIX), bf16),
        pltpu.SemaphoreType.DMA((3,)),
        pltpu.SemaphoreType.DMA((3,)),
    ]


def first_pass(clips, n_clip, xs, xf, m, perm, wl, wa, wp, wfa, weight,
               x_out, f_out, z_out, zp_out, st_out, base_out, mom, row, col, corner,
               keep, taps, ends, base, one, two, line, side, *refs):
    i = pl.program_id(0)
    cols = xs.shape[1]
    slab = m.shape[0]
    rows = cols * slab
    high = keep.shape[0]
    ex = Exchange(n_clip, True, refs[:8], refs[8:])
    here = cols * jnp.sum(m[...], axis=0, keepdims=True)
    count = high * here

    @pl.when(i == 0)
    def _():
        ex.signal()
        frames_matrix(wfa, taps, ends)

    @pl.when(i < high)
    def _():
        mask_in = spread(m[...], C_IN).astype(bf16)
        for w in range(cols):
            keep[i, w, :, :C_IN] = xs[:, w].reshape(slab, C_IN) * mask_in
            phases = dot(perm[...], xf[:, w].reshape(ALPHA * slab, C_FAST)).astype(bf16)
            for p in range(ALPHA):
                f_out[w, :, p * C_FAST : (p + 1) * C_FAST] = phases[p * slab : (p + 1) * slab]
        fast = f_out[...].reshape(rows, WIDE_FAST)
        lat = dot(fast[:, : 3 * C_FAST], wl[2:5].reshape(3 * C_FAST, C_LAT)).reshape(cols, slab, C_LAT)
        back = dot(fast[:, 2 * C_FAST :], wl[0:2].reshape(2 * C_FAST, C_LAT)).reshape(cols, slab, C_LAT)
        keep[i, :, :, C_IN:] = (lat + later(back, clips)).astype(bf16)
        x_out[...] = keep[i]
        joined = keep[i].reshape(rows, C_JOIN)
        za = dot(joined, wa[1]).reshape(cols, slab, C_MID)
        za = za + later(dot(joined, wa[0]).reshape(cols, slab, C_MID), clips)
        za = za + sooner(dot(joined, wa[2]).reshape(cols, slab, C_MID), clips)
        fa = dot_nt(fast, taps[...]).reshape(cols, slab, 128)
        fa = fa + later(dot_nt(fast[:, 3 * C_FAST :], ends[0]).reshape(cols, slab, 128), clips)
        fa = fa + sooner(dot_nt(fast[:, :C_FAST], ends[1]).reshape(cols, slab, 128), clips)
        z_out[:, :, :C_MID] = za
        z_out[:, :, C_MID:] = fa
        keep_rims(ex, i, high, z_out, line, side)
        add_moments(i == 0, ((0, za, 0), (C_MID, fa, 1)), m, here, base, one, two)

    @pl.when(i == high)
    def _():
        finish_moments(ex.part, base[...], one[...], two[...], count, ((0, C_MID, 0), (C_MID, 128, 1)))
        ex.meet()
        ex.send_near()
        ex.send_rims(line, side)

    @pl.when(i == high + 2)
    def _():
        ex.send_far()

    @pl.when(i >= high)
    def _():
        joined = keep[i - high].reshape(rows, C_JOIN)
        zp = dot(joined, wp[...]).reshape(cols, slab, C_IN)
        add_moments(i == high, ((MIX, zp, 0),), m, here, base, one, two)
        zp_out[...] = (zp - base[:, MIX:]).astype(bf16)

    @pl.when(i == 2 * high - 1)
    def _():
        s1 = one[:, MIX:] / spread(count, C_IN)
        st_out[0:1] = base[:, MIX:] + s1
        st_out[1:2] = two[:, MIX:] / spread(count, C_IN) - s1 * s1
        base_out[...] = base[:, MIX:]
        ex.finish(mom, weight)
        ex.finish_rims((row, col, corner))


def keep_rims(ex, i, high, block, line, side):
    side[i] = block[(block.shape[0] - 1) * (1 - ex.wa)]

    @pl.when(i == (high - 1) * (1 - ex.ha))
    def _():
        line[...] = block[...]


def add_moments(first, parts, m, here, base, one, two):
    @pl.when(first)
    def _():
        for at, z, fast in parts:
            width = z.shape[-1]
            mean = rows_sum(z * spread(m[...], width)) / spread(here, width)
            if fast:
                mean = phase_sum(mean) * 0.25
            base[:, at : at + width] = mean
            one[:, at : at + width] = jnp.zeros((1, width), f32)
            two[:, at : at + width] = jnp.zeros((1, width), f32)

    for at, z, _ in parts:
        width = z.shape[-1]
        off = (z - base[:, at : at + width]) * spread(m[...], width)
        one[:, at : at + width] += rows_sum(off)
        two[:, at : at + width] += rows_sum(off * off)


def finish_moments(st, base, one, two, count, parts):
    for at, width, fast in parts:
        s1 = one[:, at : at + width]
        s2 = two[:, at : at + width]
        if fast:
            s1 = phase_sum(s1) * 0.25
            s2 = phase_sum(s2) * 0.25
        n = spread(count.astype(f32), width)
        s1 = s1 / n
        st[0:1, at : at + width] = base[:, at : at + width] + s1
        st[1:2, at : at + width] = s2 / n - s1 * s1


def affine(moments, gain, shift, at, width):
    mean = moments[0:1, at : at + width]
    scale = lax.rsqrt(moments[1:2, at : at + width] + eps_norm)
    return mean, scale, gain[...], shift[...]


def second_pass(n_clip, z1_hbm, row, col, corner, mom, gain, shift, m, wb, wfb, stp, weight, cot,
                a_out, z_out, mom_out, zrow, zcol, zcorner, cot_out, z1, z1_sem, one, two, *refs):
    i = pl.program_id(0)
    high, cols, slab, _ = z1.shape
    rows = cols * slab
    ex = Exchange(n_clip, True, refs[:8], refs[8:])

    def fetch(h):
        return pltpu.make_async_copy(z1_hbm.at[h], z1.at[h], z1_sem.at[h])

    @pl.when(i == 0)
    def _():
        for h in range(high):
            fetch(h).start()
        ex.signal()
        mean, scale, g, b = affine(mom, gain, shift, 0, MIX)
        mult = scale * g
        mask = spread(m[...], MIX)

        def act(z):
            v = (z - mean) * mult + b
            return (v * sigmoid(v) * mask).astype(bf16)

        far = high + 1
        a_out[far * ex.ha] = jnp.zeros((cols + 2, slab, MIX), bf16)
        a_out[:, far * ex.wa] = jnp.zeros((high + 2, slab, MIX), bf16)
        a_out[far * (1 - ex.ha), 1 : 1 + cols] = act(row[...])
        a_out[1 : 1 + high, far * (1 - ex.wa)] = act(col[...])
        a_out[far * (1 - ex.ha), far * (1 - ex.wa)] = act(corner[...])

        def fill(h, carry):
            fetch(h).wait()
            a_out[h + 1, 1 : 1 + cols] = act(z1[h])
            return carry

        lax.fori_loop(0, high, fill, 0)

        def space(h, carry):
            slow = jnp.zeros((rows, C_MID), f32)
            fast = jnp.zeros((rows, 128), f32)
            for a in range(3):
                for c in range(3):
                    v = a_out[h + a, c : c + cols].reshape(rows, MIX)
                    slow = slow + dot(v[:, :C_MID], wb[a, c])
                    fast = fast + dot(v[:, C_MID:], wfb[3 * a + c])
            z_out[h, :, :, :C_MID] = slow.reshape(cols, slab, C_MID)
            z_out[h, :, :, C_MID:] = fast.reshape(cols, slab, 128)
            return carry

        lax.fori_loop(0, high, space, 0)
        here = cols * jnp.sum(m[...], axis=0, keepdims=True)
        base = rows_sum(z_out[0] * mask) / spread(here, MIX)
        base = jnp.concatenate([base[:, :C_MID], phase_sum(base[:, C_MID:]) * 0.25], axis=1)
        one[...] = jnp.zeros_like(one)
        two[...] = jnp.zeros_like(two)

        def gather(h, carry):
            off = (z_out[h] - base) * mask
            one[...] += rows_sum(off)
            two[...] += rows_sum(off * off)
            return carry

        lax.fori_loop(0, high, gather, 0)
        finish_moments(ex.part, base, one[...], two[...], high * here, ((0, C_MID, 0), (C_MID, 128, 1)))
        ex.part[:, MIX:] = stp[...]
        ex.meet()
        ex.send_near()
        ex.send_rims(z_out.at[(high - 1) * (1 - ex.ha)], z_out.at[:, (cols - 1) * (1 - ex.wa)])

    @pl.when(i == 3)
    def _():
        ex.send_far()

    @pl.when(i > 0)
    def _():
        for w in range(cols):
            cot_out[w] = cot[:, w].reshape(slab, C_IN)

    @pl.when(i == high)
    def _():
        ex.finish(mom_out, weight)
        ex.finish_rims((zrow, zcol, zcorner))


def third_pass(n_clip, z2, mom, gain, shift, m, wc, wfc, weight, fcot, perm,
               a_out, mom_out, fcot_out, big, base, one, two, *refs):
    i = pl.program_id(0)
    high = pl.num_programs(0) // 2
    cols, slab, _ = z2.shape
    rows = cols * slab
    ex = Exchange(n_clip, True, refs)
    here = cols * jnp.sum(m[...], axis=0, keepdims=True)

    @pl.when(i == 0)
    def _():
        ex.signal()
        expand_matrix(wfc, big)

    @pl.when(i < high)
    def _():
        mean, scale, g, b = affine(mom, gain, shift, 0, MIX)
        v = (z2[...] - mean) * (scale * g) + b
        a_out[...] = (v * sigmoid(v) * spread(m[...], MIX)).astype(bf16)
        a2 = a_out[...].reshape(rows, MIX)
        zc = dot(a2[:, :C_MID], wc[...]).reshape(cols, slab, C_IN)
        fc = dot(a2[:, C_MID:], big[...]).reshape(cols, slab, WIDE_FAST)

        @pl.when(i == 0)
        def _():
            base[:, :C_IN] = rows_sum(zc * spread(m[...], C_IN)) / spread(here, C_IN)
            base[:, C_IN:] = block_sum(rows_sum(fc * spread(m[...], WIDE_FAST))) / (4.0 * here)
            one[...] = jnp.zeros_like(one)
            two[...] = jnp.zeros_like(two)

        off = (zc - base[:, :C_IN]) * spread(m[...], C_IN)
        one[:, :C_IN] += rows_sum(off)
        two[:, :C_IN] += rows_sum(off * off)
        off = (fc - jnp.tile(base[:, C_IN:], (1, ALPHA))) * spread(m[...], WIDE_FAST)
        one[:, C_IN:] += block_sum(rows_sum(off)) * 0.25
        two[:, C_IN:] += block_sum(rows_sum(off * off)) * 0.25

    @pl.when(i == high)
    def _():
        finish_moments(ex.part, base[...], one[...], two[...], high * here, ((0, C_IN + C_FAST, 0),))
        ex.meet()
        ex.send_near()

    @pl.when(i == high + 2)
    def _():
        ex.send_far()

    @pl.when(i >= high)
    def _():
        for w in range(cols):
            phases = dot(perm[...], fcot[:, w].reshape(ALPHA * slab, C_FAST)).astype(bf16)
            for p in range(ALPHA):
                fcot_out[w, :, p * C_FAST : (p + 1) * C_FAST] = phases[p * slab : (p + 1) * slab]

    @pl.when(i == 2 * high - 1)
    def _():
        ex.finish(mom_out, weight)


def fourth_pass(n_clip, clips, a2, zp, base, mom2, mom3, sgain, sshift, fgain, fshift, cot, fcot, fast_in, m, perm, wc,
                wfc, weight, so, fo, gs, gf, tot, so_keep, fo_keep, sums, big, *refs):
    i = pl.program_id(0)
    high = pl.num_programs(0) // 2
    cols, slab, _ = a2.shape
    ex = Exchange(n_clip, False, refs)

    @pl.when(i == 0)
    def _():
        ex.signal()
        expand_matrix(wfc, big)
        sums[...] = jnp.zeros_like(sums)

    def tile_sum(v):
        return jnp.sum(v.reshape(slab // 8, 8, v.shape[-1]), axis=0)

    @pl.when(i < high)
    def _():
        mask = spread(m[...], C_IN)
        mask_f = spread(m[...], WIDE_FAST)
        mean_c = mom3[0:1, :C_IN]
        scale_c = lax.rsqrt(mom3[1:2, :C_IN] + eps_norm)
        mean_p = mom2[0:1, MIX:] - base[...]
        scale_p = lax.rsqrt(mom2[1:2, MIX:] + eps_norm)
        mean_f = jnp.tile(mom3[0:1, C_IN:], (1, ALPHA))
        scale_f = jnp.tile(lax.rsqrt(mom3[1:2, C_IN:] + eps_norm), (1, ALPHA))
        gain_c, gain_p = sgain[:, :C_IN], sgain[:, C_IN:]
        shift_cp = sshift[:, :C_IN] + sshift[:, C_IN:]
        gain_f = jnp.tile(fgain[...], (1, ALPHA))
        shift_f = jnp.tile(fshift[...], (1, ALPHA))
        totals = [jnp.zeros((8, C_IN), f32)] * 3 + [jnp.zeros((8, WIDE_FAST), f32)] * 2
        for w in range(cols):
            zc = (dot(a2[w, :, :C_MID], wc[...]) - mean_c) * scale_c
            zq = (zp[w].astype(f32) - mean_p) * scale_p
            ps = gain_c * zc + gain_p * zq + shift_cp
            sig = sigmoid(ps)
            so_keep[i, w] = (ps * sig * mask).astype(bf16)
            back = cot[w].astype(f32) * (sig * (1.0 + ps * (1.0 - sig)) * mask)
            gs[w] = back
            totals[0] += tile_sum(back)
            totals[1] += tile_sum(back * zc)
            totals[2] += tile_sum(back * zq)
            fc = (dot(a2[w, :, C_MID:], big[...]) - mean_f) * scale_f
            pf = gain_f * fc + shift_f + fast_in[w].astype(f32)
            sig = sigmoid(pf)
            fo_keep[i, w] = (pf * sig).astype(bf16)
            fback = fcot[w].astype(f32) * (sig * (1.0 + pf * (1.0 - sig)))
            gf[w] = fback
            totals[3] += tile_sum(fback)
            totals[4] += tile_sum(fback * fc)
        for k in range(3):
            sums[:, k * C_IN : (k + 1) * C_IN] += jnp.sum(totals[k], axis=0, keepdims=True)
        for k in range(2):
            at = 3 * C_IN + k * C_FAST
            sums[:, at : at + C_FAST] += block_sum(jnp.sum(totals[3 + k], axis=0, keepdims=True))

    @pl.when(i == high)
    def _():
        ex.part[...] = sums[...]
        ex.meet()
        ex.send_near()

    @pl.when(i == high + 2)
    def _():
        ex.send_far()

    @pl.when(i >= high)
    def _():
        for w in range(cols):
            so[:, w] = so_keep[i - high, w].reshape(slab // clips, clips, C_IN)
            wide = fo_keep[i - high, w]
            stacked = jnp.concatenate([wide[:, p * C_FAST : (p + 1) * C_FAST] for p in range(ALPHA)], axis=0)
            fo[:, w] = dot_tn(perm[...], stacked).astype(bf16).reshape(clips, slab, C_FAST)

    @pl.when(i == 2 * high - 1)
    def _():
        ex.finish(tot, weight)


def fifth_pass(n_clip, gs, gf, a2, zp, base, z2, mom2, mom3, tot4, inv, sgain, fgain, gain2, shift2, m, wc, wfc, x, weight,
               dzp_out, q_out, tot, row, col, corner, wp_out, wc_out, wfc_out,
               dzc_keep, dzp_keep, dfc_keep, a_keep, sums, big, line, side, *refs):
    i = pl.program_id(0)
    high, cols, slab, _ = dzc_keep.shape
    n = high * cols
    rows = cols * slab
    ex = Exchange(n_clip, False, refs[:8], refs[8:])

    @pl.when(i == 0)
    def _():
        ex.signal()
        expand_matrix(wfc, big)
        sums[...] = jnp.zeros_like(sums)

    @pl.when(i < high)
    def _():
        mask = spread(m[...], C_IN)
        inv_s = spread(inv[...], C_IN)
        inv_f = 0.25 * inv[...]
        mean_c = mom3[0:1, :C_IN]
        scale_c = lax.rsqrt(mom3[1:2, :C_IN] + eps_norm)
        mean_p = mom2[0:1, MIX:] - base[...]
        scale_p = lax.rsqrt(mom2[1:2, MIX:] + eps_norm)
        mean_f = jnp.tile(mom3[0:1, C_IN:], (1, ALPHA))
        scale_f = jnp.tile(lax.rsqrt(mom3[1:2, C_IN:] + eps_norm), (1, ALPHA))
        mult_c = sgain[:, :C_IN] * scale_c
        mult_p = sgain[:, C_IN:] * scale_p
        mult_f = jnp.tile(fgain[...], (1, ALPHA)) * scale_f
        first_s = tot4[:, :C_IN] * inv_s
        second_c = tot4[:, C_IN : 2 * C_IN] * inv_s
        second_p = tot4[:, 2 * C_IN : 3 * C_IN] * inv_s
        first_f = jnp.tile(tot4[:, 3 * C_IN : 3 * C_IN + C_FAST] * inv_f, (1, ALPHA))
        second_f = jnp.tile(tot4[:, 3 * C_IN + C_FAST :] * inv_f, (1, ALPHA))
        mask_f = spread(m[...], WIDE_FAST)
        a_keep[i] = a2[...]
        for w in range(cols):
            zc = (dot(a2[w, :, :C_MID], wc[...]) - mean_c) * scale_c
            zq = (zp[w].astype(f32) - mean_p) * scale_p
            g = gs[w]
            dzc_keep[i, w] = (mult_c * (g - mask * (first_s + zc * second_c))).astype(bf16)
            dzp = (mult_p * (g - mask * (first_s + zq * second_p))).astype(bf16)
            dzp_keep[i, w] = dzp
            dzp_out[w] = dzp
            fc = (dot(a2[w, :, C_MID:], big[...]) - mean_f) * scale_f
            dfc_keep[i, w] = (mult_f * (gf[w] - mask_f * (first_f + fc * second_f))).astype(bf16)
        da = dot_nt(dzc_keep[i].reshape(rows, C_IN), wc[...]).reshape(cols, slab, C_MID)
        df = dot_nt(dfc_keep[i].reshape(rows, WIDE_FAST), big[...]).reshape(cols, slab, 128)
        grads = jnp.concatenate([da, df], axis=2)
        slope_back(grads, z2[...], mom2, gain2, shift2, m, q_out, sums)
        keep_rims(ex, i, high, q_out, line, side)

    @pl.when(i == high)
    def _():
        ex.part[...] = sums[...]
        ex.meet()
        ex.send_near()
        ex.send_rims(line, side)

    @pl.when(i == high + 2)
    def _():
        ex.send_far()

    @pl.when(i >= high)
    def _():
        wp_out[...] = dot_tn(
            x[...].reshape(n * slab, C_MID), dzp_keep[...].reshape(n * slab, C_IN)
        ).astype(bf16)

    @pl.when(i == pl.num_programs(0) - 1)
    def _():
        a = a_keep[...].reshape(n * slab, MIX)
        wc_out[...] = dot_tn(a[:, :C_MID], dzc_keep[...].reshape(n * slab, C_IN)).astype(bf16)
        wide = dot_tn(a[:, C_MID:], dfc_keep[...].reshape(n * slab, WIDE_FAST))
        wfc_out[...] = sum(
            wide[p * C_FMID : (p + 1) * C_FMID, p * C_FAST : (p + 1) * C_FAST] for p in range(ALPHA)
        )
        ex.finish(tot, weight)
        ex.finish_rims((row, col, corner))


def slope_back(grads, z, mom, gain, shift, m, q_out, sums):
    mean, scale, g, b = affine(mom, gain, shift, 0, MIX)
    zhat = (z - mean) * scale
    v = g * zhat + b
    sig = sigmoid(v)
    q = grads * (sig * (1.0 + v * (1.0 - sig)) * spread(m[...], MIX))
    q_out[...] = q
    for k, s in enumerate((rows_sum(q), rows_sum(q * zhat))):
        at = k * MIX
        sums[:, at : at + C_MID] += s[:, :C_MID]
        sums[:, at + C_MID : at + MIX] += phase_sum(s[:, C_MID:])


def norm_terms(mom, gain, tot, inv):
    mean = mom[0:1, :MIX]
    scale = lax.rsqrt(mom[1:2, :MIX] + eps_norm)
    share = jnp.concatenate([spread(inv[...], C_MID), 0.25 * inv[...]], axis=1)
    return mean, scale, gain[...] * scale, tot[:, :MIX] * share, tot[:, MIX:] * share


def sixth_pass(n_clip, q2_hbm, z2_hbm, z1_hbm, a1_hbm, qrow, qcol, qcorner, zrow, zcol, zcorner, mom1, mom2, tot5, inv,
               gain1, shift1, gain2, m, wb, wfb, weight, q_out, tot, wb_out, wfb_out,
               wide, q2, z2, z1, a1, q2_sem, z2_sem, z1_sem, a1_sem, sums, *refs):
    i = pl.program_id(0)
    high, cols, slab, _ = z1.shape
    rows = cols * slab
    ex = Exchange(n_clip, False, refs)

    moved = ((q2_hbm, q2, q2_sem), (z2_hbm, z2, z2_sem), (z1_hbm, z1, z1_sem))

    def fetch(k, h):
        a, b, s = moved[k]
        return pltpu.make_async_copy(a.at[h], b.at[h], s.at[h])

    def fetch_a1():
        return pltpu.make_async_copy(a1_hbm, a1, a1_sem.at[0])

    @pl.when(i == 0)
    def _():
        for h in range(high):
            fetch(0, h).start()
            fetch(1, h).start()
        for h in range(high):
            fetch(2, h).start()
        fetch_a1().start()
        ex.signal()
        mean, scale, mult, first, second = norm_terms(mom2, gain2, tot5, inv)
        mask = spread(m[...], MIX)

        def grad(q, z):
            return (mult * (q - mask * (first + (z - mean) * scale * second))).astype(bf16)

        far = high + 1
        wide[far * ex.ha] = jnp.zeros((cols + 2, slab, MIX), bf16)
        wide[:, far * ex.wa] = jnp.zeros((high + 2, slab, MIX), bf16)
        wide[far * (1 - ex.ha), 1 : 1 + cols] = grad(qrow[...], zrow[...])
        wide[1 : 1 + high, far * (1 - ex.wa)] = grad(qcol[...], zcol[...])
        wide[far * (1 - ex.ha), far * (1 - ex.wa)] = grad(qcorner[...], zcorner[...])

        def fill(h, carry):
            fetch(0, h).wait()
            fetch(1, h).wait()
            wide[h + 1, 1 : 1 + cols] = grad(q2[h], z2[h])
            return carry

        lax.fori_loop(0, high, fill, 0)
        sums[...] = jnp.zeros_like(sums)

        def space(h, carry):
            fetch(2, h).wait()
            slow = jnp.zeros((rows, C_MID), f32)
            fast = jnp.zeros((rows, 128), f32)
            for a in range(3):
                for c in range(3):
                    v = wide[h + 2 - a, 2 - c : 2 - c + cols].reshape(rows, MIX)
                    slow = slow + dot_nt(v[:, :C_MID], wb[a, c])
                    fast = fast + dot_nt(v[:, C_MID:], wfb[3 * a + c])
            grads = jnp.concatenate([slow, fast], axis=1).reshape(cols, slab, MIX)
            slope_back(grads, z1[h], mom1, gain1, shift1, m, q_out.at[h], sums)
            return carry

        lax.fori_loop(0, high, space, 0)
        ex.part[...] = sums[...]
        ex.meet()
        ex.send_near()
        fetch_a1().wait()

    @pl.when(i == 3)
    def _():
        ex.send_far()

    @pl.when(i > 0)
    def _():
        tap = i - 1
        v = a1[pl.ds(tap // 3, high), pl.ds(lax.rem(tap, 3), cols)].reshape(high * rows, MIX)
        d = wide[1 : 1 + high, 1 : 1 + cols].reshape(high * rows, MIX)
        wb_out[...] = dot_tn(v[:, :C_MID], d[:, :C_MID]).astype(bf16)
        both = dot_tn(v[:, C_MID:], d[:, C_MID:])
        wfb_out[tap] = sum(
            both[p * C_FMID : (p + 1) * C_FMID, p * C_FMID : (p + 1) * C_FMID] for p in range(ALPHA)
        )

    @pl.when(i == 9)
    def _():
        ex.finish(tot, weight)


def first_back(clips, q1, z1, mom1, tot, inv, gain1, m, perm, dzp, gf, wl, wa, wp, wfa, sx, fx, da_out, dl_out, df_out,
               taps, ends):
    h = pl.program_id(0)
    cols, slab, _ = q1.shape
    rows = cols * slab

    @pl.when(h == 0)
    def _():
        frames_matrix(wfa, taps, ends)

    mean, scale, mult, first, second = norm_terms(mom1, gain1, tot, inv)
    zhat = (z1[...] - mean) * scale
    dz = mult * (q1[...] - spread(m[...], MIX) * (first + zhat * second))
    up, down = sooner(dz, clips), later(dz, clips)
    for k, v in enumerate((up, dz, down)):
        da_out[:, :, k * C_MID : (k + 1) * C_MID] = v[:, :, :C_MID].astype(bf16)
        df_out[:, :, k * 128 : (k + 1) * 128] = v[:, :, C_MID:].astype(bf16)
    dj = dot_nt(dzp[...].reshape(rows, C_IN), wp[...])
    for k in range(3):
        dj = dj + dot_nt(da_out[:, :, k * C_MID : (k + 1) * C_MID].reshape(rows, C_MID), wa[k])
    mask = spread(m[...], C_IN)
    dj = dj.reshape(cols, slab, C_JOIN)
    for w in range(cols):
        sx[:, w] = (dj[w, :, :C_IN] * mask).astype(bf16).reshape(slab // clips, clips, C_IN)
    dlat = dj[:, :, C_IN:].astype(bf16).astype(f32)
    dl_out[:, :, :C_LAT] = dlat.astype(bf16)
    dl_out[:, :, C_LAT:] = sooner(dlat, clips).astype(bf16)
    df = df_out[...].reshape(rows, 3 * 128)
    dl = dl_out[...].reshape(rows, 2 * C_LAT)
    total = gf[...].reshape(rows, WIDE_FAST).astype(f32) + dot(df[:, 128:256], taps[...])
    head = dot_nt(dl[:, :C_LAT], wl[2:5].reshape(3 * C_FAST, C_LAT))
    tail = dot_nt(dl[:, C_LAT:], wl[0:2].reshape(2 * C_FAST, C_LAT))
    blocks = [total[:, p * C_FAST : (p + 1) * C_FAST] for p in range(ALPHA)]
    for p in range(3):
        blocks[p] = blocks[p] + head[:, p * C_FAST : (p + 1) * C_FAST]
    for p in range(2):
        blocks[2 + p] = blocks[2 + p] + tail[:, p * C_FAST : (p + 1) * C_FAST]
    blocks[3] = blocks[3] + dot(df[:, :128], ends[0])
    blocks[0] = blocks[0] + dot(df[:, 256:], ends[1])
    blocks = [v.astype(bf16) for v in blocks]
    for w in range(cols):
        stacked = jnp.concatenate([v[w * slab : (w + 1) * slab] for v in blocks], axis=0)
        fx[:, w] = dot_tn(perm[...], stacked).astype(bf16).reshape(clips, slab, C_FAST)


def first_weights(x, f, da, dl, df, dwfc, dwfb, wa_out, wl_out, small_out):
    i = pl.program_id(0)
    n, slab, _ = x.shape
    rows = n * slab
    for k in range(3):
        wa_out[k] = dot_tn(x[...].reshape(rows, C_MID), da[:, :, k * C_MID : (k + 1) * C_MID].reshape(rows, C_MID)).astype(bf16)

    @pl.when(i == pl.num_programs(0) - 1)
    def _():
        fast = f[...].reshape(rows, WIDE_FAST)
        d = dl[...].reshape(rows, 2 * C_LAT)
        wl_out[2:5] = dot_tn(fast[:, : 3 * C_FAST], d[:, :C_LAT]).reshape(3, C_FAST, C_LAT).astype(bf16)
        wl_out[0:2] = dot_tn(fast[:, 2 * C_FAST :], d[:, C_LAT:]).reshape(2, C_FAST, C_LAT).astype(bf16)
        g = df[...].reshape(rows, 3 * 128)
        mid = dot_tn(g[:, 128:256], fast)
        sums = [jnp.zeros((C_FMID, C_FAST), f32) for _ in range(3)]
        for p in range(ALPHA):
            for s in range(max(p - 1, 0), min(p + 2, ALPHA)):
                sums[s - p + 1] += mid[p * C_FMID : (p + 1) * C_FMID, s * C_FAST : (s + 1) * C_FAST]
        sums[0] += dot_tn(g[:, :128], fast[:, 3 * C_FAST :])[:C_FMID]
        sums[2] += dot_tn(g[:, 256:], fast[:, :C_FAST])[3 * C_FMID :]
        small_out[...] = jnp.zeros_like(small_out)
        for k in range(3):
            small_out[k * C_FMID : (k + 1) * C_FMID] = sums[k].astype(bf16)
        small_out[3 * C_FMID : 4 * C_FMID] = dwfc[...].astype(bf16)
        for k in range(9):
            at = (4 + k) * C_FMID
            small_out[at : at + C_FMID, :C_FMID] = dwfb[k].astype(bf16)


UNIT = 512


def bit_of(axis, power):
    return lax.rem(lax.axis_index(axis) // (1 << power), 2)


def partner_of(axis, power, bit):
    where = {name: lax.axis_index(name) for name in ("clip", "ha", "wa")}
    where[axis] = where[axis] + (1 - 2 * bit) * (1 << power)
    return (where["clip"], where["ha"], where["wa"])


def stage_orders(n_clip, sets):
    rest = [("wa", 0)] + [("clip", b) for b in range(n_clip.bit_length() - 1)]
    turn, last = rest[:3], rest[3:]
    return [[("ha", 0)] + turn[s % len(turn) :] + turn[: s % len(turn)] + last for s in range(sets)]


def chunk_of(rows):
    best = 16
    for k in range(16, min(rows, 256) + 1, 16):
        if rows % k == 0:
            best = k
    return best


def land_plan(n_clip, sizes):
    stages = len(stage_orders(n_clip, 1)[0])
    starts, total = [], 0
    for size in sizes:
        starts.append(total)
        for _ in range(stages):
            size = size // 2 if size % 32 == 0 else size
            total += size
    return starts, total


def reduce_sets(n_clip, starts, sizes, mine, land, done, rs_send, rs_recv, ag_send, ag_recv):
    orders = stage_orders(n_clip, len(starts))
    stages = len(orders[0])
    low = [jnp.int32(v) for v in starts]
    size = list(sizes)
    at = land_plan(n_clip, sizes)[0]
    trail = [[] for _ in starts]
    sent = []

    def rows(ref, begin, count):
        return ref.at[pl.ds(pl.multiple_of(begin, 16), count)]

    def send(s, k):
        axis, power = orders[s][k]
        bit = bit_of(axis, power)
        halve = size[s] % 32 == 0
        count = size[s] // 2 if halve else size[s]
        begin = low[s] + (1 - bit) * count if halve else low[s]
        copy = pltpu.make_async_remote_copy(
            src_ref=rows(mine, begin, count), dst_ref=rows(land, at[s], count),
            send_sem=rs_send.at[s, k], recv_sem=rs_recv.at[s, k],
            device_id=partner_of(axis, power, bit), device_id_type=MESH,
        )
        copy.start()
        trail[s].append((copy, low[s], count, halve, axis, power, bit, at[s]))
        if halve:
            low[s] = low[s] + bit * count
            size[s] = count
        at[s] += count

    def gather(s, k):
        copy, _, count, halve, axis, power, bit, begin = trail[s][k]
        copy.wait_recv()
        if not halve:
            copy.wait_send()
        step = chunk_of(count)

        def add(i, carry):
            own = pl.ds(pl.multiple_of(low[s] + i * step, 16), step)
            came = pl.ds(pl.multiple_of(begin + i * step, 16), step)
            mine[own, :] = (mine[own, :].astype(f32) + land[came, :].astype(f32)).astype(bf16)
            return carry

        lax.fori_loop(0, count // step, add, 0)
        if halve:
            sent.append(copy)

    for s in range(len(starts)):
        send(s, 0)
    for k in range(stages):
        for s in range(len(starts)):
            gather(s, k)
            if k + 1 < stages:
                send(s, k + 1)
    for copy in sent:
        copy.wait_send()

    for s in range(len(starts)):
        step = chunk_of(size[s])

        def keep(i, carry):
            own = pl.ds(pl.multiple_of(low[s] + i * step, 16), step)
            done[own, :] = mine[own, :]
            return carry

        lax.fori_loop(0, size[s] // step, keep, 0)

    copies = []
    pending = [None] * len(starts)

    def spread_out(s, k):
        _, before, count, halve, axis, power, bit, _ = trail[s][k]
        if not halve:
            return
        copy = pltpu.make_async_remote_copy(
            src_ref=rows(done, low[s], count), dst_ref=rows(done, low[s], count),
            send_sem=ag_send.at[s, k], recv_sem=ag_recv.at[s, k],
            device_id=partner_of(axis, power, bit), device_id_type=MESH,
        )
        copy.start()
        other = before + (1 - bit) * count
        pending[s] = pltpu.make_async_remote_copy(
            src_ref=rows(done, other, count), dst_ref=rows(done, other, count),
            send_sem=ag_send.at[s, k], recv_sem=ag_recv.at[s, k],
            device_id=partner_of(axis, power, bit), device_id_type=MESH,
        )
        low[s] = before
        copies.append(copy)

    for s in range(len(starts)):
        spread_out(s, stages - 1)
    for k in range(stages - 1, -1, -1):
        for s in range(len(starts)):
            if pending[s] is not None:
                pending[s].wait_recv()
                pending[s] = None
            if k > 0:
                spread_out(s, k - 1)
    for copy in copies:
        copy.wait_send()


def greet(n_clip):
    barrier = pltpu.get_barrier_semaphore()
    stages = stage_orders(n_clip, 1)[0]
    for axis, power in stages:
        bit = bit_of(axis, power)
        pl.semaphore_signal(barrier, inc=1, device_id=partner_of(axis, power, bit), device_id_type=MESH)
    pl.semaphore_wait(barrier, len(stages))


def weight_pieces(dws_rows):
    pieces = []
    row = 0
    for which, count in ((0, C_JOIN), (1, C_MID)):
        for b in range(C_IN // 256):
            pieces.append((row, count, which, (slice(None), slice(b * 256, (b + 1) * 256))))
            row += count
    for i in range(3):
        for j in range(3):
            pieces.append((row, C_MID, 2, (i, j)))
            row += C_MID
    for k in range(3):
        pieces.append((row, C_JOIN, 3, (k,)))
        row += C_JOIN
    for k in range(5):
        pieces.append((row, C_FAST, 4, (k,)))
        row += C_FAST
    return pieces, row


def reduce_weights(n_clip, starts, sizes, dwp, dwc, dwb, dwa, dwl, dws, done,
                   mine, land, rs_send, rs_recv, ag_send, ag_recv):
    sources = (dwp, dwc, dwb, dwa, dwl)
    pieces, row = weight_pieces(dws.shape[0])
    for begin, count, which, at in pieces:
        mine[begin : begin + count, :] = sources[which].at[at][...]
    half = dws.shape[0] // 2
    mine[row : row + half, :128] = dws[:half]
    mine[row : row + half, 128:] = dws[half:]
    end = row + half
    if end < mine.shape[0]:
        mine[end:, :] = jnp.zeros((mine.shape[0] - end, 256), bf16)
    greet(n_clip)
    reduce_sets(n_clip, starts, sizes, mine, land, done, rs_send, rs_recv, ag_send, ag_recv)


def unpack_weights(done, wp_out, wc_out, wb_out, wa_out, wl_out, ws_out):
    targets = (wp_out, wc_out, wb_out, wa_out, wl_out)
    pieces, row = weight_pieces(ws_out.shape[0])
    for begin, count, which, at in pieces:
        targets[which].at[at][...] = done[begin : begin + count, :].astype(f32)
    half = ws_out.shape[0] // 2
    ws_out[:half] = done[row : row + half, :128].astype(f32)
    ws_out[half:] = done[row : row + half, 128:].astype(f32)


def vmem_spec():
    return pl.BlockSpec(memory_space=pltpu.VMEM)


def shaped(shape, kind):
    return jax.ShapeDtypeStruct(shape, kind)


def run_reduce(ident, n_clip, arrays):
    total = sum(v.size for v in arrays) // 256
    units = -(-total // UNIT)
    share = [-(-units // 3), -(-(units - units // 3) // 2), units // 3]
    share[1] = units - share[0] - share[2]
    sizes = [v * UNIT for v in share]
    starts = [0, sizes[0], sizes[0] + sizes[1]]
    rows = units * UNIT
    land_rows = land_plan(n_clip, sizes)[1]
    stages = len(stage_orders(n_clip, 1)[0])
    sems = [pltpu.SemaphoreType.DMA((3, stages))] * 4
    vm = vmem_spec()
    done = pl.pallas_call(
        functools.partial(reduce_weights, n_clip, starts, sizes),
        in_specs=[vm] * len(arrays),
        out_specs=vm,
        out_shape=shaped((rows, 256), bf16),
        scratch_shapes=[pltpu.VMEM((v, 256), bf16) for v in (rows, land_rows)] + sems,
        compiler_params=pltpu.CompilerParams(
            collective_id=ident, has_side_effects=True, vmem_limit_bytes=60 * MIB
        ),
        name=f"reduce{ident}",
    )(*arrays)
    return pl.pallas_call(
        unpack_weights,
        in_specs=[vm],
        out_specs=(vm,) * len(arrays),
        out_shape=tuple(shaped(v.shape, f32) for v in arrays),
        compiler_params=params(60),
        name="unpack_weights",
    )(done)


def whole(shape):
    return pl.BlockSpec(shape, lambda h: (0,) * len(shape))


def per_line(shape):
    return pl.BlockSpec((None,) + tuple(shape), lambda h: (h,) + (0,) * len(shape))


def params(limit):
    return pltpu.CompilerParams(vmem_limit_bytes=60 * MIB)


def on_device(
    slow_input,
    fast_input,
    frame_counts,
    lateral_weight,
    slow_a_weight,
    slow_b_weight,
    slow_c_weight,
    slow_proj_weight,
    fast_a_weight,
    fast_b_weight,
    fast_c_weight,
    slow_gain,
    slow_shift,
    fast_gain,
    fast_shift,
    slow_cotangent,
    fast_cotangent,
):
    n_clip = lax.axis_size("clip")
    clips, frames, high, cols, _ = slow_input.shape
    slab = clips * frames
    own = lax.dynamic_slice_in_dim(frame_counts, lax.axis_index("clip") * clips, clips)
    row_t = jnp.arange(slab) // clips
    row_c = jnp.arange(slab) % clips
    real = row_t < own[row_c]
    m = jnp.broadcast_to(real.astype(f32)[:, None], (slab, 128))
    col_c = jnp.arange(ALPHA * slab) // (ALPHA * frames)
    col_f = jnp.arange(ALPHA * slab) % (ALPHA * frames)
    want_f = (ALPHA * row_t[None, :] + jnp.arange(ALPHA)[:, None]).reshape(-1)
    want_c = jnp.tile(row_c, ALPHA)
    perm = (
        (want_f[:, None] == col_f[None, :]) & (want_c[:, None] == col_c[None, :]) & jnp.tile(real, ALPHA)[:, None]
    ).astype(bf16)
    real_total = jnp.sum(frame_counts).astype(f32)
    weight = jnp.broadcast_to(
        (jnp.sum(frame_counts.reshape(n_clip, clips), axis=1).astype(f32) / real_total)[:, None, None], (n_clip, 1, 128)
    )
    inv = jnp.full((1, 128), 1.0, f32) / (real_total * (H * W))
    def mixed(slow, fast, k):
        lo = fast[k * C_FMID : (k + 1) * C_FMID]
        return jnp.concatenate([slow[k * C_MID : (k + 1) * C_MID], jnp.tile(lo, ALPHA)])[None]

    gain1, shift1 = mixed(slow_gain, fast_gain, 0), mixed(slow_shift, fast_shift, 0)
    gain2, shift2 = mixed(slow_gain, fast_gain, 1), mixed(slow_shift, fast_shift, 1)
    sgain, sshift = slow_gain[None, 2 * C_MID :], slow_shift[None, 2 * C_MID :]
    fgain, fshift = fast_gain[None, 2 * C_FMID :], fast_shift[None, 2 * C_FMID :]
    wfa = fast_a_weight.transpose(0, 2, 1)
    eye = jnp.eye(ALPHA, dtype=bf16)
    wfb = (eye[None, :, None, :, None] * fast_b_weight.reshape(9, 1, C_FMID, 1, C_FMID)).reshape(9, 128, 128)

    xs = slow_input.transpose(1, 2, 3, 0, 4)
    xf = fast_input.transpose(0, 2, 3, 1, 4)
    cot = slow_cotangent.transpose(1, 2, 3, 0, 4)
    fcot = fast_cotangent.transpose(0, 2, 3, 1, 4)
    def lines(c, kind):
        return shaped((high, cols, slab, c), kind)

    m_spec = whole((slab, 128))
    vm = vmem_spec()
    hbm = pl.BlockSpec(memory_space=pl.ANY)

    def early_line(shape):
        return pl.BlockSpec((None,) + tuple(shape), lambda i: (jnp.minimum(i, high - 1),) + (0,) * len(shape))

    def late_line(shape, begin):
        return pl.BlockSpec((None,) + tuple(shape), lambda i: (jnp.maximum(i - begin, 0),) + (0,) * len(shape))

    def slow_block(index):
        return pl.BlockSpec((frames, None, cols, clips, C_IN), lambda i: (0, index(i), 0, 0, 0))

    def fast_block(index):
        return pl.BlockSpec((clips, None, cols, ALPHA * frames, C_FAST), lambda i: (0, index(i), 0, 0, 0))

    def early(i):
        return jnp.minimum(i, high - 1)

    def after(begin):
        return lambda i: jnp.maximum(i - begin, 0)

    def remote(ident):
        return pltpu.CompilerParams(collective_id=ident, has_side_effects=True, vmem_limit_bytes=60 * MIB)

    rim_shapes = (shaped((cols, slab, MIX), f32), shaped((high, slab, MIX), f32), shaped((slab, MIX), f32))
    edge_scratch = [pltpu.VMEM((cols, slab, MIX), f32), pltpu.VMEM((high, slab, MIX), f32)]
    rims = rim_scratch(cols, slab)
    L1 = MIX + C_IN
    x, f, z1, zp, stp, base, mom1, row1, col1, corner1 = pl.pallas_call(
        functools.partial(first_pass, clips, n_clip),
        grid=(2 * high,),
        in_specs=[slow_block(early), fast_block(early)] + [vm] * 7,
        out_specs=(
            early_line((cols, slab, C_JOIN)), early_line((cols, slab, WIDE_FAST)), early_line((cols, slab, MIX)),
            late_line((cols, slab, C_IN), high), vm, vm, vm, vm, vm, vm,
        ),
        out_shape=(
            lines(C_JOIN, bf16), lines(WIDE_FAST, bf16), lines(MIX, f32), lines(C_IN, bf16), shaped((2, C_IN), f32),
            shaped((1, C_IN), f32), shaped((2, MIX), f32),
        ) + rim_shapes,
        scratch_shapes=[
            pltpu.VMEM((high, cols, slab, C_JOIN), bf16), pltpu.VMEM((128, WIDE_FAST), bf16),
            pltpu.VMEM((2, 128, C_FAST), bf16), pltpu.VMEM((1, L1), f32), pltpu.VMEM((1, L1), f32),
            pltpu.VMEM((1, L1), f32),
        ] + edge_scratch + exchange_scratch(n_clip, 2, MIX) + rims,
        compiler_params=remote(1),
        name="first_pass",
    )(xs, xf, m, perm, lateral_weight, slow_a_weight, slow_proj_weight, wfa, weight)

    a1, z2, mom2, zrow, zcol, zcorner, cot = pl.pallas_call(
        functools.partial(second_pass, n_clip),
        grid=(high + 1,),
        in_specs=[hbm] + [vm] * 11 + [slow_block(after(1))],
        out_specs=(vm, vm, vm, vm, vm, vm, late_line((cols, slab, C_IN), 1)),
        out_shape=(
            shaped((high + 2, cols + 2, slab, MIX), bf16), lines(MIX, f32), shaped((2, L1), f32),
        ) + rim_shapes + (lines(C_IN, bf16),),
        scratch_shapes=[
            pltpu.VMEM((high, cols, slab, MIX), f32), pltpu.SemaphoreType.DMA((high,)), pltpu.VMEM((1, MIX), f32),
            pltpu.VMEM((1, MIX), f32),
        ] + exchange_scratch(n_clip, 2, L1) + rims,
        compiler_params=remote(2),
        name="second_pass",
    )(z1, row1, col1, corner1, mom1, gain1, shift1, m, slow_b_weight, wfb, stp, weight, cot)

    L3 = C_IN + C_FAST
    a2, mom3, fcot = pl.pallas_call(
        functools.partial(third_pass, n_clip),
        grid=(2 * high,),
        in_specs=[early_line((cols, slab, MIX))] + [vm] * 7 + [fast_block(after(high)), vm],
        out_specs=(early_line((cols, slab, MIX)), vm, late_line((cols, slab, WIDE_FAST), high)),
        out_shape=(lines(MIX, bf16), shaped((2, L3), f32), lines(WIDE_FAST, bf16)),
        scratch_shapes=[pltpu.VMEM((128, WIDE_FAST), bf16)] + [pltpu.VMEM((1, L3), f32)] * 3
        + exchange_scratch(n_clip, 2, L3),
        compiler_params=remote(3),
        name="third_pass",
    )(z2, mom2, gain2, shift2, m, slow_c_weight, fast_c_weight, weight, fcot, perm)

    L4 = 3 * C_IN + 2 * C_FAST
    so, fo, gs, gf, tot4 = pl.pallas_call(
        functools.partial(fourth_pass, n_clip, clips),
        grid=(2 * high,),
        in_specs=[early_line((cols, slab, MIX)), early_line((cols, slab, C_IN))] + [vm] * 7 + [
            early_line((cols, slab, C_IN)), early_line((cols, slab, WIDE_FAST)), early_line((cols, slab, WIDE_FAST)),
        ] + [vm] * 5,
        out_specs=(
            slow_block(after(high)), fast_block(after(high)), early_line((cols, slab, C_IN)),
            early_line((cols, slab, WIDE_FAST)), vm,
        ),
        out_shape=(
            shaped(xs.shape, bf16), shaped(xf.shape, bf16), lines(C_IN, f32), lines(WIDE_FAST, f32),
            shaped((1, L4), f32),
        ),
        scratch_shapes=[
            pltpu.VMEM((high, cols, slab, C_IN), bf16), pltpu.VMEM((high, cols, slab, WIDE_FAST), bf16),
            pltpu.VMEM((1, L4), f32), pltpu.VMEM((128, WIDE_FAST), bf16),
        ] + exchange_scratch(n_clip, 1, L4),
        compiler_params=remote(4),
        name="fourth_pass",
    )(
        a2, zp, base, mom2, mom3, sgain, sshift, fgain, fshift, cot, fcot, f, m, perm, slow_c_weight, fast_c_weight, weight,
    )

    n = high * cols

    def flat(v):
        return v.reshape((n,) + v.shape[2:])

    steps = C_JOIN // C_MID
    dzp, q2, tot5, qrow, qcol, qcorner, dwp, dwc, dwfc = pl.pallas_call(
        functools.partial(fifth_pass, n_clip),
        grid=(high + steps,),
        in_specs=[
            early_line((cols, slab, C_IN)), early_line((cols, slab, WIDE_FAST)), early_line((cols, slab, MIX)),
            early_line((cols, slab, C_IN)), vm, early_line((cols, slab, MIX)),
        ] + [vm] * 11 + [pl.BlockSpec((n, slab, C_MID), lambda i: (0, 0, jnp.maximum(i - high, 0))), vm],
        out_specs=(
            early_line((cols, slab, C_IN)), early_line((cols, slab, MIX)), vm, vm, vm, vm,
            pl.BlockSpec((C_MID, C_IN), lambda i: (jnp.maximum(i - high, 0), 0)), vm, vm,
        ),
        out_shape=(lines(C_IN, bf16), lines(MIX, f32), shaped((1, 2 * MIX), f32)) + rim_shapes + (
            shaped((C_JOIN, C_IN), bf16), shaped((C_MID, C_IN), bf16), shaped((C_FMID, C_FAST), f32),
        ),
        scratch_shapes=[
            pltpu.VMEM((high, cols, slab, C_IN), bf16), pltpu.VMEM((high, cols, slab, C_IN), bf16),
            pltpu.VMEM((high, cols, slab, WIDE_FAST), bf16), pltpu.VMEM((high, cols, slab, MIX), bf16),
            pltpu.VMEM((1, 2 * MIX), f32), pltpu.VMEM((128, WIDE_FAST), bf16),
        ] + edge_scratch + exchange_scratch(n_clip, 1, 2 * MIX) + rims,
        compiler_params=remote(5),
        name="fifth_pass",
    )(
        gs, gf, a2, zp, base, z2, mom2, mom3, tot4, inv, sgain, fgain, gain2, shift2, m, slow_c_weight, fast_c_weight,
        flat(x), weight,
    )

    q1, tot6, dwb, dwfb = pl.pallas_call(
        functools.partial(sixth_pass, n_clip),
        grid=(10,),
        in_specs=[hbm] * 4 + [vm] * 17,
        out_specs=(
            vm, vm, pl.BlockSpec((None, None, C_MID, C_MID), lambda i: (jnp.maximum(i - 1, 0) // 3, lax.rem(jnp.maximum(i - 1, 0), 3), 0, 0)),
            vm,
        ),
        out_shape=(
            lines(MIX, f32), shaped((1, 2 * MIX), f32), shaped((3, 3, C_MID, C_MID), bf16),
            shaped((9, C_FMID, C_FMID), f32),
        ),
        scratch_shapes=[pltpu.VMEM((high + 2, cols + 2, slab, MIX), bf16)]
        + [pltpu.VMEM((high, cols, slab, MIX), f32)] * 3
        + [pltpu.VMEM((high + 2, cols + 2, slab, MIX), bf16)]
        + [pltpu.SemaphoreType.DMA((high,))] * 3
        + [pltpu.SemaphoreType.DMA((1,)), pltpu.VMEM((1, 2 * MIX), f32)]
        + exchange_scratch(n_clip, 1, 2 * MIX),
        compiler_params=remote(6),
        name="sixth_pass",
    )(
        q2, z2, z1, a1, qrow, qcol, qcorner, zrow, zcol, zcorner, mom1, mom2, tot5, inv, gain1, shift1, gain2, m,
        slow_b_weight, wfb, weight,
    )

    perm_spec = whole((ALPHA * slab, ALPHA * slab))
    sx, fx, da, dl, df = pl.pallas_call(
        functools.partial(first_back, clips),
        grid=(high,),
        in_specs=[
            per_line((cols, slab, MIX)), per_line((cols, slab, MIX)), whole((2, MIX)), whole((1, 2 * MIX)),
            whole((1, 128)), whole((1, MIX)), m_spec, perm_spec, per_line((cols, slab, C_IN)),
            per_line((cols, slab, WIDE_FAST)), whole((5, C_FAST, C_LAT)), whole((3, C_JOIN, C_MID)),
            whole((C_JOIN, C_IN)), whole((3, C_FMID, C_FAST)),
        ],
        out_specs=(
            slow_block(early), fast_block(early), per_line((cols, slab, 3 * C_MID)), per_line((cols, slab, 2 * C_LAT)),
            per_line((cols, slab, 3 * 128)),
        ),
        out_shape=(
            shaped(xs.shape, bf16), shaped(xf.shape, bf16), lines(3 * C_MID, bf16), lines(2 * C_LAT, bf16),
            lines(3 * 128, bf16),
        ),
        scratch_shapes=[pltpu.VMEM((128, WIDE_FAST), bf16), pltpu.VMEM((2, 128, C_FAST), bf16)],
        compiler_params=params(40),
        name="first_back",
    )(q1, z1, mom1, tot6, inv, gain1, m, perm, dzp, gf, lateral_weight, slow_a_weight, slow_proj_weight, wfa)

    dwa, dwl, dws = pl.pallas_call(
        first_weights,
        grid=(C_JOIN // C_MID,),
        in_specs=[
            pl.BlockSpec((n, slab, C_MID), lambda i: (0, 0, i)), whole((n, slab, WIDE_FAST)),
            whole((n, slab, 3 * C_MID)), whole((n, slab, 2 * C_LAT)), whole((n, slab, 3 * 128)),
            whole((C_FMID, C_FAST)), whole((9, C_FMID, C_FMID)),
        ],
        out_specs=(
            pl.BlockSpec((3, C_MID, C_MID), lambda i: (0, i, 0)), whole((5, C_FAST, C_LAT)), whole((512, C_FAST)),
        ),
        out_shape=(
            shaped((3, C_JOIN, C_MID), bf16), shaped((5, C_FAST, C_LAT), bf16), shaped((512, C_FAST), bf16),
        ),
        compiler_params=params(48),
        name="first_weights",
    )(flat(x), flat(f), flat(da), flat(dl), flat(df), dwfc, dwfb)

    dwp, dwc, dwb, dwa, dwl, dws = run_reduce(7, n_clip, (dwp, dwc, dwb, dwa, dwl, dws))
    dwfa = dws[: 3 * C_FMID].reshape(3, C_FMID, C_FAST)
    dwfc = dws[3 * C_FMID : 4 * C_FMID]
    dwfb = dws[4 * C_FMID : 13 * C_FMID, :C_FMID]

    def joined_sums(k):
        first = [tot6[0, k * MIX : (k + 1) * MIX], tot5[0, k * MIX : (k + 1) * MIX]]
        last = tot4[0, :C_IN] if k == 0 else tot4[0, C_IN : 2 * C_IN]
        proj = tot4[0, :C_IN] if k == 0 else tot4[0, 2 * C_IN : 3 * C_IN]
        at = 3 * C_IN + k * C_FAST
        slow = jnp.concatenate([first[0][:C_MID], first[1][:C_MID], last, proj])
        lo = C_MID + C_FMID
        fast = jnp.concatenate([first[0][C_MID:lo], first[1][C_MID:lo], tot4[0, at : at + C_FAST]])
        return slow, fast

    slow_shift_grad, fast_shift_grad = joined_sums(0)
    slow_gain_grad, fast_gain_grad = joined_sums(1)
    return (
        so.transpose(3, 0, 1, 2, 4),
        fo.transpose(0, 3, 1, 2, 4),
        sx.transpose(3, 0, 1, 2, 4),
        fx.transpose(0, 3, 1, 2, 4),
        dwl,
        dwa,
        dwb,
        dwc,
        dwp,
        dwfa.transpose(0, 2, 1),
        dwfb.reshape(3, 3, C_FMID, C_FMID),
        dwfc,
        slow_gain_grad,
        slow_shift_grad,
        fast_gain_grad,
        fast_shift_grad,
    )


def solution(mesh):
    tiles = P("clip", None, "ha", "wa", None)
    return jax.shard_map(
        on_device,
        mesh=mesh,
        in_specs=(tiles, tiles) + (P(),) * 13 + (tiles, tiles),
        out_specs=(tiles,) * 4 + (P(),) * 12,
        check_vma=False,
    )
```

```python
import functools

import jax
import jax.numpy as jnp
from jax import lax
from jax.experimental import pallas as pl
from jax.experimental.pallas import tpu as pltpu
from jax.sharding import PartitionSpec as P

ALPHA = 4
H = 14
W = 14
C_IN = 1024
C_LAT = 256
C_MID = 256
C_FAST = 128
C_FMID = 32
C_JOIN = C_IN + C_LAT
MIX = C_MID + ALPHA * C_FMID
WIDE_FAST = ALPHA * C_FAST

eps_norm = 1e-05
f32 = jnp.float32
bf16 = jnp.bfloat16
MESH = pl.DeviceIdType.MESH
MIB = 1 << 20


def dot(a, b):
    return lax.dot_general(a, b, (((1,), (0,)), ((), ())), preferred_element_type=f32)


def dot_nt(a, b):
    return lax.dot_general(a, b, (((1,), (1,)), ((), ())), preferred_element_type=f32)


def dot_tn(a, b):
    return lax.dot_general(a, b, (((0,), (0,)), ((), ())), preferred_element_type=f32)


def sigmoid(v):
    return 0.5 + 0.5 * jnp.tanh(0.5 * v)


def later(y, clips):
    return jnp.concatenate([jnp.zeros_like(y[:, :clips]), y[:, : y.shape[1] - clips]], axis=1)


def sooner(y, clips):
    return jnp.concatenate([y[:, clips:], jnp.zeros_like(y[:, :clips])], axis=1)


def rows_sum(v):
    return jnp.sum(jnp.sum(v, axis=0), axis=0, keepdims=True)


def phase_sum(v):
    out = v
    for k in range(1, ALPHA):
        out = out + pltpu.roll(v, k * C_FMID, 1)
    return out


def block_sum(v):
    return sum(v[:, p * C_FAST : (p + 1) * C_FAST] for p in range(ALPHA))


def spread(mask, width):
    return jnp.tile(mask, (1, width // 128))


def frames_matrix(wfa_ref, out_ref, ends_ref):
    out_ref[...] = jnp.zeros_like(out_ref)
    ends_ref[...] = jnp.zeros_like(ends_ref)
    for p in range(ALPHA):
        for s in range(max(p - 1, 0), min(p + 2, ALPHA)):
            out_ref[p * C_FMID : (p + 1) * C_FMID, s * C_FAST : (s + 1) * C_FAST] = wfa_ref[s - p + 1]
    ends_ref[0, 0:C_FMID] = wfa_ref[0]
    ends_ref[1, 3 * C_FMID :] = wfa_ref[2]


def expand_matrix(wfc_ref, out_ref):
    out_ref[...] = jnp.zeros_like(out_ref)
    for p in range(ALPHA):
        out_ref[p * C_FMID : (p + 1) * C_FMID, p * C_FAST : (p + 1) * C_FAST] = wfc_ref[...]


class Exchange:
    def __init__(self, n_clip, moments, refs, rim_refs=None):
        self.n = n_clip
        self.moments = moments
        self.part, self.near, self.mid, self.far, self.near_send, self.near_recv, self.far_send, self.far_recv = refs
        self.clip, self.ha, self.wa = lax.axis_index("clip"), lax.axis_index("ha"), lax.axis_index("wa")
        self.me = 2 * self.ha + self.wa
        self.peers = [(1 - self.ha, self.wa), (self.ha, 1 - self.wa), (1 - self.ha, 1 - self.wa)]
        self.others = [lax.rem(self.clip + d, n_clip) for d in range(1, n_clip)]
        if rim_refs is not None:
            self.packs, self.lands, self.rim_send, self.rim_recv = rim_refs

    def signal(self):
        barrier = pltpu.get_barrier_semaphore()
        for a, b in self.peers:
            pl.semaphore_signal(barrier, inc=1, device_id=(self.clip, a, b), device_id_type=MESH)
        for other in self.others:
            pl.semaphore_signal(barrier, inc=1, device_id=(other, self.ha, self.wa), device_id_type=MESH)

    def meet(self):
        pl.semaphore_wait(pltpu.get_barrier_semaphore(), 3 + self.n - 1)

    def near_copy(self, k, slot):
        a, b = self.peers[k]
        return pltpu.make_async_remote_copy(
            src_ref=self.part, dst_ref=self.near.at[slot], send_sem=self.near_send.at[k],
            recv_sem=self.near_recv.at[slot], device_id=(self.clip, a, b), device_id_type=MESH,
        )

    def far_copy(self, d, slot):
        return pltpu.make_async_remote_copy(
            src_ref=self.mid, dst_ref=self.far.at[slot], send_sem=self.far_send.at[d],
            recv_sem=self.far_recv.at[slot], device_id=(self.others[d], self.ha, self.wa), device_id_type=MESH,
        )

    def rim_copy(self, k):
        a, b = self.peers[k]
        size = 1 if k == 2 else self.packs.shape[1]
        return pltpu.make_async_remote_copy(
            src_ref=self.packs.at[k, pl.ds(0, size)], dst_ref=self.lands.at[k, pl.ds(0, size)],
            send_sem=self.rim_send.at[k], recv_sem=self.rim_recv.at[k], device_id=(self.clip, a, b),
            device_id_type=MESH,
        )

    def send_near(self):
        for k in range(3):
            self.near_copy(k, self.me).start()
        self.near[self.me] = self.part[...]

    def send_rims(self, line, side):
        count = self.packs.shape[1]
        centre = self.part[0:1, :MIX] if self.moments else jnp.zeros((1, MIX), f32)
        self.packs[0] = (line[...] - centre).astype(bf16)
        self.packs[1] = (side[...] - centre).astype(bf16)
        self.packs[2, 0] = self.packs[0, (count - 1) * (1 - self.wa)]
        for k in range(3):
            self.rim_copy(k).start()

    def send_far(self):
        for k, (a, b) in enumerate(self.peers):
            self.near_copy(k, 2 * a + b).wait_recv()
        near = self.near
        if self.moments:
            mean = (near[0, 0:1] + near[1, 0:1] + near[2, 0:1] + near[3, 0:1]) * 0.25
            self.mid[0:1] = mean
            self.mid[1:2] = sum(near[k, 1:2] + (near[k, 0:1] - mean) ** 2 for k in range(4)) * 0.25
        else:
            self.mid[...] = near[0] + near[1] + near[2] + near[3]
        for d in range(self.n - 1):
            self.far_copy(d, self.clip).start()
        self.far[self.clip] = self.mid[...]

    def finish(self, out, weight):
        for d, other in enumerate(self.others):
            self.far_copy(d, other).wait_recv()
        width = out.shape[1]
        far = self.far
        if self.moments:
            mean = sum(far[k, 0:1] * spread(weight[k], width) for k in range(self.n))
            out[0:1] = mean
            out[1:2] = sum((far[k, 1:2] + (far[k, 0:1] - mean) ** 2) * spread(weight[k], width) for k in range(self.n))
        else:
            out[...] = sum(far[k] for k in range(self.n))
        for k in range(3):
            self.near_copy(k, self.me).wait_send()
        for d in range(self.n - 1):
            self.far_copy(d, self.clip).wait_send()

    def finish_rims(self, rims):
        for k, (a, b) in enumerate(self.peers):
            self.rim_copy(k).wait_recv()
            centre = self.near[2 * a + b, 0:1, :MIX] if self.moments else jnp.zeros((1, MIX), f32)
            land = self.lands[k, 0] if k == 2 else self.lands[k]
            rims[k][...] = land.astype(f32) + centre
        for k in range(3):
            self.rim_copy(k).wait_send()


def exchange_scratch(n_clip, count, width):
    return [
        pltpu.VMEM((count, width), f32),
        pltpu.VMEM((4, count, width), f32),
        pltpu.VMEM((count, width), f32),
        pltpu.VMEM((n_clip, count, width), f32),
        pltpu.SemaphoreType.DMA((3,)),
        pltpu.SemaphoreType.DMA((4,)),
        pltpu.SemaphoreType.DMA((n_clip,)),
        pltpu.SemaphoreType.DMA((n_clip,)),
    ]


def rim_scratch(side, slab):
    return [
        pltpu.VMEM((3, side, slab, MIX), bf16),
        pltpu.VMEM((3, side, slab, MIX), bf16),
        pltpu.SemaphoreType.DMA((3,)),
        pltpu.SemaphoreType.DMA((3,)),
    ]


def first_pass(clips, n_clip, xs, xf, m, perm, wl, wa, wp, wfa, weight,
               x_out, f_out, z_out, zp_out, st_out, base_out, mom, row, col, corner,
               keep, taps, ends, base, one, two, line, side, *refs):
    i = pl.program_id(0)
    cols = xs.shape[1]
    slab = m.shape[0]
    rows = cols * slab
    high = keep.shape[0]
    ex = Exchange(n_clip, True, refs[:8], refs[8:])
    here = cols * jnp.sum(m[...], axis=0, keepdims=True)
    count = high * here

    @pl.when(i == 0)
    def _():
        ex.signal()
        frames_matrix(wfa, taps, ends)

    @pl.when(i < high)
    def _():
        mask_in = spread(m[...], C_IN).astype(bf16)
        for w in range(cols):
            keep[i, w, :, :C_IN] = xs[:, w].reshape(slab, C_IN) * mask_in
            phases = dot(perm[...], xf[:, w].reshape(ALPHA * slab, C_FAST)).astype(bf16)
            for p in range(ALPHA):
                f_out[w, :, p * C_FAST : (p + 1) * C_FAST] = phases[p * slab : (p + 1) * slab]
        fast = f_out[...].reshape(rows, WIDE_FAST)
        lat = dot(fast[:, : 3 * C_FAST], wl[2:5].reshape(3 * C_FAST, C_LAT)).reshape(cols, slab, C_LAT)
        back = dot(fast[:, 2 * C_FAST :], wl[0:2].reshape(2 * C_FAST, C_LAT)).reshape(cols, slab, C_LAT)
        keep[i, :, :, C_IN:] = (lat + later(back, clips)).astype(bf16)
        x_out[...] = keep[i]
        joined = keep[i].reshape(rows, C_JOIN)
        za = dot(joined, wa[1]).reshape(cols, slab, C_MID)
        za = za + later(dot(joined, wa[0]).reshape(cols, slab, C_MID), clips)
        za = za + sooner(dot(joined, wa[2]).reshape(cols, slab, C_MID), clips)
        fa = dot_nt(fast, taps[...]).reshape(cols, slab, 128)
        fa = fa + later(dot_nt(fast[:, 3 * C_FAST :], ends[0]).reshape(cols, slab, 128), clips)
        fa = fa + sooner(dot_nt(fast[:, :C_FAST], ends[1]).reshape(cols, slab, 128), clips)
        z_out[:, :, :C_MID] = za
        z_out[:, :, C_MID:] = fa
        keep_rims(ex, i, high, z_out, line, side)
        add_moments(i == 0, ((0, za, 0), (C_MID, fa, 1)), m, here, base, one, two)

    @pl.when(i == high)
    def _():
        finish_moments(ex.part, base[...], one[...], two[...], count, ((0, C_MID, 0), (C_MID, 128, 1)))
        ex.meet()
        ex.send_near()
        ex.send_rims(line, side)

    @pl.when(i == high + 2)
    def _():
        ex.send_far()

    @pl.when(i >= high)
    def _():
        joined = keep[i - high].reshape(rows, C_JOIN)
        zp = dot(joined, wp[...]).reshape(cols, slab, C_IN)
        add_moments(i == high, ((MIX, zp, 0),), m, here, base, one, two)
        zp_out[...] = (zp - base[:, MIX:]).astype(bf16)

    @pl.when(i == 2 * high - 1)
    def _():
        s1 = one[:, MIX:] / spread(count, C_IN)
        st_out[0:1] = base[:, MIX:] + s1
        st_out[1:2] = two[:, MIX:] / spread(count, C_IN) - s1 * s1
        base_out[...] = base[:, MIX:]
        ex.finish(mom, weight)
        ex.finish_rims((row, col, corner))


def keep_rims(ex, i, high, block, line, side):
    side[i] = block[(block.shape[0] - 1) * (1 - ex.wa)]

    @pl.when(i == (high - 1) * (1 - ex.ha))
    def _():
        line[...] = block[...]


def add_moments(first, parts, m, here, base, one, two):
    @pl.when(first)
    def _():
        for at, z, fast in parts:
            width = z.shape[-1]
            mean = rows_sum(z * spread(m[...], width)) / spread(here, width)
            if fast:
                mean = phase_sum(mean) * 0.25
            base[:, at : at + width] = mean
            one[:, at : at + width] = jnp.zeros((1, width), f32)
            two[:, at : at + width] = jnp.zeros((1, width), f32)

    for at, z, _ in parts:
        width = z.shape[-1]
        off = (z - base[:, at : at + width]) * spread(m[...], width)
        one[:, at : at + width] += rows_sum(off)
        two[:, at : at + width] += rows_sum(off * off)


def finish_moments(st, base, one, two, count, parts):
    for at, width, fast in parts:
        s1 = one[:, at : at + width]
        s2 = two[:, at : at + width]
        if fast:
            s1 = phase_sum(s1) * 0.25
            s2 = phase_sum(s2) * 0.25
        n = spread(count.astype(f32), width)
        s1 = s1 / n
        st[0:1, at : at + width] = base[:, at : at + width] + s1
        st[1:2, at : at + width] = s2 / n - s1 * s1


def affine(moments, gain, shift, at, width):
    mean = moments[0:1, at : at + width]
    scale = lax.rsqrt(moments[1:2, at : at + width] + eps_norm)
    return mean, scale, gain, shift


def second_pass(n_clip, z1_hbm, row, col, corner, mom, mids, m, wb, wfb, stp, weight, cot,
                a_out, z_out, mom_out, zrow, zcol, zcorner, cot_out, z1, z1_sem, one, two, *refs):
    i = pl.program_id(0)
    high, cols, slab, _ = z1.shape
    rows = cols * slab
    ex = Exchange(n_clip, True, refs[:8], refs[8:])

    def fetch(h):
        return pltpu.make_async_copy(z1_hbm.at[h], z1.at[h], z1_sem.at[h])

    @pl.when(i == 0)
    def _():
        for h in range(high):
            fetch(h).start()
        ex.signal()
        mean, scale, g, b = affine(mom, mids[0], mids[1], 0, MIX)
        mult = scale * g
        mask = spread(m[...], MIX)

        def act(z):
            v = (z - mean) * mult + b
            return (v * sigmoid(v) * mask).astype(bf16)

        far = high + 1
        a_out[far * ex.ha] = jnp.zeros((cols + 2, slab, MIX), bf16)
        a_out[:, far * ex.wa] = jnp.zeros((high + 2, slab, MIX), bf16)
        a_out[far * (1 - ex.ha), 1 : 1 + cols] = act(row[...])
        a_out[1 : 1 + high, far * (1 - ex.wa)] = act(col[...])
        a_out[far * (1 - ex.ha), far * (1 - ex.wa)] = act(corner[...])

        def fill(h, carry):
            fetch(h).wait()
            a_out[h + 1, 1 : 1 + cols] = act(z1[h])
            return carry

        lax.fori_loop(0, high, fill, 0)

        def space(h, carry):
            slow = jnp.zeros((rows, C_MID), f32)
            fast = jnp.zeros((rows, 128), f32)
            for a in range(3):
                for c in range(3):
                    v = a_out[h + a, c : c + cols].reshape(rows, MIX)
                    slow = slow + dot(v[:, :C_MID], wb[a, c])
                    fast = fast + dot(v[:, C_MID:], wfb[3 * a + c])
            z_out[h, :, :, :C_MID] = slow.reshape(cols, slab, C_MID)
            z_out[h, :, :, C_MID:] = fast.reshape(cols, slab, 128)
            return carry

        lax.fori_loop(0, high, space, 0)
        here = cols * jnp.sum(m[...], axis=0, keepdims=True)
        base = rows_sum(z_out[0] * mask) / spread(here, MIX)
        base = jnp.concatenate([base[:, :C_MID], phase_sum(base[:, C_MID:]) * 0.25], axis=1)
        one[...] = jnp.zeros_like(one)
        two[...] = jnp.zeros_like(two)

        def gather(h, carry):
            off = (z_out[h] - base) * mask
            one[...] += rows_sum(off)
            two[...] += rows_sum(off * off)
            return carry

        lax.fori_loop(0, high, gather, 0)
        finish_moments(ex.part, base, one[...], two[...], high * here, ((0, C_MID, 0), (C_MID, 128, 1)))
        ex.part[:, MIX:] = stp[...]
        ex.meet()
        ex.send_near()
        ex.send_rims(z_out.at[(high - 1) * (1 - ex.ha)], z_out.at[:, (cols - 1) * (1 - ex.wa)])

    @pl.when(i == 3)
    def _():
        ex.send_far()

    @pl.when(i > 0)
    def _():
        for w in range(cols):
            cot_out[w] = cot[:, w].reshape(slab, C_IN)

    @pl.when(i == high)
    def _():
        ex.finish(mom_out, weight)
        ex.finish_rims((zrow, zcol, zcorner))


def third_pass(n_clip, z2, mom, mids, m, wc, wfc, weight, fcot, perm,
               a_out, mom_out, fcot_out, big, base, one, two, *refs):
    i = pl.program_id(0)
    high = pl.num_programs(0) // 2
    cols, slab, _ = z2.shape
    rows = cols * slab
    ex = Exchange(n_clip, True, refs)
    here = cols * jnp.sum(m[...], axis=0, keepdims=True)

    @pl.when(i == 0)
    def _():
        ex.signal()
        expand_matrix(wfc, big)

    @pl.when(i < high)
    def _():
        mean, scale, g, b = affine(mom, mids[2], mids[3], 0, MIX)
        v = (z2[...] - mean) * (scale * g) + b
        a_out[...] = (v * sigmoid(v) * spread(m[...], MIX)).astype(bf16)
        a2 = a_out[...].reshape(rows, MIX)
        zc = dot(a2[:, :C_MID], wc[...]).reshape(cols, slab, C_IN)
        fc = dot(a2[:, C_MID:], big[...]).reshape(cols, slab, WIDE_FAST)

        @pl.when(i == 0)
        def _():
            base[:, :C_IN] = rows_sum(zc * spread(m[...], C_IN)) / spread(here, C_IN)
            base[:, C_IN:] = block_sum(rows_sum(fc * spread(m[...], WIDE_FAST))) / (4.0 * here)
            one[...] = jnp.zeros_like(one)
            two[...] = jnp.zeros_like(two)

        off = (zc - base[:, :C_IN]) * spread(m[...], C_IN)
        one[:, :C_IN] += rows_sum(off)
        two[:, :C_IN] += rows_sum(off * off)
        off = (fc - jnp.tile(base[:, C_IN:], (1, ALPHA))) * spread(m[...], WIDE_FAST)
        one[:, C_IN:] += block_sum(rows_sum(off)) * 0.25
        two[:, C_IN:] += block_sum(rows_sum(off * off)) * 0.25

    @pl.when(i == high)
    def _():
        finish_moments(ex.part, base[...], one[...], two[...], high * here, ((0, C_IN + C_FAST, 0),))
        ex.meet()
        ex.send_near()

    @pl.when(i == high + 2)
    def _():
        ex.send_far()

    @pl.when(i >= high)
    def _():
        for w in range(cols):
            phases = dot(perm[...], fcot[:, w].reshape(ALPHA * slab, C_FAST)).astype(bf16)
            for p in range(ALPHA):
                fcot_out[w, :, p * C_FAST : (p + 1) * C_FAST] = phases[p * slab : (p + 1) * slab]

    @pl.when(i == 2 * high - 1)
    def _():
        ex.finish(mom_out, weight)


def fourth_pass(n_clip, clips, a2, zp, base, mom2, mom3, sgain, sshift, fends, cot, fcot, fast_in, m, perm, wc,
                wfc, weight, so, fo, gs, gf, tot, so_keep, fo_keep, sums, big, *refs):
    i = pl.program_id(0)
    high = pl.num_programs(0) // 2
    cols, slab, _ = a2.shape
    ex = Exchange(n_clip, False, refs)

    @pl.when(i == 0)
    def _():
        ex.signal()
        expand_matrix(wfc, big)
        sums[...] = jnp.zeros_like(sums)

    def tile_sum(v):
        return jnp.sum(v.reshape(slab // 8, 8, v.shape[-1]), axis=0)

    @pl.when(i < high)
    def _():
        mask = spread(m[...], C_IN)
        mask_f = spread(m[...], WIDE_FAST)
        mean_c = mom3[0:1, :C_IN]
        scale_c = lax.rsqrt(mom3[1:2, :C_IN] + eps_norm)
        mean_p = mom2[0:1, MIX:] - base[...]
        scale_p = lax.rsqrt(mom2[1:2, MIX:] + eps_norm)
        mean_f = jnp.tile(mom3[0:1, C_IN:], (1, ALPHA))
        scale_f = jnp.tile(lax.rsqrt(mom3[1:2, C_IN:] + eps_norm), (1, ALPHA))
        mid, far = 2 * C_MID, 2 * C_MID + C_IN
        gain_c, gain_p = sgain[:, mid:far], sgain[:, far:]
        shift_cp = sshift[:, mid:far] + sshift[:, far:]
        gain_f = jnp.tile(fends[0], (1, ALPHA))
        shift_f = jnp.tile(fends[1], (1, ALPHA))
        totals = [jnp.zeros((8, C_IN), f32)] * 3 + [jnp.zeros((8, WIDE_FAST), f32)] * 2
        for w in range(cols):
            zc = (dot(a2[w, :, :C_MID], wc[...]) - mean_c) * scale_c
            zq = (zp[w].astype(f32) - mean_p) * scale_p
            ps = gain_c * zc + gain_p * zq + shift_cp
            sig = sigmoid(ps)
            so_keep[i, w] = (ps * sig * mask).astype(bf16)
            back = cot[w].astype(f32) * (sig * (1.0 + ps * (1.0 - sig)) * mask)
            gs[w] = back
            totals[0] += tile_sum(back)
            totals[1] += tile_sum(back * zc)
            totals[2] += tile_sum(back * zq)
            fc = (dot(a2[w, :, C_MID:], big[...]) - mean_f) * scale_f
            pf = gain_f * fc + shift_f + fast_in[w].astype(f32)
            sig = sigmoid(pf)
            fo_keep[i, w] = (pf * sig).astype(bf16)
            fback = fcot[w].astype(f32) * (sig * (1.0 + pf * (1.0 - sig)))
            gf[w] = fback
            totals[3] += tile_sum(fback)
            totals[4] += tile_sum(fback * fc)
        for k in range(3):
            sums[:, k * C_IN : (k + 1) * C_IN] += jnp.sum(totals[k], axis=0, keepdims=True)
        for k in range(2):
            at = 3 * C_IN + k * C_FAST
            sums[:, at : at + C_FAST] += block_sum(jnp.sum(totals[3 + k], axis=0, keepdims=True))

    @pl.when(i == high)
    def _():
        ex.part[...] = sums[...]
        ex.meet()
        ex.send_near()

    @pl.when(i == high + 2)
    def _():
        ex.send_far()

    @pl.when(i >= high)
    def _():
        for w in range(cols):
            so[:, w] = so_keep[i - high, w].reshape(slab // clips, clips, C_IN)
            wide = fo_keep[i - high, w]
            stacked = jnp.concatenate([wide[:, p * C_FAST : (p + 1) * C_FAST] for p in range(ALPHA)], axis=0)
            fo[:, w] = dot_tn(perm[...], stacked).astype(bf16).reshape(clips, slab, C_FAST)

    @pl.when(i == 2 * high - 1)
    def _():
        ex.finish(tot, weight)


def fifth_pass(n_clip, gs, gf, a2, zp, base, z2, mom2, mom3, tot4, inv, sgain, fends, mids, m, wc, wfc, x, weight,
               dzp_out, q_out, tot, row, col, corner, w_out, wfc_out,
               dzc_keep, dzp_keep, dfc_keep, a_keep, sums, big, line, side, *refs):
    i = pl.program_id(0)
    high, cols, slab, _ = dzc_keep.shape
    n = high * cols
    rows = cols * slab
    ex = Exchange(n_clip, False, refs[:8], refs[8:])

    @pl.when(i == 0)
    def _():
        ex.signal()
        expand_matrix(wfc, big)
        sums[...] = jnp.zeros_like(sums)

    @pl.when(i < high)
    def _():
        mask = spread(m[...], C_IN)
        inv_s = spread(inv[...], C_IN)
        inv_f = 0.25 * inv[...]
        mean_c = mom3[0:1, :C_IN]
        scale_c = lax.rsqrt(mom3[1:2, :C_IN] + eps_norm)
        mean_p = mom2[0:1, MIX:] - base[...]
        scale_p = lax.rsqrt(mom2[1:2, MIX:] + eps_norm)
        mean_f = jnp.tile(mom3[0:1, C_IN:], (1, ALPHA))
        scale_f = jnp.tile(lax.rsqrt(mom3[1:2, C_IN:] + eps_norm), (1, ALPHA))
        mult_c = sgain[:, 2 * C_MID : 2 * C_MID + C_IN] * scale_c
        mult_p = sgain[:, 2 * C_MID + C_IN :] * scale_p
        mult_f = jnp.tile(fends[0], (1, ALPHA)) * scale_f
        first_s = tot4[:, :C_IN] * inv_s
        second_c = tot4[:, C_IN : 2 * C_IN] * inv_s
        second_p = tot4[:, 2 * C_IN : 3 * C_IN] * inv_s
        first_f = jnp.tile(tot4[:, 3 * C_IN : 3 * C_IN + C_FAST] * inv_f, (1, ALPHA))
        second_f = jnp.tile(tot4[:, 3 * C_IN + C_FAST :] * inv_f, (1, ALPHA))
        mask_f = spread(m[...], WIDE_FAST)
        a_keep[i] = a2[...]
        for w in range(cols):
            zc = (dot(a2[w, :, :C_MID], wc[...]) - mean_c) * scale_c
            zq = (zp[w].astype(f32) - mean_p) * scale_p
            g = gs[w]
            dzc_keep[i, w] = (mult_c * (g - mask * (first_s + zc * second_c))).astype(bf16)
            dzp = (mult_p * (g - mask * (first_s + zq * second_p))).astype(bf16)
            dzp_keep[i, w] = dzp
            dzp_out[w] = dzp
            fc = (dot(a2[w, :, C_MID:], big[...]) - mean_f) * scale_f
            dfc_keep[i, w] = (mult_f * (gf[w] - mask_f * (first_f + fc * second_f))).astype(bf16)
        da = dot_nt(dzc_keep[i].reshape(rows, C_IN), wc[...]).reshape(cols, slab, C_MID)
        df = dot_nt(dfc_keep[i].reshape(rows, WIDE_FAST), big[...]).reshape(cols, slab, 128)
        grads = jnp.concatenate([da, df], axis=2)
        slope_back(grads, z2[...], mom2, mids[2], mids[3], m, q_out, sums)
        keep_rims(ex, i, high, q_out, line, side)

    @pl.when(i == high)
    def _():
        ex.part[...] = sums[...]
        ex.meet()
        ex.send_near()
        ex.send_rims(line, side)

    @pl.when(i == high + 2)
    def _():
        ex.send_far()

    @pl.when(i >= high)
    def _():
        c = i - high
        got = dot_tn(x[...].reshape(n * slab, C_MID), dzp_keep[...].reshape(n * slab, C_IN)).astype(bf16)
        for b in range(C_IN // 256):
            at = pl.multiple_of(b * C_JOIN + c * C_MID, C_MID)
            w_out[pl.ds(at, C_MID), :] = got[:, b * 256 : (b + 1) * 256]

    @pl.when(i == pl.num_programs(0) - 1)
    def _():
        a = a_keep[...].reshape(n * slab, MIX)
        got = dot_tn(a[:, :C_MID], dzc_keep[...].reshape(n * slab, C_IN)).astype(bf16)
        for b in range(C_IN // 256):
            at = 4 * C_JOIN + b * C_MID
            w_out[at : at + C_MID, :] = got[:, b * 256 : (b + 1) * 256]
        wide = dot_tn(a[:, C_MID:], dfc_keep[...].reshape(n * slab, WIDE_FAST))
        wfc_out[...] = sum(
            wide[p * C_FMID : (p + 1) * C_FMID, p * C_FAST : (p + 1) * C_FAST] for p in range(ALPHA)
        )
        ex.finish(tot, weight)
        ex.finish_rims((row, col, corner))


def slope_back(grads, z, mom, gain, shift, m, q_out, sums):
    mean, scale, g, b = affine(mom, gain, shift, 0, MIX)
    zhat = (z - mean) * scale
    v = g * zhat + b
    sig = sigmoid(v)
    q = grads * (sig * (1.0 + v * (1.0 - sig)) * spread(m[...], MIX))
    q_out[...] = q
    for k, s in enumerate((rows_sum(q), rows_sum(q * zhat))):
        at = k * MIX
        sums[:, at : at + C_MID] += s[:, :C_MID]
        sums[:, at + C_MID : at + MIX] += phase_sum(s[:, C_MID:])


def norm_terms(mom, gain, tot, inv):
    mean = mom[0:1, :MIX]
    scale = lax.rsqrt(mom[1:2, :MIX] + eps_norm)
    share = jnp.concatenate([spread(inv[...], C_MID), 0.25 * inv[...]], axis=1)
    return mean, scale, gain * scale, tot[:, :MIX] * share, tot[:, MIX:] * share


def sixth_pass(n_clip, early_sizes, q2_hbm, z2_hbm, z1_hbm, a1_hbm, qrow, qcol, qcorner, zrow, zcol, zcorner, mom1, mom2, tot5, inv,
               mids, m, wb, wfb, weight, dwfc, w_hbm, q_out, tot, wb_out, kept_out,
               fast_sums, wide, q2, z2, z1, a1, q2_sem, z2_sem, z1_sem, a1_sem, sums, mine, land, *refs):
    i = pl.program_id(0)
    high, cols, slab, _ = z1.shape
    rows = cols * slab
    ex = Exchange(n_clip, False, refs[:8])
    early = Reducer(n_clip, early_sizes, mine, land, None, refs[8:10] + (None, None))
    end = early.stages - 1

    def fetch_w():
        return pltpu.make_async_copy(w_hbm, mine, a1_sem.at[1])

    moved = ((q2_hbm, q2, q2_sem), (z2_hbm, z2, z2_sem), (z1_hbm, z1, z1_sem))

    def fetch(k, h):
        a, b, s = moved[k]
        return pltpu.make_async_copy(a.at[h], b.at[h], s.at[h])

    def fetch_a1():
        return pltpu.make_async_copy(a1_hbm, a1, a1_sem.at[0])

    @pl.when(i == 0)
    def _():
        fetch_w().start()
        wb_out[9 * C_MID :, :] = jnp.zeros((wb_out.shape[0] - 9 * C_MID, 256), bf16)
        for h in range(high):
            fetch(0, h).start()
            fetch(1, h).start()
        for h in range(high):
            fetch(2, h).start()
        fetch_a1().start()
        ex.signal()
        mean, scale, mult, first, second = norm_terms(mom2, mids[2], tot5, inv)
        mask = spread(m[...], MIX)

        def grad(q, z):
            return (mult * (q - mask * (first + (z - mean) * scale * second))).astype(bf16)

        far = high + 1
        wide[far * ex.ha] = jnp.zeros((cols + 2, slab, MIX), bf16)
        wide[:, far * ex.wa] = jnp.zeros((high + 2, slab, MIX), bf16)
        wide[far * (1 - ex.ha), 1 : 1 + cols] = grad(qrow[...], zrow[...])
        wide[1 : 1 + high, far * (1 - ex.wa)] = grad(qcol[...], zcol[...])
        wide[far * (1 - ex.ha), far * (1 - ex.wa)] = grad(qcorner[...], zcorner[...])
        fetch_w().wait()
        ex.meet()
        early.send(0)

        def fill(h, carry):
            fetch(0, h).wait()
            fetch(1, h).wait()
            wide[h + 1, 1 : 1 + cols] = grad(q2[h], z2[h])
            return carry

        lax.fori_loop(0, high, fill, 0)
        sums[...] = jnp.zeros_like(sums)

        def space(h, carry):
            fetch(2, h).wait()
            slow = jnp.zeros((rows, C_MID), f32)
            fast = jnp.zeros((rows, 128), f32)
            for a in range(3):
                for c in range(3):
                    v = wide[h + 2 - a, 2 - c : 2 - c + cols].reshape(rows, MIX)
                    slow = slow + dot_nt(v[:, :C_MID], wb[a, c])
                    fast = fast + dot_nt(v[:, C_MID:], wfb[3 * a + c])
            grads = jnp.concatenate([slow, fast], axis=1).reshape(cols, slab, MIX)
            slope_back(grads, z1[h], mom1, mids[0], mids[1], m, q_out.at[h], sums)
            return carry

        lax.fori_loop(0, 3, space, 0)
        early.gather(0)
        lax.fori_loop(3, high, space, 0)
        ex.part[...] = sums[...]
        ex.send_near()
        fetch_a1().wait()

    @pl.when(i == 3)
    def _():
        ex.send_far()

    @pl.when(i > 0)
    def _():
        tap = i - 1
        v = a1[pl.ds(tap // 3, high), pl.ds(lax.rem(tap, 3), cols)].reshape(high * rows, MIX)
        d = wide[1 : 1 + high, 1 : 1 + cols].reshape(high * rows, MIX)
        wb_out[pl.ds(pl.multiple_of(tap * C_MID, C_MID), C_MID), :] = dot_tn(v[:, :C_MID], d[:, :C_MID]).astype(bf16)
        both = dot_tn(v[:, C_MID:], d[:, C_MID:])
        fast_sums[tap] = sum(
            both[p * C_FMID : (p + 1) * C_FMID, p * C_FMID : (p + 1) * C_FMID] for p in range(ALPHA)
        )

    for k, step in ((1, 1), (2, 5), (3, 7)):

        @pl.when(i == step)
        def _():
            early.gather(k)

    @pl.when(i == 9)
    def _():
        ex.finish(tot, weight)
        for k in range(4, end + 1):
            early.gather(k)
        early.export(kept_out)
        for q in range(10):
            r, c, width = small_place(q)
            wb_out[r : r + C_FMID, c : c + width] = (fast_sums[q] if q < 9 else dwfc[...]).astype(bf16)


def bit_of(axis, power):
    return lax.rem(lax.axis_index(axis) // (1 << power), 2)


def partner_of(axis, power):
    where = {name: lax.axis_index(name) for name in ("clip", "ha", "wa")}
    where[axis] = where[axis] + (1 - 2 * bit_of(axis, power)) * (1 << power)
    return (where["clip"], where["ha"], where["wa"])


def stage_orders(n_clip, sets):
    rest = [("wa", 0)] + [("clip", b) for b in range(n_clip.bit_length() - 1)]
    turn, last = rest[:3], rest[3:]
    return [[("ha", 0)] + turn[s % len(turn) :] + turn[: s % len(turn)] + last for s in range(sets)]


def chunk_of(rows):
    return max(k for k in range(16, min(rows, 256) + 1, 16) if rows % k == 0)


class Reducer:
    def __init__(self, n_clip, sizes, mine, land, done, sems):
        self.mine, self.land, self.done = mine, land, done
        self.rs_sent, self.rs_came, self.ag_sent, self.ag_came = sems
        self.sets = range(len(sizes))
        self.orders = stage_orders(n_clip, len(sizes))
        self.stages = len(self.orders[0])
        self.plan, self.starts, self.kept = Reducer.layout(n_clip, sizes)

    @staticmethod
    def layout(n_clip, sizes):
        stages = len(stage_orders(n_clip, 1)[0])
        plan, starts, kept = [], [], []
        start = land = 0
        for size in sizes:
            starts.append(start)
            start += size
            row = []
            for _ in range(stages):
                halve = size % 32 == 0
                size = size // 2 if halve else size
                row.append((halve, size, land))
                land += size
            plan.append(row)
            kept.append(size)
        return plan, starts, kept

    @staticmethod
    def scratch(n_clip, sizes):
        plan = Reducer.layout(n_clip, sizes)[0]
        last = plan[-1][-1]
        return pltpu.VMEM((last[1] + last[2], 256), bf16)

    @staticmethod
    def sems(n_clip, sizes, count=4):
        stages = len(stage_orders(n_clip, 1)[0])
        return [pltpu.SemaphoreType.DMA((len(sizes), stages)) for _ in range(count)]

    def low(self, s, k):
        low = jnp.int32(self.starts[s])
        for j in range(k):
            halve, count, _ = self.plan[s][j]
            if halve:
                low = low + bit_of(*self.orders[s][j]) * count
        return low

    @staticmethod
    def rows(ref, begin, count):
        return ref.at[pl.ds(pl.multiple_of(begin, 16), count)]

    def scatter_copy(self, s, k):
        halve, count, land = self.plan[s][k]
        axis, power = self.orders[s][k]
        begin = self.low(s, k)
        if halve:
            begin = begin + (1 - bit_of(axis, power)) * count
        return pltpu.make_async_remote_copy(
            src_ref=self.rows(self.mine, begin, count), dst_ref=self.rows(self.land, land, count),
            send_sem=self.rs_sent.at[s, k], recv_sem=self.rs_came.at[s, k],
            device_id=partner_of(axis, power), device_id_type=MESH,
        )

    def send(self, k):
        for s in self.sets:
            self.scatter_copy(s, k).start()

    def gather(self, k):
        for s in self.sets:
            halve, count, land = self.plan[s][k]
            copy = self.scatter_copy(s, k)
            copy.wait_recv()
            copy.wait_send()
            begin = self.low(s, k + 1)
            step = chunk_of(count)

            def add(i, carry):
                own = pl.ds(pl.multiple_of(begin + i * step, 16), step)
                came = pl.ds(pl.multiple_of(land + i * step, 16), step)
                self.mine[own, :] = (self.mine[own, :].astype(f32) + self.land[came, :].astype(f32)).astype(bf16)
                return carry

            lax.fori_loop(0, count // step, add, 0)
            if k + 1 < self.stages:
                self.scatter_copy(s, k + 1).start()

    def export(self, out):
        at = 0
        for s in self.sets:
            count = self.kept[s]
            out[at : at + count] = self.mine[pl.ds(pl.multiple_of(self.low(s, self.stages), 16), count), :]
            at += count

    def load(self, kept):
        at = 0
        for s in self.sets:
            count = self.kept[s]
            self.done[pl.ds(pl.multiple_of(self.low(s, self.stages), 16), count), :] = kept[at : at + count]
            at += count

    def keep(self):
        for s in self.sets:
            own = pl.ds(pl.multiple_of(self.low(s, self.stages), 16), self.kept[s])
            self.done[own, :] = self.mine[own, :]

    def regain(self):
        self.keep()
        self.spread(self.stages - 1)

    def gather_copy(self, s, k, other):
        halve, count, _ = self.plan[s][k]
        axis, power = self.orders[s][k]
        bit = bit_of(axis, power)
        begin = self.low(s, k) + ((1 - bit) if other else bit) * count
        return pltpu.make_async_remote_copy(
            src_ref=self.rows(self.done, begin, count), dst_ref=self.rows(self.done, begin, count),
            send_sem=self.ag_sent.at[s, k], recv_sem=self.ag_came.at[s, k],
            device_id=partner_of(axis, power), device_id_type=MESH,
        )

    def spread(self, k):
        for s in self.sets:
            if self.plan[s][k][0]:
                self.gather_copy(s, k, False).start()

    def take(self, k):
        for s in self.sets:
            if self.plan[s][k][0]:
                self.gather_copy(s, k, True).wait_recv()
                self.gather_copy(s, k, False).wait_send()
            if k > 0 and self.plan[s][k - 1][0]:
                self.gather_copy(s, k - 1, False).start()


SPACE_STEPS = (2, 5, 7, 8, 10)
FIRST_STEPS = (5, 7, 9, 12, 14)
HALF_STEPS = (10, 11, 13, 14, 15)
SPACE_BACK = (11, 13, 14, 15, 16, 17)
HALF_BACK = (15, 16, 17, 18, 18, 18)
LATE_STEPS = (14, 16, 18)


def seventh_pass(clips, n_clip, early_sizes, space_sizes, half_sizes, late_sizes, q1, z1, dzp, gf, x, f, kept, space_hbm, mom1, tot6, inv,
                 mids, m, perm, wl, wa, wp, wfa, sx, fx, out1, out_b, out_h, out_a,
                 done1, done_b, done_h, done_a, da, dl, df, taps, ends, mine_b, land_b, mine_h, land_h, mine_a, land_a, load_sem, *sems):
    i = pl.program_id(0)
    cols, slab, _ = q1.shape
    high = da.shape[0]
    rows = cols * slab
    every = high * rows
    steps = C_JOIN // C_MID
    late = high + steps
    sems = iter(sems)
    first = Reducer(n_clip, early_sizes, None, None, done1, (None, None, next(sems), next(sems)))
    space = Reducer(n_clip, space_sizes, mine_b, land_b, done_b, [next(sems) for _ in range(4)])
    half = Reducer(n_clip, half_sizes, mine_h, land_h, done_h, [next(sems) for _ in range(4)])
    last = Reducer(n_clip, late_sizes, mine_a, land_a, done_a, [next(sems) for _ in range(4)])
    end = last.stages - 1

    @pl.when(i == 0)
    def _():
        load = pltpu.make_async_copy(space_hbm, mine_b, load_sem.at[0])
        load.start()
        greet_signal(n_clip)
        frames_matrix(wfa, taps, ends)
        first.load(kept)
        greet_wait(n_clip)
        first.spread(end)
        load.wait()
        space.send(0)

    plan = {}

    def book(ops, steps):
        for j, op in enumerate(ops):
            plan.setdefault(steps[j * len(steps) // len(ops)], []).append(op)

    book([functools.partial(space.gather, k) for k in range(end + 1)], SPACE_STEPS)
    book([functools.partial(first.take, k) for k in range(end, -1, -1)], FIRST_STEPS)
    book([functools.partial(half.gather, k) for k in range(end + 1)], HALF_STEPS)
    book([space.regain] + [functools.partial(space.take, k) for k in range(end, -1, -1)], SPACE_BACK)
    book([half.regain] + [functools.partial(half.take, k) for k in range(end, -1, -1)], HALF_BACK)
    book([functools.partial(last.gather, k) for k in range(3)], LATE_STEPS)
    final = pl.num_programs(0) - 1
    for step, ops in sorted(plan.items()):

        @pl.when((i == step) & (i < final))
        def _():
            for op in ops:
                op()

    @pl.when(i < high)
    def _():
        mean, scale, mult, one, two = norm_terms(mom1, mids[0], tot6, inv)
        zhat = (z1[...] - mean) * scale
        dz = mult * (q1[...] - spread(m[...], MIX) * (one + zhat * two))
        up, down = sooner(dz, clips), later(dz, clips)
        for k, v in enumerate((up, dz, down)):
            da[i, :, :, k * C_MID : (k + 1) * C_MID] = v[:, :, :C_MID].astype(bf16)
            df[i, :, :, k * 128 : (k + 1) * 128] = v[:, :, C_MID:].astype(bf16)
        dlat = dot_nt(dzp[...].reshape(rows, C_IN), wp[C_IN:])
        for k in range(3):
            dlat = dlat + dot_nt(da[i, :, :, k * C_MID : (k + 1) * C_MID].reshape(rows, C_MID), wa[k, C_IN:])
        dlat = dlat.astype(bf16).astype(f32).reshape(cols, slab, C_LAT)
        dl[i, :, :, :C_LAT] = dlat.astype(bf16)
        dl[i, :, :, C_LAT:] = sooner(dlat, clips).astype(bf16)

    @pl.when((i >= high) & (i < late))
    def _():
        c = i - high
        got = dot_tn(x[...].reshape(every, C_MID), da[...].reshape(every, 3 * C_MID)).astype(bf16)

        @pl.when(c < 2)
        def _():
            for k in range(3):
                mine_h[pl.ds(pl.multiple_of((2 * k + c) * C_MID, C_MID), C_MID), :] = got[:, k * C_MID : (k + 1) * C_MID]

        @pl.when(c >= 2)
        def _():
            for k in range(3):
                at = pl.multiple_of((3 * k + c - 2) * C_MID, C_MID)
                mine_a[pl.ds(at, C_MID), :] = got[:, k * C_MID : (k + 1) * C_MID]

        @pl.when(c == 1)
        def _():
            half.send(0)

    @pl.when(i == late - 1)
    def _():
        fast = f[...].reshape(every, WIDE_FAST)
        d = dl[...].reshape(every, 2 * C_LAT)
        at = 9 * C_MID
        mine_a[at + 2 * C_FAST : at + 5 * C_FAST, :] = dot_tn(fast[:, : 3 * C_FAST], d[:, :C_LAT]).astype(bf16)
        mine_a[at : at + 2 * C_FAST, :] = dot_tn(fast[:, 2 * C_FAST :], d[:, C_LAT:]).astype(bf16)
        at += 5 * C_FAST
        g = df[...].reshape(every, 3 * 128)
        mid = dot_tn(g[:, 128:256], fast)
        sums = [jnp.zeros((C_FMID, C_FAST), f32) for _ in range(3)]
        for p in range(ALPHA):
            for s in range(max(p - 1, 0), min(p + 2, ALPHA)):
                sums[s - p + 1] += mid[p * C_FMID : (p + 1) * C_FMID, s * C_FAST : (s + 1) * C_FAST]
        sums[0] += dot_tn(g[:, :128], fast[:, 3 * C_FAST :])[:C_FMID]
        sums[2] += dot_tn(g[:, 256:], fast[:, :C_FAST])[3 * C_FMID :]
        mine_a[at:, :] = jnp.zeros((mine_a.shape[0] - at, 256), bf16)
        for q in range(3):
            mine_a[at + q * C_FMID : at + (q + 1) * C_FMID, :C_FAST] = sums[q].astype(bf16)
        last.send(0)

    @pl.when(i >= late)
    def _():
        h = i - late
        dj = dot_nt(dzp[...].reshape(rows, C_IN), wp[:C_IN])
        for k in range(3):
            dj = dj + dot_nt(da[h, :, :, k * C_MID : (k + 1) * C_MID].reshape(rows, C_MID), wa[k, :C_IN])
        mask = spread(m[...], C_IN)
        dj = dj.reshape(cols, slab, C_IN)
        for w in range(cols):
            sx[:, w] = (dj[w] * mask).astype(bf16).reshape(slab // clips, clips, C_IN)
        g = df[h].reshape(rows, 3 * 128)
        d = dl[h].reshape(rows, 2 * C_LAT)
        total = gf[...].reshape(rows, WIDE_FAST) + dot(g[:, 128:256], taps[...])
        head = dot_nt(d[:, :C_LAT], wl[2:5].reshape(3 * C_FAST, C_LAT))
        tail = dot_nt(d[:, C_LAT:], wl[0:2].reshape(2 * C_FAST, C_LAT))
        blocks = [total[:, p * C_FAST : (p + 1) * C_FAST] for p in range(ALPHA)]
        for p in range(3):
            blocks[p] = blocks[p] + head[:, p * C_FAST : (p + 1) * C_FAST]
        for p in range(2):
            blocks[2 + p] = blocks[2 + p] + tail[:, p * C_FAST : (p + 1) * C_FAST]
        blocks[3] = blocks[3] + dot(g[:, :128], ends[0])
        blocks[0] = blocks[0] + dot(g[:, 256:], ends[1])
        blocks = [v.astype(bf16) for v in blocks]
        for w in range(cols):
            stacked = jnp.concatenate([v[w * slab : (w + 1) * slab] for v in blocks], axis=0)
            fx[:, w] = dot_tn(perm[...], stacked).astype(bf16).reshape(clips, slab, C_FAST)

    @pl.when(i == final)
    def _():
        for step, ops in sorted(plan.items()):
            if step >= 2 * high + steps - 1:
                for op in ops:
                    op()
        for k in range(3, end + 1):
            last.gather(k)
        last.regain()
        for k in range(end, -1, -1):
            last.take(k)
        saves = [
            pltpu.make_async_copy(a, b, load_sem.at[k])
            for k, (a, b) in enumerate(((done1, out1), (done_b, out_b), (done_h, out_h), (done_a, out_a)))
        ]
        for save in saves:
            save.start()
        for save in saves:
            save.wait()


def small_place(q):
    return 9 * C_MID + (q % 5) * C_FMID, (q // 5) * 128, C_FMID if q < 9 else C_FAST


def greet_signal(n_clip):
    barrier = pltpu.get_barrier_semaphore()
    for axis, power in stage_orders(n_clip, 1)[0]:
        pl.semaphore_signal(barrier, inc=1, device_id=partner_of(axis, power), device_id_type=MESH)


def greet_wait(n_clip):
    pl.semaphore_wait(pltpu.get_barrier_semaphore(), len(stage_orders(n_clip, 1)[0]))


def finish_outputs(so, fo, sx, fx, done1, done_b, done_h, done_a, tot4, tot5, tot6, so_out, fo_out, sx_out, fx_out,
                   wp_hbm, wc_hbm, wb_hbm, wa_hbm, wl_hbm, wfa_out, wfc_out, wfb_out, sgain_out, sshift_out, fgain_out,
                   fshift_out, wp, wc, wb, wa, wl, sem):
    i = pl.program_id(0)
    moves = ((wp, wp_hbm), (wc, wc_hbm), (wb, wb_hbm), (wa, wa_hbm), (wl, wl_hbm))

    def move(k):
        return pltpu.make_async_copy(moves[k][0], moves[k][1], sem.at[k])

    @pl.when(i == 0)
    def _():
        for b in range(C_IN // 256):
            wp[:, b * 256 : (b + 1) * 256] = done1[b * C_JOIN : (b + 1) * C_JOIN, :].astype(f32)
        move(0).start()
        for b in range(C_IN // 256):
            at = 4 * C_JOIN + b * C_MID
            wc[:, b * 256 : (b + 1) * 256] = done1[at : at + C_MID, :].astype(f32)
        move(1).start()

    @pl.when(i == 1)
    def _():
        for t in range(9):
            wb[t // 3, t % 3] = done_b[t * C_MID : (t + 1) * C_MID, :].astype(f32)
        move(2).start()

    @pl.when(i == 2)
    def _():
        for k in range(3):
            wa[k, : 2 * C_MID] = done_h[2 * k * C_MID : 2 * (k + 1) * C_MID, :].astype(f32)
            wa[k, 2 * C_MID :] = done_a[3 * k * C_MID : 3 * (k + 1) * C_MID, :].astype(f32)
        move(3).start()
        at = 9 * C_MID
        for k in range(5):
            wl[k] = done_a[at + k * C_FAST : at + (k + 1) * C_FAST, :].astype(f32)
        move(4).start()

    @pl.when(i == 3)
    def _():
        at = 9 * C_MID + 5 * C_FAST
        for q in range(3):
            wfa_out[q] = done_a[at + q * C_FMID : at + (q + 1) * C_FMID, :C_FAST].astype(f32)
        for q in range(10):
            r, c, width = small_place(q)
            piece = done_b[r : r + C_FMID, c : c + width].astype(f32)
            if q < 9:
                wfb_out[q] = piece
            else:
                wfc_out[...] = piece
        lane = lax.broadcasted_iota(jnp.int32, (1, 128), 1)
        for k, slow, fast in ((0, sshift_out, fshift_out), (1, sgain_out, fgain_out)):
            at = k * MIX
            row = 0
            for source, begin, width in (
                (tot6, at, C_MID), (tot5, at, C_MID), (tot4, k * C_IN, C_IN), (tot4, 2 * k * C_IN, C_IN)
            ):
                for c in range(begin, begin + width, 128):
                    slow[row : row + 1] = source[:, c : c + 128]
                    row += 1
            c = pltpu.roll(tot4[:, 3 * C_IN + k * C_FAST : 3 * C_IN + (k + 1) * C_FAST], 2 * C_FMID, 1)
            a, b = tot6[:, at + C_MID : at + MIX], tot5[:, at + C_MID : at + MIX]
            fast[:, :128] = jnp.where(lane < C_FMID, a, jnp.where(lane < 2 * C_FMID, b, c))
            fast[:, 128:] = c[:, : 2 * C_FMID]

    so_out[...] = so[...]
    fo_out[...] = fo[...]
    sx_out[...] = sx[...]
    fx_out[...] = fx[...]

    @pl.when(i == pl.num_programs(0) - 1)
    def _():
        for k in range(5):
            move(k).wait()


def prepare(clips, n_clip, counts, sgain_rows, sshift_rows, fgain, fshift, wb, m, perm, weight, inv, mids, last, wide,
            sgain, sshift):
    for k in range(sgain_rows.shape[0]):
        sgain[:, k * 128 : (k + 1) * 128] = sgain_rows[k : k + 1]
        sshift[:, k * 128 : (k + 1) * 128] = sshift_rows[k : k + 1]
    slab = m.shape[0]
    frames = slab // clips
    me = lax.axis_index("clip") * clips
    shift = clips.bit_length() - 1

    def real(shape):
        r = lax.broadcasted_iota(jnp.int32, shape, 0)
        own = jnp.zeros(shape, jnp.int32)
        for c in range(clips):
            own = jnp.where((r & (clips - 1)) == c, counts[me + c], own)
        return r, (r >> shift) < own

    m[...] = real(m.shape)[1].astype(f32)
    width = perm.shape[1]
    r, there = real((slab, width))
    col = lax.broadcasted_iota(jnp.int32, (slab, width), 1)
    for p in range(ALPHA):
        want = (r & (clips - 1)) * (ALPHA * frames) + ALPHA * (r >> shift) + p
        perm[p * slab : (p + 1) * slab] = ((want == col) & there).astype(f32).astype(bf16)
    groups = []
    for g in range(n_clip):
        part = counts[g * clips]
        for c in range(1, clips):
            part = part + counts[g * clips + c]
        groups.append(part)
    total = groups[0]
    for part in groups[1:]:
        total = total + part
    whole_count = jnp.full((1, 128), total, jnp.int32).astype(f32)
    inv[...] = 1.0 / (whole_count * (H * W))
    for g in range(n_clip):
        weight[g] = jnp.full((1, 128), groups[g], jnp.int32).astype(f32) / whole_count
    lane = lax.broadcasted_iota(jnp.int32, (1, 128), 1)
    for k in range(2):
        for j, (slow, fast) in enumerate(((sgain, fgain), (sshift, fshift))):
            mine = (lane >= k * C_FMID) & (lane < (k + 1) * C_FMID)
            mids[2 * k + j, :, :C_MID] = slow[:, k * C_MID : (k + 1) * C_MID]
            mids[2 * k + j, :, C_MID:] = phase_sum(jnp.where(mine, fast[:, :128], 0.0))
    for j, fast in enumerate((fgain, fshift)):
        last[j] = fast[:, 2 * C_FMID :]
    for t in range(9):
        w = wb[t]
        for p in range(ALPHA):
            parts = [jnp.zeros((C_FMID, C_FMID), bf16)] * ALPHA
            parts[p] = w
            wide[t, p * C_FMID : (p + 1) * C_FMID] = jnp.concatenate(parts, axis=1)


def vmem_spec():
    return pl.BlockSpec(memory_space=pltpu.VMEM)


def shaped(shape, kind):
    return jax.ShapeDtypeStruct(shape, kind)


def whole(shape):
    return pl.BlockSpec(shape, lambda h: (0,) * len(shape))


def per_line(shape):
    return pl.BlockSpec((None,) + tuple(shape), lambda h: (h,) + (0,) * len(shape))


def params(limit):
    return pltpu.CompilerParams(vmem_limit_bytes=60 * MIB)


def on_device(
    slow_input,
    fast_input,
    frame_counts,
    lateral_weight,
    slow_a_weight,
    slow_b_weight,
    slow_c_weight,
    slow_proj_weight,
    fast_a_weight,
    fast_b_weight,
    fast_c_weight,
    slow_gain,
    slow_shift,
    fast_gain,
    fast_shift,
    slow_cotangent,
    fast_cotangent,
):
    n_clip = lax.axis_size("clip")
    clips, frames, high, cols, _ = slow_input.shape
    slab = clips * frames
    lanes = slow_gain.reshape(-1, 128), slow_shift.reshape(-1, 128)
    slow_row = shaped((1, slow_gain.shape[0]), f32)
    vm = vmem_spec()
    m, perm, weight, inv, mids, ends, wfb, sgain, sshift = pl.pallas_call(
        functools.partial(prepare, clips, n_clip),
        in_specs=[pl.BlockSpec(memory_space=pltpu.SMEM)] + [vm] * 5,
        out_specs=(vm,) * 9,
        out_shape=(
            shaped((slab, 128), f32), shaped((ALPHA * slab, ALPHA * slab), bf16), shaped((n_clip, 1, 128), f32),
            shaped((1, 128), f32), shaped((4, 1, MIX), f32), shaped((2, 1, C_FAST), f32), shaped((9, 128, 128), bf16),
            slow_row, slow_row,
        ),
        compiler_params=params(60),
        name="prepare",
    )(frame_counts, *lanes, fast_gain[None], fast_shift[None], fast_b_weight.reshape(9, C_FMID, C_FMID))
    wfa = fast_a_weight.transpose(0, 2, 1)
    xs = slow_input.transpose(1, 2, 3, 0, 4)
    xf = fast_input.transpose(0, 2, 3, 1, 4)
    cot = slow_cotangent.transpose(1, 2, 3, 0, 4)
    fcot = fast_cotangent.transpose(0, 2, 3, 1, 4)
    def lines(c, kind):
        return shaped((high, cols, slab, c), kind)

    m_spec = whole((slab, 128))
    vm = vmem_spec()
    hbm = pl.BlockSpec(memory_space=pl.ANY)

    def early_line(shape):
        return pl.BlockSpec((None,) + tuple(shape), lambda i: (jnp.minimum(i, high - 1),) + (0,) * len(shape))

    def late_line(shape, begin):
        return pl.BlockSpec((None,) + tuple(shape), lambda i: (jnp.maximum(i - begin, 0),) + (0,) * len(shape))

    def slow_block(index):
        return pl.BlockSpec((frames, None, cols, clips, C_IN), lambda i: (0, index(i), 0, 0, 0))

    def fast_block(index):
        return pl.BlockSpec((clips, None, cols, ALPHA * frames, C_FAST), lambda i: (0, index(i), 0, 0, 0))

    def early(i):
        return jnp.minimum(i, high - 1)

    def after(begin):
        return lambda i: jnp.maximum(i - begin, 0)

    def remote(ident):
        return pltpu.CompilerParams(collective_id=ident, has_side_effects=True, vmem_limit_bytes=60 * MIB)

    rim_shapes = (shaped((cols, slab, MIX), f32), shaped((high, slab, MIX), f32), shaped((slab, MIX), f32))
    edge_scratch = [pltpu.VMEM((cols, slab, MIX), f32), pltpu.VMEM((high, slab, MIX), f32)]
    rims = rim_scratch(cols, slab)
    L1 = MIX + C_IN
    x, f, z1, zp, stp, base, mom1, row1, col1, corner1 = pl.pallas_call(
        functools.partial(first_pass, clips, n_clip),
        grid=(2 * high,),
        in_specs=[slow_block(early), fast_block(early)] + [vm] * 7,
        out_specs=(
            early_line((cols, slab, C_JOIN)), early_line((cols, slab, WIDE_FAST)), early_line((cols, slab, MIX)),
            late_line((cols, slab, C_IN), high), vm, vm, vm, vm, vm, vm,
        ),
        out_shape=(
            lines(C_JOIN, bf16), lines(WIDE_FAST, bf16), lines(MIX, f32), lines(C_IN, bf16), shaped((2, C_IN), f32),
            shaped((1, C_IN), f32), shaped((2, MIX), f32),
        ) + rim_shapes,
        scratch_shapes=[
            pltpu.VMEM((high, cols, slab, C_JOIN), bf16), pltpu.VMEM((128, WIDE_FAST), bf16),
            pltpu.VMEM((2, 128, C_FAST), bf16), pltpu.VMEM((1, L1), f32), pltpu.VMEM((1, L1), f32),
            pltpu.VMEM((1, L1), f32),
        ] + edge_scratch + exchange_scratch(n_clip, 2, MIX) + rims,
        compiler_params=remote(1),
        name="first_pass",
    )(xs, xf, m, perm, lateral_weight, slow_a_weight, slow_proj_weight, wfa, weight)

    a1, z2, mom2, zrow, zcol, zcorner, cot = pl.pallas_call(
        functools.partial(second_pass, n_clip),
        grid=(high + 1,),
        in_specs=[hbm] + [vm] * 10 + [slow_block(after(1))],
        out_specs=(vm, vm, vm, vm, vm, vm, late_line((cols, slab, C_IN), 1)),
        out_shape=(
            shaped((high + 2, cols + 2, slab, MIX), bf16), lines(MIX, f32), shaped((2, L1), f32),
        ) + rim_shapes + (lines(C_IN, bf16),),
        scratch_shapes=[
            pltpu.VMEM((high, cols, slab, MIX), f32), pltpu.SemaphoreType.DMA((high,)), pltpu.VMEM((1, MIX), f32),
            pltpu.VMEM((1, MIX), f32),
        ] + exchange_scratch(n_clip, 2, L1) + rims,
        compiler_params=remote(2),
        name="second_pass",
    )(z1, row1, col1, corner1, mom1, mids, m, slow_b_weight, wfb, stp, weight, cot)

    L3 = C_IN + C_FAST
    a2, mom3, fcot = pl.pallas_call(
        functools.partial(third_pass, n_clip),
        grid=(2 * high,),
        in_specs=[early_line((cols, slab, MIX))] + [vm] * 6 + [fast_block(after(high)), vm],
        out_specs=(early_line((cols, slab, MIX)), vm, late_line((cols, slab, WIDE_FAST), high)),
        out_shape=(lines(MIX, bf16), shaped((2, L3), f32), lines(WIDE_FAST, bf16)),
        scratch_shapes=[pltpu.VMEM((128, WIDE_FAST), bf16)] + [pltpu.VMEM((1, L3), f32)] * 3
        + exchange_scratch(n_clip, 2, L3),
        compiler_params=remote(3),
        name="third_pass",
    )(z2, mom2, mids, m, slow_c_weight, fast_c_weight, weight, fcot, perm)

    L4 = 3 * C_IN + 2 * C_FAST
    so, fo, gs, gf, tot4 = pl.pallas_call(
        functools.partial(fourth_pass, n_clip, clips),
        grid=(2 * high,),
        in_specs=[early_line((cols, slab, MIX)), early_line((cols, slab, C_IN))] + [vm] * 6 + [
            early_line((cols, slab, C_IN)), early_line((cols, slab, WIDE_FAST)), early_line((cols, slab, WIDE_FAST)),
        ] + [vm] * 5,
        out_specs=(
            slow_block(after(high)), fast_block(after(high)), early_line((cols, slab, C_IN)),
            early_line((cols, slab, WIDE_FAST)), vm,
        ),
        out_shape=(
            shaped(xs.shape, bf16), shaped(xf.shape, bf16), lines(C_IN, f32), lines(WIDE_FAST, f32),
            shaped((1, L4), f32),
        ),
        scratch_shapes=[
            pltpu.VMEM((high, cols, slab, C_IN), bf16), pltpu.VMEM((high, cols, slab, WIDE_FAST), bf16),
            pltpu.VMEM((1, L4), f32), pltpu.VMEM((128, WIDE_FAST), bf16),
        ] + exchange_scratch(n_clip, 1, L4),
        compiler_params=remote(4),
        name="fourth_pass",
    )(
        a2, zp, base, mom2, mom3, sgain, sshift, ends, cot, fcot, f, m, perm, slow_c_weight, fast_c_weight, weight,
    )

    n = high * cols
    early_sizes = (2048, 2048, 2048)
    space_sizes = (1024, 1024, 512)
    half_sizes = (512, 512, 512)
    late_sizes = (1024, 1024, 1024)

    def flat(v):
        return v.reshape((n,) + v.shape[2:])

    steps = C_JOIN // C_MID
    dzp, q2, tot5, qrow, qcol, qcorner, dw1, dwfc = pl.pallas_call(
        functools.partial(fifth_pass, n_clip),
        grid=(high + steps,),
        in_specs=[
            early_line((cols, slab, C_IN)), early_line((cols, slab, WIDE_FAST)), early_line((cols, slab, MIX)),
            early_line((cols, slab, C_IN)), vm, early_line((cols, slab, MIX)),
        ] + [vm] * 10 + [pl.BlockSpec((n, slab, C_MID), lambda i: (0, 0, jnp.clip(i - high, 0, steps - 1))), vm],
        out_specs=(
            early_line((cols, slab, C_IN)), early_line((cols, slab, MIX)), vm, vm, vm, vm, vm, vm,
        ),
        out_shape=(lines(C_IN, bf16), lines(MIX, f32), shaped((1, 2 * MIX), f32)) + rim_shapes + (
            shaped((sum(early_sizes), 256), bf16), shaped((C_FMID, C_FAST), f32),
        ),
        scratch_shapes=[
            pltpu.VMEM((high, cols, slab, C_IN), bf16), pltpu.VMEM((high, cols, slab, C_IN), bf16),
            pltpu.VMEM((high, cols, slab, WIDE_FAST), bf16), pltpu.VMEM((high, cols, slab, MIX), bf16),
            pltpu.VMEM((1, 2 * MIX), f32), pltpu.VMEM((128, WIDE_FAST), bf16),
        ] + edge_scratch + exchange_scratch(n_clip, 1, 2 * MIX) + rims,
        compiler_params=remote(5),
        name="fifth_pass",
    )(
        gs, gf, a2, zp, base, z2, mom2, mom3, tot4, inv, sgain, ends, mids, m, slow_c_weight, fast_c_weight,
        flat(x), weight,
    )

    q1, tot6, dwb, kept = pl.pallas_call(
        functools.partial(sixth_pass, n_clip, early_sizes),
        grid=(10,),
        in_specs=[hbm] * 4 + [vm] * 16 + [hbm],
        out_specs=(vm,) * 4,
        out_shape=(
            lines(MIX, f32), shaped((1, 2 * MIX), f32), shaped((sum(space_sizes), 256), bf16),
            shaped((sum(Reducer.layout(n_clip, early_sizes)[2]), 256), bf16),
        ),
        scratch_shapes=[pltpu.VMEM((9, C_FMID, C_FMID), f32), pltpu.VMEM((high + 2, cols + 2, slab, MIX), bf16)]
        + [pltpu.VMEM((high, cols, slab, MIX), f32)] * 3
        + [pltpu.VMEM((high + 2, cols + 2, slab, MIX), bf16)]
        + [pltpu.SemaphoreType.DMA((high,))] * 3
        + [pltpu.SemaphoreType.DMA((2,)), pltpu.VMEM((1, 2 * MIX), f32)]
        + [pltpu.VMEM((sum(early_sizes), 256), bf16), Reducer.scratch(n_clip, early_sizes)]
        + exchange_scratch(n_clip, 1, 2 * MIX) + Reducer.sems(n_clip, early_sizes, 2),
        compiler_params=remote(6),
        name="sixth_pass",
    )(
        q2, z2, z1, a1, qrow, qcol, qcorner, zrow, zcol, zcorner, mom1, mom2, tot5, inv, mids, m,
        slow_b_weight, wfb, weight, dwfc, dw1,
    )

    def twice_line(shape):
        begin = high + steps
        return pl.BlockSpec(
            (None,) + tuple(shape),
            lambda i: (jnp.where(i < begin, jnp.minimum(i, high - 1), i - begin),) + (0,) * len(shape),
        )

    sx, fx, done1, done_b, done_h, done_a = pl.pallas_call(
        functools.partial(seventh_pass, clips, n_clip, early_sizes, space_sizes, half_sizes, late_sizes),
        grid=(2 * high + steps,),
        in_specs=[
            early_line((cols, slab, MIX)), early_line((cols, slab, MIX)), twice_line((cols, slab, C_IN)),
            late_line((cols, slab, WIDE_FAST), high + steps),
            pl.BlockSpec((n, slab, C_MID), lambda i: (0, 0, jnp.clip(i - high, 0, steps - 1))), vm, vm, hbm,
        ] + [vm] * 10,
        out_specs=(slow_block(after(high + steps)), fast_block(after(high + steps)), hbm, hbm, hbm, hbm),
        out_shape=(
            shaped(xs.shape, bf16), shaped(xf.shape, bf16), shaped((sum(early_sizes), 256), bf16),
            shaped((sum(space_sizes), 256), bf16), shaped((sum(half_sizes), 256), bf16), shaped((sum(late_sizes), 256), bf16),
        ),
        scratch_shapes=[
            pltpu.VMEM((sum(v), 256), bf16) for v in (early_sizes, space_sizes, half_sizes, late_sizes)
        ] + [
            pltpu.VMEM((high, cols, slab, 3 * C_MID), bf16), pltpu.VMEM((high, cols, slab, 2 * C_LAT), bf16),
            pltpu.VMEM((high, cols, slab, 3 * 128), bf16), pltpu.VMEM((128, WIDE_FAST), bf16),
            pltpu.VMEM((2, 128, C_FAST), bf16), pltpu.VMEM((sum(space_sizes), 256), bf16),
            Reducer.scratch(n_clip, space_sizes), pltpu.VMEM((sum(half_sizes), 256), bf16),
            Reducer.scratch(n_clip, half_sizes), pltpu.VMEM((sum(late_sizes), 256), bf16),
            Reducer.scratch(n_clip, late_sizes), pltpu.SemaphoreType.DMA((4,)),
        ] + Reducer.sems(n_clip, early_sizes, 2) + Reducer.sems(n_clip, space_sizes) + Reducer.sems(n_clip, half_sizes)
        + Reducer.sems(n_clip, late_sizes),
        compiler_params=remote(7),
        name="seventh_pass",
    )(
        q1, z1, dzp, gf, flat(x), flat(f), kept, dwb, mom1, tot6, inv, mids, m, perm, lateral_weight, slow_a_weight,
        slow_proj_weight, wfa,
    )

    slow_rows, fast_row = shaped(lanes[0].shape, f32), shaped((1, fast_gain.shape[0]), f32)
    def here(i):
        return i

    weights = (
        shaped((C_JOIN, C_IN), f32), shaped((C_MID, C_IN), f32), shaped((3, 3, C_MID, C_MID), f32),
        shaped((3, C_JOIN, C_MID), f32), shaped((5, C_FAST, C_LAT), f32),
    )
    maps = [slow_block(here), fast_block(here)] * 2
    so, fo, sx, fx, dwp, dwc, dwb, dwa, dwl, dwfa, dwfc, dwfb, dsg, dss, dfg, dfs = pl.pallas_call(
        finish_outputs,
        grid=(high,),
        in_specs=maps + [vm] * 7,
        out_specs=tuple(maps) + (hbm,) * 5 + (vm,) * 7,
        out_shape=(shaped(xs.shape, bf16), shaped(xf.shape, bf16)) * 2 + weights + (
            shaped((3, C_FMID, C_FAST), f32), shaped((C_FMID, C_FAST), f32), shaped((9, C_FMID, C_FMID), f32),
            slow_rows, slow_rows, fast_row, fast_row,
        ),
        scratch_shapes=[pltpu.VMEM(v.shape, f32) for v in weights] + [pltpu.SemaphoreType.DMA((5,))],
        compiler_params=params(60),
        name="finish_outputs",
    )(so, fo, sx, fx, done1, done_b, done_h, done_a, tot4, tot5, tot6)
    return (
        so.transpose(3, 0, 1, 2, 4),
        fo.transpose(0, 3, 1, 2, 4),
        sx.transpose(3, 0, 1, 2, 4),
        fx.transpose(0, 3, 1, 2, 4),
        dwl,
        dwa,
        dwb,
        dwc,
        dwp,
        dwfa.transpose(0, 2, 1),
        dwfb.reshape(3, 3, C_FMID, C_FMID),
        dwfc,
        dsg.reshape(-1),
        dss.reshape(-1),
        dfg[0],
        dfs[0],
    )


def solution(mesh):
    tiles = P("clip", None, "ha", "wa", None)
    return jax.shard_map(
        on_device,
        mesh=mesh,
        in_specs=(tiles, tiles) + (P(),) * 13 + (tiles, tiles),
        out_specs=(tiles,) * 4 + (P(),) * 12,
        check_vma=False,
    )
```

```python
import functools

import jax
import jax.numpy as jnp
from jax import lax
from jax.experimental import pallas as pl
from jax.experimental.pallas import tpu as pltpu
from jax.sharding import PartitionSpec as P

ALPHA = 4
H = 14
W = 14
C_IN = 1024
C_LAT = 256
C_MID = 256
C_FAST = 128
C_FMID = 32
C_JOIN = C_IN + C_LAT
MIX = C_MID + ALPHA * C_FMID
WIDE_FAST = ALPHA * C_FAST

eps_norm = 1e-05
f32 = jnp.float32
bf16 = jnp.bfloat16
MESH = pl.DeviceIdType.MESH
MIB = 1 << 20


def dot(a, b):
    return lax.dot_general(a, b, (((1,), (0,)), ((), ())), preferred_element_type=f32)


def dot_nt(a, b):
    return lax.dot_general(a, b, (((1,), (1,)), ((), ())), preferred_element_type=f32)


def dot_tn(a, b):
    return lax.dot_general(a, b, (((0,), (0,)), ((), ())), preferred_element_type=f32)


def sigmoid(v):
    return 0.5 + 0.5 * jnp.tanh(0.5 * v)


def later(y, clips):
    return jnp.concatenate([jnp.zeros_like(y[:, :clips]), y[:, : y.shape[1] - clips]], axis=1)


def sooner(y, clips):
    return jnp.concatenate([y[:, clips:], jnp.zeros_like(y[:, :clips])], axis=1)


def rows_sum(v):
    return jnp.sum(jnp.sum(v, axis=0), axis=0, keepdims=True)


def phase_sum(v):
    out = v
    for k in range(1, ALPHA):
        out = out + pltpu.roll(v, k * C_FMID, 1)
    return out


def block_sum(v):
    return sum(v[:, p * C_FAST : (p + 1) * C_FAST] for p in range(ALPHA))


def spread(mask, width):
    return jnp.tile(mask, (1, width // 128))


def frames_matrix(wfa_ref, out_ref, ends_ref):
    out_ref[...] = jnp.zeros_like(out_ref)
    ends_ref[...] = jnp.zeros_like(ends_ref)
    for p in range(ALPHA):
        for s in range(max(p - 1, 0), min(p + 2, ALPHA)):
            out_ref[p * C_FMID : (p + 1) * C_FMID, s * C_FAST : (s + 1) * C_FAST] = wfa_ref[s - p + 1]
    ends_ref[0, 0:C_FMID] = wfa_ref[0]
    ends_ref[1, 3 * C_FMID :] = wfa_ref[2]


def expand_matrix(wfc_ref, out_ref):
    out_ref[...] = jnp.zeros_like(out_ref)
    for p in range(ALPHA):
        out_ref[p * C_FMID : (p + 1) * C_FMID, p * C_FAST : (p + 1) * C_FAST] = wfc_ref[...]


class Exchange:
    def __init__(self, n_clip, moments, refs, rim_refs=None):
        self.n = n_clip
        self.moments = moments
        self.part, self.near, self.mid, self.far, self.near_send, self.near_recv, self.far_send, self.far_recv = refs
        self.clip, self.ha, self.wa = lax.axis_index("clip"), lax.axis_index("ha"), lax.axis_index("wa")
        self.me = 2 * self.ha + self.wa
        self.peers = [(1 - self.ha, self.wa), (self.ha, 1 - self.wa), (1 - self.ha, 1 - self.wa)]
        self.others = [lax.rem(self.clip + d, n_clip) for d in range(1, n_clip)]
        if rim_refs is not None:
            self.packs, self.lands, self.rim_send, self.rim_recv = rim_refs

    def signal(self):
        barrier = pltpu.get_barrier_semaphore()
        for a, b in self.peers:
            pl.semaphore_signal(barrier, inc=1, device_id=(self.clip, a, b), device_id_type=MESH)
        for other in self.others:
            pl.semaphore_signal(barrier, inc=1, device_id=(other, self.ha, self.wa), device_id_type=MESH)

    def meet(self):
        pl.semaphore_wait(pltpu.get_barrier_semaphore(), 3 + self.n - 1)

    def near_copy(self, k, slot):
        a, b = self.peers[k]
        return pltpu.make_async_remote_copy(
            src_ref=self.part, dst_ref=self.near.at[slot], send_sem=self.near_send.at[k],
            recv_sem=self.near_recv.at[slot], device_id=(self.clip, a, b), device_id_type=MESH,
        )

    def far_copy(self, d, slot):
        return pltpu.make_async_remote_copy(
            src_ref=self.mid, dst_ref=self.far.at[slot], send_sem=self.far_send.at[d],
            recv_sem=self.far_recv.at[slot], device_id=(self.others[d], self.ha, self.wa), device_id_type=MESH,
        )

    def rim_copy(self, k):
        a, b = self.peers[k]
        size = 1 if k == 2 else self.packs.shape[1]
        return pltpu.make_async_remote_copy(
            src_ref=self.packs.at[k, pl.ds(0, size)], dst_ref=self.lands.at[k, pl.ds(0, size)],
            send_sem=self.rim_send.at[k], recv_sem=self.rim_recv.at[k], device_id=(self.clip, a, b),
            device_id_type=MESH,
        )

    def send_near(self):
        for k in range(3):
            self.near_copy(k, self.me).start()
        self.near[self.me] = self.part[...]

    def send_rims(self, line, side):
        count = self.packs.shape[1]
        centre = self.part[0:1, :MIX] if self.moments else jnp.zeros((1, MIX), f32)
        self.packs[0] = (line[...] - centre).astype(bf16)
        self.packs[1] = (side[...] - centre).astype(bf16)
        self.packs[2, 0] = self.packs[0, (count - 1) * (1 - self.wa)]
        for k in range(3):
            self.rim_copy(k).start()

    def send_far(self):
        for k, (a, b) in enumerate(self.peers):
            self.near_copy(k, 2 * a + b).wait_recv()
        near = self.near
        if self.moments:
            mean = (near[0, 0:1] + near[1, 0:1] + near[2, 0:1] + near[3, 0:1]) * 0.25
            self.mid[0:1] = mean
            self.mid[1:2] = sum(near[k, 1:2] + (near[k, 0:1] - mean) ** 2 for k in range(4)) * 0.25
        else:
            self.mid[...] = near[0] + near[1] + near[2] + near[3]
        for d in range(self.n - 1):
            self.far_copy(d, self.clip).start()
        self.far[self.clip] = self.mid[...]

    def finish(self, out, weight):
        for d, other in enumerate(self.others):
            self.far_copy(d, other).wait_recv()
        width = out.shape[1]
        far = self.far
        if self.moments:
            mean = sum(far[k, 0:1] * spread(weight[k], width) for k in range(self.n))
            out[0:1] = mean
            out[1:2] = sum((far[k, 1:2] + (far[k, 0:1] - mean) ** 2) * spread(weight[k], width) for k in range(self.n))
        else:
            out[...] = sum(far[k] for k in range(self.n))
        for k in range(3):
            self.near_copy(k, self.me).wait_send()
        for d in range(self.n - 1):
            self.far_copy(d, self.clip).wait_send()

    def finish_rims(self, rims):
        for k, (a, b) in enumerate(self.peers):
            self.rim_copy(k).wait_recv()
            centre = self.near[2 * a + b, 0:1, :MIX] if self.moments else jnp.zeros((1, MIX), f32)
            land = self.lands[k, 0] if k == 2 else self.lands[k]
            rims[k][...] = land.astype(f32) + centre
        for k in range(3):
            self.rim_copy(k).wait_send()


def exchange_scratch(n_clip, count, width):
    return [
        pltpu.VMEM((count, width), f32),
        pltpu.VMEM((4, count, width), f32),
        pltpu.VMEM((count, width), f32),
        pltpu.VMEM((n_clip, count, width), f32),
        pltpu.SemaphoreType.DMA((3,)),
        pltpu.SemaphoreType.DMA((4,)),
        pltpu.SemaphoreType.DMA((n_clip,)),
        pltpu.SemaphoreType.DMA((n_clip,)),
    ]


def rim_scratch(side, slab):
    return [
        pltpu.VMEM((3, side, slab, MIX), bf16),
        pltpu.VMEM((3, side, slab, MIX), bf16),
        pltpu.SemaphoreType.DMA((3,)),
        pltpu.SemaphoreType.DMA((3,)),
    ]


def first_pass(clips, n_clip, xs, xf, m, perm, wl, wa, wp, wfa, weight,
               x_out, f_out, z_out, zp_out, st_out, base_out, mom, row, col, corner,
               keep, taps, ends, base, one, two, line, side, *refs):
    i = pl.program_id(0)
    cols = xs.shape[1]
    slab = m.shape[0]
    rows = cols * slab
    high = keep.shape[0]
    ex = Exchange(n_clip, True, refs[:8], refs[8:])
    here = cols * jnp.sum(m[...], axis=0, keepdims=True)
    count = high * here

    @pl.when(i == 0)
    def _():
        ex.signal()
        frames_matrix(wfa, taps, ends)

    @pl.when(i < high)
    def _():
        mask_in = spread(m[...], C_IN).astype(bf16)
        for w in range(cols):
            keep[i, w, :, :C_IN] = xs[:, w].reshape(slab, C_IN) * mask_in
            phases = dot(perm[...], xf[:, w].reshape(ALPHA * slab, C_FAST)).astype(bf16)
            for p in range(ALPHA):
                f_out[w, :, p * C_FAST : (p + 1) * C_FAST] = phases[p * slab : (p + 1) * slab]
        fast = f_out[...].reshape(rows, WIDE_FAST)
        lat = dot(fast[:, : 3 * C_FAST], wl[2:5].reshape(3 * C_FAST, C_LAT)).reshape(cols, slab, C_LAT)
        back = dot(fast[:, 2 * C_FAST :], wl[0:2].reshape(2 * C_FAST, C_LAT)).reshape(cols, slab, C_LAT)
        keep[i, :, :, C_IN:] = (lat + later(back, clips)).astype(bf16)
        x_out[...] = keep[i]
        joined = keep[i].reshape(rows, C_JOIN)
        za = dot(joined, wa[1]).reshape(cols, slab, C_MID)
        za = za + later(dot(joined, wa[0]).reshape(cols, slab, C_MID), clips)
        za = za + sooner(dot(joined, wa[2]).reshape(cols, slab, C_MID), clips)
        fa = dot_nt(fast, taps[...]).reshape(cols, slab, 128)
        fa = fa + later(dot_nt(fast[:, 3 * C_FAST :], ends[0]).reshape(cols, slab, 128), clips)
        fa = fa + sooner(dot_nt(fast[:, :C_FAST], ends[1]).reshape(cols, slab, 128), clips)
        z_out[:, :, :C_MID] = za
        z_out[:, :, C_MID:] = fa
        keep_rims(ex, i, high, z_out, line, side)
        add_moments(i == 0, ((0, za, 0), (C_MID, fa, 1)), m, here, base, one, two)

    @pl.when(i == high)
    def _():
        finish_moments(ex.part, base[...], one[...], two[...], count, ((0, C_MID, 0), (C_MID, 128, 1)))
        ex.meet()
        ex.send_near()
        ex.send_rims(line, side)

    @pl.when(i == high + 2)
    def _():
        ex.send_far()

    @pl.when(i >= high)
    def _():
        joined = keep[i - high].reshape(rows, C_JOIN)
        zp = dot(joined, wp[...]).reshape(cols, slab, C_IN)
        add_moments(i == high, ((MIX, zp, 0),), m, here, base, one, two)
        zp_out[...] = (zp - base[:, MIX:]).astype(bf16)

    @pl.when(i == 2 * high - 1)
    def _():
        s1 = one[:, MIX:] / spread(count, C_IN)
        st_out[0:1] = base[:, MIX:] + s1
        st_out[1:2] = two[:, MIX:] / spread(count, C_IN) - s1 * s1
        base_out[...] = base[:, MIX:]
        ex.finish(mom, weight)
        ex.finish_rims((row, col, corner))


def keep_rims(ex, i, high, block, line, side):
    side[i] = block[(block.shape[0] - 1) * (1 - ex.wa)]

    @pl.when(i == (high - 1) * (1 - ex.ha))
    def _():
        line[...] = block[...]


def add_moments(first, parts, m, here, base, one, two):
    @pl.when(first)
    def _():
        for at, z, fast in parts:
            width = z.shape[-1]
            mean = rows_sum(z * spread(m[...], width)) / spread(here, width)
            if fast:
                mean = phase_sum(mean) * 0.25
            base[:, at : at + width] = mean
            one[:, at : at + width] = jnp.zeros((1, width), f32)
            two[:, at : at + width] = jnp.zeros((1, width), f32)

    for at, z, _ in parts:
        width = z.shape[-1]
        off = (z - base[:, at : at + width]) * spread(m[...], width)
        one[:, at : at + width] += rows_sum(off)
        two[:, at : at + width] += rows_sum(off * off)


def finish_moments(st, base, one, two, count, parts):
    for at, width, fast in parts:
        s1 = one[:, at : at + width]
        s2 = two[:, at : at + width]
        if fast:
            s1 = phase_sum(s1) * 0.25
            s2 = phase_sum(s2) * 0.25
        n = spread(count.astype(f32), width)
        s1 = s1 / n
        st[0:1, at : at + width] = base[:, at : at + width] + s1
        st[1:2, at : at + width] = s2 / n - s1 * s1


def affine(moments, gain, shift, at, width):
    mean = moments[0:1, at : at + width]
    scale = lax.rsqrt(moments[1:2, at : at + width] + eps_norm)
    return mean, scale, gain, shift


def second_pass(n_clip, z1_hbm, row, col, corner, mom, mids, m, wb, wfb, stp, weight, cot,
                a_out, z_out, mom_out, zrow, zcol, zcorner, cot_out, z1, z1_sem, one, two, *refs):
    i = pl.program_id(0)
    high, cols, slab, _ = z1.shape
    rows = cols * slab
    ex = Exchange(n_clip, True, refs[:8], refs[8:])

    def fetch(h):
        return pltpu.make_async_copy(z1_hbm.at[h], z1.at[h], z1_sem.at[h])

    @pl.when(i == 0)
    def _():
        for h in range(high):
            fetch(h).start()
        ex.signal()
        mean, scale, g, b = affine(mom, mids[0], mids[1], 0, MIX)
        mult = scale * g
        mask = spread(m[...], MIX)

        def act(z):
            v = (z - mean) * mult + b
            return (v * sigmoid(v) * mask).astype(bf16)

        far = high + 1
        a_out[far * ex.ha] = jnp.zeros((cols + 2, slab, MIX), bf16)
        a_out[:, far * ex.wa] = jnp.zeros((high + 2, slab, MIX), bf16)
        a_out[far * (1 - ex.ha), 1 : 1 + cols] = act(row[...])
        a_out[1 : 1 + high, far * (1 - ex.wa)] = act(col[...])
        a_out[far * (1 - ex.ha), far * (1 - ex.wa)] = act(corner[...])

        def fill(h, carry):
            fetch(h).wait()
            a_out[h + 1, 1 : 1 + cols] = act(z1[h])
            return carry

        lax.fori_loop(0, high, fill, 0)

        def space(h, carry):
            slow = jnp.zeros((rows, C_MID), f32)
            fast = jnp.zeros((rows, 128), f32)
            for a in range(3):
                for c in range(3):
                    v = a_out[h + a, c : c + cols].reshape(rows, MIX)
                    slow = slow + dot(v[:, :C_MID], wb[a, c])
                    fast = fast + dot(v[:, C_MID:], wfb[3 * a + c])
            z_out[h, :, :, :C_MID] = slow.reshape(cols, slab, C_MID)
            z_out[h, :, :, C_MID:] = fast.reshape(cols, slab, 128)
            return carry

        lax.fori_loop(0, high, space, 0)
        here = cols * jnp.sum(m[...], axis=0, keepdims=True)
        base = rows_sum(z_out[0] * mask) / spread(here, MIX)
        base = jnp.concatenate([base[:, :C_MID], phase_sum(base[:, C_MID:]) * 0.25], axis=1)
        one[...] = jnp.zeros_like(one)
        two[...] = jnp.zeros_like(two)

        def gather(h, carry):
            off = (z_out[h] - base) * mask
            one[...] += rows_sum(off)
            two[...] += rows_sum(off * off)
            return carry

        lax.fori_loop(0, high, gather, 0)
        finish_moments(ex.part, base, one[...], two[...], high * here, ((0, C_MID, 0), (C_MID, 128, 1)))
        ex.part[:, MIX:] = stp[...]
        ex.meet()
        ex.send_near()
        ex.send_rims(z_out.at[(high - 1) * (1 - ex.ha)], z_out.at[:, (cols - 1) * (1 - ex.wa)])

    @pl.when(i == 3)
    def _():
        ex.send_far()

    @pl.when(i > 0)
    def _():
        half_mask = (0.5 * spread(m[...], C_IN)).astype(bf16)
        for w in range(cols):
            cot_out[w] = cot[:, w].reshape(slab, C_IN) * half_mask

    @pl.when(i == high)
    def _():
        ex.finish(mom_out, weight)
        ex.finish_rims((zrow, zcol, zcorner))


def third_pass(n_clip, z2, mom, mids, m, wc, wfc, weight, fcot, perm,
               a_out, mom_out, fcot_out, big, base, one, two, *refs):
    i = pl.program_id(0)
    high = pl.num_programs(0) // 2
    cols, slab, _ = z2.shape
    rows = cols * slab
    ex = Exchange(n_clip, True, refs)
    here = cols * jnp.sum(m[...], axis=0, keepdims=True)

    @pl.when(i == 0)
    def _():
        ex.signal()
        expand_matrix(wfc, big)

    @pl.when(i < high)
    def _():
        mean, scale, g, b = affine(mom, mids[2], mids[3], 0, MIX)
        v = (z2[...] - mean) * (scale * g) + b
        a_out[...] = (v * sigmoid(v) * spread(m[...], MIX)).astype(bf16)
        a2 = a_out[...].reshape(rows, MIX)
        zc = dot(a2[:, :C_MID], wc[...]).reshape(cols, slab, C_IN)
        fc = dot(a2[:, C_MID:], big[...]).reshape(cols, slab, WIDE_FAST)

        @pl.when(i == 0)
        def _():
            base[:, :C_IN] = rows_sum(zc * spread(m[...], C_IN)) / spread(here, C_IN)
            base[:, C_IN:] = block_sum(rows_sum(fc * spread(m[...], WIDE_FAST))) / (4.0 * here)
            one[...] = jnp.zeros_like(one)
            two[...] = jnp.zeros_like(two)

        off = (zc - base[:, :C_IN]) * spread(m[...], C_IN)
        one[:, :C_IN] += rows_sum(off)
        two[:, :C_IN] += rows_sum(off * off)
        off = (fc - jnp.tile(base[:, C_IN:], (1, ALPHA))) * spread(m[...], WIDE_FAST)
        one[:, C_IN:] += block_sum(rows_sum(off)) * 0.25
        two[:, C_IN:] += block_sum(rows_sum(off * off)) * 0.25

    @pl.when(i == high)
    def _():
        finish_moments(ex.part, base[...], one[...], two[...], high * here, ((0, C_IN + C_FAST, 0),))
        ex.meet()
        ex.send_near()

    @pl.when(i == high + 2)
    def _():
        ex.send_far()

    @pl.when(i >= high)
    def _():
        for w in range(cols):
            phases = dot(perm[...], fcot[:, w].reshape(ALPHA * slab, C_FAST)).astype(bf16)
            for p in range(ALPHA):
                fcot_out[w, :, p * C_FAST : (p + 1) * C_FAST] = 0.5 * phases[p * slab : (p + 1) * slab]

    @pl.when(i == 2 * high - 1)
    def _():
        ex.finish(mom_out, weight)


def fourth_pass(n_clip, clips, a2, zp, base, mom2, mom3, sgain, sshift, fends, cot, fcot, fast_in, m, perm, wc,
                wfc, weight, so, fo, gs, gf, tot, so_keep, fo_keep, sums, big, z_line, f_line, *refs):
    i = pl.program_id(0)
    high = pl.num_programs(0) // 2
    cols, slab, _ = a2.shape
    ex = Exchange(n_clip, False, refs)

    @pl.when(i == 0)
    def _():
        ex.signal()
        expand_matrix(wfc, big)
        sums[...] = jnp.zeros_like(sums)

    def tile_sum(v):
        return jnp.sum(v.reshape(slab // 8, 8, v.shape[-1]), axis=0)

    @pl.when(i < high)
    def _():
        mid, far = 2 * C_MID, 2 * C_MID + C_IN
        mean_c = mom3[0:1, :C_IN]
        scale_c = lax.rsqrt(mom3[1:2, :C_IN] + eps_norm)
        mean_p = mom2[0:1, MIX:] - base[...]
        scale_p = lax.rsqrt(mom2[1:2, MIX:] + eps_norm)
        mean_f = jnp.tile(mom3[0:1, C_IN:], (1, ALPHA))
        scale_f = jnp.tile(lax.rsqrt(mom3[1:2, C_IN:] + eps_norm), (1, ALPHA))
        mult_c = 0.5 * sgain[:, mid:far] * scale_c
        mult_p = 0.5 * sgain[:, far:] * scale_p
        shift_cp = 0.5 * (sshift[:, mid:far] + sshift[:, far:])
        mult_f = 0.5 * jnp.tile(fends[0], (1, ALPHA)) * scale_f
        shift_f = 0.5 * jnp.tile(fends[1], (1, ALPHA))

        def gate(v, g):
            u = 1.0 + jnp.tanh(v)
            o = v * u
            return o, g * (u + o * (2.0 - u))

        totals = [jnp.zeros((8, C_IN), f32)] * 3 + [jnp.zeros((8, WIDE_FAST), f32)] * 2
        rows = a2[...].reshape(cols * slab, MIX)
        z_line[...] = dot(rows[:, :C_MID], wc[...]).reshape(cols, slab, C_IN)
        f_line[...] = dot(rows[:, C_MID:], big[...]).reshape(cols, slab, WIDE_FAST)
        for w in range(cols):
            zc = z_line[w] - mean_c
            zq = zp[w].astype(f32) - mean_p
            res, back = gate(mult_c * zc + mult_p * zq + shift_cp, cot[w].astype(f32))
            so_keep[i, w] = res.astype(bf16)
            gs[w] = back
            totals[0] += tile_sum(back)
            totals[1] += tile_sum(back * zc)
            totals[2] += tile_sum(back * zq)
            fc = f_line[w] - mean_f
            res, fback = gate(mult_f * fc + shift_f + 0.5 * fast_in[w].astype(f32), fcot[w].astype(f32))
            fo_keep[i, w] = res.astype(bf16)
            gf[w] = fback
            totals[3] += tile_sum(fback)
            totals[4] += tile_sum(fback * fc)
        scales = (None, scale_c, scale_p)
        for k in range(3):
            total = jnp.sum(totals[k], axis=0, keepdims=True)
            sums[:, k * C_IN : (k + 1) * C_IN] += total if k == 0 else total * scales[k]
        for k in range(2):
            at = 3 * C_IN + k * C_FAST
            total = jnp.sum(totals[3 + k], axis=0, keepdims=True)
            sums[:, at : at + C_FAST] += block_sum(total if k == 0 else total * scale_f)

    @pl.when(i == high)
    def _():
        ex.part[...] = sums[...]
        ex.meet()
        ex.send_near()

    @pl.when(i == high + 2)
    def _():
        ex.send_far()

    @pl.when(i >= high)
    def _():
        mask = spread(m[...], C_IN).astype(bf16)
        for w in range(cols):
            so[:, w] = (so_keep[i - high, w] * mask).reshape(slab // clips, clips, C_IN)
            wide = fo_keep[i - high, w]
            stacked = jnp.concatenate([wide[:, p * C_FAST : (p + 1) * C_FAST] for p in range(ALPHA)], axis=0)
            fo[:, w] = dot_tn(perm[...], stacked).astype(bf16).reshape(clips, slab, C_FAST)

    @pl.when(i == 2 * high - 1)
    def _():
        ex.finish(tot, weight)


def fifth_pass(n_clip, gs, gf, a2, zp, base, z2, mom2, mom3, tot4, inv, sgain, fends, mids, m, wc, wfc, x, weight,
               dzp_out, q_out, tot, row, col, corner, w_out, wfc_out,
               dzc_keep, dzp_keep, dfc_keep, a_keep, sums, big, z_line, f_line, line, side, *refs):
    i = pl.program_id(0)
    high, cols, slab, _ = dzc_keep.shape
    n = high * cols
    rows = cols * slab
    ex = Exchange(n_clip, False, refs[:8], refs[8:])

    @pl.when(i == 0)
    def _():
        ex.signal()
        expand_matrix(wfc, big)
        sums[...] = jnp.zeros_like(sums)

    @pl.when(i < high)
    def _():
        mask = spread(m[...], C_IN)
        inv_s = spread(inv[...], C_IN)
        inv_f = 0.25 * inv[...]
        mean_c = mom3[0:1, :C_IN]
        scale_c = lax.rsqrt(mom3[1:2, :C_IN] + eps_norm)
        mean_p = mom2[0:1, MIX:] - base[...]
        scale_p = lax.rsqrt(mom2[1:2, MIX:] + eps_norm)
        mean_f = jnp.tile(mom3[0:1, C_IN:], (1, ALPHA))
        scale_f = jnp.tile(lax.rsqrt(mom3[1:2, C_IN:] + eps_norm), (1, ALPHA))
        mult_c = sgain[:, 2 * C_MID : 2 * C_MID + C_IN] * scale_c
        mult_p = sgain[:, 2 * C_MID + C_IN :] * scale_p
        mult_f = jnp.tile(fends[0], (1, ALPHA)) * scale_f
        first_s = tot4[:, :C_IN] * inv_s
        second_c = mult_c * scale_c * tot4[:, C_IN : 2 * C_IN] * inv_s
        second_p = mult_p * scale_p * tot4[:, 2 * C_IN : 3 * C_IN] * inv_s
        first_f = mult_f * jnp.tile(tot4[:, 3 * C_IN : 3 * C_IN + C_FAST] * inv_f, (1, ALPHA))
        second_f = mult_f * scale_f * jnp.tile(tot4[:, 3 * C_IN + C_FAST :] * inv_f, (1, ALPHA))
        first_c = mult_c * first_s - mean_c * second_c
        first_p = mult_p * first_s - mean_p * second_p
        first_f = first_f - mean_f * second_f
        mask_f = spread(m[...], WIDE_FAST)
        a_keep[i] = a2[...]
        flat = a2[...].reshape(rows, MIX)
        z_line[...] = dot(flat[:, :C_MID], wc[...]).reshape(cols, slab, C_IN)
        f_line[...] = dot(flat[:, C_MID:], big[...]).reshape(cols, slab, WIDE_FAST)
        for w in range(cols):
            zc = z_line[w]
            g = gs[w]
            dzc_keep[i, w] = (mult_c * g - mask * (first_c + zc * second_c)).astype(bf16)
            dzp = (mult_p * g - mask * (first_p + zp[w].astype(f32) * second_p)).astype(bf16)
            dzp_keep[i, w] = dzp
            dzp_out[w] = dzp
            fc = f_line[w]
            dfc_keep[i, w] = (mult_f * gf[w] - mask_f * (first_f + fc * second_f)).astype(bf16)
        da = dot_nt(dzc_keep[i].reshape(rows, C_IN), wc[...]).reshape(cols, slab, C_MID)
        df = dot_nt(dfc_keep[i].reshape(rows, WIDE_FAST), big[...]).reshape(cols, slab, 128)
        grads = jnp.concatenate([da, df], axis=2)
        slope_back(grads, z2[...], mom2, mids[2], mids[3], m, q_out, sums)
        keep_rims(ex, i, high, q_out, line, side)

    @pl.when(i == high)
    def _():
        ex.part[...] = sums[...]
        ex.meet()
        ex.send_near()
        ex.send_rims(line, side)

    @pl.when(i == high + 2)
    def _():
        ex.send_far()

    @pl.when(i >= high)
    def _():
        c = i - high
        got = dot_tn(x[...].reshape(n * slab, C_MID), dzp_keep[...].reshape(n * slab, C_IN)).astype(bf16)
        for b in range(C_IN // 256):
            at = pl.multiple_of(b * C_JOIN + c * C_MID, C_MID)
            w_out[pl.ds(at, C_MID), :] = got[:, b * 256 : (b + 1) * 256]

    @pl.when(i == pl.num_programs(0) - 1)
    def _():
        a = a_keep[...].reshape(n * slab, MIX)
        got = dot_tn(a[:, :C_MID], dzc_keep[...].reshape(n * slab, C_IN)).astype(bf16)
        for b in range(C_IN // 256):
            at = 4 * C_JOIN + b * C_MID
            w_out[at : at + C_MID, :] = got[:, b * 256 : (b + 1) * 256]
        wide = dot_tn(a[:, C_MID:], dfc_keep[...].reshape(n * slab, WIDE_FAST))
        wfc_out[...] = sum(
            wide[p * C_FMID : (p + 1) * C_FMID, p * C_FAST : (p + 1) * C_FAST] for p in range(ALPHA)
        )
        ex.finish(tot, weight)
        ex.finish_rims((row, col, corner))


def slope_back(grads, z, mom, gain, shift, m, q_out, sums):
    mean, scale, g, b = affine(mom, gain, shift, 0, MIX)
    zhat = (z - mean) * scale
    v = g * zhat + b
    sig = sigmoid(v)
    q = grads * (sig * (1.0 + v * (1.0 - sig)) * spread(m[...], MIX))
    q_out[...] = q
    for k, s in enumerate((rows_sum(q), rows_sum(q * zhat))):
        at = k * MIX
        sums[:, at : at + C_MID] += s[:, :C_MID]
        sums[:, at + C_MID : at + MIX] += phase_sum(s[:, C_MID:])


def norm_terms(mom, gain, tot, inv):
    mean = mom[0:1, :MIX]
    scale = lax.rsqrt(mom[1:2, :MIX] + eps_norm)
    share = jnp.concatenate([spread(inv[...], C_MID), 0.25 * inv[...]], axis=1)
    return mean, scale, gain * scale, tot[:, :MIX] * share, tot[:, MIX:] * share


def sixth_pass(n_clip, early_sizes, q2_hbm, z2_hbm, z1_hbm, a1_hbm, qrow, qcol, qcorner, zrow, zcol, zcorner, mom1, mom2, tot5, inv,
               mids, m, wb, wfb, weight, dwfc, w_hbm, q_out, tot, wb_out, kept_out,
               fast_sums, wide, q2, z2, z1, a1, q2_sem, z2_sem, z1_sem, a1_sem, sums, mine, land, *refs):
    i = pl.program_id(0)
    high, cols, slab, _ = z1.shape
    rows = cols * slab
    ex = Exchange(n_clip, False, refs[:8])
    early = Reducer(n_clip, early_sizes, mine, land, None, refs[8:10] + (None, None))
    end = early.stages - 1

    def fetch_w():
        return pltpu.make_async_copy(w_hbm, mine, a1_sem.at[1])

    moved = ((q2_hbm, q2, q2_sem), (z2_hbm, z2, z2_sem), (z1_hbm, z1, z1_sem))

    def fetch(k, h):
        a, b, s = moved[k]
        return pltpu.make_async_copy(a.at[h], b.at[h], s.at[h])

    def fetch_a1():
        return pltpu.make_async_copy(a1_hbm, a1, a1_sem.at[0])

    @pl.when(i == 0)
    def _():
        fetch_w().start()
        wb_out[9 * C_MID :, :] = jnp.zeros((wb_out.shape[0] - 9 * C_MID, 256), bf16)
        for h in range(high):
            fetch(0, h).start()
            fetch(1, h).start()
        for h in range(high):
            fetch(2, h).start()
        fetch_a1().start()
        ex.signal()
        mean, scale, mult, first, second = norm_terms(mom2, mids[2], tot5, inv)
        mask = spread(m[...], MIX)

        def grad(q, z):
            return (mult * (q - mask * (first + (z - mean) * scale * second))).astype(bf16)

        far = high + 1
        wide[far * ex.ha] = jnp.zeros((cols + 2, slab, MIX), bf16)
        wide[:, far * ex.wa] = jnp.zeros((high + 2, slab, MIX), bf16)
        wide[far * (1 - ex.ha), 1 : 1 + cols] = grad(qrow[...], zrow[...])
        wide[1 : 1 + high, far * (1 - ex.wa)] = grad(qcol[...], zcol[...])
        wide[far * (1 - ex.ha), far * (1 - ex.wa)] = grad(qcorner[...], zcorner[...])
        fetch_w().wait()
        ex.meet()
        early.send(0)

        def fill(h, carry):
            fetch(0, h).wait()
            fetch(1, h).wait()
            wide[h + 1, 1 : 1 + cols] = grad(q2[h], z2[h])
            return carry

        lax.fori_loop(0, high, fill, 0)
        sums[...] = jnp.zeros_like(sums)

        def space(h, carry):
            fetch(2, h).wait()
            slow = jnp.zeros((rows, C_MID), f32)
            fast = jnp.zeros((rows, 128), f32)
            for a in range(3):
                for c in range(3):
                    v = wide[h + 2 - a, 2 - c : 2 - c + cols].reshape(rows, MIX)
                    slow = slow + dot_nt(v[:, :C_MID], wb[a, c])
                    fast = fast + dot_nt(v[:, C_MID:], wfb[3 * a + c])
            grads = jnp.concatenate([slow, fast], axis=1).reshape(cols, slab, MIX)
            slope_back(grads, z1[h], mom1, mids[0], mids[1], m, q_out.at[h], sums)
            return carry

        lax.fori_loop(0, 3, space, 0)
        early.gather(0)
        lax.fori_loop(3, high, space, 0)
        ex.part[...] = sums[...]
        ex.send_near()
        fetch_a1().wait()

    @pl.when(i == 3)
    def _():
        ex.send_far()

    @pl.when(i > 0)
    def _():
        tap = i - 1
        v = a1[pl.ds(tap // 3, high), pl.ds(lax.rem(tap, 3), cols)].reshape(high * rows, MIX)
        d = wide[1 : 1 + high, 1 : 1 + cols].reshape(high * rows, MIX)
        wb_out[pl.ds(pl.multiple_of(tap * C_MID, C_MID), C_MID), :] = dot_tn(v[:, :C_MID], d[:, :C_MID]).astype(bf16)
        both = dot_tn(v[:, C_MID:], d[:, C_MID:])
        fast_sums[tap] = sum(
            both[p * C_FMID : (p + 1) * C_FMID, p * C_FMID : (p + 1) * C_FMID] for p in range(ALPHA)
        )

    for k, step in ((1, 1), (2, 5), (3, 7)):

        @pl.when(i == step)
        def _():
            early.gather(k)

    @pl.when(i == 9)
    def _():
        ex.finish(tot, weight)
        for k in range(4, end + 1):
            early.gather(k)
        early.export(kept_out)
        for q in range(10):
            r, c, width = small_place(q)
            wb_out[r : r + C_FMID, c : c + width] = (fast_sums[q] if q < 9 else dwfc[...]).astype(bf16)


def bit_of(axis, power):
    return lax.rem(lax.axis_index(axis) // (1 << power), 2)


def partner_of(axis, power):
    where = {name: lax.axis_index(name) for name in ("clip", "ha", "wa")}
    where[axis] = where[axis] + (1 - 2 * bit_of(axis, power)) * (1 << power)
    return (where["clip"], where["ha"], where["wa"])


def stage_orders(n_clip, sets):
    rest = [("wa", 0)] + [("clip", b) for b in range(n_clip.bit_length() - 1)]
    turn, last = rest[:3], rest[3:]
    return [[("ha", 0)] + turn[s % len(turn) :] + turn[: s % len(turn)] + last for s in range(sets)]


def chunk_of(rows):
    return max(k for k in range(16, min(rows, 256) + 1, 16) if rows % k == 0)


class Reducer:
    def __init__(self, n_clip, sizes, mine, land, done, sems):
        self.mine, self.land, self.done = mine, land, done
        self.rs_sent, self.rs_came, self.ag_sent, self.ag_came = sems
        self.sets = range(len(sizes))
        self.orders = stage_orders(n_clip, len(sizes))
        self.stages = len(self.orders[0])
        self.plan, self.starts, self.kept = Reducer.layout(n_clip, sizes)

    @staticmethod
    def layout(n_clip, sizes):
        stages = len(stage_orders(n_clip, 1)[0])
        plan, starts, kept = [], [], []
        start = land = 0
        for size in sizes:
            starts.append(start)
            start += size
            row = []
            for _ in range(stages):
                halve = size % 32 == 0
                size = size // 2 if halve else size
                row.append((halve, size, land))
                land += size
            plan.append(row)
            kept.append(size)
        return plan, starts, kept

    @staticmethod
    def scratch(n_clip, sizes):
        plan = Reducer.layout(n_clip, sizes)[0]
        last = plan[-1][-1]
        return pltpu.VMEM((last[1] + last[2], 256), bf16)

    @staticmethod
    def sems(n_clip, sizes, count=4):
        stages = len(stage_orders(n_clip, 1)[0])
        return [pltpu.SemaphoreType.DMA((len(sizes), stages)) for _ in range(count)]

    def low(self, s, k):
        low = jnp.int32(self.starts[s])
        for j in range(k):
            halve, count, _ = self.plan[s][j]
            if halve:
                low = low + bit_of(*self.orders[s][j]) * count
        return low

    @staticmethod
    def rows(ref, begin, count):
        return ref.at[pl.ds(pl.multiple_of(begin, 16), count)]

    def scatter_copy(self, s, k):
        halve, count, land = self.plan[s][k]
        axis, power = self.orders[s][k]
        begin = self.low(s, k)
        if halve:
            begin = begin + (1 - bit_of(axis, power)) * count
        return pltpu.make_async_remote_copy(
            src_ref=self.rows(self.mine, begin, count), dst_ref=self.rows(self.land, land, count),
            send_sem=self.rs_sent.at[s, k], recv_sem=self.rs_came.at[s, k],
            device_id=partner_of(axis, power), device_id_type=MESH,
        )

    def send(self, k):
        for s in self.sets:
            self.scatter_copy(s, k).start()

    def gather(self, k):
        for s in self.sets:
            halve, count, land = self.plan[s][k]
            copy = self.scatter_copy(s, k)
            copy.wait_recv()
            copy.wait_send()
            begin = self.low(s, k + 1)
            step = chunk_of(count)

            def add(i, carry):
                own = pl.ds(pl.multiple_of(begin + i * step, 16), step)
                came = pl.ds(pl.multiple_of(land + i * step, 16), step)
                self.mine[own, :] = (self.mine[own, :].astype(f32) + self.land[came, :].astype(f32)).astype(bf16)
                return carry

            lax.fori_loop(0, count // step, add, 0)
            if k + 1 < self.stages:
                self.scatter_copy(s, k + 1).start()

    def export(self, out):
        at = 0
        for s in self.sets:
            count = self.kept[s]
            out[at : at + count] = self.mine[pl.ds(pl.multiple_of(self.low(s, self.stages), 16), count), :]
            at += count

    def load(self, kept):
        at = 0
        for s in self.sets:
            count = self.kept[s]
            self.done[pl.ds(pl.multiple_of(self.low(s, self.stages), 16), count), :] = kept[at : at + count]
            at += count

    def keep(self):
        for s in self.sets:
            own = pl.ds(pl.multiple_of(self.low(s, self.stages), 16), self.kept[s])
            self.done[own, :] = self.mine[own, :]

    def regain(self):
        self.keep()
        self.spread(self.stages - 1)

    def gather_copy(self, s, k, other):
        halve, count, _ = self.plan[s][k]
        axis, power = self.orders[s][k]
        bit = bit_of(axis, power)
        begin = self.low(s, k) + ((1 - bit) if other else bit) * count
        return pltpu.make_async_remote_copy(
            src_ref=self.rows(self.done, begin, count), dst_ref=self.rows(self.done, begin, count),
            send_sem=self.ag_sent.at[s, k], recv_sem=self.ag_came.at[s, k],
            device_id=partner_of(axis, power), device_id_type=MESH,
        )

    def spread(self, k):
        for s in self.sets:
            if self.plan[s][k][0]:
                self.gather_copy(s, k, False).start()

    def take(self, k):
        for s in self.sets:
            if self.plan[s][k][0]:
                self.gather_copy(s, k, True).wait_recv()
                self.gather_copy(s, k, False).wait_send()
            if k > 0 and self.plan[s][k - 1][0]:
                self.gather_copy(s, k - 1, False).start()


SPACE_STEPS = (5, 9, 12, 15, 18, 18, 18, 18, 18, 18, 18)
FIRST_STEPS = (5, 9, 12, 15, 18)
HALF_STEPS = (12, 15, 18, 18, 18, 18, 18, 18, 18, 18, 18)
LATE_STEPS = (15, 18, 18, 18, 18, 18, 18, 18, 18, 18, 18)


def seventh_pass(clips, n_clip, early_sizes, space_sizes, half_sizes, late_sizes, q1, z1, dzp, gf, x, f, kept, space_hbm, mom1, tot6, inv,
                 mids, m, perm, wl, wa, wp, wfa, sx, fx, out1, out_b, out_h, out_a,
                 done1, done_b, done_h, done_a, da, dl, df, taps, ends, mine_b, land_b, mine_h, land_h, mine_a, land_a, load_sem, *sems):
    i = pl.program_id(0)
    cols, slab, _ = q1.shape
    high = da.shape[0]
    rows = cols * slab
    every = high * rows
    steps = C_JOIN // C_MID
    late = high + steps
    sems = iter(sems)
    first = Reducer(n_clip, early_sizes, None, None, done1, (None, None, next(sems), next(sems)))
    space = Reducer(n_clip, space_sizes, mine_b, land_b, done_b, [next(sems) for _ in range(4)])
    half = Reducer(n_clip, half_sizes, mine_h, land_h, done_h, [next(sems) for _ in range(4)])
    last = Reducer(n_clip, late_sizes, mine_a, land_a, done_a, [next(sems) for _ in range(4)])
    end = last.stages - 1

    @pl.when(i == 0)
    def _():
        load = pltpu.make_async_copy(space_hbm, mine_b, load_sem.at[0])
        load.start()
        greet_signal(n_clip)
        frames_matrix(wfa, taps, ends)
        first.load(kept)
        greet_wait(n_clip)
        first.spread(end)
        load.wait()
        space.send(0)

    plan, rest = {}, []
    final = pl.num_programs(0) - 1

    def book(ops, steps):
        left = []
        for j, op in enumerate(ops):
            step = steps[j * len(steps) // len(ops)]
            if step >= 2 * high + C_JOIN // C_MID - 1:
                left.append(op)
            else:
                plan.setdefault(step, []).append(op)
        rest.append(left)

    down, up = range(end + 1), range(end, -1, -1)
    book(
        [functools.partial(space.gather, k) for k in down] + [space.regain]
        + [functools.partial(space.take, k) for k in up], SPACE_STEPS,
    )
    book([functools.partial(first.take, k) for k in up], FIRST_STEPS)
    book(
        [functools.partial(half.gather, k) for k in down] + [half.regain]
        + [functools.partial(half.take, k) for k in up], HALF_STEPS,
    )
    book(
        [functools.partial(last.gather, k) for k in down] + [last.regain]
        + [functools.partial(last.take, k) for k in up], LATE_STEPS,
    )
    for step, ops in sorted(plan.items()):

        @pl.when(i == step)
        def _():
            for op in ops:
                op()

    @pl.when(i < high)
    def _():
        mean, scale, mult, one, two = norm_terms(mom1, mids[0], tot6, inv)
        zhat = (z1[...] - mean) * scale
        dz = mult * (q1[...] - spread(m[...], MIX) * (one + zhat * two))
        up, down = sooner(dz, clips), later(dz, clips)
        for k, v in enumerate((up, dz, down)):
            da[i, :, :, k * C_MID : (k + 1) * C_MID] = v[:, :, :C_MID].astype(bf16)
            df[i, :, :, k * 128 : (k + 1) * 128] = v[:, :, C_MID:].astype(bf16)
        dlat = dot_nt(dzp[...].reshape(rows, C_IN), wp[C_IN:])
        for k in range(3):
            dlat = dlat + dot_nt(da[i, :, :, k * C_MID : (k + 1) * C_MID].reshape(rows, C_MID), wa[k, C_IN:])
        dlat = dlat.astype(bf16).astype(f32).reshape(cols, slab, C_LAT)
        dl[i, :, :, :C_LAT] = dlat.astype(bf16)
        dl[i, :, :, C_LAT:] = sooner(dlat, clips).astype(bf16)

    @pl.when((i >= high) & (i < late))
    def _():
        c = i - high
        got = dot_tn(x[...].reshape(every, C_MID), da[...].reshape(every, 3 * C_MID)).astype(bf16)

        @pl.when(c < 2)
        def _():
            for k in range(3):
                mine_h[pl.ds(pl.multiple_of((2 * k + c) * C_MID, C_MID), C_MID), :] = got[:, k * C_MID : (k + 1) * C_MID]

        @pl.when(c >= 2)
        def _():
            for k in range(3):
                at = pl.multiple_of((3 * k + c - 2) * C_MID, C_MID)
                mine_a[pl.ds(at, C_MID), :] = got[:, k * C_MID : (k + 1) * C_MID]

        @pl.when(c == 1)
        def _():
            half.send(0)

    @pl.when(i == late - 1)
    def _():
        fast = f[...].reshape(every, WIDE_FAST)
        d = dl[...].reshape(every, 2 * C_LAT)
        at = 9 * C_MID
        mine_a[at + 2 * C_FAST : at + 5 * C_FAST, :] = dot_tn(fast[:, : 3 * C_FAST], d[:, :C_LAT]).astype(bf16)
        mine_a[at : at + 2 * C_FAST, :] = dot_tn(fast[:, 2 * C_FAST :], d[:, C_LAT:]).astype(bf16)
        at += 5 * C_FAST
        g = df[...].reshape(every, 3 * 128)
        mid = dot_tn(g[:, 128:256], fast)
        sums = [jnp.zeros((C_FMID, C_FAST), f32) for _ in range(3)]
        for p in range(ALPHA):
            for s in range(max(p - 1, 0), min(p + 2, ALPHA)):
                sums[s - p + 1] += mid[p * C_FMID : (p + 1) * C_FMID, s * C_FAST : (s + 1) * C_FAST]
        sums[0] += dot_tn(g[:, :128], fast[:, 3 * C_FAST :])[:C_FMID]
        sums[2] += dot_tn(g[:, 256:], fast[:, :C_FAST])[3 * C_FMID :]
        mine_a[at:, :] = jnp.zeros((mine_a.shape[0] - at, 256), bf16)
        for q in range(3):
            mine_a[at + q * C_FMID : at + (q + 1) * C_FMID, :C_FAST] = sums[q].astype(bf16)
        last.send(0)

    @pl.when(i >= late)
    def _():
        h = i - late
        dj = dot_nt(dzp[...].reshape(rows, C_IN), wp[:C_IN])
        for k in range(3):
            dj = dj + dot_nt(da[h, :, :, k * C_MID : (k + 1) * C_MID].reshape(rows, C_MID), wa[k, :C_IN])
        mask = spread(m[...], C_IN)
        dj = dj.reshape(cols, slab, C_IN)
        for w in range(cols):
            sx[:, w] = (dj[w] * mask).astype(bf16).reshape(slab // clips, clips, C_IN)
        g = df[h].reshape(rows, 3 * 128)
        d = dl[h].reshape(rows, 2 * C_LAT)
        total = gf[...].reshape(rows, WIDE_FAST) + dot(g[:, 128:256], taps[...])
        head = dot_nt(d[:, :C_LAT], wl[2:5].reshape(3 * C_FAST, C_LAT))
        tail = dot_nt(d[:, C_LAT:], wl[0:2].reshape(2 * C_FAST, C_LAT))
        blocks = [total[:, p * C_FAST : (p + 1) * C_FAST] for p in range(ALPHA)]
        for p in range(3):
            blocks[p] = blocks[p] + head[:, p * C_FAST : (p + 1) * C_FAST]
        for p in range(2):
            blocks[2 + p] = blocks[2 + p] + tail[:, p * C_FAST : (p + 1) * C_FAST]
        blocks[3] = blocks[3] + dot(g[:, :128], ends[0])
        blocks[0] = blocks[0] + dot(g[:, 256:], ends[1])
        blocks = [v.astype(bf16) for v in blocks]
        for w in range(cols):
            stacked = jnp.concatenate([v[w * slab : (w + 1) * slab] for v in blocks], axis=0)
            fx[:, w] = dot_tn(perm[...], stacked).astype(bf16).reshape(clips, slab, C_FAST)

    @pl.when(i == final)
    def _():
        for k in range(max(len(left) for left in rest)):
            for left in rest:
                if k < len(left):
                    left[k]()
        saves = [
            pltpu.make_async_copy(a, b, load_sem.at[k])
            for k, (a, b) in enumerate(((done1, out1), (done_b, out_b), (done_h, out_h), (done_a, out_a)))
        ]
        for save in saves:
            save.start()
        for save in saves:
            save.wait()


def small_place(q):
    return 9 * C_MID + (q % 5) * C_FMID, (q // 5) * 128, C_FMID if q < 9 else C_FAST


def greet_signal(n_clip):
    barrier = pltpu.get_barrier_semaphore()
    for axis, power in stage_orders(n_clip, 1)[0]:
        pl.semaphore_signal(barrier, inc=1, device_id=partner_of(axis, power), device_id_type=MESH)


def greet_wait(n_clip):
    pl.semaphore_wait(pltpu.get_barrier_semaphore(), len(stage_orders(n_clip, 1)[0]))


def finish_outputs(so, fo, sx, fx, done1, done_b, done_h, done_a, tot4, tot5, tot6, so_out, fo_out, sx_out, fx_out,
                   wp_hbm, wc_hbm, wb_hbm, wa_hbm, wl_hbm, wfa_out, wfc_out, wfb_out, sgain_out, sshift_out, fgain_out,
                   fshift_out, wp, wc, wb, wa, wl, sem):
    i = pl.program_id(0)
    moves = ((wp, wp_hbm), (wc, wc_hbm), (wb, wb_hbm), (wa, wa_hbm), (wl, wl_hbm))

    def move(k):
        return pltpu.make_async_copy(moves[k][0], moves[k][1], sem.at[k])

    @pl.when(i == 0)
    def _():
        for b in range(C_IN // 256):
            wp[:, b * 256 : (b + 1) * 256] = done1[b * C_JOIN : (b + 1) * C_JOIN, :].astype(f32)
        move(0).start()
        for b in range(C_IN // 256):
            at = 4 * C_JOIN + b * C_MID
            wc[:, b * 256 : (b + 1) * 256] = done1[at : at + C_MID, :].astype(f32)
        move(1).start()

    @pl.when(i == 1)
    def _():
        for t in range(9):
            wb[t // 3, t % 3] = done_b[t * C_MID : (t + 1) * C_MID, :].astype(f32)
        move(2).start()

    @pl.when(i == 2)
    def _():
        for k in range(3):
            wa[k, : 2 * C_MID] = done_h[2 * k * C_MID : 2 * (k + 1) * C_MID, :].astype(f32)
            wa[k, 2 * C_MID :] = done_a[3 * k * C_MID : 3 * (k + 1) * C_MID, :].astype(f32)
        move(3).start()
        at = 9 * C_MID
        for k in range(5):
            wl[k] = done_a[at + k * C_FAST : at + (k + 1) * C_FAST, :].astype(f32)
        move(4).start()

    @pl.when(i == 3)
    def _():
        at = 9 * C_MID + 5 * C_FAST
        for q in range(3):
            wfa_out[q] = done_a[at + q * C_FMID : at + (q + 1) * C_FMID, :C_FAST].astype(f32)
        for q in range(10):
            r, c, width = small_place(q)
            piece = done_b[r : r + C_FMID, c : c + width].astype(f32)
            if q < 9:
                wfb_out[q] = piece
            else:
                wfc_out[...] = piece
        lane = lax.broadcasted_iota(jnp.int32, (1, 128), 1)
        for k, slow, fast in ((0, sshift_out, fshift_out), (1, sgain_out, fgain_out)):
            at = k * MIX
            row = 0
            for source, begin, width in (
                (tot6, at, C_MID), (tot5, at, C_MID), (tot4, k * C_IN, C_IN), (tot4, 2 * k * C_IN, C_IN)
            ):
                for c in range(begin, begin + width, 128):
                    slow[row : row + 1] = source[:, c : c + 128]
                    row += 1
            c = pltpu.roll(tot4[:, 3 * C_IN + k * C_FAST : 3 * C_IN + (k + 1) * C_FAST], 2 * C_FMID, 1)
            a, b = tot6[:, at + C_MID : at + MIX], tot5[:, at + C_MID : at + MIX]
            fast[:, :128] = jnp.where(lane < C_FMID, a, jnp.where(lane < 2 * C_FMID, b, c))
            fast[:, 128:] = c[:, : 2 * C_FMID]

    so_out[...] = so[...]
    fo_out[...] = fo[...]
    sx_out[...] = sx[...]
    fx_out[...] = fx[...]

    @pl.when(i == pl.num_programs(0) - 1)
    def _():
        for k in range(5):
            move(k).wait()


def prepare(clips, n_clip, counts, sgain_rows, sshift_rows, fgain, fshift, wb, m, perm, weight, inv, mids, last, wide,
            sgain, sshift):
    for k in range(sgain_rows.shape[0]):
        sgain[:, k * 128 : (k + 1) * 128] = sgain_rows[k : k + 1]
        sshift[:, k * 128 : (k + 1) * 128] = sshift_rows[k : k + 1]
    slab = m.shape[0]
    frames = slab // clips
    me = lax.axis_index("clip") * clips
    shift = clips.bit_length() - 1

    def real(shape):
        r = lax.broadcasted_iota(jnp.int32, shape, 0)
        own = jnp.zeros(shape, jnp.int32)
        for c in range(clips):
            own = jnp.where((r & (clips - 1)) == c, counts[me + c], own)
        return r, (r >> shift) < own

    m[...] = real(m.shape)[1].astype(f32)
    width = perm.shape[1]
    r, there = real((slab, width))
    col = lax.broadcasted_iota(jnp.int32, (slab, width), 1)
    for p in range(ALPHA):
        want = (r & (clips - 1)) * (ALPHA * frames) + ALPHA * (r >> shift) + p
        perm[p * slab : (p + 1) * slab] = ((want == col) & there).astype(f32).astype(bf16)
    groups = []
    for g in range(n_clip):
        part = counts[g * clips]
        for c in range(1, clips):
            part = part + counts[g * clips + c]
        groups.append(part)
    total = groups[0]
    for part in groups[1:]:
        total = total + part
    whole_count = jnp.full((1, 128), total, jnp.int32).astype(f32)
    inv[...] = 1.0 / (whole_count * (H * W))
    for g in range(n_clip):
        weight[g] = jnp.full((1, 128), groups[g], jnp.int32).astype(f32) / whole_count
    lane = lax.broadcasted_iota(jnp.int32, (1, 128), 1)
    for k in range(2):
        for j, (slow, fast) in enumerate(((sgain, fgain), (sshift, fshift))):
            mine = (lane >= k * C_FMID) & (lane < (k + 1) * C_FMID)
            mids[2 * k + j, :, :C_MID] = slow[:, k * C_MID : (k + 1) * C_MID]
            mids[2 * k + j, :, C_MID:] = phase_sum(jnp.where(mine, fast[:, :128], 0.0))
    for j, fast in enumerate((fgain, fshift)):
        last[j] = fast[:, 2 * C_FMID :]
    for t in range(9):
        w = wb[t]
        for p in range(ALPHA):
            parts = [jnp.zeros((C_FMID, C_FMID), bf16)] * ALPHA
            parts[p] = w
            wide[t, p * C_FMID : (p + 1) * C_FMID] = jnp.concatenate(parts, axis=1)


def vmem_spec():
    return pl.BlockSpec(memory_space=pltpu.VMEM)


def shaped(shape, kind):
    return jax.ShapeDtypeStruct(shape, kind)


def whole(shape):
    return pl.BlockSpec(shape, lambda h: (0,) * len(shape))


def per_line(shape):
    return pl.BlockSpec((None,) + tuple(shape), lambda h: (h,) + (0,) * len(shape))


def params(limit):
    return pltpu.CompilerParams(vmem_limit_bytes=60 * MIB)


def on_device(
    slow_input,
    fast_input,
    frame_counts,
    lateral_weight,
    slow_a_weight,
    slow_b_weight,
    slow_c_weight,
    slow_proj_weight,
    fast_a_weight,
    fast_b_weight,
    fast_c_weight,
    slow_gain,
    slow_shift,
    fast_gain,
    fast_shift,
    slow_cotangent,
    fast_cotangent,
):
    n_clip = lax.axis_size("clip")
    clips, frames, high, cols, _ = slow_input.shape
    slab = clips * frames
    lanes = slow_gain.reshape(-1, 128), slow_shift.reshape(-1, 128)
    slow_row = shaped((1, slow_gain.shape[0]), f32)
    vm = vmem_spec()
    m, perm, weight, inv, mids, ends, wfb, sgain, sshift = pl.pallas_call(
        functools.partial(prepare, clips, n_clip),
        in_specs=[pl.BlockSpec(memory_space=pltpu.SMEM)] + [vm] * 5,
        out_specs=(vm,) * 9,
        out_shape=(
            shaped((slab, 128), f32), shaped((ALPHA * slab, ALPHA * slab), bf16), shaped((n_clip, 1, 128), f32),
            shaped((1, 128), f32), shaped((4, 1, MIX), f32), shaped((2, 1, C_FAST), f32), shaped((9, 128, 128), bf16),
            slow_row, slow_row,
        ),
        compiler_params=params(60),
        name="prepare",
    )(frame_counts, *lanes, fast_gain[None], fast_shift[None], fast_b_weight.reshape(9, C_FMID, C_FMID))
    wfa = fast_a_weight.transpose(0, 2, 1)
    xs = slow_input.transpose(1, 2, 3, 0, 4)
    xf = fast_input.transpose(0, 2, 3, 1, 4)
    cot = slow_cotangent.transpose(1, 2, 3, 0, 4)
    fcot = fast_cotangent.transpose(0, 2, 3, 1, 4)
    def lines(c, kind):
        return shaped((high, cols, slab, c), kind)

    m_spec = whole((slab, 128))
    vm = vmem_spec()
    hbm = pl.BlockSpec(memory_space=pl.ANY)

    def early_line(shape):
        return pl.BlockSpec((None,) + tuple(shape), lambda i: (jnp.minimum(i, high - 1),) + (0,) * len(shape))

    def late_line(shape, begin):
        return pl.BlockSpec((None,) + tuple(shape), lambda i: (jnp.maximum(i - begin, 0),) + (0,) * len(shape))

    def slow_block(index):
        return pl.BlockSpec((frames, None, cols, clips, C_IN), lambda i: (0, index(i), 0, 0, 0))

    def fast_block(index):
        return pl.BlockSpec((clips, None, cols, ALPHA * frames, C_FAST), lambda i: (0, index(i), 0, 0, 0))

    def early(i):
        return jnp.minimum(i, high - 1)

    def after(begin):
        return lambda i: jnp.maximum(i - begin, 0)

    def remote(ident):
        return pltpu.CompilerParams(collective_id=ident, has_side_effects=True, vmem_limit_bytes=60 * MIB)

    rim_shapes = (shaped((cols, slab, MIX), f32), shaped((high, slab, MIX), f32), shaped((slab, MIX), f32))
    edge_scratch = [pltpu.VMEM((cols, slab, MIX), f32), pltpu.VMEM((high, slab, MIX), f32)]
    rims = rim_scratch(cols, slab)
    L1 = MIX + C_IN
    x, f, z1, zp, stp, base, mom1, row1, col1, corner1 = pl.pallas_call(
        functools.partial(first_pass, clips, n_clip),
        grid=(2 * high,),
        in_specs=[slow_block(early), fast_block(early)] + [vm] * 7,
        out_specs=(
            early_line((cols, slab, C_JOIN)), early_line((cols, slab, WIDE_FAST)), early_line((cols, slab, MIX)),
            late_line((cols, slab, C_IN), high), vm, vm, vm, vm, vm, vm,
        ),
        out_shape=(
            lines(C_JOIN, bf16), lines(WIDE_FAST, bf16), lines(MIX, f32), lines(C_IN, bf16), shaped((2, C_IN), f32),
            shaped((1, C_IN), f32), shaped((2, MIX), f32),
        ) + rim_shapes,
        scratch_shapes=[
            pltpu.VMEM((high, cols, slab, C_JOIN), bf16), pltpu.VMEM((128, WIDE_FAST), bf16),
            pltpu.VMEM((2, 128, C_FAST), bf16), pltpu.VMEM((1, L1), f32), pltpu.VMEM((1, L1), f32),
            pltpu.VMEM((1, L1), f32),
        ] + edge_scratch + exchange_scratch(n_clip, 2, MIX) + rims,
        compiler_params=remote(1),
        name="first_pass",
    )(xs, xf, m, perm, lateral_weight, slow_a_weight, slow_proj_weight, wfa, weight)

    a1, z2, mom2, zrow, zcol, zcorner, cot = pl.pallas_call(
        functools.partial(second_pass, n_clip),
        grid=(high + 1,),
        in_specs=[hbm] + [vm] * 10 + [slow_block(after(1))],
        out_specs=(vm, vm, vm, vm, vm, vm, late_line((cols, slab, C_IN), 1)),
        out_shape=(
            shaped((high + 2, cols + 2, slab, MIX), bf16), lines(MIX, f32), shaped((2, L1), f32),
        ) + rim_shapes + (lines(C_IN, bf16),),
        scratch_shapes=[
            pltpu.VMEM((high, cols, slab, MIX), f32), pltpu.SemaphoreType.DMA((high,)), pltpu.VMEM((1, MIX), f32),
            pltpu.VMEM((1, MIX), f32),
        ] + exchange_scratch(n_clip, 2, L1) + rims,
        compiler_params=remote(2),
        name="second_pass",
    )(z1, row1, col1, corner1, mom1, mids, m, slow_b_weight, wfb, stp, weight, cot)

    L3 = C_IN + C_FAST
    a2, mom3, fcot = pl.pallas_call(
        functools.partial(third_pass, n_clip),
        grid=(2 * high,),
        in_specs=[early_line((cols, slab, MIX))] + [vm] * 6 + [fast_block(after(high)), vm],
        out_specs=(early_line((cols, slab, MIX)), vm, late_line((cols, slab, WIDE_FAST), high)),
        out_shape=(lines(MIX, bf16), shaped((2, L3), f32), lines(WIDE_FAST, bf16)),
        scratch_shapes=[pltpu.VMEM((128, WIDE_FAST), bf16)] + [pltpu.VMEM((1, L3), f32)] * 3
        + exchange_scratch(n_clip, 2, L3),
        compiler_params=remote(3),
        name="third_pass",
    )(z2, mom2, mids, m, slow_c_weight, fast_c_weight, weight, fcot, perm)

    L4 = 3 * C_IN + 2 * C_FAST
    so, fo, gs, gf, tot4 = pl.pallas_call(
        functools.partial(fourth_pass, n_clip, clips),
        grid=(2 * high,),
        in_specs=[early_line((cols, slab, MIX)), early_line((cols, slab, C_IN))] + [vm] * 6 + [
            early_line((cols, slab, C_IN)), early_line((cols, slab, WIDE_FAST)), early_line((cols, slab, WIDE_FAST)),
        ] + [vm] * 5,
        out_specs=(
            slow_block(after(high)), fast_block(after(high)), early_line((cols, slab, C_IN)),
            early_line((cols, slab, WIDE_FAST)), vm,
        ),
        out_shape=(
            shaped(xs.shape, bf16), shaped(xf.shape, bf16), lines(C_IN, f32), lines(WIDE_FAST, f32),
            shaped((1, L4), f32),
        ),
        scratch_shapes=[
            pltpu.VMEM((high, cols, slab, C_IN), bf16), pltpu.VMEM((high, cols, slab, WIDE_FAST), bf16),
            pltpu.VMEM((1, L4), f32), pltpu.VMEM((128, WIDE_FAST), bf16), pltpu.VMEM((cols, slab, C_IN), f32),
            pltpu.VMEM((cols, slab, WIDE_FAST), f32),
        ] + exchange_scratch(n_clip, 1, L4),
        compiler_params=remote(4),
        name="fourth_pass",
    )(
        a2, zp, base, mom2, mom3, sgain, sshift, ends, cot, fcot, f, m, perm, slow_c_weight, fast_c_weight, weight,
    )

    n = high * cols
    early_sizes = (2048, 2048, 2048)
    space_sizes = (1024, 1024, 512)
    half_sizes = (512, 512, 512)
    late_sizes = (1024, 1024, 1024)

    def flat(v):
        return v.reshape((n,) + v.shape[2:])

    steps = C_JOIN // C_MID
    dzp, q2, tot5, qrow, qcol, qcorner, dw1, dwfc = pl.pallas_call(
        functools.partial(fifth_pass, n_clip),
        grid=(high + steps,),
        in_specs=[
            early_line((cols, slab, C_IN)), early_line((cols, slab, WIDE_FAST)), early_line((cols, slab, MIX)),
            early_line((cols, slab, C_IN)), vm, early_line((cols, slab, MIX)),
        ] + [vm] * 10 + [pl.BlockSpec((n, slab, C_MID), lambda i: (0, 0, jnp.clip(i - high, 0, steps - 1))), vm],
        out_specs=(
            early_line((cols, slab, C_IN)), early_line((cols, slab, MIX)), vm, vm, vm, vm, vm, vm,
        ),
        out_shape=(lines(C_IN, bf16), lines(MIX, f32), shaped((1, 2 * MIX), f32)) + rim_shapes + (
            shaped((sum(early_sizes), 256), bf16), shaped((C_FMID, C_FAST), f32),
        ),
        scratch_shapes=[
            pltpu.VMEM((high, cols, slab, C_IN), bf16), pltpu.VMEM((high, cols, slab, C_IN), bf16),
            pltpu.VMEM((high, cols, slab, WIDE_FAST), bf16), pltpu.VMEM((high, cols, slab, MIX), bf16),
            pltpu.VMEM((1, 2 * MIX), f32), pltpu.VMEM((128, WIDE_FAST), bf16), pltpu.VMEM((cols, slab, C_IN), f32),
            pltpu.VMEM((cols, slab, WIDE_FAST), f32),
        ] + edge_scratch + exchange_scratch(n_clip, 1, 2 * MIX) + rims,
        compiler_params=remote(5),
        name="fifth_pass",
    )(
        gs, gf, a2, zp, base, z2, mom2, mom3, tot4, inv, sgain, ends, mids, m, slow_c_weight, fast_c_weight,
        flat(x), weight,
    )

    q1, tot6, dwb, kept = pl.pallas_call(
        functools.partial(sixth_pass, n_clip, early_sizes),
        grid=(10,),
        in_specs=[hbm] * 4 + [vm] * 16 + [hbm],
        out_specs=(vm,) * 4,
        out_shape=(
            lines(MIX, f32), shaped((1, 2 * MIX), f32), shaped((sum(space_sizes), 256), bf16),
            shaped((sum(Reducer.layout(n_clip, early_sizes)[2]), 256), bf16),
        ),
        scratch_shapes=[pltpu.VMEM((9, C_FMID, C_FMID), f32), pltpu.VMEM((high + 2, cols + 2, slab, MIX), bf16)]
        + [pltpu.VMEM((high, cols, slab, MIX), f32)] * 3
        + [pltpu.VMEM((high + 2, cols + 2, slab, MIX), bf16)]
        + [pltpu.SemaphoreType.DMA((high,))] * 3
        + [pltpu.SemaphoreType.DMA((2,)), pltpu.VMEM((1, 2 * MIX), f32)]
        + [pltpu.VMEM((sum(early_sizes), 256), bf16), Reducer.scratch(n_clip, early_sizes)]
        + exchange_scratch(n_clip, 1, 2 * MIX) + Reducer.sems(n_clip, early_sizes, 2),
        compiler_params=remote(6),
        name="sixth_pass",
    )(
        q2, z2, z1, a1, qrow, qcol, qcorner, zrow, zcol, zcorner, mom1, mom2, tot5, inv, mids, m,
        slow_b_weight, wfb, weight, dwfc, dw1,
    )

    def twice_line(shape):
        begin = high + steps
        return pl.BlockSpec(
            (None,) + tuple(shape),
            lambda i: (jnp.where(i < begin, jnp.minimum(i, high - 1), i - begin),) + (0,) * len(shape),
        )

    sx, fx, done1, done_b, done_h, done_a = pl.pallas_call(
        functools.partial(seventh_pass, clips, n_clip, early_sizes, space_sizes, half_sizes, late_sizes),
        grid=(2 * high + steps,),
        in_specs=[
            early_line((cols, slab, MIX)), early_line((cols, slab, MIX)), twice_line((cols, slab, C_IN)),
            late_line((cols, slab, WIDE_FAST), high + steps),
            pl.BlockSpec((n, slab, C_MID), lambda i: (0, 0, jnp.clip(i - high, 0, steps - 1))), vm, vm, hbm,
        ] + [vm] * 10,
        out_specs=(slow_block(after(high + steps)), fast_block(after(high + steps)), hbm, hbm, hbm, hbm),
        out_shape=(
            shaped(xs.shape, bf16), shaped(xf.shape, bf16), shaped((sum(early_sizes), 256), bf16),
            shaped((sum(space_sizes), 256), bf16), shaped((sum(half_sizes), 256), bf16), shaped((sum(late_sizes), 256), bf16),
        ),
        scratch_shapes=[
            pltpu.VMEM((sum(v), 256), bf16) for v in (early_sizes, space_sizes, half_sizes, late_sizes)
        ] + [
            pltpu.VMEM((high, cols, slab, 3 * C_MID), bf16), pltpu.VMEM((high, cols, slab, 2 * C_LAT), bf16),
            pltpu.VMEM((high, cols, slab, 3 * 128), bf16), pltpu.VMEM((128, WIDE_FAST), bf16),
            pltpu.VMEM((2, 128, C_FAST), bf16), pltpu.VMEM((sum(space_sizes), 256), bf16),
            Reducer.scratch(n_clip, space_sizes), pltpu.VMEM((sum(half_sizes), 256), bf16),
            Reducer.scratch(n_clip, half_sizes), pltpu.VMEM((sum(late_sizes), 256), bf16),
            Reducer.scratch(n_clip, late_sizes), pltpu.SemaphoreType.DMA((4,)),
        ] + Reducer.sems(n_clip, early_sizes, 2) + Reducer.sems(n_clip, space_sizes) + Reducer.sems(n_clip, half_sizes)
        + Reducer.sems(n_clip, late_sizes),
        compiler_params=remote(7),
        name="seventh_pass",
    )(
        q1, z1, dzp, gf, flat(x), flat(f), kept, dwb, mom1, tot6, inv, mids, m, perm, lateral_weight, slow_a_weight,
        slow_proj_weight, wfa,
    )

    slow_rows, fast_row = shaped(lanes[0].shape, f32), shaped((1, fast_gain.shape[0]), f32)
    def here(i):
        return i

    weights = (
        shaped((C_JOIN, C_IN), f32), shaped((C_MID, C_IN), f32), shaped((3, 3, C_MID, C_MID), f32),
        shaped((3, C_JOIN, C_MID), f32), shaped((5, C_FAST, C_LAT), f32),
    )
    maps = [slow_block(here), fast_block(here)] * 2
    so, fo, sx, fx, dwp, dwc, dwb, dwa, dwl, dwfa, dwfc, dwfb, dsg, dss, dfg, dfs = pl.pallas_call(
        finish_outputs,
        grid=(high,),
        in_specs=maps + [vm] * 7,
        out_specs=tuple(maps) + (hbm,) * 5 + (vm,) * 7,
        out_shape=(shaped(xs.shape, bf16), shaped(xf.shape, bf16)) * 2 + weights + (
            shaped((3, C_FMID, C_FAST), f32), shaped((C_FMID, C_FAST), f32), shaped((9, C_FMID, C_FMID), f32),
            slow_rows, slow_rows, fast_row, fast_row,
        ),
        scratch_shapes=[pltpu.VMEM(v.shape, f32) for v in weights] + [pltpu.SemaphoreType.DMA((5,))],
        compiler_params=params(60),
        name="finish_outputs",
    )(so, fo, sx, fx, done1, done_b, done_h, done_a, tot4, tot5, tot6)
    return (
        so.transpose(3, 0, 1, 2, 4),
        fo.transpose(0, 3, 1, 2, 4),
        sx.transpose(3, 0, 1, 2, 4),
        fx.transpose(0, 3, 1, 2, 4),
        dwl,
        dwa,
        dwb,
        dwc,
        dwp,
        dwfa.transpose(0, 2, 1),
        dwfb.reshape(3, 3, C_FMID, C_FMID),
        dwfc,
        dsg.reshape(-1),
        dss.reshape(-1),
        dfg[0],
        dfs[0],
    )


def solution(mesh):
    tiles = P("clip", None, "ha", "wa", None)
    return jax.shard_map(
        on_device,
        mesh=mesh,
        in_specs=(tiles, tiles) + (P(),) * 13 + (tiles, tiles),
        out_specs=(tiles,) * 4 + (P(),) * 12,
        check_vma=False,
    )
```

```python
import functools

import jax
import jax.numpy as jnp
from jax import lax
from jax.experimental import pallas as pl
from jax.experimental.pallas import tpu as pltpu
from jax.sharding import PartitionSpec as P

ALPHA = 4
H = 14
W = 14
C_IN = 1024
C_LAT = 256
C_MID = 256
C_FAST = 128
C_FMID = 32
C_JOIN = C_IN + C_LAT
MIX = C_MID + ALPHA * C_FMID
WIDE_FAST = ALPHA * C_FAST

eps_norm = 1e-05
f32 = jnp.float32
bf16 = jnp.bfloat16
MESH = pl.DeviceIdType.MESH
MIB = 1 << 20


def dot(a, b):
    return lax.dot_general(a, b, (((1,), (0,)), ((), ())), preferred_element_type=f32)


def dot_nt(a, b):
    return lax.dot_general(a, b, (((1,), (1,)), ((), ())), preferred_element_type=f32)


def dot_tn(a, b):
    return lax.dot_general(a, b, (((0,), (0,)), ((), ())), preferred_element_type=f32)


def sigmoid(v):
    return 0.5 + 0.5 * jnp.tanh(0.5 * v)


def later(y, clips):
    return jnp.concatenate([jnp.zeros_like(y[:, :clips]), y[:, : y.shape[1] - clips]], axis=1)


def sooner(y, clips):
    return jnp.concatenate([y[:, clips:], jnp.zeros_like(y[:, :clips])], axis=1)


def rows_sum(v):
    return jnp.sum(jnp.sum(v, axis=0), axis=0, keepdims=True)


def phase_sum(v):
    out = v
    for k in range(1, ALPHA):
        out = out + pltpu.roll(v, k * C_FMID, 1)
    return out


def block_sum(v):
    return sum(v[:, p * C_FAST : (p + 1) * C_FAST] for p in range(ALPHA))


def spread(mask, width):
    return jnp.tile(mask, (1, width // 128))


def frames_matrix(wfa_ref, out_ref, ends_ref):
    out_ref[...] = jnp.zeros_like(out_ref)
    ends_ref[...] = jnp.zeros_like(ends_ref)
    for p in range(ALPHA):
        for s in range(max(p - 1, 0), min(p + 2, ALPHA)):
            out_ref[p * C_FMID : (p + 1) * C_FMID, s * C_FAST : (s + 1) * C_FAST] = wfa_ref[s - p + 1]
    ends_ref[0, 0:C_FMID] = wfa_ref[0]
    ends_ref[1, 3 * C_FMID :] = wfa_ref[2]


def expand_matrix(wfc_ref, out_ref):
    out_ref[...] = jnp.zeros_like(out_ref)
    for p in range(ALPHA):
        out_ref[p * C_FMID : (p + 1) * C_FMID, p * C_FAST : (p + 1) * C_FAST] = wfc_ref[...]


class Exchange:
    def __init__(self, n_clip, moments, refs, rim_refs=None):
        self.n = n_clip
        self.moments = moments
        self.part, self.near, self.mid, self.far, self.near_send, self.near_recv, self.far_send, self.far_recv = refs
        self.clip, self.ha, self.wa = lax.axis_index("clip"), lax.axis_index("ha"), lax.axis_index("wa")
        self.me = 2 * self.ha + self.wa
        self.peers = [(1 - self.ha, self.wa), (self.ha, 1 - self.wa), (1 - self.ha, 1 - self.wa)]
        self.others = [lax.rem(self.clip + d, n_clip) for d in range(1, n_clip)]
        if rim_refs is not None:
            self.packs, self.lands, self.rim_send, self.rim_recv = rim_refs

    def signal(self):
        barrier = pltpu.get_barrier_semaphore()
        for a, b in self.peers:
            pl.semaphore_signal(barrier, inc=1, device_id=(self.clip, a, b), device_id_type=MESH)
        for other in self.others:
            pl.semaphore_signal(barrier, inc=1, device_id=(other, self.ha, self.wa), device_id_type=MESH)

    def meet(self):
        pl.semaphore_wait(pltpu.get_barrier_semaphore(), 3 + self.n - 1)

    def near_copy(self, k, slot):
        a, b = self.peers[k]
        return pltpu.make_async_remote_copy(
            src_ref=self.part, dst_ref=self.near.at[slot], send_sem=self.near_send.at[k],
            recv_sem=self.near_recv.at[slot], device_id=(self.clip, a, b), device_id_type=MESH,
        )

    def far_copy(self, d, slot):
        return pltpu.make_async_remote_copy(
            src_ref=self.mid, dst_ref=self.far.at[slot], send_sem=self.far_send.at[d],
            recv_sem=self.far_recv.at[slot], device_id=(self.others[d], self.ha, self.wa), device_id_type=MESH,
        )

    def rim_copy(self, k):
        a, b = self.peers[k]
        size = 1 if k == 2 else self.packs.shape[1]
        return pltpu.make_async_remote_copy(
            src_ref=self.packs.at[k, pl.ds(0, size)], dst_ref=self.lands.at[k, pl.ds(0, size)],
            send_sem=self.rim_send.at[k], recv_sem=self.rim_recv.at[k], device_id=(self.clip, a, b),
            device_id_type=MESH,
        )

    def send_near(self):
        for k in range(3):
            self.near_copy(k, self.me).start()
        self.near[self.me] = self.part[...]

    def send_rims(self, line, side):
        count = self.packs.shape[1]
        centre = self.part[0:1, :MIX] if self.moments else jnp.zeros((1, MIX), f32)
        self.packs[0] = (line[...] - centre).astype(bf16)
        self.packs[1] = (side[...] - centre).astype(bf16)
        self.packs[2, 0] = self.packs[0, (count - 1) * (1 - self.wa)]
        for k in range(3):
            self.rim_copy(k).start()

    def send_far(self):
        for k, (a, b) in enumerate(self.peers):
            self.near_copy(k, 2 * a + b).wait_recv()
        near = self.near
        if self.moments:
            mean = (near[0, 0:1] + near[1, 0:1] + near[2, 0:1] + near[3, 0:1]) * 0.25
            self.mid[0:1] = mean
            self.mid[1:2] = sum(near[k, 1:2] + (near[k, 0:1] - mean) ** 2 for k in range(4)) * 0.25
        else:
            self.mid[...] = near[0] + near[1] + near[2] + near[3]
        for d in range(self.n - 1):
            self.far_copy(d, self.clip).start()
        self.far[self.clip] = self.mid[...]

    def finish(self, out, weight):
        for d, other in enumerate(self.others):
            self.far_copy(d, other).wait_recv()
        width = out.shape[1]
        far = self.far
        if self.moments:
            mean = sum(far[k, 0:1] * spread(weight[k], width) for k in range(self.n))
            out[0:1] = mean
            out[1:2] = sum((far[k, 1:2] + (far[k, 0:1] - mean) ** 2) * spread(weight[k], width) for k in range(self.n))
        else:
            out[...] = sum(far[k] for k in range(self.n))
        for k in range(3):
            self.near_copy(k, self.me).wait_send()
        for d in range(self.n - 1):
            self.far_copy(d, self.clip).wait_send()

    def finish_rims(self, rims):
        for k, (a, b) in enumerate(self.peers):
            self.rim_copy(k).wait_recv()
            centre = self.near[2 * a + b, 0:1, :MIX] if self.moments else jnp.zeros((1, MIX), f32)
            land = self.lands[k, 0] if k == 2 else self.lands[k]
            rims[k][...] = land.astype(f32) + centre
        for k in range(3):
            self.rim_copy(k).wait_send()


def exchange_scratch(n_clip, count, width):
    return [
        pltpu.VMEM((count, width), f32),
        pltpu.VMEM((4, count, width), f32),
        pltpu.VMEM((count, width), f32),
        pltpu.VMEM((n_clip, count, width), f32),
        pltpu.SemaphoreType.DMA((3,)),
        pltpu.SemaphoreType.DMA((4,)),
        pltpu.SemaphoreType.DMA((n_clip,)),
        pltpu.SemaphoreType.DMA((n_clip,)),
    ]


def rim_scratch(side, slab):
    return [
        pltpu.VMEM((3, side, slab, MIX), bf16),
        pltpu.VMEM((3, side, slab, MIX), bf16),
        pltpu.SemaphoreType.DMA((3,)),
        pltpu.SemaphoreType.DMA((3,)),
    ]


def first_pass(clips, n_clip, xs, xf, m, perm, wl, wa, wp, wfa, weight,
               x_out, f_out, z_out, zp_out, st_out, base_out, mom, row, col, corner,
               keep, taps, ends, base, one, two, line, side, *refs):
    i = pl.program_id(0)
    cols = xs.shape[1]
    slab = m.shape[0]
    rows = cols * slab
    high = keep.shape[0]
    ex = Exchange(n_clip, True, refs[:8], refs[8:])
    here = cols * jnp.sum(m[...], axis=0, keepdims=True)
    count = high * here

    @pl.when(i == 0)
    def _():
        ex.signal()
        frames_matrix(wfa, taps, ends)

    @pl.when(i < high)
    def _():
        mask_in = spread(m[...], C_IN).astype(bf16)
        for w in range(cols):
            keep[i, w, :, :C_IN] = xs[:, w].reshape(slab, C_IN) * mask_in
            phases = dot(perm[...], xf[:, w].reshape(ALPHA * slab, C_FAST)).astype(bf16)
            for p in range(ALPHA):
                f_out[w, :, p * C_FAST : (p + 1) * C_FAST] = phases[p * slab : (p + 1) * slab]
        fast = f_out[...].reshape(rows, WIDE_FAST)
        lat = dot(fast[:, : 3 * C_FAST], wl[2:5].reshape(3 * C_FAST, C_LAT)).reshape(cols, slab, C_LAT)
        back = dot(fast[:, 2 * C_FAST :], wl[0:2].reshape(2 * C_FAST, C_LAT)).reshape(cols, slab, C_LAT)
        keep[i, :, :, C_IN:] = (lat + later(back, clips)).astype(bf16)
        x_out[...] = keep[i]
        joined = keep[i].reshape(rows, C_JOIN)
        za = dot(joined, wa[1]).reshape(cols, slab, C_MID)
        za = za + later(dot(joined, wa[0]).reshape(cols, slab, C_MID), clips)
        za = za + sooner(dot(joined, wa[2]).reshape(cols, slab, C_MID), clips)
        fa = dot_nt(fast, taps[...]).reshape(cols, slab, 128)
        fa = fa + later(dot_nt(fast[:, 3 * C_FAST :], ends[0]).reshape(cols, slab, 128), clips)
        fa = fa + sooner(dot_nt(fast[:, :C_FAST], ends[1]).reshape(cols, slab, 128), clips)
        z_out[:, :, :C_MID] = za
        z_out[:, :, C_MID:] = fa
        keep_rims(ex, i, high, z_out, line, side)
        add_moments(i == 0, ((0, za, 0), (C_MID, fa, 1)), m, here, base, one, two)

    @pl.when(i == high)
    def _():
        finish_moments(ex.part, base[...], one[...], two[...], count, ((0, C_MID, 0), (C_MID, 128, 1)))
        ex.meet()
        ex.send_near()
        ex.send_rims(line, side)

    @pl.when(i == high + 2)
    def _():
        ex.send_far()

    @pl.when(i >= high)
    def _():
        joined = keep[i - high].reshape(rows, C_JOIN)
        zp = dot(joined, wp[...]).reshape(cols, slab, C_IN)
        add_moments(i == high, ((MIX, zp, 0),), m, here, base, one, two, zp_out)

    @pl.when(i == 2 * high - 1)
    def _():
        s1 = one[:, MIX:] / spread(count, C_IN)
        st_out[0:1] = base[:, MIX:] + s1
        st_out[1:2] = two[:, MIX:] / spread(count, C_IN) - s1 * s1
        base_out[...] = base[:, MIX:]
        ex.finish(mom, weight)
        ex.finish_rims((row, col, corner))


def keep_rims(ex, i, high, block, line, side):
    side[i] = block[(block.shape[0] - 1) * (1 - ex.wa)]

    @pl.when(i == (high - 1) * (1 - ex.ha))
    def _():
        line[...] = block[...]


def add_moments(first, parts, m, here, base, one, two, kept=None):
    @pl.when(first)
    def _():
        for at, z, fast in parts:
            width = z.shape[-1]
            mean = rows_sum(z * spread(m[...], width)) / spread(here, width)
            if fast:
                mean = phase_sum(mean) * 0.25
            base[:, at : at + width] = mean
            one[:, at : at + width] = jnp.zeros((1, width), f32)
            two[:, at : at + width] = jnp.zeros((1, width), f32)

    for at, z, _ in parts:
        width = z.shape[-1]
        off = z - base[:, at : at + width]
        if kept is not None:
            kept[...] = off.astype(bf16)
        off = off * spread(m[...], width)
        one[:, at : at + width] += rows_sum(off)
        two[:, at : at + width] += rows_sum(off * off)


def finish_moments(st, base, one, two, count, parts):
    for at, width, fast in parts:
        s1 = one[:, at : at + width]
        s2 = two[:, at : at + width]
        if fast:
            s1 = phase_sum(s1) * 0.25
            s2 = phase_sum(s2) * 0.25
        n = spread(count.astype(f32), width)
        s1 = s1 / n
        st[0:1, at : at + width] = base[:, at : at + width] + s1
        st[1:2, at : at + width] = s2 / n - s1 * s1


def affine(moments, gain, shift, at, width):
    mean = moments[0:1, at : at + width]
    scale = lax.rsqrt(moments[1:2, at : at + width] + eps_norm)
    return mean, scale, gain, shift


def second_pass(n_clip, z1_hbm, row, col, corner, mom, mids, m, wb, wfb, stp, weight, cot,
                a_out, z_out, mom_out, zrow, zcol, zcorner, cot_out, z1, z1_sem, one, two, *refs):
    i = pl.program_id(0)
    high, cols, slab, _ = z1.shape
    rows = cols * slab
    ex = Exchange(n_clip, True, refs[:8], refs[8:])

    def fetch(h):
        return pltpu.make_async_copy(z1_hbm.at[h], z1.at[h], z1_sem.at[h])

    @pl.when(i == 0)
    def _():
        for h in range(high):
            fetch(h).start()
        ex.signal()
        mean, scale, g, b = affine(mom, mids[0], mids[1], 0, MIX)
        mult = scale * g
        mask = spread(m[...], MIX)

        def act(z):
            v = (z - mean) * mult + b
            return (v * sigmoid(v) * mask).astype(bf16)

        far = high + 1
        a_out[far * ex.ha] = jnp.zeros((cols + 2, slab, MIX), bf16)
        a_out[:, far * ex.wa] = jnp.zeros((high + 2, slab, MIX), bf16)
        a_out[far * (1 - ex.ha), 1 : 1 + cols] = act(row[...])
        a_out[1 : 1 + high, far * (1 - ex.wa)] = act(col[...])
        a_out[far * (1 - ex.ha), far * (1 - ex.wa)] = act(corner[...])

        def fill(h, carry):
            fetch(h).wait()
            a_out[h + 1, 1 : 1 + cols] = act(z1[h])
            return carry

        lax.fori_loop(0, high, fill, 0)

        def space(h, carry):
            slow = jnp.zeros((rows, C_MID), f32)
            fast = jnp.zeros((rows, 128), f32)
            for a in range(3):
                v = [a_out[h + a, c : c + cols].reshape(rows, MIX) for c in range(3)]
                slow = slow + dot(
                    jnp.concatenate([u[:, :C_MID] for u in v], axis=1), wb[a].reshape(3 * C_MID, C_MID)
                )
                fast = fast + dot(
                    jnp.concatenate([u[:, C_MID:] for u in v], axis=1), wfb[3 * a : 3 * a + 3].reshape(3 * 128, 128)
                )
            z_out[h, :, :, :C_MID] = slow.reshape(cols, slab, C_MID)
            z_out[h, :, :, C_MID:] = fast.reshape(cols, slab, 128)
            return carry

        lax.fori_loop(0, high, space, 0)
        here = cols * jnp.sum(m[...], axis=0, keepdims=True)
        base = rows_sum(z_out[0] * mask) / spread(here, MIX)
        base = jnp.concatenate([base[:, :C_MID], phase_sum(base[:, C_MID:]) * 0.25], axis=1)
        one[...] = jnp.zeros_like(one)
        two[...] = jnp.zeros_like(two)

        def gather(h, carry):
            off = (z_out[h] - base) * mask
            one[...] += rows_sum(off)
            two[...] += rows_sum(off * off)
            return carry

        lax.fori_loop(0, high, gather, 0)
        finish_moments(ex.part, base, one[...], two[...], high * here, ((0, C_MID, 0), (C_MID, 128, 1)))
        ex.part[:, MIX:] = stp[...]
        ex.meet()
        ex.send_near()
        ex.send_rims(z_out.at[(high - 1) * (1 - ex.ha)], z_out.at[:, (cols - 1) * (1 - ex.wa)])

    @pl.when(i == 3)
    def _():
        ex.send_far()

    @pl.when(i > 0)
    def _():
        half_mask = (0.5 * spread(m[...], C_IN)).astype(bf16)
        for w in range(cols):
            cot_out[w] = cot[:, w].reshape(slab, C_IN) * half_mask

    @pl.when(i == high)
    def _():
        ex.finish(mom_out, weight)
        ex.finish_rims((zrow, zcol, zcorner))


def third_pass(n_clip, z2, mom, mids, m, wc, wfc, weight, fcot, perm,
               a_out, mom_out, fcot_out, big, base, one, two, *refs):
    i = pl.program_id(0)
    high = pl.num_programs(0) // 2
    cols, slab, _ = z2.shape
    rows = cols * slab
    ex = Exchange(n_clip, True, refs)
    here = cols * jnp.sum(m[...], axis=0, keepdims=True)

    @pl.when(i == 0)
    def _():
        ex.signal()
        expand_matrix(wfc, big)

    @pl.when(i < high)
    def _():
        mean, scale, g, b = affine(mom, mids[2], mids[3], 0, MIX)
        v = (z2[...] - mean) * (scale * g) + b
        a_out[...] = (v * sigmoid(v) * spread(m[...], MIX)).astype(bf16)
        a2 = a_out[...].reshape(rows, MIX)
        zc = dot(a2[:, :C_MID], wc[...]).reshape(cols, slab, C_IN)
        fc = dot(a2[:, C_MID:], big[...]).reshape(cols, slab, WIDE_FAST)

        @pl.when(i == 0)
        def _():
            base[:, :C_IN] = rows_sum(zc * spread(m[...], C_IN)) / spread(here, C_IN)
            base[:, C_IN:] = block_sum(rows_sum(fc * spread(m[...], WIDE_FAST))) / (4.0 * here)
            one[...] = jnp.zeros_like(one)
            two[...] = jnp.zeros_like(two)

        off = (zc - base[:, :C_IN]) * spread(m[...], C_IN)
        one[:, :C_IN] += rows_sum(off)
        two[:, :C_IN] += rows_sum(off * off)
        off = (fc - jnp.tile(base[:, C_IN:], (1, ALPHA))) * spread(m[...], WIDE_FAST)
        one[:, C_IN:] += block_sum(rows_sum(off)) * 0.25
        two[:, C_IN:] += block_sum(rows_sum(off * off)) * 0.25

    @pl.when(i == high)
    def _():
        finish_moments(ex.part, base[...], one[...], two[...], high * here, ((0, C_IN + C_FAST, 0),))
        ex.meet()
        ex.send_near()

    @pl.when(i == high + 2)
    def _():
        ex.send_far()

    @pl.when(i >= high)
    def _():
        for w in range(cols):
            phases = dot(perm[...], fcot[:, w].reshape(ALPHA * slab, C_FAST)).astype(bf16)
            for p in range(ALPHA):
                fcot_out[w, :, p * C_FAST : (p + 1) * C_FAST] = 0.5 * phases[p * slab : (p + 1) * slab]

    @pl.when(i == 2 * high - 1)
    def _():
        ex.finish(mom_out, weight)


def fourth_pass(n_clip, clips, a2, zp, base, mom2, mom3, sgain, sshift, fends, cot, fcot, fast_in, m, perm, wc,
                wfc, weight, so, fo, gs, gf, tot, so_keep, fo_keep, sums, big, z_line, f_line, *refs):
    i = pl.program_id(0)
    high = pl.num_programs(0) // 2
    cols, slab, _ = a2.shape
    ex = Exchange(n_clip, False, refs)

    @pl.when(i == 0)
    def _():
        ex.signal()
        expand_matrix(wfc, big)
        sums[...] = jnp.zeros_like(sums)

    def tile_sum(v):
        return jnp.sum(v.reshape(slab // 8, 8, v.shape[-1]), axis=0)

    @pl.when(i < high)
    def _():
        mid, far = 2 * C_MID, 2 * C_MID + C_IN
        mean_c = mom3[0:1, :C_IN]
        scale_c = lax.rsqrt(mom3[1:2, :C_IN] + eps_norm)
        mean_p = mom2[0:1, MIX:] - base[...]
        scale_p = lax.rsqrt(mom2[1:2, MIX:] + eps_norm)
        mean_f = jnp.tile(mom3[0:1, C_IN:], (1, ALPHA))
        scale_f = jnp.tile(lax.rsqrt(mom3[1:2, C_IN:] + eps_norm), (1, ALPHA))
        mult_c = 0.5 * sgain[:, mid:far] * scale_c
        mult_p = 0.5 * sgain[:, far:] * scale_p
        shift_cp = 0.5 * (sshift[:, mid:far] + sshift[:, far:])
        mult_f = 0.5 * jnp.tile(fends[0], (1, ALPHA)) * scale_f
        shift_f = 0.5 * jnp.tile(fends[1], (1, ALPHA))

        def gate(v, g):
            u = 1.0 + jnp.tanh(v)
            o = v * u
            return o, g * (u + o * (2.0 - u))

        totals = [jnp.zeros((8, C_IN), f32)] * 3 + [jnp.zeros((8, WIDE_FAST), f32)] * 2
        rows = a2[...].reshape(cols * slab, MIX)
        z_line[...] = dot(rows[:, :C_MID], wc[...]).reshape(cols, slab, C_IN)
        f_line[...] = dot(rows[:, C_MID:], big[...]).reshape(cols, slab, WIDE_FAST)
        for w in range(cols):
            zc = z_line[w] - mean_c
            zq = zp[w].astype(f32) - mean_p
            res, back = gate(mult_c * zc + mult_p * zq + shift_cp, cot[w].astype(f32))
            so_keep[i, w] = res.astype(bf16)
            gs[w] = back
            totals[0] += tile_sum(back)
            totals[1] += tile_sum(back * zc)
            totals[2] += tile_sum(back * zq)
            fc = f_line[w] - mean_f
            res, fback = gate(mult_f * fc + shift_f + 0.5 * fast_in[w].astype(f32), fcot[w].astype(f32))
            fo_keep[i, w] = res.astype(bf16)
            gf[w] = fback
            totals[3] += tile_sum(fback)
            totals[4] += tile_sum(fback * fc)
        scales = (None, scale_c, scale_p)
        for k in range(3):
            total = jnp.sum(totals[k], axis=0, keepdims=True)
            sums[:, k * C_IN : (k + 1) * C_IN] += total if k == 0 else total * scales[k]
        for k in range(2):
            at = 3 * C_IN + k * C_FAST
            total = jnp.sum(totals[3 + k], axis=0, keepdims=True)
            sums[:, at : at + C_FAST] += block_sum(total if k == 0 else total * scale_f)

    @pl.when(i == high)
    def _():
        ex.part[...] = sums[...]
        ex.meet()
        ex.send_near()

    @pl.when(i == high + 2)
    def _():
        ex.send_far()

    @pl.when(i >= high)
    def _():
        mask = spread(m[...], C_IN).astype(bf16)
        for w in range(cols):
            so[:, w] = (so_keep[i - high, w] * mask).reshape(slab // clips, clips, C_IN)
            wide = fo_keep[i - high, w]
            stacked = jnp.concatenate([wide[:, p * C_FAST : (p + 1) * C_FAST] for p in range(ALPHA)], axis=0)
            fo[:, w] = dot_tn(perm[...], stacked).astype(bf16).reshape(clips, slab, C_FAST)

    @pl.when(i == 2 * high - 1)
    def _():
        ex.finish(tot, weight)


def fifth_pass(n_clip, gs, gf, a2, zp, base, z2, mom2, mom3, tot4, inv, sgain, fends, mids, m, wc, wfc, x, weight,
               dzp_out, q_out, tot, row, col, corner, w_out, wfc_out,
               dzc_keep, dzp_keep, dfc_keep, a_keep, sums, big, z_line, f_line, line, side, *refs):
    i = pl.program_id(0)
    high, cols, slab, _ = dzc_keep.shape
    n = high * cols
    rows = cols * slab
    ex = Exchange(n_clip, False, refs[:8], refs[8:])

    @pl.when(i == 0)
    def _():
        ex.signal()
        expand_matrix(wfc, big)
        sums[...] = jnp.zeros_like(sums)

    @pl.when(i < high)
    def _():
        mask = spread(m[...], C_IN)
        inv_s = spread(inv[...], C_IN)
        inv_f = 0.25 * inv[...]
        mean_c = mom3[0:1, :C_IN]
        scale_c = lax.rsqrt(mom3[1:2, :C_IN] + eps_norm)
        mean_p = mom2[0:1, MIX:] - base[...]
        scale_p = lax.rsqrt(mom2[1:2, MIX:] + eps_norm)
        mean_f = jnp.tile(mom3[0:1, C_IN:], (1, ALPHA))
        scale_f = jnp.tile(lax.rsqrt(mom3[1:2, C_IN:] + eps_norm), (1, ALPHA))
        mult_c = sgain[:, 2 * C_MID : 2 * C_MID + C_IN] * scale_c
        mult_p = sgain[:, 2 * C_MID + C_IN :] * scale_p
        mult_f = jnp.tile(fends[0], (1, ALPHA)) * scale_f
        first_s = tot4[:, :C_IN] * inv_s
        second_c = mult_c * scale_c * tot4[:, C_IN : 2 * C_IN] * inv_s
        second_p = mult_p * scale_p * tot4[:, 2 * C_IN : 3 * C_IN] * inv_s
        first_f = mult_f * jnp.tile(tot4[:, 3 * C_IN : 3 * C_IN + C_FAST] * inv_f, (1, ALPHA))
        second_f = mult_f * scale_f * jnp.tile(tot4[:, 3 * C_IN + C_FAST :] * inv_f, (1, ALPHA))
        first_c = mult_c * first_s - mean_c * second_c
        first_p = mult_p * first_s - mean_p * second_p
        first_f = first_f - mean_f * second_f
        mask_f = spread(m[...], WIDE_FAST)
        a_keep[i] = a2[...]
        flat = a2[...].reshape(rows, MIX)
        z_line[...] = dot(flat[:, :C_MID], wc[...]).reshape(cols, slab, C_IN)
        f_line[...] = dot(flat[:, C_MID:], big[...]).reshape(cols, slab, WIDE_FAST)
        for w in range(cols):
            zc = z_line[w]
            g = gs[w]
            dzc_keep[i, w] = (mult_c * g - mask * (first_c + zc * second_c)).astype(bf16)
            dzp = (mult_p * g - mask * (first_p + zp[w].astype(f32) * second_p)).astype(bf16)
            dzp_keep[i, w] = dzp
            dzp_out[w] = dzp
            fc = f_line[w]
            dfc_keep[i, w] = (mult_f * gf[w] - mask_f * (first_f + fc * second_f)).astype(bf16)
        da = dot_nt(dzc_keep[i].reshape(rows, C_IN), wc[...]).reshape(cols, slab, C_MID)
        df = dot_nt(dfc_keep[i].reshape(rows, WIDE_FAST), big[...]).reshape(cols, slab, 128)
        grads = jnp.concatenate([da, df], axis=2)
        slope_back(grads, z2[...], mom2, mids[2], mids[3], m, q_out, sums)
        keep_rims(ex, i, high, q_out, line, side)

    @pl.when(i == high)
    def _():
        ex.part[...] = sums[...]
        ex.meet()
        ex.send_near()
        ex.send_rims(line, side)

    @pl.when(i == high + 2)
    def _():
        ex.send_far()

    @pl.when(i >= high)
    def _():
        c = i - high
        got = dot_tn(x[...].reshape(n * slab, C_MID), dzp_keep[...].reshape(n * slab, C_IN)).astype(bf16)
        for b in range(C_IN // 256):
            at = pl.multiple_of(b * C_JOIN + c * C_MID, C_MID)
            w_out[pl.ds(at, C_MID), :] = got[:, b * 256 : (b + 1) * 256]

    @pl.when(i == pl.num_programs(0) - 1)
    def _():
        a = a_keep[...].reshape(n * slab, MIX)
        got = dot_tn(a[:, :C_MID], dzc_keep[...].reshape(n * slab, C_IN)).astype(bf16)
        for b in range(C_IN // 256):
            at = 4 * C_JOIN + b * C_MID
            w_out[at : at + C_MID, :] = got[:, b * 256 : (b + 1) * 256]
        wide = dot_tn(a[:, C_MID:], dfc_keep[...].reshape(n * slab, WIDE_FAST))
        wfc_out[...] = sum(
            wide[p * C_FMID : (p + 1) * C_FMID, p * C_FAST : (p + 1) * C_FAST] for p in range(ALPHA)
        )
        ex.finish(tot, weight)
        ex.finish_rims((row, col, corner))


def slope_back(grads, z, mom, gain, shift, m, q_out, sums):
    mean, scale, g, b = affine(mom, gain, shift, 0, MIX)
    zhat = (z - mean) * scale
    v = g * zhat + b
    sig = sigmoid(v)
    q = grads * (sig * (1.0 + v * (1.0 - sig)) * spread(m[...], MIX))
    q_out[...] = q
    for k, s in enumerate((rows_sum(q), rows_sum(q * zhat))):
        at = k * MIX
        sums[:, at : at + C_MID] += s[:, :C_MID]
        sums[:, at + C_MID : at + MIX] += phase_sum(s[:, C_MID:])


def norm_terms(mom, gain, tot, inv):
    mean = mom[0:1, :MIX]
    scale = lax.rsqrt(mom[1:2, :MIX] + eps_norm)
    share = jnp.concatenate([spread(inv[...], C_MID), 0.25 * inv[...]], axis=1)
    return mean, scale, gain * scale, tot[:, :MIX] * share, tot[:, MIX:] * share


def sixth_pass(n_clip, early_sizes, q2_hbm, z2_hbm, z1_hbm, a1_hbm, qrow, qcol, qcorner, zrow, zcol, zcorner, mom1, mom2, tot5, inv,
               mids, m, wb, wfb, weight, dwfc, w_hbm, q_out, tot, wb_out, kept_out,
               fast_sums, wide, q2, z2, z1, a1, q2_sem, z2_sem, z1_sem, a1_sem, sums, mine, land, *refs):
    i = pl.program_id(0)
    high, cols, slab, _ = z1.shape
    rows = cols * slab
    ex = Exchange(n_clip, False, refs[:8])
    early = Reducer(n_clip, early_sizes, mine, land, None, refs[8:10] + (None, None))
    end = early.stages - 1

    def fetch_w():
        return pltpu.make_async_copy(w_hbm, mine, a1_sem.at[1])

    moved = ((q2_hbm, q2, q2_sem), (z2_hbm, z2, z2_sem), (z1_hbm, z1, z1_sem))

    def fetch(k, h):
        a, b, s = moved[k]
        return pltpu.make_async_copy(a.at[h], b.at[h], s.at[h])

    def fetch_a1():
        return pltpu.make_async_copy(a1_hbm, a1, a1_sem.at[0])

    @pl.when(i == 0)
    def _():
        fetch_w().start()
        wb_out[9 * C_MID :, :] = jnp.zeros((wb_out.shape[0] - 9 * C_MID, 256), bf16)
        for h in range(high):
            fetch(0, h).start()
            fetch(1, h).start()
        for h in range(high):
            fetch(2, h).start()
        fetch_a1().start()
        ex.signal()
        mean, scale, mult, first, second = norm_terms(mom2, mids[2], tot5, inv)
        mask = spread(m[...], MIX)

        def grad(q, z):
            return (mult * (q - mask * (first + (z - mean) * scale * second))).astype(bf16)

        far = high + 1
        wide[far * ex.ha] = jnp.zeros((cols + 2, slab, MIX), bf16)
        wide[:, far * ex.wa] = jnp.zeros((high + 2, slab, MIX), bf16)
        wide[far * (1 - ex.ha), 1 : 1 + cols] = grad(qrow[...], zrow[...])
        wide[1 : 1 + high, far * (1 - ex.wa)] = grad(qcol[...], zcol[...])
        wide[far * (1 - ex.ha), far * (1 - ex.wa)] = grad(qcorner[...], zcorner[...])
        fetch_w().wait()
        ex.meet()
        early.send(0)

        def fill(h, carry):
            fetch(0, h).wait()
            fetch(1, h).wait()
            wide[h + 1, 1 : 1 + cols] = grad(q2[h], z2[h])
            return carry

        lax.fori_loop(0, high, fill, 0)
        sums[...] = jnp.zeros_like(sums)

        def space(h, carry):
            fetch(2, h).wait()
            slow = jnp.zeros((rows, C_MID), f32)
            fast = jnp.zeros((rows, 128), f32)
            for a in range(3):
                v = [wide[h + 2 - a, 2 - c : 2 - c + cols].reshape(rows, MIX) for c in range(3)]
                slow = slow + dot_nt(
                    jnp.concatenate([u[:, :C_MID] for u in v], axis=1),
                    jnp.concatenate([wb[a, c] for c in range(3)], axis=1),
                )
                fast = fast + dot_nt(
                    jnp.concatenate([u[:, C_MID:] for u in v], axis=1),
                    jnp.concatenate([wfb[3 * a + c] for c in range(3)], axis=1),
                )
            grads = jnp.concatenate([slow, fast], axis=1).reshape(cols, slab, MIX)
            slope_back(grads, z1[h], mom1, mids[0], mids[1], m, q_out.at[h], sums)
            return carry

        lax.fori_loop(0, 3, space, 0)
        early.gather(0)
        lax.fori_loop(3, high, space, 0)
        ex.part[...] = sums[...]
        ex.send_near()
        fetch_a1().wait()

    @pl.when(i == 3)
    def _():
        ex.send_far()

    @pl.when(i > 0)
    def _():
        tap = i - 1
        v = a1[pl.ds(tap // 3, high), pl.ds(lax.rem(tap, 3), cols)].reshape(high * rows, MIX)
        d = wide[1 : 1 + high, 1 : 1 + cols].reshape(high * rows, MIX)
        wb_out[pl.ds(pl.multiple_of(tap * C_MID, C_MID), C_MID), :] = dot_tn(v[:, :C_MID], d[:, :C_MID]).astype(bf16)
        both = dot_tn(v[:, C_MID:], d[:, C_MID:])
        fast_sums[tap] = sum(
            both[p * C_FMID : (p + 1) * C_FMID, p * C_FMID : (p + 1) * C_FMID] for p in range(ALPHA)
        )

    for k, step in ((1, 1), (2, 5), (3, 7)):

        @pl.when(i == step)
        def _():
            early.gather(k)

    @pl.when(i == 9)
    def _():
        ex.finish(tot, weight)
        for k in range(4, end + 1):
            early.gather(k)
        early.export(kept_out)
        for q in range(10):
            r, c, width = small_place(q)
            wb_out[r : r + C_FMID, c : c + width] = (fast_sums[q] if q < 9 else dwfc[...]).astype(bf16)


def bit_of(axis, power):
    return lax.rem(lax.axis_index(axis) // (1 << power), 2)


def partner_of(axis, power):
    where = {name: lax.axis_index(name) for name in ("clip", "ha", "wa")}
    where[axis] = where[axis] + (1 - 2 * bit_of(axis, power)) * (1 << power)
    return (where["clip"], where["ha"], where["wa"])


def stage_orders(n_clip, sets):
    rest = [("wa", 0)] + [("clip", b) for b in range(n_clip.bit_length() - 1)]
    turn, last = rest[:3], rest[3:]
    return [[("ha", 0)] + turn[s % len(turn) :] + turn[: s % len(turn)] + last for s in range(sets)]


def chunk_of(rows):
    return max(k for k in range(16, min(rows, 256) + 1, 16) if rows % k == 0)


class Reducer:
    def __init__(self, n_clip, sizes, mine, land, done, sems):
        self.mine, self.land, self.done = mine, land, done
        self.rs_sent, self.rs_came, self.ag_sent, self.ag_came = sems
        self.sets = range(len(sizes))
        self.orders = stage_orders(n_clip, len(sizes))
        self.stages = len(self.orders[0])
        self.plan, self.starts, self.kept = Reducer.layout(n_clip, sizes)

    @staticmethod
    def layout(n_clip, sizes):
        stages = len(stage_orders(n_clip, 1)[0])
        plan, starts, kept = [], [], []
        start = land = 0
        for size in sizes:
            starts.append(start)
            start += size
            row = []
            for _ in range(stages):
                halve = size % 32 == 0
                size = size // 2 if halve else size
                row.append((halve, size, land))
                land += size
            plan.append(row)
            kept.append(size)
        return plan, starts, kept

    @staticmethod
    def scratch(n_clip, sizes):
        plan = Reducer.layout(n_clip, sizes)[0]
        last = plan[-1][-1]
        return pltpu.VMEM((last[1] + last[2], 256), bf16)

    @staticmethod
    def sems(n_clip, sizes, count=4):
        stages = len(stage_orders(n_clip, 1)[0])
        return [pltpu.SemaphoreType.DMA((len(sizes), stages)) for _ in range(count)]

    def low(self, s, k):
        low = jnp.int32(self.starts[s])
        for j in range(k):
            halve, count, _ = self.plan[s][j]
            if halve:
                low = low + bit_of(*self.orders[s][j]) * count
        return low

    @staticmethod
    def rows(ref, begin, count):
        return ref.at[pl.ds(pl.multiple_of(begin, 16), count)]

    def scatter_copy(self, s, k):
        halve, count, land = self.plan[s][k]
        axis, power = self.orders[s][k]
        begin = self.low(s, k)
        if halve:
            begin = begin + (1 - bit_of(axis, power)) * count
        return pltpu.make_async_remote_copy(
            src_ref=self.rows(self.mine, begin, count), dst_ref=self.rows(self.land, land, count),
            send_sem=self.rs_sent.at[s, k], recv_sem=self.rs_came.at[s, k],
            device_id=partner_of(axis, power), device_id_type=MESH,
        )

    def send(self, k):
        for s in self.sets:
            self.scatter_copy(s, k).start()

    def gather(self, k):
        for s in self.sets:
            halve, count, land = self.plan[s][k]
            copy = self.scatter_copy(s, k)
            copy.wait_recv()
            copy.wait_send()
            begin = self.low(s, k + 1)
            step = chunk_of(count)

            def add(i, carry):
                own = pl.ds(pl.multiple_of(begin + i * step, 16), step)
                came = pl.ds(pl.multiple_of(land + i * step, 16), step)
                self.mine[own, :] = (self.mine[own, :].astype(f32) + self.land[came, :].astype(f32)).astype(bf16)
                return carry

            lax.fori_loop(0, count // step, add, 0)
            if k + 1 < self.stages:
                self.scatter_copy(s, k + 1).start()

    def export(self, out):
        at = 0
        for s in self.sets:
            count = self.kept[s]
            out[at : at + count] = self.mine[pl.ds(pl.multiple_of(self.low(s, self.stages), 16), count), :]
            at += count

    def load(self, kept):
        at = 0
        for s in self.sets:
            count = self.kept[s]
            self.done[pl.ds(pl.multiple_of(self.low(s, self.stages), 16), count), :] = kept[at : at + count]
            at += count

    def keep(self):
        for s in self.sets:
            own = pl.ds(pl.multiple_of(self.low(s, self.stages), 16), self.kept[s])
            self.done[own, :] = self.mine[own, :]

    def regain(self):
        self.keep()
        self.spread(self.stages - 1)

    def gather_copy(self, s, k, other):
        halve, count, _ = self.plan[s][k]
        axis, power = self.orders[s][k]
        bit = bit_of(axis, power)
        begin = self.low(s, k) + ((1 - bit) if other else bit) * count
        return pltpu.make_async_remote_copy(
            src_ref=self.rows(self.done, begin, count), dst_ref=self.rows(self.done, begin, count),
            send_sem=self.ag_sent.at[s, k], recv_sem=self.ag_came.at[s, k],
            device_id=partner_of(axis, power), device_id_type=MESH,
        )

    def spread(self, k):
        for s in self.sets:
            if self.plan[s][k][0]:
                self.gather_copy(s, k, False).start()

    def take(self, k):
        for s in self.sets:
            if self.plan[s][k][0]:
                self.gather_copy(s, k, True).wait_recv()
                self.gather_copy(s, k, False).wait_send()
            if k > 0 and self.plan[s][k - 1][0]:
                self.gather_copy(s, k - 1, False).start()


SPACE_STEPS = (5, 9, 12, 15, 18, 18, 18, 18, 18, 18, 18)
FIRST_STEPS = (5, 9, 12, 15, 18)
HALF_STEPS = (12, 15, 17, 18, 18, 18, 18, 18, 18, 18, 18)
LATE_STEPS = (15, 17, 18, 18, 18, 18, 18, 18, 18, 18, 18)


def seventh_pass(clips, n_clip, early_sizes, space_sizes, half_sizes, late_sizes, q1, z1, dzp, gf, x, f, kept, space_hbm, mom1, tot6, inv,
                 mids, m, perm, wl, wa, wp, wfa, sx, fx, out1, out_b, out_h, out_a,
                 done1, done_b, done_h, done_a, da, dl, df, taps, ends, mine_b, land_b, mine_h, land_h, mine_a, land_a, load_sem, *sems):
    i = pl.program_id(0)
    cols, slab, _ = q1.shape
    high = da.shape[0]
    rows = cols * slab
    every = high * rows
    steps = C_JOIN // C_MID
    late = high + steps
    sems = iter(sems)
    first = Reducer(n_clip, early_sizes, None, None, done1, (None, None, next(sems), next(sems)))
    space = Reducer(n_clip, space_sizes, mine_b, land_b, done_b, [next(sems) for _ in range(4)])
    half = Reducer(n_clip, half_sizes, mine_h, land_h, done_h, [next(sems) for _ in range(4)])
    last = Reducer(n_clip, late_sizes, mine_a, land_a, done_a, [next(sems) for _ in range(4)])
    end = last.stages - 1

    @pl.when(i == 0)
    def _():
        load = pltpu.make_async_copy(space_hbm, mine_b, load_sem.at[0])
        load.start()
        greet_signal(n_clip)
        frames_matrix(wfa, taps, ends)
        first.load(kept)
        greet_wait(n_clip)
        first.spread(end)
        load.wait()
        space.send(0)

    plan, rest = {}, []
    final = pl.num_programs(0) - 1

    def book(ops, steps):
        left = []
        for j, op in enumerate(ops):
            step = steps[j * len(steps) // len(ops)]
            if step >= 2 * high + C_JOIN // C_MID - 1:
                left.append(op)
            else:
                plan.setdefault(step, []).append(op)
        rest.append(left)

    down, up = range(end + 1), range(end, -1, -1)
    book(
        [functools.partial(space.gather, k) for k in down] + [space.regain]
        + [functools.partial(space.take, k) for k in up], SPACE_STEPS,
    )
    book([functools.partial(first.take, k) for k in up], FIRST_STEPS)
    book(
        [functools.partial(half.gather, k) for k in down] + [half.regain]
        + [functools.partial(half.take, k) for k in up], HALF_STEPS,
    )
    book(
        [functools.partial(last.gather, k) for k in down] + [last.regain]
        + [functools.partial(last.take, k) for k in up], LATE_STEPS,
    )
    for step, ops in sorted(plan.items()):

        @pl.when(i == step)
        def _():
            for op in ops:
                op()

    @pl.when(i < high)
    def _():
        mean, scale, mult, one, two = norm_terms(mom1, mids[0], tot6, inv)
        zhat = (z1[...] - mean) * scale
        dz = mult * (q1[...] - spread(m[...], MIX) * (one + zhat * two))
        up, down = sooner(dz, clips), later(dz, clips)
        for k, v in enumerate((up, dz, down)):
            da[i, :, :, k * C_MID : (k + 1) * C_MID] = v[:, :, :C_MID].astype(bf16)
            df[i, :, :, k * 128 : (k + 1) * 128] = v[:, :, C_MID:].astype(bf16)
        dlat = dot_nt(
            jnp.concatenate([dzp[...].reshape(rows, C_IN), da[i].reshape(rows, 3 * C_MID)], axis=1),
            jnp.concatenate([wp[C_IN:]] + [wa[k, C_IN:] for k in range(3)], axis=1),
        )
        dlat = dlat.astype(bf16).astype(f32).reshape(cols, slab, C_LAT)
        dl[i, :, :, :C_LAT] = dlat.astype(bf16)
        dl[i, :, :, C_LAT:] = sooner(dlat, clips).astype(bf16)

    @pl.when((i >= high) & (i < late))
    def _():
        c = i - high
        got = dot_tn(x[...].reshape(every, C_MID), da[...].reshape(every, 3 * C_MID)).astype(bf16)

        @pl.when(c < 2)
        def _():
            for k in range(3):
                mine_h[pl.ds(pl.multiple_of((2 * k + c) * C_MID, C_MID), C_MID), :] = got[:, k * C_MID : (k + 1) * C_MID]

        @pl.when(c >= 2)
        def _():
            for k in range(3):
                at = pl.multiple_of((3 * k + c - 2) * C_MID, C_MID)
                mine_a[pl.ds(at, C_MID), :] = got[:, k * C_MID : (k + 1) * C_MID]

        @pl.when(c == 1)
        def _():
            half.send(0)

    @pl.when(i == late - 1)
    def _():
        fast = f[...].reshape(every, WIDE_FAST)
        d = dl[...].reshape(every, 2 * C_LAT)
        at = 9 * C_MID
        mine_a[at + 2 * C_FAST : at + 5 * C_FAST, :] = dot_tn(fast[:, : 3 * C_FAST], d[:, :C_LAT]).astype(bf16)
        mine_a[at : at + 2 * C_FAST, :] = dot_tn(fast[:, 2 * C_FAST :], d[:, C_LAT:]).astype(bf16)
        at += 5 * C_FAST
        g = df[...].reshape(every, 3 * 128)
        mid = dot_tn(g[:, 128:256], fast)
        sums = [jnp.zeros((C_FMID, C_FAST), f32) for _ in range(3)]
        for p in range(ALPHA):
            for s in range(max(p - 1, 0), min(p + 2, ALPHA)):
                sums[s - p + 1] += mid[p * C_FMID : (p + 1) * C_FMID, s * C_FAST : (s + 1) * C_FAST]
        sums[0] += dot_tn(g[:, :128], fast[:, 3 * C_FAST :])[:C_FMID]
        sums[2] += dot_tn(g[:, 256:], fast[:, :C_FAST])[3 * C_FMID :]
        mine_a[at:, :] = jnp.zeros((mine_a.shape[0] - at, 256), bf16)
        for q in range(3):
            mine_a[at + q * C_FMID : at + (q + 1) * C_FMID, :C_FAST] = sums[q].astype(bf16)
        last.send(0)

    @pl.when(i >= late)
    def _():
        h = i - late
        dj = dot_nt(
            jnp.concatenate([dzp[...].reshape(rows, C_IN), da[h].reshape(rows, 3 * C_MID)], axis=1),
            jnp.concatenate([wp[:C_IN]] + [wa[k, :C_IN] for k in range(3)], axis=1),
        )
        mask = spread(m[...], C_IN)
        dj = dj.reshape(cols, slab, C_IN)
        for w in range(cols):
            sx[:, w] = (dj[w] * mask).astype(bf16).reshape(slab // clips, clips, C_IN)
        g = df[h].reshape(rows, 3 * 128)
        d = dl[h].reshape(rows, 2 * C_LAT)
        total = gf[...].reshape(rows, WIDE_FAST) + dot(g[:, 128:256], taps[...])
        head = dot_nt(d[:, :C_LAT], wl[2:5].reshape(3 * C_FAST, C_LAT))
        tail = dot_nt(d[:, C_LAT:], wl[0:2].reshape(2 * C_FAST, C_LAT))
        blocks = [total[:, p * C_FAST : (p + 1) * C_FAST] for p in range(ALPHA)]
        for p in range(3):
            blocks[p] = blocks[p] + head[:, p * C_FAST : (p + 1) * C_FAST]
        for p in range(2):
            blocks[2 + p] = blocks[2 + p] + tail[:, p * C_FAST : (p + 1) * C_FAST]
        blocks[3] = blocks[3] + dot(g[:, :128], ends[0])
        blocks[0] = blocks[0] + dot(g[:, 256:], ends[1])
        blocks = [v.astype(bf16) for v in blocks]
        for w in range(cols):
            stacked = jnp.concatenate([v[w * slab : (w + 1) * slab] for v in blocks], axis=0)
            fx[:, w] = dot_tn(perm[...], stacked).astype(bf16).reshape(clips, slab, C_FAST)

    @pl.when(i == final)
    def _():
        for k in range(max(len(left) for left in rest)):
            for left in rest:
                if k < len(left):
                    left[k]()
        saves = [
            pltpu.make_async_copy(a, b, load_sem.at[k])
            for k, (a, b) in enumerate(((done1, out1), (done_b, out_b), (done_h, out_h), (done_a, out_a)))
        ]
        for save in saves:
            save.start()
        for save in saves:
            save.wait()


def small_place(q):
    return 9 * C_MID + (q % 5) * C_FMID, (q // 5) * 128, C_FMID if q < 9 else C_FAST


def greet_signal(n_clip):
    barrier = pltpu.get_barrier_semaphore()
    for axis, power in stage_orders(n_clip, 1)[0]:
        pl.semaphore_signal(barrier, inc=1, device_id=partner_of(axis, power), device_id_type=MESH)


def greet_wait(n_clip):
    pl.semaphore_wait(pltpu.get_barrier_semaphore(), len(stage_orders(n_clip, 1)[0]))


def finish_outputs(so, fo, sx, fx, done1, done_b, done_h, done_a, tot4, tot5, tot6, so_out, fo_out, sx_out, fx_out,
                   wp_hbm, wc_hbm, wb_hbm, wa_hbm, wl_hbm, wfa_out, wfc_out, wfb_out, sgain_out, sshift_out, fgain_out,
                   fshift_out, wp, wc, wb, wa, wl, sem):
    i = pl.program_id(0)
    moves = ((wp, wp_hbm), (wc, wc_hbm), (wb, wb_hbm), (wa, wa_hbm), (wl, wl_hbm))

    def move(k):
        return pltpu.make_async_copy(moves[k][0], moves[k][1], sem.at[k])

    @pl.when(i == 0)
    def _():
        for b in range(C_IN // 256):
            wp[:, b * 256 : (b + 1) * 256] = done1[b * C_JOIN : (b + 1) * C_JOIN, :].astype(f32)
        move(0).start()
        for b in range(C_IN // 256):
            at = 4 * C_JOIN + b * C_MID
            wc[:, b * 256 : (b + 1) * 256] = done1[at : at + C_MID, :].astype(f32)
        move(1).start()

    @pl.when(i == 1)
    def _():
        for t in range(9):
            wb[t // 3, t % 3] = done_b[t * C_MID : (t + 1) * C_MID, :].astype(f32)
        move(2).start()

    @pl.when(i == 2)
    def _():
        for k in range(3):
            wa[k, : 2 * C_MID] = done_h[2 * k * C_MID : 2 * (k + 1) * C_MID, :].astype(f32)
            wa[k, 2 * C_MID :] = done_a[3 * k * C_MID : 3 * (k + 1) * C_MID, :].astype(f32)
        move(3).start()
        at = 9 * C_MID
        for k in range(5):
            wl[k] = done_a[at + k * C_FAST : at + (k + 1) * C_FAST, :].astype(f32)
        move(4).start()

    @pl.when(i == 3)
    def _():
        at = 9 * C_MID + 5 * C_FAST
        for q in range(3):
            wfa_out[q] = done_a[at + q * C_FMID : at + (q + 1) * C_FMID, :C_FAST].astype(f32)
        for q in range(10):
            r, c, width = small_place(q)
            piece = done_b[r : r + C_FMID, c : c + width].astype(f32)
            if q < 9:
                wfb_out[q] = piece
            else:
                wfc_out[...] = piece
        lane = lax.broadcasted_iota(jnp.int32, (1, 128), 1)
        for k, slow, fast in ((0, sshift_out, fshift_out), (1, sgain_out, fgain_out)):
            at = k * MIX
            row = 0
            for source, begin, width in (
                (tot6, at, C_MID), (tot5, at, C_MID), (tot4, k * C_IN, C_IN), (tot4, 2 * k * C_IN, C_IN)
            ):
                for c in range(begin, begin + width, 128):
                    slow[row : row + 1] = source[:, c : c + 128]
                    row += 1
            c = pltpu.roll(tot4[:, 3 * C_IN + k * C_FAST : 3 * C_IN + (k + 1) * C_FAST], 2 * C_FMID, 1)
            a, b = tot6[:, at + C_MID : at + MIX], tot5[:, at + C_MID : at + MIX]
            fast[:, :128] = jnp.where(lane < C_FMID, a, jnp.where(lane < 2 * C_FMID, b, c))
            fast[:, 128:] = c[:, : 2 * C_FMID]

    so_out[...] = so[...]
    fo_out[...] = fo[...]
    sx_out[...] = sx[...]
    fx_out[...] = fx[...]

    @pl.when(i == pl.num_programs(0) - 1)
    def _():
        for k in range(5):
            move(k).wait()


def prepare(clips, n_clip, counts, sgain_rows, sshift_rows, fgain, fshift, wb, m, perm, weight, inv, mids, last, wide,
            sgain, sshift):
    for k in range(sgain_rows.shape[0]):
        sgain[:, k * 128 : (k + 1) * 128] = sgain_rows[k : k + 1]
        sshift[:, k * 128 : (k + 1) * 128] = sshift_rows[k : k + 1]
    slab = m.shape[0]
    frames = slab // clips
    me = lax.axis_index("clip") * clips
    shift = clips.bit_length() - 1

    def real(shape):
        r = lax.broadcasted_iota(jnp.int32, shape, 0)
        own = jnp.zeros(shape, jnp.int32)
        for c in range(clips):
            own = jnp.where((r & (clips - 1)) == c, counts[me + c], own)
        return r, (r >> shift) < own

    m[...] = real(m.shape)[1].astype(f32)
    width = perm.shape[1]
    r, there = real((slab, width))
    col = lax.broadcasted_iota(jnp.int32, (slab, width), 1)
    for p in range(ALPHA):
        want = (r & (clips - 1)) * (ALPHA * frames) + ALPHA * (r >> shift) + p
        perm[p * slab : (p + 1) * slab] = ((want == col) & there).astype(f32).astype(bf16)
    groups = []
    for g in range(n_clip):
        part = counts[g * clips]
        for c in range(1, clips):
            part = part + counts[g * clips + c]
        groups.append(part)
    total = groups[0]
    for part in groups[1:]:
        total = total + part
    whole_count = jnp.full((1, 128), total, jnp.int32).astype(f32)
    inv[...] = 1.0 / (whole_count * (H * W))
    for g in range(n_clip):
        weight[g] = jnp.full((1, 128), groups[g], jnp.int32).astype(f32) / whole_count
    lane = lax.broadcasted_iota(jnp.int32, (1, 128), 1)
    for k in range(2):
        for j, (slow, fast) in enumerate(((sgain, fgain), (sshift, fshift))):
            mine = (lane >= k * C_FMID) & (lane < (k + 1) * C_FMID)
            mids[2 * k + j, :, :C_MID] = slow[:, k * C_MID : (k + 1) * C_MID]
            mids[2 * k + j, :, C_MID:] = phase_sum(jnp.where(mine, fast[:, :128], 0.0))
    for j, fast in enumerate((fgain, fshift)):
        last[j] = fast[:, 2 * C_FMID :]
    for t in range(9):
        w = wb[t]
        for p in range(ALPHA):
            parts = [jnp.zeros((C_FMID, C_FMID), bf16)] * ALPHA
            parts[p] = w
            wide[t, p * C_FMID : (p + 1) * C_FMID] = jnp.concatenate(parts, axis=1)


def vmem_spec():
    return pl.BlockSpec(memory_space=pltpu.VMEM)


def shaped(shape, kind):
    return jax.ShapeDtypeStruct(shape, kind)


def whole(shape):
    return pl.BlockSpec(shape, lambda h: (0,) * len(shape))


def per_line(shape):
    return pl.BlockSpec((None,) + tuple(shape), lambda h: (h,) + (0,) * len(shape))


def params(limit):
    return pltpu.CompilerParams(vmem_limit_bytes=60 * MIB)


def on_device(
    slow_input,
    fast_input,
    frame_counts,
    lateral_weight,
    slow_a_weight,
    slow_b_weight,
    slow_c_weight,
    slow_proj_weight,
    fast_a_weight,
    fast_b_weight,
    fast_c_weight,
    slow_gain,
    slow_shift,
    fast_gain,
    fast_shift,
    slow_cotangent,
    fast_cotangent,
):
    n_clip = lax.axis_size("clip")
    clips, frames, high, cols, _ = slow_input.shape
    slab = clips * frames
    lanes = slow_gain.reshape(-1, 128), slow_shift.reshape(-1, 128)
    slow_row = shaped((1, slow_gain.shape[0]), f32)
    vm = vmem_spec()
    m, perm, weight, inv, mids, ends, wfb, sgain, sshift = pl.pallas_call(
        functools.partial(prepare, clips, n_clip),
        in_specs=[pl.BlockSpec(memory_space=pltpu.SMEM)] + [vm] * 5,
        out_specs=(vm,) * 9,
        out_shape=(
            shaped((slab, 128), f32), shaped((ALPHA * slab, ALPHA * slab), bf16), shaped((n_clip, 1, 128), f32),
            shaped((1, 128), f32), shaped((4, 1, MIX), f32), shaped((2, 1, C_FAST), f32), shaped((9, 128, 128), bf16),
            slow_row, slow_row,
        ),
        compiler_params=params(60),
        name="prepare",
    )(frame_counts, *lanes, fast_gain[None], fast_shift[None], fast_b_weight.reshape(9, C_FMID, C_FMID))
    wfa = fast_a_weight.transpose(0, 2, 1)
    xs = slow_input.transpose(1, 2, 3, 0, 4)
    xf = fast_input.transpose(0, 2, 3, 1, 4)
    cot = slow_cotangent.transpose(1, 2, 3, 0, 4)
    fcot = fast_cotangent.transpose(0, 2, 3, 1, 4)
    def lines(c, kind):
        return shaped((high, cols, slab, c), kind)

    m_spec = whole((slab, 128))
    vm = vmem_spec()
    hbm = pl.BlockSpec(memory_space=pl.ANY)

    def early_line(shape):
        return pl.BlockSpec((None,) + tuple(shape), lambda i: (jnp.minimum(i, high - 1),) + (0,) * len(shape))

    def late_line(shape, begin):
        return pl.BlockSpec((None,) + tuple(shape), lambda i: (jnp.maximum(i - begin, 0),) + (0,) * len(shape))

    def slow_block(index):
        return pl.BlockSpec((frames, None, cols, clips, C_IN), lambda i: (0, index(i), 0, 0, 0))

    def fast_block(index):
        return pl.BlockSpec((clips, None, cols, ALPHA * frames, C_FAST), lambda i: (0, index(i), 0, 0, 0))

    def early(i):
        return jnp.minimum(i, high - 1)

    def after(begin):
        return lambda i: jnp.maximum(i - begin, 0)

    def remote(ident):
        return pltpu.CompilerParams(collective_id=ident, has_side_effects=True, vmem_limit_bytes=60 * MIB)

    rim_shapes = (shaped((cols, slab, MIX), f32), shaped((high, slab, MIX), f32), shaped((slab, MIX), f32))
    edge_scratch = [pltpu.VMEM((cols, slab, MIX), f32), pltpu.VMEM((high, slab, MIX), f32)]
    rims = rim_scratch(cols, slab)
    L1 = MIX + C_IN
    x, f, z1, zp, stp, base, mom1, row1, col1, corner1 = pl.pallas_call(
        functools.partial(first_pass, clips, n_clip),
        grid=(2 * high,),
        in_specs=[slow_block(early), fast_block(early)] + [vm] * 7,
        out_specs=(
            early_line((cols, slab, C_JOIN)), early_line((cols, slab, WIDE_FAST)), early_line((cols, slab, MIX)),
            late_line((cols, slab, C_IN), high), vm, vm, vm, vm, vm, vm,
        ),
        out_shape=(
            lines(C_JOIN, bf16), lines(WIDE_FAST, bf16), lines(MIX, f32), lines(C_IN, bf16), shaped((2, C_IN), f32),
            shaped((1, C_IN), f32), shaped((2, MIX), f32),
        ) + rim_shapes,
        scratch_shapes=[
            pltpu.VMEM((high, cols, slab, C_JOIN), bf16), pltpu.VMEM((128, WIDE_FAST), bf16),
            pltpu.VMEM((2, 128, C_FAST), bf16), pltpu.VMEM((1, L1), f32), pltpu.VMEM((1, L1), f32),
            pltpu.VMEM((1, L1), f32),
        ] + edge_scratch + exchange_scratch(n_clip, 2, MIX) + rims,
        compiler_params=remote(1),
        name="first_pass",
    )(xs, xf, m, perm, lateral_weight, slow_a_weight, slow_proj_weight, wfa, weight)

    a1, z2, mom2, zrow, zcol, zcorner, cot = pl.pallas_call(
        functools.partial(second_pass, n_clip),
        grid=(high + 1,),
        in_specs=[hbm] + [vm] * 10 + [slow_block(after(1))],
        out_specs=(vm, vm, vm, vm, vm, vm, late_line((cols, slab, C_IN), 1)),
        out_shape=(
            shaped((high + 2, cols + 2, slab, MIX), bf16), lines(MIX, f32), shaped((2, L1), f32),
        ) + rim_shapes + (lines(C_IN, bf16),),
        scratch_shapes=[
            pltpu.VMEM((high, cols, slab, MIX), f32), pltpu.SemaphoreType.DMA((high,)), pltpu.VMEM((1, MIX), f32),
            pltpu.VMEM((1, MIX), f32),
        ] + exchange_scratch(n_clip, 2, L1) + rims,
        compiler_params=remote(2),
        name="second_pass",
    )(z1, row1, col1, corner1, mom1, mids, m, slow_b_weight, wfb, stp, weight, cot)

    L3 = C_IN + C_FAST
    a2, mom3, fcot = pl.pallas_call(
        functools.partial(third_pass, n_clip),
        grid=(2 * high,),
        in_specs=[early_line((cols, slab, MIX))] + [vm] * 6 + [fast_block(after(high)), vm],
        out_specs=(early_line((cols, slab, MIX)), vm, late_line((cols, slab, WIDE_FAST), high)),
        out_shape=(lines(MIX, bf16), shaped((2, L3), f32), lines(WIDE_FAST, bf16)),
        scratch_shapes=[pltpu.VMEM((128, WIDE_FAST), bf16)] + [pltpu.VMEM((1, L3), f32)] * 3
        + exchange_scratch(n_clip, 2, L3),
        compiler_params=remote(3),
        name="third_pass",
    )(z2, mom2, mids, m, slow_c_weight, fast_c_weight, weight, fcot, perm)

    L4 = 3 * C_IN + 2 * C_FAST
    so, fo, gs, gf, tot4 = pl.pallas_call(
        functools.partial(fourth_pass, n_clip, clips),
        grid=(2 * high,),
        in_specs=[early_line((cols, slab, MIX)), early_line((cols, slab, C_IN))] + [vm] * 6 + [
            early_line((cols, slab, C_IN)), early_line((cols, slab, WIDE_FAST)), early_line((cols, slab, WIDE_FAST)),
        ] + [vm] * 5,
        out_specs=(
            slow_block(after(high)), fast_block(after(high)), early_line((cols, slab, C_IN)),
            early_line((cols, slab, WIDE_FAST)), vm,
        ),
        out_shape=(
            shaped(xs.shape, bf16), shaped(xf.shape, bf16), lines(C_IN, f32), lines(WIDE_FAST, f32),
            shaped((1, L4), f32),
        ),
        scratch_shapes=[
            pltpu.VMEM((high, cols, slab, C_IN), bf16), pltpu.VMEM((high, cols, slab, WIDE_FAST), bf16),
            pltpu.VMEM((1, L4), f32), pltpu.VMEM((128, WIDE_FAST), bf16), pltpu.VMEM((cols, slab, C_IN), f32),
            pltpu.VMEM((cols, slab, WIDE_FAST), f32),
        ] + exchange_scratch(n_clip, 1, L4),
        compiler_params=remote(4),
        name="fourth_pass",
    )(
        a2, zp, base, mom2, mom3, sgain, sshift, ends, cot, fcot, f, m, perm, slow_c_weight, fast_c_weight, weight,
    )

    n = high * cols
    early_sizes = (2048, 2048, 2048)
    space_sizes = (1024, 1024, 512)
    half_sizes = (512, 512, 512)
    late_sizes = (1024, 1024, 1024)

    def flat(v):
        return v.reshape((n,) + v.shape[2:])

    steps = C_JOIN // C_MID
    dzp, q2, tot5, qrow, qcol, qcorner, dw1, dwfc = pl.pallas_call(
        functools.partial(fifth_pass, n_clip),
        grid=(high + steps,),
        in_specs=[
            early_line((cols, slab, C_IN)), early_line((cols, slab, WIDE_FAST)), early_line((cols, slab, MIX)),
            early_line((cols, slab, C_IN)), vm, early_line((cols, slab, MIX)),
        ] + [vm] * 10 + [pl.BlockSpec((n, slab, C_MID), lambda i: (0, 0, jnp.clip(i - high, 0, steps - 1))), vm],
        out_specs=(
            early_line((cols, slab, C_IN)), early_line((cols, slab, MIX)), vm, vm, vm, vm, vm, vm,
        ),
        out_shape=(lines(C_IN, bf16), lines(MIX, f32), shaped((1, 2 * MIX), f32)) + rim_shapes + (
            shaped((sum(early_sizes), 256), bf16), shaped((C_FMID, C_FAST), f32),
        ),
        scratch_shapes=[
            pltpu.VMEM((high, cols, slab, C_IN), bf16), pltpu.VMEM((high, cols, slab, C_IN), bf16),
            pltpu.VMEM((high, cols, slab, WIDE_FAST), bf16), pltpu.VMEM((high, cols, slab, MIX), bf16),
            pltpu.VMEM((1, 2 * MIX), f32), pltpu.VMEM((128, WIDE_FAST), bf16), pltpu.VMEM((cols, slab, C_IN), f32),
            pltpu.VMEM((cols, slab, WIDE_FAST), f32),
        ] + edge_scratch + exchange_scratch(n_clip, 1, 2 * MIX) + rims,
        compiler_params=remote(5),
        name="fifth_pass",
    )(
        gs, gf, a2, zp, base, z2, mom2, mom3, tot4, inv, sgain, ends, mids, m, slow_c_weight, fast_c_weight,
        flat(x), weight,
    )

    q1, tot6, dwb, kept = pl.pallas_call(
        functools.partial(sixth_pass, n_clip, early_sizes),
        grid=(10,),
        in_specs=[hbm] * 4 + [vm] * 16 + [hbm],
        out_specs=(vm,) * 4,
        out_shape=(
            lines(MIX, f32), shaped((1, 2 * MIX), f32), shaped((sum(space_sizes), 256), bf16),
            shaped((sum(Reducer.layout(n_clip, early_sizes)[2]), 256), bf16),
        ),
        scratch_shapes=[pltpu.VMEM((9, C_FMID, C_FMID), f32), pltpu.VMEM((high + 2, cols + 2, slab, MIX), bf16)]
        + [pltpu.VMEM((high, cols, slab, MIX), f32)] * 3
        + [pltpu.VMEM((high + 2, cols + 2, slab, MIX), bf16)]
        + [pltpu.SemaphoreType.DMA((high,))] * 3
        + [pltpu.SemaphoreType.DMA((2,)), pltpu.VMEM((1, 2 * MIX), f32)]
        + [pltpu.VMEM((sum(early_sizes), 256), bf16), Reducer.scratch(n_clip, early_sizes)]
        + exchange_scratch(n_clip, 1, 2 * MIX) + Reducer.sems(n_clip, early_sizes, 2),
        compiler_params=remote(6),
        name="sixth_pass",
    )(
        q2, z2, z1, a1, qrow, qcol, qcorner, zrow, zcol, zcorner, mom1, mom2, tot5, inv, mids, m,
        slow_b_weight, wfb, weight, dwfc, dw1,
    )

    def twice_line(shape):
        begin = high + steps
        return pl.BlockSpec(
            (None,) + tuple(shape),
            lambda i: (jnp.where(i < begin, jnp.minimum(i, high - 1), i - begin),) + (0,) * len(shape),
        )

    sx, fx, done1, done_b, done_h, done_a = pl.pallas_call(
        functools.partial(seventh_pass, clips, n_clip, early_sizes, space_sizes, half_sizes, late_sizes),
        grid=(2 * high + steps,),
        in_specs=[
            early_line((cols, slab, MIX)), early_line((cols, slab, MIX)), twice_line((cols, slab, C_IN)),
            late_line((cols, slab, WIDE_FAST), high + steps),
            pl.BlockSpec((n, slab, C_MID), lambda i: (0, 0, jnp.clip(i - high, 0, steps - 1))), vm, vm, hbm,
        ] + [vm] * 10,
        out_specs=(slow_block(after(high + steps)), fast_block(after(high + steps)), hbm, hbm, hbm, hbm),
        out_shape=(
            shaped(xs.shape, bf16), shaped(xf.shape, bf16), shaped((sum(early_sizes), 256), bf16),
            shaped((sum(space_sizes), 256), bf16), shaped((sum(half_sizes), 256), bf16), shaped((sum(late_sizes), 256), bf16),
        ),
        scratch_shapes=[
            pltpu.VMEM((sum(v), 256), bf16) for v in (early_sizes, space_sizes, half_sizes, late_sizes)
        ] + [
            pltpu.VMEM((high, cols, slab, 3 * C_MID), bf16), pltpu.VMEM((high, cols, slab, 2 * C_LAT), bf16),
            pltpu.VMEM((high, cols, slab, 3 * 128), bf16), pltpu.VMEM((128, WIDE_FAST), bf16),
            pltpu.VMEM((2, 128, C_FAST), bf16), pltpu.VMEM((sum(space_sizes), 256), bf16),
            Reducer.scratch(n_clip, space_sizes), pltpu.VMEM((sum(half_sizes), 256), bf16),
            Reducer.scratch(n_clip, half_sizes), pltpu.VMEM((sum(late_sizes), 256), bf16),
            Reducer.scratch(n_clip, late_sizes), pltpu.SemaphoreType.DMA((4,)),
        ] + Reducer.sems(n_clip, early_sizes, 2) + Reducer.sems(n_clip, space_sizes) + Reducer.sems(n_clip, half_sizes)
        + Reducer.sems(n_clip, late_sizes),
        compiler_params=remote(7),
        name="seventh_pass",
    )(
        q1, z1, dzp, gf, flat(x), flat(f), kept, dwb, mom1, tot6, inv, mids, m, perm, lateral_weight, slow_a_weight,
        slow_proj_weight, wfa,
    )

    slow_rows, fast_row = shaped(lanes[0].shape, f32), shaped((1, fast_gain.shape[0]), f32)
    def here(i):
        return i

    weights = (
        shaped((C_JOIN, C_IN), f32), shaped((C_MID, C_IN), f32), shaped((3, 3, C_MID, C_MID), f32),
        shaped((3, C_JOIN, C_MID), f32), shaped((5, C_FAST, C_LAT), f32),
    )
    maps = [slow_block(here), fast_block(here)] * 2
    so, fo, sx, fx, dwp, dwc, dwb, dwa, dwl, dwfa, dwfc, dwfb, dsg, dss, dfg, dfs = pl.pallas_call(
        finish_outputs,
        grid=(high,),
        in_specs=maps + [vm] * 7,
        out_specs=tuple(maps) + (hbm,) * 5 + (vm,) * 7,
        out_shape=(shaped(xs.shape, bf16), shaped(xf.shape, bf16)) * 2 + weights + (
            shaped((3, C_FMID, C_FAST), f32), shaped((C_FMID, C_FAST), f32), shaped((9, C_FMID, C_FMID), f32),
            slow_rows, slow_rows, fast_row, fast_row,
        ),
        scratch_shapes=[pltpu.VMEM(v.shape, f32) for v in weights] + [pltpu.SemaphoreType.DMA((5,))],
        compiler_params=params(60),
        name="finish_outputs",
    )(so, fo, sx, fx, done1, done_b, done_h, done_a, tot4, tot5, tot6)
    return (
        so.transpose(3, 0, 1, 2, 4),
        fo.transpose(0, 3, 1, 2, 4),
        sx.transpose(3, 0, 1, 2, 4),
        fx.transpose(0, 3, 1, 2, 4),
        dwl,
        dwa,
        dwb,
        dwc,
        dwp,
        dwfa.transpose(0, 2, 1),
        dwfb.reshape(3, 3, C_FMID, C_FMID),
        dwfc,
        dsg.reshape(-1),
        dss.reshape(-1),
        dfg[0],
        dfs[0],
    )


def solution(mesh):
    tiles = P("clip", None, "ha", "wa", None)
    return jax.shard_map(
        on_device,
        mesh=mesh,
        in_specs=(tiles, tiles) + (P(),) * 13 + (tiles, tiles),
        out_specs=(tiles,) * 4 + (P(),) * 12,
        check_vma=False,
    )
```

```python
import functools

import jax
import jax.numpy as jnp
from jax import lax
from jax.experimental import pallas as pl
from jax.experimental.pallas import tpu as pltpu
from jax.sharding import PartitionSpec as P

ALPHA = 4
H = 14
W = 14
C_IN = 1024
C_LAT = 256
C_MID = 256
C_FAST = 128
C_FMID = 32
C_JOIN = C_IN + C_LAT
MIX = C_MID + ALPHA * C_FMID
WIDE_FAST = ALPHA * C_FAST

eps_norm = 1e-05
f32 = jnp.float32
bf16 = jnp.bfloat16
MESH = pl.DeviceIdType.MESH
MIB = 1 << 20


def dot(a, b):
    return lax.dot_general(a, b, (((1,), (0,)), ((), ())), preferred_element_type=f32)


def dot_nt(a, b):
    return lax.dot_general(a, b, (((1,), (1,)), ((), ())), preferred_element_type=f32)


def dot_tn(a, b):
    return lax.dot_general(a, b, (((0,), (0,)), ((), ())), preferred_element_type=f32)


def sigmoid(v):
    return 0.5 + 0.5 * jnp.tanh(0.5 * v)


def later(y, clips):
    return jnp.concatenate([jnp.zeros_like(y[:, :clips]), y[:, : y.shape[1] - clips]], axis=1)


def sooner(y, clips):
    return jnp.concatenate([y[:, clips:], jnp.zeros_like(y[:, :clips])], axis=1)


def rows_sum(v):
    return jnp.sum(jnp.sum(v, axis=0), axis=0, keepdims=True)


def phase_sum(v):
    out = v
    for k in range(1, ALPHA):
        out = out + pltpu.roll(v, k * C_FMID, 1)
    return out


def block_sum(v):
    return sum(v[:, p * C_FAST : (p + 1) * C_FAST] for p in range(ALPHA))


def spread(mask, width):
    return jnp.tile(mask, (1, width // 128))


def frames_matrix(wfa_ref, out_ref, ends_ref):
    out_ref[...] = jnp.zeros_like(out_ref)
    ends_ref[...] = jnp.zeros_like(ends_ref)
    for p in range(ALPHA):
        for s in range(max(p - 1, 0), min(p + 2, ALPHA)):
            out_ref[p * C_FMID : (p + 1) * C_FMID, s * C_FAST : (s + 1) * C_FAST] = wfa_ref[s - p + 1]
    ends_ref[0, 0:C_FMID] = wfa_ref[0]
    ends_ref[1, 3 * C_FMID :] = wfa_ref[2]


def expand_matrix(wfc_ref, out_ref):
    out_ref[...] = jnp.zeros_like(out_ref)
    for p in range(ALPHA):
        out_ref[p * C_FMID : (p + 1) * C_FMID, p * C_FAST : (p + 1) * C_FAST] = wfc_ref[...]


class Exchange:
    def __init__(self, n_clip, moments, refs, rim_refs=None):
        self.n = n_clip
        self.moments = moments
        self.part, self.near, self.mid, self.far, self.near_send, self.near_recv, self.far_send, self.far_recv = refs
        self.clip, self.ha, self.wa = lax.axis_index("clip"), lax.axis_index("ha"), lax.axis_index("wa")
        self.me = 2 * self.ha + self.wa
        self.peers = [(1 - self.ha, self.wa), (self.ha, 1 - self.wa), (1 - self.ha, 1 - self.wa)]
        self.others = [lax.rem(self.clip + d, n_clip) for d in range(1, n_clip)]
        if rim_refs is not None:
            self.packs, self.lands, self.rim_send, self.rim_recv = rim_refs

    def signal(self):
        barrier = pltpu.get_barrier_semaphore()
        for a, b in self.peers:
            pl.semaphore_signal(barrier, inc=1, device_id=(self.clip, a, b), device_id_type=MESH)
        for other in self.others:
            pl.semaphore_signal(barrier, inc=1, device_id=(other, self.ha, self.wa), device_id_type=MESH)

    def meet(self):
        pl.semaphore_wait(pltpu.get_barrier_semaphore(), 3 + self.n - 1)

    def near_copy(self, k, slot):
        a, b = self.peers[k]
        return pltpu.make_async_remote_copy(
            src_ref=self.part, dst_ref=self.near.at[slot], send_sem=self.near_send.at[k],
            recv_sem=self.near_recv.at[slot], device_id=(self.clip, a, b), device_id_type=MESH,
        )

    def far_copy(self, d, slot):
        return pltpu.make_async_remote_copy(
            src_ref=self.mid, dst_ref=self.far.at[slot], send_sem=self.far_send.at[d],
            recv_sem=self.far_recv.at[slot], device_id=(self.others[d], self.ha, self.wa), device_id_type=MESH,
        )

    def rim_copy(self, k):
        a, b = self.peers[k]
        size = 1 if k == 2 else self.packs.shape[1]
        return pltpu.make_async_remote_copy(
            src_ref=self.packs.at[k, pl.ds(0, size)], dst_ref=self.lands.at[k, pl.ds(0, size)],
            send_sem=self.rim_send.at[k], recv_sem=self.rim_recv.at[k], device_id=(self.clip, a, b),
            device_id_type=MESH,
        )

    def send_near(self):
        for k in range(3):
            self.near_copy(k, self.me).start()
        self.near[self.me] = self.part[...]

    def send_rims(self, line, side):
        count = self.packs.shape[1]
        centre = self.part[0:1, :MIX] if self.moments else jnp.zeros((1, MIX), f32)
        self.packs[0] = (line[...] - centre).astype(bf16)
        self.packs[1] = (side[...] - centre).astype(bf16)
        self.packs[2, 0] = self.packs[0, (count - 1) * (1 - self.wa)]
        for k in range(3):
            self.rim_copy(k).start()

    def send_far(self):
        for k, (a, b) in enumerate(self.peers):
            self.near_copy(k, 2 * a + b).wait_recv()
        near = self.near
        if self.moments:
            mean = (near[0, 0:1] + near[1, 0:1] + near[2, 0:1] + near[3, 0:1]) * 0.25
            self.mid[0:1] = mean
            self.mid[1:2] = sum(near[k, 1:2] + (near[k, 0:1] - mean) ** 2 for k in range(4)) * 0.25
        else:
            self.mid[...] = near[0] + near[1] + near[2] + near[3]
        for d in range(self.n - 1):
            self.far_copy(d, self.clip).start()
        self.far[self.clip] = self.mid[...]

    def finish(self, out, weight):
        for d, other in enumerate(self.others):
            self.far_copy(d, other).wait_recv()
        width = out.shape[1]
        far = self.far
        if self.moments:
            mean = sum(far[k, 0:1] * spread(weight[k], width) for k in range(self.n))
            out[0:1] = mean
            out[1:2] = sum((far[k, 1:2] + (far[k, 0:1] - mean) ** 2) * spread(weight[k], width) for k in range(self.n))
        else:
            out[...] = sum(far[k] for k in range(self.n))
        for k in range(3):
            self.near_copy(k, self.me).wait_send()
        for d in range(self.n - 1):
            self.far_copy(d, self.clip).wait_send()

    def finish_rims(self, rims):
        for k, (a, b) in enumerate(self.peers):
            self.rim_copy(k).wait_recv()
            centre = self.near[2 * a + b, 0:1, :MIX] if self.moments else jnp.zeros((1, MIX), f32)
            land = self.lands[k, 0] if k == 2 else self.lands[k]
            rims[k][...] = land.astype(f32) + centre
        for k in range(3):
            self.rim_copy(k).wait_send()


def exchange_scratch(n_clip, count, width):
    return [
        pltpu.VMEM((count, width), f32),
        pltpu.VMEM((4, count, width), f32),
        pltpu.VMEM((count, width), f32),
        pltpu.VMEM((n_clip, count, width), f32),
        pltpu.SemaphoreType.DMA((3,)),
        pltpu.SemaphoreType.DMA((4,)),
        pltpu.SemaphoreType.DMA((n_clip,)),
        pltpu.SemaphoreType.DMA((n_clip,)),
    ]


def rim_scratch(side, slab):
    return [
        pltpu.VMEM((3, side, slab, MIX), bf16),
        pltpu.VMEM((3, side, slab, MIX), bf16),
        pltpu.SemaphoreType.DMA((3,)),
        pltpu.SemaphoreType.DMA((3,)),
    ]


def first_pass(clips, n_clip, xs, xf, m, perm, wl, wa, wp_hbm, wfa, weight,
               x_out, f_out, z_out, zp_out, st_out, base_out, mom, row, col, corner,
               wp, wp_sem, keep, taps, ends, base, one, two, line, side, *refs):
    i = pl.program_id(0)
    cols = xs.shape[1]
    slab = m.shape[0]
    rows = cols * slab
    high = keep.shape[0]
    ex = Exchange(n_clip, True, refs[:8], refs[8:])
    here = cols * jnp.sum(m[...], axis=0, keepdims=True)
    count = high * here

    def fetch_wp():
        return pltpu.make_async_copy(wp_hbm, wp, wp_sem.at[0])

    @pl.when(i == 0)
    def _():
        fetch_wp().start()
        ex.signal()
        frames_matrix(wfa, taps, ends)

    @pl.when(i < high)
    def _():
        mask_in = spread(m[...], C_IN).astype(bf16)
        for w in range(cols):
            keep[i, w, :, :C_IN] = xs[:, w].reshape(slab, C_IN) * mask_in
            phases = dot(perm[...], xf[:, w].reshape(ALPHA * slab, C_FAST)).astype(bf16)
            for p in range(ALPHA):
                f_out[w, :, p * C_FAST : (p + 1) * C_FAST] = phases[p * slab : (p + 1) * slab]
        fast = f_out[...].reshape(rows, WIDE_FAST)
        lat = dot(fast[:, : 3 * C_FAST], wl[2:5].reshape(3 * C_FAST, C_LAT)).reshape(cols, slab, C_LAT)
        back = dot(fast[:, 2 * C_FAST :], wl[0:2].reshape(2 * C_FAST, C_LAT)).reshape(cols, slab, C_LAT)
        keep[i, :, :, C_IN:] = (lat + later(back, clips)).astype(bf16)
        x_out[...] = keep[i]
        joined = keep[i].reshape(rows, C_JOIN)
        za = dot(joined, wa[1]).reshape(cols, slab, C_MID)
        za = za + later(dot(joined, wa[0]).reshape(cols, slab, C_MID), clips)
        za = za + sooner(dot(joined, wa[2]).reshape(cols, slab, C_MID), clips)
        fa = dot_nt(fast, taps[...]).reshape(cols, slab, 128)
        fa = fa + later(dot_nt(fast[:, 3 * C_FAST :], ends[0]).reshape(cols, slab, 128), clips)
        fa = fa + sooner(dot_nt(fast[:, :C_FAST], ends[1]).reshape(cols, slab, 128), clips)
        z_out[:, :, :C_MID] = za
        z_out[:, :, C_MID:] = fa
        keep_rims(ex, i, high, z_out, line, side)
        add_moments(i == 0, ((0, za, 0), (C_MID, fa, 1)), m, here, base, one, two)

    @pl.when(i == high)
    def _():
        finish_moments(ex.part, base[...], one[...], two[...], count, ((0, C_MID, 0), (C_MID, 128, 1)))
        ex.meet()
        ex.send_near()
        ex.send_rims(line, side)
        fetch_wp().wait()

    @pl.when(i == high + 2)
    def _():
        ex.send_far()

    @pl.when(i >= high)
    def _():
        joined = keep[i - high].reshape(rows, C_JOIN)
        zp = dot(joined, wp[...]).reshape(cols, slab, C_IN)
        add_moments(i == high, ((MIX, zp, 0),), m, here, base, one, two, zp_out)

    @pl.when(i == 2 * high - 1)
    def _():
        s1 = one[:, MIX:] / spread(count, C_IN)
        st_out[0:1] = base[:, MIX:] + s1
        st_out[1:2] = two[:, MIX:] / spread(count, C_IN) - s1 * s1
        base_out[...] = base[:, MIX:]
        ex.finish(mom, weight)
        ex.finish_rims((row, col, corner))


def keep_rims(ex, i, high, block, line, side):
    side[i] = block[(block.shape[0] - 1) * (1 - ex.wa)]

    @pl.when(i == (high - 1) * (1 - ex.ha))
    def _():
        line[...] = block[...]


def add_moments(first, parts, m, here, base, one, two, kept=None):
    @pl.when(first)
    def _():
        for at, z, fast in parts:
            width = z.shape[-1]
            mean = rows_sum(z * spread(m[...], width)) / spread(here, width)
            if fast:
                mean = phase_sum(mean) * 0.25
            base[:, at : at + width] = mean
            one[:, at : at + width] = jnp.zeros((1, width), f32)
            two[:, at : at + width] = jnp.zeros((1, width), f32)

    for at, z, _ in parts:
        width = z.shape[-1]
        off = z - base[:, at : at + width]
        if kept is not None:
            kept[...] = off.astype(bf16)
        off = off * spread(m[...], width)
        one[:, at : at + width] += rows_sum(off)
        two[:, at : at + width] += rows_sum(off * off)


def finish_moments(st, base, one, two, count, parts):
    for at, width, fast in parts:
        s1 = one[:, at : at + width]
        s2 = two[:, at : at + width]
        if fast:
            s1 = phase_sum(s1) * 0.25
            s2 = phase_sum(s2) * 0.25
        n = spread(count.astype(f32), width)
        s1 = s1 / n
        st[0:1, at : at + width] = base[:, at : at + width] + s1
        st[1:2, at : at + width] = s2 / n - s1 * s1


def affine(moments, gain, shift, at, width):
    mean = moments[0:1, at : at + width]
    scale = lax.rsqrt(moments[1:2, at : at + width] + eps_norm)
    return mean, scale, gain, shift


def second_pass(n_clip, z1_hbm, row, col, corner, mom, mids, m, wb, wfb, stp, weight, cot,
                a_hbm, z_hbm, mom_out, zrow, zcol, zcorner, cot_out, a_out, z_out, save_sem, z1, z1_sem, one, two, *refs):
    i = pl.program_id(0)
    high, cols, slab, _ = z1.shape
    rows = cols * slab
    ex = Exchange(n_clip, True, refs[:8], refs[8:])

    def fetch(h):
        return pltpu.make_async_copy(z1_hbm.at[h], z1.at[h], z1_sem.at[h])

    def save(k):
        source, target = ((a_out, a_hbm), (z_out, z_hbm))[k]
        return pltpu.make_async_copy(source, target, save_sem.at[k])

    @pl.when(i == 0)
    def _():
        for h in range(high):
            fetch(h).start()
        ex.signal()
        mean, scale, g, b = affine(mom, mids[0], mids[1], 0, MIX)
        mult = scale * g
        mask = spread(m[...], MIX)

        def act(z):
            v = (z - mean) * mult + b
            return (v * sigmoid(v) * mask).astype(bf16)

        far = high + 1
        a_out[far * ex.ha] = jnp.zeros((cols + 2, slab, MIX), bf16)
        a_out[:, far * ex.wa] = jnp.zeros((high + 2, slab, MIX), bf16)
        a_out[far * (1 - ex.ha), 1 : 1 + cols] = act(row[...])
        a_out[1 : 1 + high, far * (1 - ex.wa)] = act(col[...])
        a_out[far * (1 - ex.ha), far * (1 - ex.wa)] = act(corner[...])

        def fill(h, carry):
            fetch(h).wait()
            a_out[h + 1, 1 : 1 + cols] = act(z1[h])
            return carry

        lax.fori_loop(0, high, fill, 0)

        def space(h, carry):
            slow = jnp.zeros((rows, C_MID), f32)
            fast = jnp.zeros((rows, 128), f32)
            for a in range(3):
                v = [a_out[h + a, c : c + cols].reshape(rows, MIX) for c in range(3)]
                slow = slow + dot(
                    jnp.concatenate([u[:, :C_MID] for u in v], axis=1), wb[a].reshape(3 * C_MID, C_MID)
                )
                fast = fast + dot(
                    jnp.concatenate([u[:, C_MID:] for u in v], axis=1), wfb[3 * a : 3 * a + 3].reshape(3 * 128, 128)
                )
            z_out[h, :, :, :C_MID] = slow.reshape(cols, slab, C_MID)
            z_out[h, :, :, C_MID:] = fast.reshape(cols, slab, 128)
            return carry

        lax.fori_loop(0, high, space, 0)
        here = cols * jnp.sum(m[...], axis=0, keepdims=True)
        base = rows_sum(z_out[0] * mask) / spread(here, MIX)
        base = jnp.concatenate([base[:, :C_MID], phase_sum(base[:, C_MID:]) * 0.25], axis=1)
        one[...] = jnp.zeros_like(one)
        two[...] = jnp.zeros_like(two)

        def gather(h, carry):
            off = (z_out[h] - base) * mask
            one[...] += rows_sum(off)
            two[...] += rows_sum(off * off)
            return carry

        lax.fori_loop(0, high, gather, 0)
        finish_moments(ex.part, base, one[...], two[...], high * here, ((0, C_MID, 0), (C_MID, 128, 1)))
        ex.part[:, MIX:] = stp[...]
        ex.meet()
        ex.send_near()
        ex.send_rims(z_out.at[(high - 1) * (1 - ex.ha)], z_out.at[:, (cols - 1) * (1 - ex.wa)])
        save(0).start()
        save(1).start()

    @pl.when(i == 3)
    def _():
        ex.send_far()

    @pl.when(i > 0)
    def _():
        half_mask = (0.5 * spread(m[...], C_IN)).astype(bf16)
        for w in range(cols):
            cot_out[w] = cot[:, w].reshape(slab, C_IN) * half_mask

    @pl.when(i == high)
    def _():
        ex.finish(mom_out, weight)
        ex.finish_rims((zrow, zcol, zcorner))
        save(0).wait()
        save(1).wait()


def third_pass(n_clip, z2, mom, mids, m, wc, wfc, weight, fcot, perm,
               a_out, mom_out, fcot_out, big, base, one, two, *refs):
    i = pl.program_id(0)
    high = pl.num_programs(0) // 2
    cols, slab, _ = z2.shape
    rows = cols * slab
    ex = Exchange(n_clip, True, refs)
    here = cols * jnp.sum(m[...], axis=0, keepdims=True)

    @pl.when(i == 0)
    def _():
        ex.signal()
        expand_matrix(wfc, big)

    @pl.when(i < high)
    def _():
        mean, scale, g, b = affine(mom, mids[2], mids[3], 0, MIX)
        v = (z2[...] - mean) * (scale * g) + b
        a_out[...] = (v * sigmoid(v) * spread(m[...], MIX)).astype(bf16)
        a2 = a_out[...].reshape(rows, MIX)
        zc = dot(a2[:, :C_MID], wc[...]).reshape(cols, slab, C_IN)
        fc = dot(a2[:, C_MID:], big[...]).reshape(cols, slab, WIDE_FAST)

        @pl.when(i == 0)
        def _():
            base[:, :C_IN] = rows_sum(zc * spread(m[...], C_IN)) / spread(here, C_IN)
            base[:, C_IN:] = block_sum(rows_sum(fc * spread(m[...], WIDE_FAST))) / (4.0 * here)
            one[...] = jnp.zeros_like(one)
            two[...] = jnp.zeros_like(two)

        off = (zc - base[:, :C_IN]) * spread(m[...], C_IN)
        one[:, :C_IN] += rows_sum(off)
        two[:, :C_IN] += rows_sum(off * off)
        off = (fc - jnp.tile(base[:, C_IN:], (1, ALPHA))) * spread(m[...], WIDE_FAST)
        one[:, C_IN:] += block_sum(rows_sum(off)) * 0.25
        two[:, C_IN:] += block_sum(rows_sum(off * off)) * 0.25

    @pl.when(i == high)
    def _():
        finish_moments(ex.part, base[...], one[...], two[...], high * here, ((0, C_IN + C_FAST, 0),))
        ex.meet()
        ex.send_near()

    @pl.when(i == high + 2)
    def _():
        ex.send_far()

    @pl.when(i >= high)
    def _():
        for w in range(cols):
            phases = dot(perm[...], fcot[:, w].reshape(ALPHA * slab, C_FAST)).astype(bf16)
            for p in range(ALPHA):
                fcot_out[w, :, p * C_FAST : (p + 1) * C_FAST] = 0.5 * phases[p * slab : (p + 1) * slab]

    @pl.when(i == 2 * high - 1)
    def _():
        ex.finish(mom_out, weight)


def fourth_pass(n_clip, clips, a2, zp, base, mom2, mom3, sgain, sshift, fends, cot, fcot, fast_in, m, perm, wc,
                wfc, weight, so, fo, gs, gf, tot, so_keep, fo_keep, sums, big, z_line, f_line, *refs):
    i = pl.program_id(0)
    high = pl.num_programs(0) // 2
    cols, slab, _ = a2.shape
    ex = Exchange(n_clip, False, refs)

    @pl.when(i == 0)
    def _():
        ex.signal()
        expand_matrix(wfc, big)
        sums[...] = jnp.zeros_like(sums)

    def tile_sum(v):
        return jnp.sum(v.reshape(slab // 8, 8, v.shape[-1]), axis=0)

    @pl.when(i < high)
    def _():
        mid, far = 2 * C_MID, 2 * C_MID + C_IN
        mean_c = mom3[0:1, :C_IN]
        scale_c = lax.rsqrt(mom3[1:2, :C_IN] + eps_norm)
        mean_p = mom2[0:1, MIX:] - base[...]
        scale_p = lax.rsqrt(mom2[1:2, MIX:] + eps_norm)
        mean_f = jnp.tile(mom3[0:1, C_IN:], (1, ALPHA))
        scale_f = jnp.tile(lax.rsqrt(mom3[1:2, C_IN:] + eps_norm), (1, ALPHA))
        mult_c = 0.5 * sgain[:, mid:far] * scale_c
        mult_p = 0.5 * sgain[:, far:] * scale_p
        shift_cp = 0.5 * (sshift[:, mid:far] + sshift[:, far:])
        mult_f = 0.5 * jnp.tile(fends[0], (1, ALPHA)) * scale_f
        shift_f = 0.5 * jnp.tile(fends[1], (1, ALPHA))

        def gate(v, g):
            u = 1.0 + jnp.tanh(v)
            o = v * u
            return o, g * (u + o * (2.0 - u))

        totals = [jnp.zeros((8, C_IN), f32)] * 3 + [jnp.zeros((8, WIDE_FAST), f32)] * 2
        rows = a2[...].reshape(cols * slab, MIX)
        z_line[...] = dot(rows[:, :C_MID], wc[...]).reshape(cols, slab, C_IN)
        f_line[...] = dot(rows[:, C_MID:], big[...]).reshape(cols, slab, WIDE_FAST)
        for w in range(cols):
            zc = z_line[w] - mean_c
            zq = zp[w].astype(f32) - mean_p
            res, back = gate(mult_c * zc + mult_p * zq + shift_cp, cot[w].astype(f32))
            so_keep[i, w] = res.astype(bf16)
            gs[w] = back
            totals[0] += tile_sum(back)
            totals[1] += tile_sum(back * zc)
            totals[2] += tile_sum(back * zq)
            fc = f_line[w] - mean_f
            res, fback = gate(mult_f * fc + shift_f + 0.5 * fast_in[w].astype(f32), fcot[w].astype(f32))
            fo_keep[i, w] = res.astype(bf16)
            gf[w] = fback
            totals[3] += tile_sum(fback)
            totals[4] += tile_sum(fback * fc)
        scales = (None, scale_c, scale_p)
        for k in range(3):
            total = jnp.sum(totals[k], axis=0, keepdims=True)
            sums[:, k * C_IN : (k + 1) * C_IN] += total if k == 0 else total * scales[k]
        for k in range(2):
            at = 3 * C_IN + k * C_FAST
            total = jnp.sum(totals[3 + k], axis=0, keepdims=True)
            sums[:, at : at + C_FAST] += block_sum(total if k == 0 else total * scale_f)

    @pl.when(i == high)
    def _():
        ex.part[...] = sums[...]
        ex.meet()
        ex.send_near()

    @pl.when(i == high + 2)
    def _():
        ex.send_far()

    @pl.when(i >= high)
    def _():
        mask = spread(m[...], C_IN).astype(bf16)
        for w in range(cols):
            so[:, w] = (so_keep[i - high, w] * mask).reshape(slab // clips, clips, C_IN)
            wide = fo_keep[i - high, w]
            stacked = jnp.concatenate([wide[:, p * C_FAST : (p + 1) * C_FAST] for p in range(ALPHA)], axis=0)
            fo[:, w] = dot_tn(perm[...], stacked).astype(bf16).reshape(clips, slab, C_FAST)

    @pl.when(i == 2 * high - 1)
    def _():
        ex.finish(tot, weight)


def fifth_pass(n_clip, gs, gf, a2, zp, base, z2, mom2, mom3, tot4, inv, sgain, fends, mids, m, wc, wfc, x, weight,
               dzp_out, q_out, tot, row, col, corner, w_out, wfc_out,
               dzc_keep, dzp_keep, dfc_keep, a_keep, sums, big, z_line, f_line, line, side, *refs):
    i = pl.program_id(0)
    high, cols, slab, _ = dzc_keep.shape
    n = high * cols
    rows = cols * slab
    ex = Exchange(n_clip, False, refs[:8], refs[8:])

    @pl.when(i == 0)
    def _():
        ex.signal()
        expand_matrix(wfc, big)
        sums[...] = jnp.zeros_like(sums)

    @pl.when(i < high)
    def _():
        mask = spread(m[...], C_IN)
        inv_s = spread(inv[...], C_IN)
        inv_f = 0.25 * inv[...]
        mean_c = mom3[0:1, :C_IN]
        scale_c = lax.rsqrt(mom3[1:2, :C_IN] + eps_norm)
        mean_p = mom2[0:1, MIX:] - base[...]
        scale_p = lax.rsqrt(mom2[1:2, MIX:] + eps_norm)
        mean_f = jnp.tile(mom3[0:1, C_IN:], (1, ALPHA))
        scale_f = jnp.tile(lax.rsqrt(mom3[1:2, C_IN:] + eps_norm), (1, ALPHA))
        mult_c = sgain[:, 2 * C_MID : 2 * C_MID + C_IN] * scale_c
        mult_p = sgain[:, 2 * C_MID + C_IN :] * scale_p
        mult_f = jnp.tile(fends[0], (1, ALPHA)) * scale_f
        first_s = tot4[:, :C_IN] * inv_s
        second_c = mult_c * scale_c * tot4[:, C_IN : 2 * C_IN] * inv_s
        second_p = mult_p * scale_p * tot4[:, 2 * C_IN : 3 * C_IN] * inv_s
        first_f = mult_f * jnp.tile(tot4[:, 3 * C_IN : 3 * C_IN + C_FAST] * inv_f, (1, ALPHA))
        second_f = mult_f * scale_f * jnp.tile(tot4[:, 3 * C_IN + C_FAST :] * inv_f, (1, ALPHA))
        first_c = mult_c * first_s - mean_c * second_c
        first_p = mult_p * first_s - mean_p * second_p
        first_f = first_f - mean_f * second_f
        mask_f = spread(m[...], WIDE_FAST)
        a_keep[i] = a2[...]
        flat = a2[...].reshape(rows, MIX)
        z_line[...] = dot(flat[:, :C_MID], wc[...]).reshape(cols, slab, C_IN)
        f_line[...] = dot(flat[:, C_MID:], big[...]).reshape(cols, slab, WIDE_FAST)
        for w in range(cols):
            zc = z_line[w]
            g = gs[w]
            dzc_keep[i, w] = (mult_c * g - mask * (first_c + zc * second_c)).astype(bf16)
            dzp = (mult_p * g - mask * (first_p + zp[w].astype(f32) * second_p)).astype(bf16)
            dzp_keep[i, w] = dzp
            dzp_out[w] = dzp
            fc = f_line[w]
            dfc_keep[i, w] = (mult_f * gf[w] - mask_f * (first_f + fc * second_f)).astype(bf16)
        da = dot_nt(dzc_keep[i].reshape(rows, C_IN), wc[...]).reshape(cols, slab, C_MID)
        df = dot_nt(dfc_keep[i].reshape(rows, WIDE_FAST), big[...]).reshape(cols, slab, 128)
        grads = jnp.concatenate([da, df], axis=2)
        slope_back(grads, z2[...], mom2, mids[2], mids[3], m, q_out, sums)
        keep_rims(ex, i, high, q_out, line, side)

    @pl.when(i == high)
    def _():
        ex.part[...] = sums[...]
        ex.meet()
        ex.send_near()
        ex.send_rims(line, side)

    @pl.when(i == high + 2)
    def _():
        ex.send_far()

    @pl.when(i >= high)
    def _():
        c = i - high
        got = dot_tn(x[...].reshape(n * slab, C_MID), dzp_keep[...].reshape(n * slab, C_IN)).astype(bf16)
        for b in range(C_IN // 256):
            at = pl.multiple_of(b * C_JOIN + c * C_MID, C_MID)
            w_out[pl.ds(at, C_MID), :] = got[:, b * 256 : (b + 1) * 256]

    @pl.when(i == pl.num_programs(0) - 1)
    def _():
        a = a_keep[...].reshape(n * slab, MIX)
        got = dot_tn(a[:, :C_MID], dzc_keep[...].reshape(n * slab, C_IN)).astype(bf16)
        for b in range(C_IN // 256):
            at = 4 * C_JOIN + b * C_MID
            w_out[at : at + C_MID, :] = got[:, b * 256 : (b + 1) * 256]
        wide = dot_tn(a[:, C_MID:], dfc_keep[...].reshape(n * slab, WIDE_FAST))
        wfc_out[...] = sum(
            wide[p * C_FMID : (p + 1) * C_FMID, p * C_FAST : (p + 1) * C_FAST] for p in range(ALPHA)
        )
        ex.finish(tot, weight)
        ex.finish_rims((row, col, corner))


def slope_back(grads, z, mom, gain, shift, m, q_out, sums):
    mean, scale, g, b = affine(mom, gain, shift, 0, MIX)
    zhat = (z - mean) * scale
    v = g * zhat + b
    sig = sigmoid(v)
    q = grads * (sig * (1.0 + v * (1.0 - sig)) * spread(m[...], MIX))
    q_out[...] = q
    for k, s in enumerate((rows_sum(q), rows_sum(q * zhat))):
        at = k * MIX
        sums[:, at : at + C_MID] += s[:, :C_MID]
        sums[:, at + C_MID : at + MIX] += phase_sum(s[:, C_MID:])


def norm_terms(mom, gain, tot, inv):
    mean = mom[0:1, :MIX]
    scale = lax.rsqrt(mom[1:2, :MIX] + eps_norm)
    share = jnp.concatenate([spread(inv[...], C_MID), 0.25 * inv[...]], axis=1)
    return mean, scale, gain * scale, tot[:, :MIX] * share, tot[:, MIX:] * share


def sixth_pass(n_clip, early_sizes, q2_hbm, z2_hbm, z1_hbm, a1_hbm, qrow, qcol, qcorner, zrow, zcol, zcorner, mom1, mom2, tot5, inv,
               mids, m, wb, wfb, weight, dwfc, w_hbm, q_hbm, tot, wb_out, kept_out,
               q_out, fast_sums, wide, q2, z2, z1, a1, q2_sem, z2_sem, z1_sem, a1_sem, sums, mine, land, *refs):
    i = pl.program_id(0)
    high, cols, slab, _ = z1.shape
    rows = cols * slab
    ex = Exchange(n_clip, False, refs[:8])
    early = Reducer(n_clip, early_sizes, mine, land, None, refs[8:10] + (None, None))
    end = early.stages - 1

    def fetch_w():
        return pltpu.make_async_copy(w_hbm, mine, a1_sem.at[1])

    def save_q():
        return pltpu.make_async_copy(q_out, q_hbm, a1_sem.at[2])

    moved = ((q2_hbm, q2, q2_sem), (z2_hbm, z2, z2_sem), (z1_hbm, z1, z1_sem))

    def fetch(k, h):
        a, b, s = moved[k]
        return pltpu.make_async_copy(a.at[h], b.at[h], s.at[h])

    def fetch_a1():
        return pltpu.make_async_copy(a1_hbm, a1, a1_sem.at[0])

    @pl.when(i == 0)
    def _():
        fetch_w().start()
        wb_out[9 * C_MID :, :] = jnp.zeros((wb_out.shape[0] - 9 * C_MID, 256), bf16)
        for h in range(high):
            fetch(0, h).start()
            fetch(1, h).start()
        for h in range(high):
            fetch(2, h).start()
        fetch_a1().start()
        ex.signal()
        mean, scale, mult, first, second = norm_terms(mom2, mids[2], tot5, inv)
        mask = spread(m[...], MIX)

        def grad(q, z):
            return (mult * (q - mask * (first + (z - mean) * scale * second))).astype(bf16)

        far = high + 1
        wide[far * ex.ha] = jnp.zeros((cols + 2, slab, MIX), bf16)
        wide[:, far * ex.wa] = jnp.zeros((high + 2, slab, MIX), bf16)
        wide[far * (1 - ex.ha), 1 : 1 + cols] = grad(qrow[...], zrow[...])
        wide[1 : 1 + high, far * (1 - ex.wa)] = grad(qcol[...], zcol[...])
        wide[far * (1 - ex.ha), far * (1 - ex.wa)] = grad(qcorner[...], zcorner[...])
        fetch_w().wait()
        ex.meet()
        early.send(0)

        def fill(h, carry):
            fetch(0, h).wait()
            fetch(1, h).wait()
            wide[h + 1, 1 : 1 + cols] = grad(q2[h], z2[h])
            return carry

        lax.fori_loop(0, high, fill, 0)
        sums[...] = jnp.zeros_like(sums)

        def space(h, carry):
            fetch(2, h).wait()
            slow = jnp.zeros((rows, C_MID), f32)
            fast = jnp.zeros((rows, 128), f32)
            for a in range(3):
                v = [wide[h + 2 - a, 2 - c : 2 - c + cols].reshape(rows, MIX) for c in range(3)]
                slow = slow + dot_nt(
                    jnp.concatenate([u[:, :C_MID] for u in v], axis=1),
                    jnp.concatenate([wb[a, c] for c in range(3)], axis=1),
                )
                fast = fast + dot_nt(
                    jnp.concatenate([u[:, C_MID:] for u in v], axis=1),
                    jnp.concatenate([wfb[3 * a + c] for c in range(3)], axis=1),
                )
            grads = jnp.concatenate([slow, fast], axis=1).reshape(cols, slab, MIX)
            slope_back(grads, z1[h], mom1, mids[0], mids[1], m, q_out.at[h], sums)
            return carry

        lax.fori_loop(0, 3, space, 0)
        early.gather(0)
        lax.fori_loop(3, high, space, 0)
        ex.part[...] = sums[...]
        ex.send_near()
        save_q().start()
        fetch_a1().wait()

    @pl.when(i == 3)
    def _():
        ex.send_far()

    @pl.when(i > 0)
    def _():
        tap = i - 1
        v = a1[pl.ds(tap // 3, high), pl.ds(lax.rem(tap, 3), cols)].reshape(high * rows, MIX)
        d = wide[1 : 1 + high, 1 : 1 + cols].reshape(high * rows, MIX)
        wb_out[pl.ds(pl.multiple_of(tap * C_MID, C_MID), C_MID), :] = dot_tn(v[:, :C_MID], d[:, :C_MID]).astype(bf16)
        both = dot_tn(v[:, C_MID:], d[:, C_MID:])
        fast_sums[tap] = sum(
            both[p * C_FMID : (p + 1) * C_FMID, p * C_FMID : (p + 1) * C_FMID] for p in range(ALPHA)
        )

    for k, step in ((1, 1), (2, 5), (3, 7)):

        @pl.when(i == step)
        def _():
            early.gather(k)

    @pl.when(i == 9)
    def _():
        ex.finish(tot, weight)
        for k in range(4, end + 1):
            early.gather(k)
        early.export(kept_out)
        save_q().wait()
        for q in range(10):
            r, c, width = small_place(q)
            wb_out[r : r + C_FMID, c : c + width] = (fast_sums[q] if q < 9 else dwfc[...]).astype(bf16)


def bit_of(axis, power):
    return lax.rem(lax.axis_index(axis) // (1 << power), 2)


def partner_of(axis, power):
    where = {name: lax.axis_index(name) for name in ("clip", "ha", "wa")}
    where[axis] = where[axis] + (1 - 2 * bit_of(axis, power)) * (1 << power)
    return (where["clip"], where["ha"], where["wa"])


def stage_orders(n_clip, sets):
    rest = [("wa", 0)] + [("clip", b) for b in range(n_clip.bit_length() - 1)]
    turn, last = rest[:3], rest[3:]
    return [[("ha", 0)] + turn[s % len(turn) :] + turn[: s % len(turn)] + last for s in range(sets)]


def chunk_of(rows):
    return max(k for k in range(16, min(rows, 256) + 1, 16) if rows % k == 0)


class Reducer:
    def __init__(self, n_clip, sizes, mine, land, done, sems):
        self.mine, self.land, self.done = mine, land, done
        self.rs_sent, self.rs_came, self.ag_sent, self.ag_came = sems
        self.sets = range(len(sizes))
        self.orders = stage_orders(n_clip, len(sizes))
        self.stages = len(self.orders[0])
        self.plan, self.starts, self.kept = Reducer.layout(n_clip, sizes)

    @staticmethod
    def layout(n_clip, sizes):
        stages = len(stage_orders(n_clip, 1)[0])
        plan, starts, kept = [], [], []
        start = land = 0
        for size in sizes:
            starts.append(start)
            start += size
            row = []
            for _ in range(stages):
                halve = size % 32 == 0
                size = size // 2 if halve else size
                row.append((halve, size, land))
                land += size
            plan.append(row)
            kept.append(size)
        return plan, starts, kept

    @staticmethod
    def scratch(n_clip, sizes):
        plan = Reducer.layout(n_clip, sizes)[0]
        last = plan[-1][-1]
        return pltpu.VMEM((last[1] + last[2], 256), bf16)

    @staticmethod
    def sems(n_clip, sizes, count=4):
        stages = len(stage_orders(n_clip, 1)[0])
        return [pltpu.SemaphoreType.DMA((len(sizes), stages)) for _ in range(count)]

    def low(self, s, k):
        low = jnp.int32(self.starts[s])
        for j in range(k):
            halve, count, _ = self.plan[s][j]
            if halve:
                low = low + bit_of(*self.orders[s][j]) * count
        return low

    @staticmethod
    def rows(ref, begin, count):
        return ref.at[pl.ds(pl.multiple_of(begin, 16), count)]

    def scatter_copy(self, s, k):
        halve, count, land = self.plan[s][k]
        axis, power = self.orders[s][k]
        begin = self.low(s, k)
        if halve:
            begin = begin + (1 - bit_of(axis, power)) * count
        return pltpu.make_async_remote_copy(
            src_ref=self.rows(self.mine, begin, count), dst_ref=self.rows(self.land, land, count),
            send_sem=self.rs_sent.at[s, k], recv_sem=self.rs_came.at[s, k],
            device_id=partner_of(axis, power), device_id_type=MESH,
        )

    def send(self, k):
        for s in self.sets:
            self.scatter_copy(s, k).start()

    def gather(self, k):
        for s in self.sets:
            halve, count, land = self.plan[s][k]
            copy = self.scatter_copy(s, k)
            copy.wait_recv()
            copy.wait_send()
            begin = self.low(s, k + 1)
            step = chunk_of(count)

            def add(i, carry):
                own = pl.ds(pl.multiple_of(begin + i * step, 16), step)
                came = pl.ds(pl.multiple_of(land + i * step, 16), step)
                self.mine[own, :] = (self.mine[own, :].astype(f32) + self.land[came, :].astype(f32)).astype(bf16)
                return carry

            lax.fori_loop(0, count // step, add, 0)
            if k + 1 < self.stages:
                self.scatter_copy(s, k + 1).start()

    def export(self, out):
        at = 0
        for s in self.sets:
            count = self.kept[s]
            out[at : at + count] = self.mine[pl.ds(pl.multiple_of(self.low(s, self.stages), 16), count), :]
            at += count

    def load(self, kept):
        at = 0
        for s in self.sets:
            count = self.kept[s]
            self.done[pl.ds(pl.multiple_of(self.low(s, self.stages), 16), count), :] = kept[at : at + count]
            at += count

    def keep(self):
        for s in self.sets:
            own = pl.ds(pl.multiple_of(self.low(s, self.stages), 16), self.kept[s])
            self.done[own, :] = self.mine[own, :]

    def regain(self):
        self.keep()
        self.spread(self.stages - 1)

    def gather_copy(self, s, k, other):
        halve, count, _ = self.plan[s][k]
        axis, power = self.orders[s][k]
        bit = bit_of(axis, power)
        begin = self.low(s, k) + ((1 - bit) if other else bit) * count
        return pltpu.make_async_remote_copy(
            src_ref=self.rows(self.done, begin, count), dst_ref=self.rows(self.done, begin, count),
            send_sem=self.ag_sent.at[s, k], recv_sem=self.ag_came.at[s, k],
            device_id=partner_of(axis, power), device_id_type=MESH,
        )

    def spread(self, k):
        for s in self.sets:
            if self.plan[s][k][0]:
                self.gather_copy(s, k, False).start()

    def take(self, k):
        for s in self.sets:
            if self.plan[s][k][0]:
                self.gather_copy(s, k, True).wait_recv()
                self.gather_copy(s, k, False).wait_send()
            if k > 0 and self.plan[s][k - 1][0]:
                self.gather_copy(s, k - 1, False).start()


SPACE_STEPS = (5, 9, 12, 15, 18, 18, 18, 18, 18, 18, 18)
FIRST_STEPS = (5, 9, 12, 15, 18)
HALF_STEPS = (12, 15, 17, 18, 18, 18, 18, 18, 18, 18, 18)
LATE_STEPS = (15, 17, 18, 18, 18, 18, 18, 18, 18, 18, 18)


def seventh_pass(clips, n_clip, early_sizes, space_sizes, half_sizes, late_sizes, q1, z1, dzp, gf, x, f_hbm, kept, space_hbm, mom1, tot6, inv,
                 mids, m, perm, wl, wa, wp, wfa, sx, fx, out1, out_b, out_h, out_a,
                 f, done1, done_b, done_h, done_a, da, dl, df, taps, ends, mine_b, land_b, mine_h, land_h, mine_a, land_a, load_sem, *sems):
    i = pl.program_id(0)
    cols, slab, _ = q1.shape
    high = da.shape[0]
    rows = cols * slab
    every = high * rows
    steps = C_JOIN // C_MID
    late = high + steps
    sems = iter(sems)
    first = Reducer(n_clip, early_sizes, None, None, done1, (None, None, next(sems), next(sems)))
    space = Reducer(n_clip, space_sizes, mine_b, land_b, done_b, [next(sems) for _ in range(4)])
    half = Reducer(n_clip, half_sizes, mine_h, land_h, done_h, [next(sems) for _ in range(4)])
    last = Reducer(n_clip, late_sizes, mine_a, land_a, done_a, [next(sems) for _ in range(4)])
    end = last.stages - 1

    def fetch_f():
        return pltpu.make_async_copy(f_hbm, f, load_sem.at[4])

    @pl.when(i == 0)
    def _():
        load = pltpu.make_async_copy(space_hbm, mine_b, load_sem.at[0])
        load.start()
        fetch_f().start()
        greet_signal(n_clip)
        frames_matrix(wfa, taps, ends)
        first.load(kept)
        greet_wait(n_clip)
        first.spread(end)
        load.wait()
        space.send(0)

    plan, rest = {}, []
    final = pl.num_programs(0) - 1

    def book(ops, steps):
        left = []
        for j, op in enumerate(ops):
            step = steps[j * len(steps) // len(ops)]
            if step >= 2 * high + C_JOIN // C_MID - 1:
                left.append(op)
            else:
                plan.setdefault(step, []).append(op)
        rest.append(left)

    down, up = range(end + 1), range(end, -1, -1)
    book(
        [functools.partial(space.gather, k) for k in down] + [space.regain]
        + [functools.partial(space.take, k) for k in up], SPACE_STEPS,
    )
    book([functools.partial(first.take, k) for k in up], FIRST_STEPS)
    book(
        [functools.partial(half.gather, k) for k in down] + [half.regain]
        + [functools.partial(half.take, k) for k in up], HALF_STEPS,
    )
    book(
        [functools.partial(last.gather, k) for k in down] + [last.regain]
        + [functools.partial(last.take, k) for k in up], LATE_STEPS,
    )
    for step, ops in sorted(plan.items()):

        @pl.when(i == step)
        def _():
            for op in ops:
                op()

    @pl.when(i < high)
    def _():
        mean, scale, mult, one, two = norm_terms(mom1, mids[0], tot6, inv)
        zhat = (z1[...] - mean) * scale
        dz = mult * (q1[...] - spread(m[...], MIX) * (one + zhat * two))
        up, down = sooner(dz, clips), later(dz, clips)
        for k, v in enumerate((up, dz, down)):
            da[i, :, :, k * C_MID : (k + 1) * C_MID] = v[:, :, :C_MID].astype(bf16)
            df[i, :, :, k * 128 : (k + 1) * 128] = v[:, :, C_MID:].astype(bf16)
        dlat = dot_nt(
            jnp.concatenate([dzp[...].reshape(rows, C_IN), da[i].reshape(rows, 3 * C_MID)], axis=1),
            jnp.concatenate([wp[C_IN:]] + [wa[k, C_IN:] for k in range(3)], axis=1),
        )
        dlat = dlat.astype(bf16).astype(f32).reshape(cols, slab, C_LAT)
        dl[i, :, :, :C_LAT] = dlat.astype(bf16)
        dl[i, :, :, C_LAT:] = sooner(dlat, clips).astype(bf16)

    @pl.when((i >= high) & (i < late))
    def _():
        c = i - high
        got = dot_tn(x[...].reshape(every, C_MID), da[...].reshape(every, 3 * C_MID)).astype(bf16)

        @pl.when(c < 2)
        def _():
            for k in range(3):
                mine_h[pl.ds(pl.multiple_of((2 * k + c) * C_MID, C_MID), C_MID), :] = got[:, k * C_MID : (k + 1) * C_MID]

        @pl.when(c >= 2)
        def _():
            for k in range(3):
                at = pl.multiple_of((3 * k + c - 2) * C_MID, C_MID)
                mine_a[pl.ds(at, C_MID), :] = got[:, k * C_MID : (k + 1) * C_MID]

        @pl.when(c == 1)
        def _():
            half.send(0)

    @pl.when(i == late - 1)
    def _():
        fetch_f().wait()
        fast = f[...].reshape(every, WIDE_FAST)
        d = dl[...].reshape(every, 2 * C_LAT)
        at = 9 * C_MID
        mine_a[at + 2 * C_FAST : at + 5 * C_FAST, :] = dot_tn(fast[:, : 3 * C_FAST], d[:, :C_LAT]).astype(bf16)
        mine_a[at : at + 2 * C_FAST, :] = dot_tn(fast[:, 2 * C_FAST :], d[:, C_LAT:]).astype(bf16)
        at += 5 * C_FAST
        g = df[...].reshape(every, 3 * 128)
        mid = dot_tn(g[:, 128:256], fast)
        sums = [jnp.zeros((C_FMID, C_FAST), f32) for _ in range(3)]
        for p in range(ALPHA):
            for s in range(max(p - 1, 0), min(p + 2, ALPHA)):
                sums[s - p + 1] += mid[p * C_FMID : (p + 1) * C_FMID, s * C_FAST : (s + 1) * C_FAST]
        sums[0] += dot_tn(g[:, :128], fast[:, 3 * C_FAST :])[:C_FMID]
        sums[2] += dot_tn(g[:, 256:], fast[:, :C_FAST])[3 * C_FMID :]
        mine_a[at:, :] = jnp.zeros((mine_a.shape[0] - at, 256), bf16)
        for q in range(3):
            mine_a[at + q * C_FMID : at + (q + 1) * C_FMID, :C_FAST] = sums[q].astype(bf16)
        last.send(0)

    @pl.when(i >= late)
    def _():
        h = i - late
        dj = dot_nt(
            jnp.concatenate([dzp[...].reshape(rows, C_IN), da[h].reshape(rows, 3 * C_MID)], axis=1),
            jnp.concatenate([wp[:C_IN]] + [wa[k, :C_IN] for k in range(3)], axis=1),
        )
        mask = spread(m[...], C_IN)
        dj = dj.reshape(cols, slab, C_IN)
        for w in range(cols):
            sx[:, w] = (dj[w] * mask).astype(bf16).reshape(slab // clips, clips, C_IN)
        g = df[h].reshape(rows, 3 * 128)
        d = dl[h].reshape(rows, 2 * C_LAT)
        total = gf[...].reshape(rows, WIDE_FAST) + dot(g[:, 128:256], taps[...])
        head = dot_nt(d[:, :C_LAT], wl[2:5].reshape(3 * C_FAST, C_LAT))
        tail = dot_nt(d[:, C_LAT:], wl[0:2].reshape(2 * C_FAST, C_LAT))
        blocks = [total[:, p * C_FAST : (p + 1) * C_FAST] for p in range(ALPHA)]
        for p in range(3):
            blocks[p] = blocks[p] + head[:, p * C_FAST : (p + 1) * C_FAST]
        for p in range(2):
            blocks[2 + p] = blocks[2 + p] + tail[:, p * C_FAST : (p + 1) * C_FAST]
        blocks[3] = blocks[3] + dot(g[:, :128], ends[0])
        blocks[0] = blocks[0] + dot(g[:, 256:], ends[1])
        blocks = [v.astype(bf16) for v in blocks]
        for w in range(cols):
            stacked = jnp.concatenate([v[w * slab : (w + 1) * slab] for v in blocks], axis=0)
            fx[:, w] = dot_tn(perm[...], stacked).astype(bf16).reshape(clips, slab, C_FAST)

    @pl.when(i == final)
    def _():
        for k in range(max(len(left) for left in rest)):
            for left in rest:
                if k < len(left):
                    left[k]()
        saves = [
            pltpu.make_async_copy(a, b, load_sem.at[k])
            for k, (a, b) in enumerate(((done1, out1), (done_b, out_b), (done_h, out_h), (done_a, out_a)))
        ]
        for save in saves:
            save.start()
        for save in saves:
            save.wait()


def small_place(q):
    return 9 * C_MID + (q % 5) * C_FMID, (q // 5) * 128, C_FMID if q < 9 else C_FAST


def greet_signal(n_clip):
    barrier = pltpu.get_barrier_semaphore()
    for axis, power in stage_orders(n_clip, 1)[0]:
        pl.semaphore_signal(barrier, inc=1, device_id=partner_of(axis, power), device_id_type=MESH)


def greet_wait(n_clip):
    pl.semaphore_wait(pltpu.get_barrier_semaphore(), len(stage_orders(n_clip, 1)[0]))


def finish_outputs(so, fo, sx, fx, done1, done_b, done_h, done_a, tot4, tot5, tot6, so_out, fo_out, sx_out, fx_out,
                   wp_hbm, wc_hbm, wb_hbm, wa_hbm, wl_hbm, wfa_out, wfc_out, wfb_out, sgain_out, sshift_out, fgain_out,
                   fshift_out, wp, wc, wb, wa, wl, sem):
    i = pl.program_id(0)
    moves = ((wp, wp_hbm), (wc, wc_hbm), (wb, wb_hbm), (wa, wa_hbm), (wl, wl_hbm))

    def move(k):
        return pltpu.make_async_copy(moves[k][0], moves[k][1], sem.at[k])

    @pl.when(i == 0)
    def _():
        for b in range(C_IN // 256):
            wp[:, b * 256 : (b + 1) * 256] = done1[b * C_JOIN : (b + 1) * C_JOIN, :].astype(f32)
        move(0).start()
        for b in range(C_IN // 256):
            at = 4 * C_JOIN + b * C_MID
            wc[:, b * 256 : (b + 1) * 256] = done1[at : at + C_MID, :].astype(f32)
        move(1).start()

    @pl.when(i == 1)
    def _():
        for t in range(9):
            wb[t // 3, t % 3] = done_b[t * C_MID : (t + 1) * C_MID, :].astype(f32)
        move(2).start()

    @pl.when(i == 2)
    def _():
        for k in range(3):
            wa[k, : 2 * C_MID] = done_h[2 * k * C_MID : 2 * (k + 1) * C_MID, :].astype(f32)
            wa[k, 2 * C_MID :] = done_a[3 * k * C_MID : 3 * (k + 1) * C_MID, :].astype(f32)
        move(3).start()
        at = 9 * C_MID
        for k in range(5):
            wl[k] = done_a[at + k * C_FAST : at + (k + 1) * C_FAST, :].astype(f32)
        move(4).start()

    @pl.when(i == 3)
    def _():
        at = 9 * C_MID + 5 * C_FAST
        for q in range(3):
            wfa_out[q] = done_a[at + q * C_FMID : at + (q + 1) * C_FMID, :C_FAST].astype(f32)
        for q in range(10):
            r, c, width = small_place(q)
            piece = done_b[r : r + C_FMID, c : c + width].astype(f32)
            if q < 9:
                wfb_out[q] = piece
            else:
                wfc_out[...] = piece
        lane = lax.broadcasted_iota(jnp.int32, (1, 128), 1)
        for k, slow, fast in ((0, sshift_out, fshift_out), (1, sgain_out, fgain_out)):
            at = k * MIX
            row = 0
            for source, begin, width in (
                (tot6, at, C_MID), (tot5, at, C_MID), (tot4, k * C_IN, C_IN), (tot4, 2 * k * C_IN, C_IN)
            ):
                for c in range(begin, begin + width, 128):
                    slow[row : row + 1] = source[:, c : c + 128]
                    row += 1
            c = pltpu.roll(tot4[:, 3 * C_IN + k * C_FAST : 3 * C_IN + (k + 1) * C_FAST], 2 * C_FMID, 1)
            a, b = tot6[:, at + C_MID : at + MIX], tot5[:, at + C_MID : at + MIX]
            fast[:, :128] = jnp.where(lane < C_FMID, a, jnp.where(lane < 2 * C_FMID, b, c))
            fast[:, 128:] = c[:, : 2 * C_FMID]

    so_out[...] = so[...]
    fo_out[...] = fo[...]
    sx_out[...] = sx[...]
    fx_out[...] = fx[...]

    @pl.when(i == pl.num_programs(0) - 1)
    def _():
        for k in range(5):
            move(k).wait()


def prepare(clips, n_clip, counts, sgain_rows, sshift_rows, fgain, fshift, wb, m, perm, weight, inv, mids, last, wide,
            sgain, sshift):
    for k in range(sgain_rows.shape[0]):
        sgain[:, k * 128 : (k + 1) * 128] = sgain_rows[k : k + 1]
        sshift[:, k * 128 : (k + 1) * 128] = sshift_rows[k : k + 1]
    slab = m.shape[0]
    frames = slab // clips
    me = lax.axis_index("clip") * clips
    shift = clips.bit_length() - 1

    def real(shape):
        r = lax.broadcasted_iota(jnp.int32, shape, 0)
        own = jnp.zeros(shape, jnp.int32)
        for c in range(clips):
            own = jnp.where((r & (clips - 1)) == c, counts[me + c], own)
        return r, (r >> shift) < own

    m[...] = real(m.shape)[1].astype(f32)
    width = perm.shape[1]
    r, there = real((slab, width))
    col = lax.broadcasted_iota(jnp.int32, (slab, width), 1)
    for p in range(ALPHA):
        want = (r & (clips - 1)) * (ALPHA * frames) + ALPHA * (r >> shift) + p
        perm[p * slab : (p + 1) * slab] = ((want == col) & there).astype(f32).astype(bf16)
    groups = []
    for g in range(n_clip):
        part = counts[g * clips]
        for c in range(1, clips):
            part = part + counts[g * clips + c]
        groups.append(part)
    total = groups[0]
    for part in groups[1:]:
        total = total + part
    whole_count = jnp.full((1, 128), total, jnp.int32).astype(f32)
    inv[...] = 1.0 / (whole_count * (H * W))
    for g in range(n_clip):
        weight[g] = jnp.full((1, 128), groups[g], jnp.int32).astype(f32) / whole_count
    lane = lax.broadcasted_iota(jnp.int32, (1, 128), 1)
    for k in range(2):
        for j, (slow, fast) in enumerate(((sgain, fgain), (sshift, fshift))):
            mine = (lane >= k * C_FMID) & (lane < (k + 1) * C_FMID)
            mids[2 * k + j, :, :C_MID] = slow[:, k * C_MID : (k + 1) * C_MID]
            mids[2 * k + j, :, C_MID:] = phase_sum(jnp.where(mine, fast[:, :128], 0.0))
    for j, fast in enumerate((fgain, fshift)):
        last[j] = fast[:, 2 * C_FMID :]
    for t in range(9):
        w = wb[t]
        for p in range(ALPHA):
            parts = [jnp.zeros((C_FMID, C_FMID), bf16)] * ALPHA
            parts[p] = w
            wide[t, p * C_FMID : (p + 1) * C_FMID] = jnp.concatenate(parts, axis=1)


def vmem_spec():
    return pl.BlockSpec(memory_space=pltpu.VMEM)


def shaped(shape, kind):
    return jax.ShapeDtypeStruct(shape, kind)


def whole(shape):
    return pl.BlockSpec(shape, lambda h: (0,) * len(shape))


def per_line(shape):
    return pl.BlockSpec((None,) + tuple(shape), lambda h: (h,) + (0,) * len(shape))


def params(limit):
    return pltpu.CompilerParams(vmem_limit_bytes=60 * MIB)


def on_device(
    slow_input,
    fast_input,
    frame_counts,
    lateral_weight,
    slow_a_weight,
    slow_b_weight,
    slow_c_weight,
    slow_proj_weight,
    fast_a_weight,
    fast_b_weight,
    fast_c_weight,
    slow_gain,
    slow_shift,
    fast_gain,
    fast_shift,
    slow_cotangent,
    fast_cotangent,
):
    n_clip = lax.axis_size("clip")
    clips, frames, high, cols, _ = slow_input.shape
    slab = clips * frames
    lanes = slow_gain.reshape(-1, 128), slow_shift.reshape(-1, 128)
    slow_row = shaped((1, slow_gain.shape[0]), f32)
    vm = vmem_spec()
    m, perm, weight, inv, mids, ends, wfb, sgain, sshift = pl.pallas_call(
        functools.partial(prepare, clips, n_clip),
        in_specs=[pl.BlockSpec(memory_space=pltpu.SMEM)] + [vm] * 5,
        out_specs=(vm,) * 9,
        out_shape=(
            shaped((slab, 128), f32), shaped((ALPHA * slab, ALPHA * slab), bf16), shaped((n_clip, 1, 128), f32),
            shaped((1, 128), f32), shaped((4, 1, MIX), f32), shaped((2, 1, C_FAST), f32), shaped((9, 128, 128), bf16),
            slow_row, slow_row,
        ),
        compiler_params=params(60),
        name="prepare",
    )(frame_counts, *lanes, fast_gain[None], fast_shift[None], fast_b_weight.reshape(9, C_FMID, C_FMID))
    wfa = fast_a_weight.transpose(0, 2, 1)
    xs = slow_input.transpose(1, 2, 3, 0, 4)
    xf = fast_input.transpose(0, 2, 3, 1, 4)
    cot = slow_cotangent.transpose(1, 2, 3, 0, 4)
    fcot = fast_cotangent.transpose(0, 2, 3, 1, 4)
    def lines(c, kind):
        return shaped((high, cols, slab, c), kind)

    m_spec = whole((slab, 128))
    vm = vmem_spec()
    hbm = pl.BlockSpec(memory_space=pl.ANY)

    def early_line(shape):
        return pl.BlockSpec((None,) + tuple(shape), lambda i: (jnp.minimum(i, high - 1),) + (0,) * len(shape))

    def late_line(shape, begin):
        return pl.BlockSpec((None,) + tuple(shape), lambda i: (jnp.maximum(i - begin, 0),) + (0,) * len(shape))

    def slow_block(index):
        return pl.BlockSpec((frames, None, cols, clips, C_IN), lambda i: (0, index(i), 0, 0, 0))

    def fast_block(index):
        return pl.BlockSpec((clips, None, cols, ALPHA * frames, C_FAST), lambda i: (0, index(i), 0, 0, 0))

    def early(i):
        return jnp.minimum(i, high - 1)

    def after(begin):
        return lambda i: jnp.maximum(i - begin, 0)

    def remote(ident):
        return pltpu.CompilerParams(collective_id=ident, has_side_effects=True, vmem_limit_bytes=60 * MIB)

    rim_shapes = (shaped((cols, slab, MIX), f32), shaped((high, slab, MIX), f32), shaped((slab, MIX), f32))
    edge_scratch = [pltpu.VMEM((cols, slab, MIX), f32), pltpu.VMEM((high, slab, MIX), f32)]
    rims = rim_scratch(cols, slab)
    L1 = MIX + C_IN
    x, f, z1, zp, stp, base, mom1, row1, col1, corner1 = pl.pallas_call(
        functools.partial(first_pass, clips, n_clip),
        grid=(2 * high,),
        in_specs=[slow_block(early), fast_block(early)] + [vm] * 4 + [hbm] + [vm] * 2,
        out_specs=(
            early_line((cols, slab, C_JOIN)), early_line((cols, slab, WIDE_FAST)), early_line((cols, slab, MIX)),
            late_line((cols, slab, C_IN), high), vm, vm, vm, vm, vm, vm,
        ),
        out_shape=(
            lines(C_JOIN, bf16), lines(WIDE_FAST, bf16), lines(MIX, f32), lines(C_IN, bf16), shaped((2, C_IN), f32),
            shaped((1, C_IN), f32), shaped((2, MIX), f32),
        ) + rim_shapes,
        scratch_shapes=[
            pltpu.VMEM((C_JOIN, C_IN), bf16), pltpu.SemaphoreType.DMA((1,)),
            pltpu.VMEM((high, cols, slab, C_JOIN), bf16), pltpu.VMEM((128, WIDE_FAST), bf16),
            pltpu.VMEM((2, 128, C_FAST), bf16), pltpu.VMEM((1, L1), f32), pltpu.VMEM((1, L1), f32),
            pltpu.VMEM((1, L1), f32),
        ] + edge_scratch + exchange_scratch(n_clip, 2, MIX) + rims,
        compiler_params=remote(1),
        name="first_pass",
    )(xs, xf, m, perm, lateral_weight, slow_a_weight, slow_proj_weight, wfa, weight)

    a1, z2, mom2, zrow, zcol, zcorner, cot = pl.pallas_call(
        functools.partial(second_pass, n_clip),
        grid=(high + 1,),
        in_specs=[hbm] + [vm] * 10 + [slow_block(after(1))],
        out_specs=(hbm, hbm, vm, vm, vm, vm, late_line((cols, slab, C_IN), 1)),
        out_shape=(
            shaped((high + 2, cols + 2, slab, MIX), bf16), lines(MIX, f32), shaped((2, L1), f32),
        ) + rim_shapes + (lines(C_IN, bf16),),
        scratch_shapes=[
            pltpu.VMEM((high + 2, cols + 2, slab, MIX), bf16), pltpu.VMEM((high, cols, slab, MIX), f32),
            pltpu.SemaphoreType.DMA((2,)),
            pltpu.VMEM((high, cols, slab, MIX), f32), pltpu.SemaphoreType.DMA((high,)), pltpu.VMEM((1, MIX), f32),
            pltpu.VMEM((1, MIX), f32),
        ] + exchange_scratch(n_clip, 2, L1) + rims,
        compiler_params=remote(2),
        name="second_pass",
    )(z1, row1, col1, corner1, mom1, mids, m, slow_b_weight, wfb, stp, weight, cot)

    L3 = C_IN + C_FAST
    a2, mom3, fcot = pl.pallas_call(
        functools.partial(third_pass, n_clip),
        grid=(2 * high,),
        in_specs=[early_line((cols, slab, MIX))] + [vm] * 6 + [fast_block(after(high)), vm],
        out_specs=(early_line((cols, slab, MIX)), vm, late_line((cols, slab, WIDE_FAST), high)),
        out_shape=(lines(MIX, bf16), shaped((2, L3), f32), lines(WIDE_FAST, bf16)),
        scratch_shapes=[pltpu.VMEM((128, WIDE_FAST), bf16)] + [pltpu.VMEM((1, L3), f32)] * 3
        + exchange_scratch(n_clip, 2, L3),
        compiler_params=remote(3),
        name="third_pass",
    )(z2, mom2, mids, m, slow_c_weight, fast_c_weight, weight, fcot, perm)

    L4 = 3 * C_IN + 2 * C_FAST
    so, fo, gs, gf, tot4 = pl.pallas_call(
        functools.partial(fourth_pass, n_clip, clips),
        grid=(2 * high,),
        in_specs=[early_line((cols, slab, MIX)), early_line((cols, slab, C_IN))] + [vm] * 6 + [
            early_line((cols, slab, C_IN)), early_line((cols, slab, WIDE_FAST)), early_line((cols, slab, WIDE_FAST)),
        ] + [vm] * 5,
        out_specs=(
            slow_block(after(high)), fast_block(after(high)), early_line((cols, slab, C_IN)),
            early_line((cols, slab, WIDE_FAST)), vm,
        ),
        out_shape=(
            shaped(xs.shape, bf16), shaped(xf.shape, bf16), lines(C_IN, f32), lines(WIDE_FAST, f32),
            shaped((1, L4), f32),
        ),
        scratch_shapes=[
            pltpu.VMEM((high, cols, slab, C_IN), bf16), pltpu.VMEM((high, cols, slab, WIDE_FAST), bf16),
            pltpu.VMEM((1, L4), f32), pltpu.VMEM((128, WIDE_FAST), bf16), pltpu.VMEM((cols, slab, C_IN), f32),
            pltpu.VMEM((cols, slab, WIDE_FAST), f32),
        ] + exchange_scratch(n_clip, 1, L4),
        compiler_params=remote(4),
        name="fourth_pass",
    )(
        a2, zp, base, mom2, mom3, sgain, sshift, ends, cot, fcot, f, m, perm, slow_c_weight, fast_c_weight, weight,
    )

    n = high * cols
    early_sizes = (2048, 2048, 2048)
    space_sizes = (1024, 1024, 512)
    half_sizes = (512, 512, 512)
    late_sizes = (1024, 1024, 1024)

    def flat(v):
        return v.reshape((n,) + v.shape[2:])

    steps = C_JOIN // C_MID
    dzp, q2, tot5, qrow, qcol, qcorner, dw1, dwfc = pl.pallas_call(
        functools.partial(fifth_pass, n_clip),
        grid=(high + steps,),
        in_specs=[
            early_line((cols, slab, C_IN)), early_line((cols, slab, WIDE_FAST)), early_line((cols, slab, MIX)),
            early_line((cols, slab, C_IN)), vm, early_line((cols, slab, MIX)),
        ] + [vm] * 10 + [pl.BlockSpec((n, slab, C_MID), lambda i: (0, 0, jnp.clip(i - high, 0, steps - 1))), vm],
        out_specs=(
            early_line((cols, slab, C_IN)), early_line((cols, slab, MIX)), vm, vm, vm, vm, vm, vm,
        ),
        out_shape=(lines(C_IN, bf16), lines(MIX, f32), shaped((1, 2 * MIX), f32)) + rim_shapes + (
            shaped((sum(early_sizes), 256), bf16), shaped((C_FMID, C_FAST), f32),
        ),
        scratch_shapes=[
            pltpu.VMEM((high, cols, slab, C_IN), bf16), pltpu.VMEM((high, cols, slab, C_IN), bf16),
            pltpu.VMEM((high, cols, slab, WIDE_FAST), bf16), pltpu.VMEM((high, cols, slab, MIX), bf16),
            pltpu.VMEM((1, 2 * MIX), f32), pltpu.VMEM((128, WIDE_FAST), bf16), pltpu.VMEM((cols, slab, C_IN), f32),
            pltpu.VMEM((cols, slab, WIDE_FAST), f32),
        ] + edge_scratch + exchange_scratch(n_clip, 1, 2 * MIX) + rims,
        compiler_params=remote(5),
        name="fifth_pass",
    )(
        gs, gf, a2, zp, base, z2, mom2, mom3, tot4, inv, sgain, ends, mids, m, slow_c_weight, fast_c_weight,
        flat(x), weight,
    )

    q1, tot6, dwb, kept = pl.pallas_call(
        functools.partial(sixth_pass, n_clip, early_sizes),
        grid=(10,),
        in_specs=[hbm] * 4 + [vm] * 16 + [hbm],
        out_specs=(hbm,) + (vm,) * 3,
        out_shape=(
            lines(MIX, f32), shaped((1, 2 * MIX), f32), shaped((sum(space_sizes), 256), bf16),
            shaped((sum(Reducer.layout(n_clip, early_sizes)[2]), 256), bf16),
        ),
        scratch_shapes=[
            pltpu.VMEM((high, cols, slab, MIX), f32), pltpu.VMEM((9, C_FMID, C_FMID), f32),
            pltpu.VMEM((high + 2, cols + 2, slab, MIX), bf16),
        ]
        + [pltpu.VMEM((high, cols, slab, MIX), f32)] * 3
        + [pltpu.VMEM((high + 2, cols + 2, slab, MIX), bf16)]
        + [pltpu.SemaphoreType.DMA((high,))] * 3
        + [pltpu.SemaphoreType.DMA((3,)), pltpu.VMEM((1, 2 * MIX), f32)]
        + [pltpu.VMEM((sum(early_sizes), 256), bf16), Reducer.scratch(n_clip, early_sizes)]
        + exchange_scratch(n_clip, 1, 2 * MIX) + Reducer.sems(n_clip, early_sizes, 2),
        compiler_params=remote(6),
        name="sixth_pass",
    )(
        q2, z2, z1, a1, qrow, qcol, qcorner, zrow, zcol, zcorner, mom1, mom2, tot5, inv, mids, m,
        slow_b_weight, wfb, weight, dwfc, dw1,
    )

    def twice_line(shape):
        begin = high + steps
        return pl.BlockSpec(
            (None,) + tuple(shape),
            lambda i: (jnp.where(i < begin, jnp.minimum(i, high - 1), i - begin),) + (0,) * len(shape),
        )

    sx, fx, done1, done_b, done_h, done_a = pl.pallas_call(
        functools.partial(seventh_pass, clips, n_clip, early_sizes, space_sizes, half_sizes, late_sizes),
        grid=(2 * high + steps,),
        in_specs=[
            early_line((cols, slab, MIX)), early_line((cols, slab, MIX)), twice_line((cols, slab, C_IN)),
            late_line((cols, slab, WIDE_FAST), high + steps),
            pl.BlockSpec((n, slab, C_MID), lambda i: (0, 0, jnp.clip(i - high, 0, steps - 1))), hbm, vm, hbm,
        ] + [vm] * 10,
        out_specs=(slow_block(after(high + steps)), fast_block(after(high + steps)), hbm, hbm, hbm, hbm),
        out_shape=(
            shaped(xs.shape, bf16), shaped(xf.shape, bf16), shaped((sum(early_sizes), 256), bf16),
            shaped((sum(space_sizes), 256), bf16), shaped((sum(half_sizes), 256), bf16), shaped((sum(late_sizes), 256), bf16),
        ),
        scratch_shapes=[pltpu.VMEM((n, slab, WIDE_FAST), bf16)] + [
            pltpu.VMEM((sum(v), 256), bf16) for v in (early_sizes, space_sizes, half_sizes, late_sizes)
        ] + [
            pltpu.VMEM((high, cols, slab, 3 * C_MID), bf16), pltpu.VMEM((high, cols, slab, 2 * C_LAT), bf16),
            pltpu.VMEM((high, cols, slab, 3 * 128), bf16), pltpu.VMEM((128, WIDE_FAST), bf16),
            pltpu.VMEM((2, 128, C_FAST), bf16), pltpu.VMEM((sum(space_sizes), 256), bf16),
            Reducer.scratch(n_clip, space_sizes), pltpu.VMEM((sum(half_sizes), 256), bf16),
            Reducer.scratch(n_clip, half_sizes), pltpu.VMEM((sum(late_sizes), 256), bf16),
            Reducer.scratch(n_clip, late_sizes), pltpu.SemaphoreType.DMA((5,)),
        ] + Reducer.sems(n_clip, early_sizes, 2) + Reducer.sems(n_clip, space_sizes) + Reducer.sems(n_clip, half_sizes)
        + Reducer.sems(n_clip, late_sizes),
        compiler_params=remote(7),
        name="seventh_pass",
    )(
        q1, z1, dzp, gf, flat(x), flat(f), kept, dwb, mom1, tot6, inv, mids, m, perm, lateral_weight, slow_a_weight,
        slow_proj_weight, wfa,
    )

    slow_rows, fast_row = shaped(lanes[0].shape, f32), shaped((1, fast_gain.shape[0]), f32)
    def here(i):
        return i

    weights = (
        shaped((C_JOIN, C_IN), f32), shaped((C_MID, C_IN), f32), shaped((3, 3, C_MID, C_MID), f32),
        shaped((3, C_JOIN, C_MID), f32), shaped((5, C_FAST, C_LAT), f32),
    )
    maps = [slow_block(here), fast_block(here)] * 2
    so, fo, sx, fx, dwp, dwc, dwb, dwa, dwl, dwfa, dwfc, dwfb, dsg, dss, dfg, dfs = pl.pallas_call(
        finish_outputs,
        grid=(high,),
        in_specs=maps + [vm] * 7,
        out_specs=tuple(maps) + (hbm,) * 5 + (vm,) * 7,
        out_shape=(shaped(xs.shape, bf16), shaped(xf.shape, bf16)) * 2 + weights + (
            shaped((3, C_FMID, C_FAST), f32), shaped((C_FMID, C_FAST), f32), shaped((9, C_FMID, C_FMID), f32),
            slow_rows, slow_rows, fast_row, fast_row,
        ),
        scratch_shapes=[pltpu.VMEM(v.shape, f32) for v in weights] + [pltpu.SemaphoreType.DMA((5,))],
        compiler_params=params(60),
        name="finish_outputs",
    )(so, fo, sx, fx, done1, done_b, done_h, done_a, tot4, tot5, tot6)
    return (
        so.transpose(3, 0, 1, 2, 4),
        fo.transpose(0, 3, 1, 2, 4),
        sx.transpose(3, 0, 1, 2, 4),
        fx.transpose(0, 3, 1, 2, 4),
        dwl,
        dwa,
        dwb,
        dwc,
        dwp,
        dwfa.transpose(0, 2, 1),
        dwfb.reshape(3, 3, C_FMID, C_FMID),
        dwfc,
        dsg.reshape(-1),
        dss.reshape(-1),
        dfg[0],
        dfs[0],
    )


def solution(mesh):
    tiles = P("clip", None, "ha", "wa", None)
    return jax.shard_map(
        on_device,
        mesh=mesh,
        in_specs=(tiles, tiles) + (P(),) * 13 + (tiles, tiles),
        out_specs=(tiles,) * 4 + (P(),) * 12,
        check_vma=False,
    )
```

```python
import functools

import jax
import jax.numpy as jnp
from jax import lax
from jax.experimental import pallas as pl
from jax.experimental.pallas import tpu as pltpu
from jax.sharding import PartitionSpec as P

ALPHA = 4
H = 14
W = 14
C_IN = 1024
C_LAT = 256
C_MID = 256
C_FAST = 128
C_FMID = 32
C_JOIN = C_IN + C_LAT
MIX = C_MID + ALPHA * C_FMID
WIDE_FAST = ALPHA * C_FAST

eps_norm = 1e-05
f32 = jnp.float32
bf16 = jnp.bfloat16
MESH = pl.DeviceIdType.MESH
MIB = 1 << 20


def dot(a, b):
    return lax.dot_general(a, b, (((1,), (0,)), ((), ())), preferred_element_type=f32)


def dot_nt(a, b):
    return lax.dot_general(a, b, (((1,), (1,)), ((), ())), preferred_element_type=f32)


def dot_tn(a, b):
    return lax.dot_general(a, b, (((0,), (0,)), ((), ())), preferred_element_type=f32)


def sigmoid(v):
    return 0.5 + 0.5 * jnp.tanh(0.5 * v)


def later(y, clips):
    return jnp.concatenate([jnp.zeros_like(y[:, :clips]), y[:, : y.shape[1] - clips]], axis=1)


def sooner(y, clips):
    return jnp.concatenate([y[:, clips:], jnp.zeros_like(y[:, :clips])], axis=1)


def rows_sum(v):
    return jnp.sum(jnp.sum(v, axis=0), axis=0, keepdims=True)


def phase_sum(v):
    out = v
    for k in range(1, ALPHA):
        out = out + pltpu.roll(v, k * C_FMID, 1)
    return out


def block_sum(v):
    return sum(v[:, p * C_FAST : (p + 1) * C_FAST] for p in range(ALPHA))


def spread(mask, width):
    return jnp.tile(mask, (1, width // 128))


def frames_matrix(wfa_ref, out_ref, ends_ref):
    out_ref[...] = jnp.zeros_like(out_ref)
    ends_ref[...] = jnp.zeros_like(ends_ref)
    for p in range(ALPHA):
        for s in range(max(p - 1, 0), min(p + 2, ALPHA)):
            out_ref[p * C_FMID : (p + 1) * C_FMID, s * C_FAST : (s + 1) * C_FAST] = wfa_ref[s - p + 1]
    ends_ref[0, 0:C_FMID] = wfa_ref[0]
    ends_ref[1, 3 * C_FMID :] = wfa_ref[2]


def expand_matrix(wfc_ref, out_ref):
    out_ref[...] = jnp.zeros_like(out_ref)
    for p in range(ALPHA):
        out_ref[p * C_FMID : (p + 1) * C_FMID, p * C_FAST : (p + 1) * C_FAST] = wfc_ref[...]


class Exchange:
    def __init__(self, n_clip, moments, refs, rim_refs=None):
        self.n = n_clip
        self.moments = moments
        self.part, self.near, self.mid, self.far, self.near_send, self.near_recv, self.far_send, self.far_recv = refs
        self.clip, self.ha, self.wa = lax.axis_index("clip"), lax.axis_index("ha"), lax.axis_index("wa")
        self.me = 2 * self.ha + self.wa
        self.peers = [(1 - self.ha, self.wa), (self.ha, 1 - self.wa), (1 - self.ha, 1 - self.wa)]
        self.others = [lax.rem(self.clip + d, n_clip) for d in range(1, n_clip)]
        if rim_refs is not None:
            self.packs, self.lands, self.rim_send, self.rim_recv = rim_refs

    def signal(self):
        barrier = pltpu.get_barrier_semaphore()
        for a, b in self.peers:
            pl.semaphore_signal(barrier, inc=1, device_id=(self.clip, a, b), device_id_type=MESH)
        for other in self.others:
            pl.semaphore_signal(barrier, inc=1, device_id=(other, self.ha, self.wa), device_id_type=MESH)

    def meet(self):
        pl.semaphore_wait(pltpu.get_barrier_semaphore(), 3 + self.n - 1)

    def near_copy(self, k, slot):
        a, b = self.peers[k]
        return pltpu.make_async_remote_copy(
            src_ref=self.part, dst_ref=self.near.at[slot], send_sem=self.near_send.at[k],
            recv_sem=self.near_recv.at[slot], device_id=(self.clip, a, b), device_id_type=MESH,
        )

    def far_copy(self, d, slot):
        return pltpu.make_async_remote_copy(
            src_ref=self.mid, dst_ref=self.far.at[slot], send_sem=self.far_send.at[d],
            recv_sem=self.far_recv.at[slot], device_id=(self.others[d], self.ha, self.wa), device_id_type=MESH,
        )

    def rim_copy(self, k):
        a, b = self.peers[k]
        size = 1 if k == 2 else self.packs.shape[1]
        return pltpu.make_async_remote_copy(
            src_ref=self.packs.at[k, pl.ds(0, size)], dst_ref=self.lands.at[k, pl.ds(0, size)],
            send_sem=self.rim_send.at[k], recv_sem=self.rim_recv.at[k], device_id=(self.clip, a, b),
            device_id_type=MESH,
        )

    def send_near(self):
        for k in range(3):
            self.near_copy(k, self.me).start()
        self.near[self.me] = self.part[...]

    def send_rims(self, line, side):
        count = self.packs.shape[1]
        centre = self.part[0:1, :MIX] if self.moments else jnp.zeros((1, MIX), f32)
        self.packs[0] = (line[...] - centre).astype(bf16)
        self.packs[1] = (side[...] - centre).astype(bf16)
        self.packs[2, 0] = self.packs[0, (count - 1) * (1 - self.wa)]
        for k in range(3):
            self.rim_copy(k).start()

    def send_far(self):
        for k, (a, b) in enumerate(self.peers):
            self.near_copy(k, 2 * a + b).wait_recv()
        near = self.near
        if self.moments:
            mean = (near[0, 0:1] + near[1, 0:1] + near[2, 0:1] + near[3, 0:1]) * 0.25
            self.mid[0:1] = mean
            self.mid[1:2] = sum(near[k, 1:2] + (near[k, 0:1] - mean) ** 2 for k in range(4)) * 0.25
        else:
            self.mid[...] = near[0] + near[1] + near[2] + near[3]
        for d in range(self.n - 1):
            self.far_copy(d, self.clip).start()
        self.far[self.clip] = self.mid[...]

    def finish(self, out, weight):
        for d, other in enumerate(self.others):
            self.far_copy(d, other).wait_recv()
        width = out.shape[1]
        far = self.far
        if self.moments:
            mean = sum(far[k, 0:1] * spread(weight[k], width) for k in range(self.n))
            out[0:1] = mean
            out[1:2] = sum((far[k, 1:2] + (far[k, 0:1] - mean) ** 2) * spread(weight[k], width) for k in range(self.n))
        else:
            out[...] = sum(far[k] for k in range(self.n))
        for k in range(3):
            self.near_copy(k, self.me).wait_send()
        for d in range(self.n - 1):
            self.far_copy(d, self.clip).wait_send()

    def finish_rims(self, rims):
        for k, (a, b) in enumerate(self.peers):
            self.rim_copy(k).wait_recv()
            centre = self.near[2 * a + b, 0:1, :MIX] if self.moments else jnp.zeros((1, MIX), f32)
            land = self.lands[k, 0] if k == 2 else self.lands[k]
            rims[k][...] = land.astype(f32) + centre
        for k in range(3):
            self.rim_copy(k).wait_send()


def exchange_scratch(n_clip, count, width):
    return [
        pltpu.VMEM((count, width), f32),
        pltpu.VMEM((4, count, width), f32),
        pltpu.VMEM((count, width), f32),
        pltpu.VMEM((n_clip, count, width), f32),
        pltpu.SemaphoreType.DMA((3,)),
        pltpu.SemaphoreType.DMA((4,)),
        pltpu.SemaphoreType.DMA((n_clip,)),
        pltpu.SemaphoreType.DMA((n_clip,)),
    ]


def rim_scratch(side, slab):
    return [
        pltpu.VMEM((3, side, slab, MIX), bf16),
        pltpu.VMEM((3, side, slab, MIX), bf16),
        pltpu.SemaphoreType.DMA((3,)),
        pltpu.SemaphoreType.DMA((3,)),
    ]


def first_pass(clips, n_clip, xs, xf, m, perm, wl, wa, wp_hbm, wfa, weight,
               x_out, f_out, z_out, zp_out, st_out, base_out, mom, row, col, corner,
               wp, wp_sem, keep, taps, ends, base, one, two, line, side, *refs):
    i = pl.program_id(0)
    cols = xs.shape[1]
    slab = m.shape[0]
    rows = cols * slab
    high = keep.shape[0]
    ex = Exchange(n_clip, True, refs[:8], refs[8:])
    here = cols * jnp.sum(m[...], axis=0, keepdims=True)
    count = high * here

    def fetch_wp():
        return pltpu.make_async_copy(wp_hbm, wp, wp_sem.at[0])

    @pl.when(i == 0)
    def _():
        fetch_wp().start()
        ex.signal()
        frames_matrix(wfa, taps, ends)

    @pl.when(i < high)
    def _():
        mask_in = spread(m[...], C_IN).astype(bf16)
        for w in range(cols):
            keep[i, w, :, :C_IN] = xs[:, w].reshape(slab, C_IN) * mask_in
            phases = dot(perm[...], xf[:, w].reshape(ALPHA * slab, C_FAST)).astype(bf16)
            for p in range(ALPHA):
                f_out[w, :, p * C_FAST : (p + 1) * C_FAST] = phases[p * slab : (p + 1) * slab]
        fast = f_out[...].reshape(rows, WIDE_FAST)
        lat = dot(fast[:, : 3 * C_FAST], wl[2:5].reshape(3 * C_FAST, C_LAT)).reshape(cols, slab, C_LAT)
        back = dot(fast[:, 2 * C_FAST :], wl[0:2].reshape(2 * C_FAST, C_LAT)).reshape(cols, slab, C_LAT)
        keep[i, :, :, C_IN:] = (lat + later(back, clips)).astype(bf16)
        x_out[...] = keep[i]
        joined = keep[i].reshape(rows, C_JOIN)
        za = dot(joined, wa[1]).reshape(cols, slab, C_MID)
        za = za + later(dot(joined, wa[0]).reshape(cols, slab, C_MID), clips)
        za = za + sooner(dot(joined, wa[2]).reshape(cols, slab, C_MID), clips)
        fa = dot_nt(fast, taps[...]).reshape(cols, slab, 128)
        fa = fa + later(dot_nt(fast[:, 3 * C_FAST :], ends[0]).reshape(cols, slab, 128), clips)
        fa = fa + sooner(dot_nt(fast[:, :C_FAST], ends[1]).reshape(cols, slab, 128), clips)
        z_out[:, :, :C_MID] = za
        z_out[:, :, C_MID:] = fa
        keep_rims(ex, i, high, z_out, line, side)
        add_moments(i == 0, ((0, za, 0), (C_MID, fa, 1)), m, here, base, one, two)

    @pl.when(i == high)
    def _():
        finish_moments(ex.part, base[...], one[...], two[...], count, ((0, C_MID, 0), (C_MID, 128, 1)))
        ex.meet()
        ex.send_near()
        ex.send_rims(line, side)
        fetch_wp().wait()

    @pl.when(i == high + 2)
    def _():
        ex.send_far()

    @pl.when(i >= high)
    def _():
        joined = keep[i - high].reshape(rows, C_JOIN)
        zp = dot(joined, wp[...]).reshape(cols, slab, C_IN)
        add_moments(i == high, ((MIX, zp, 0),), m, here, base, one, two, zp_out)

    @pl.when(i == 2 * high - 1)
    def _():
        s1 = one[:, MIX:] / spread(count, C_IN)
        st_out[0:1] = base[:, MIX:] + s1
        st_out[1:2] = two[:, MIX:] / spread(count, C_IN) - s1 * s1
        base_out[...] = base[:, MIX:]
        ex.finish(mom, weight)
        ex.finish_rims((row, col, corner))


def keep_rims(ex, i, high, block, line, side):
    side[i] = block[(block.shape[0] - 1) * (1 - ex.wa)]

    @pl.when(i == (high - 1) * (1 - ex.ha))
    def _():
        line[...] = block[...]


def add_moments(first, parts, m, here, base, one, two, kept=None):
    @pl.when(first)
    def _():
        for at, z, fast in parts:
            width = z.shape[-1]
            mean = rows_sum(z * spread(m[...], width)) / spread(here, width)
            if fast:
                mean = phase_sum(mean) * 0.25
            base[:, at : at + width] = mean
            one[:, at : at + width] = jnp.zeros((1, width), f32)
            two[:, at : at + width] = jnp.zeros((1, width), f32)

    for at, z, _ in parts:
        width = z.shape[-1]
        off = z - base[:, at : at + width]
        if kept is not None:
            kept[...] = off.astype(bf16)
        off = off * spread(m[...], width)
        one[:, at : at + width] += rows_sum(off)
        two[:, at : at + width] += rows_sum(off * off)


def finish_moments(st, base, one, two, count, parts):
    for at, width, fast in parts:
        s1 = one[:, at : at + width]
        s2 = two[:, at : at + width]
        if fast:
            s1 = phase_sum(s1) * 0.25
            s2 = phase_sum(s2) * 0.25
        n = spread(count.astype(f32), width)
        s1 = s1 / n
        st[0:1, at : at + width] = base[:, at : at + width] + s1
        st[1:2, at : at + width] = s2 / n - s1 * s1


def affine(moments, gain, shift, at, width):
    mean = moments[0:1, at : at + width]
    scale = lax.rsqrt(moments[1:2, at : at + width] + eps_norm)
    return mean, scale, gain, shift


def second_pass(n_clip, z1_hbm, row, col, corner, mom, mids, m, wb, wfb, stp, weight, cot,
                a_hbm, z_hbm, mom_out, zrow, zcol, zcorner, cot_out, a_out, z_out, save_sem, z1, z1_sem, one, two, *refs):
    i = pl.program_id(0)
    high, cols, slab, _ = z1.shape
    rows = cols * slab
    ex = Exchange(n_clip, True, refs[:8], refs[8:])

    def fetch(h):
        return pltpu.make_async_copy(z1_hbm.at[h], z1.at[h], z1_sem.at[h])

    def save(k):
        source, target = ((a_out, a_hbm), (z_out, z_hbm))[k]
        return pltpu.make_async_copy(source, target, save_sem.at[k])

    @pl.when(i == 0)
    def _():
        for h in range(high):
            fetch(h).start()
        ex.signal()
        mean, scale, g, b = affine(mom, mids[0], mids[1], 0, MIX)
        mult = scale * g
        mask = spread(m[...], MIX)

        def act(z):
            v = (z - mean) * mult + b
            return (v * sigmoid(v) * mask).astype(bf16)

        far = high + 1
        a_out[far * ex.ha] = jnp.zeros((cols + 2, slab, MIX), bf16)
        a_out[:, far * ex.wa] = jnp.zeros((high + 2, slab, MIX), bf16)
        a_out[far * (1 - ex.ha), 1 : 1 + cols] = act(row[...])
        a_out[1 : 1 + high, far * (1 - ex.wa)] = act(col[...])
        a_out[far * (1 - ex.ha), far * (1 - ex.wa)] = act(corner[...])

        def fill(h, carry):
            fetch(h).wait()
            a_out[h + 1, 1 : 1 + cols] = act(z1[h])
            return carry

        lax.fori_loop(0, high, fill, 0)

        def space(h, carry):
            slow = jnp.zeros((rows, C_MID), f32)
            fast = jnp.zeros((rows, 128), f32)
            for a in range(3):
                v = [a_out[h + a, c : c + cols].reshape(rows, MIX) for c in range(3)]
                slow = slow + dot(
                    jnp.concatenate([u[:, :C_MID] for u in v], axis=1), wb[a].reshape(3 * C_MID, C_MID)
                )
                fast = fast + dot(
                    jnp.concatenate([u[:, C_MID:] for u in v], axis=1), wfb[3 * a : 3 * a + 3].reshape(3 * 128, 128)
                )
            z_out[h, :, :, :C_MID] = slow.reshape(cols, slab, C_MID)
            z_out[h, :, :, C_MID:] = fast.reshape(cols, slab, 128)
            return carry

        lax.fori_loop(0, high, space, 0)
        here = cols * jnp.sum(m[...], axis=0, keepdims=True)
        base = rows_sum(z_out[0] * mask) / spread(here, MIX)
        base = jnp.concatenate([base[:, :C_MID], phase_sum(base[:, C_MID:]) * 0.25], axis=1)
        one[...] = jnp.zeros_like(one)
        two[...] = jnp.zeros_like(two)

        def gather(h, carry):
            off = (z_out[h] - base) * mask
            one[...] += rows_sum(off)
            two[...] += rows_sum(off * off)
            return carry

        lax.fori_loop(0, high, gather, 0)
        finish_moments(ex.part, base, one[...], two[...], high * here, ((0, C_MID, 0), (C_MID, 128, 1)))
        ex.part[:, MIX:] = stp[...]
        ex.meet()
        ex.send_near()
        ex.send_rims(z_out.at[(high - 1) * (1 - ex.ha)], z_out.at[:, (cols - 1) * (1 - ex.wa)])
        save(0).start()
        save(1).start()

    @pl.when(i == 3)
    def _():
        ex.send_far()

    @pl.when(i > 0)
    def _():
        half_mask = (0.5 * spread(m[...], C_IN)).astype(bf16)
        for w in range(cols):
            cot_out[w] = cot[:, w].reshape(slab, C_IN) * half_mask

    @pl.when(i == high)
    def _():
        ex.finish(mom_out, weight)
        ex.finish_rims((zrow, zcol, zcorner))
        save(0).wait()
        save(1).wait()


def third_pass(n_clip, z2, mom, mids, m, wc, wfc, weight, fcot, perm,
               a_out, mom_out, fcot_out, big, base, one, two, *refs):
    i = pl.program_id(0)
    high = pl.num_programs(0) // 2
    cols, slab, _ = z2.shape
    rows = cols * slab
    ex = Exchange(n_clip, True, refs)
    here = cols * jnp.sum(m[...], axis=0, keepdims=True)

    @pl.when(i == 0)
    def _():
        ex.signal()
        expand_matrix(wfc, big)

    @pl.when(i < high)
    def _():
        mean, scale, g, b = affine(mom, mids[2], mids[3], 0, MIX)
        v = (z2[...] - mean) * (scale * g) + b
        a_out[...] = (v * sigmoid(v) * spread(m[...], MIX)).astype(bf16)
        a2 = a_out[...].reshape(rows, MIX)
        zc = dot(a2[:, :C_MID], wc[...]).reshape(cols, slab, C_IN)
        fc = dot(a2[:, C_MID:], big[...]).reshape(cols, slab, WIDE_FAST)

        @pl.when(i == 0)
        def _():
            base[:, :C_IN] = rows_sum(zc * spread(m[...], C_IN)) / spread(here, C_IN)
            base[:, C_IN:] = block_sum(rows_sum(fc * spread(m[...], WIDE_FAST))) / (4.0 * here)
            one[...] = jnp.zeros_like(one)
            two[...] = jnp.zeros_like(two)

        off = (zc - base[:, :C_IN]) * spread(m[...], C_IN)
        one[:, :C_IN] += rows_sum(off)
        two[:, :C_IN] += rows_sum(off * off)
        off = (fc - jnp.tile(base[:, C_IN:], (1, ALPHA))) * spread(m[...], WIDE_FAST)
        one[:, C_IN:] += block_sum(rows_sum(off)) * 0.25
        two[:, C_IN:] += block_sum(rows_sum(off * off)) * 0.25

    @pl.when(i == high)
    def _():
        finish_moments(ex.part, base[...], one[...], two[...], high * here, ((0, C_IN + C_FAST, 0),))
        ex.meet()
        ex.send_near()

    @pl.when(i == high + 2)
    def _():
        ex.send_far()

    @pl.when(i >= high)
    def _():
        for w in range(cols):
            phases = dot(perm[...], fcot[:, w].reshape(ALPHA * slab, C_FAST)).astype(bf16)
            for p in range(ALPHA):
                fcot_out[w, :, p * C_FAST : (p + 1) * C_FAST] = 0.5 * phases[p * slab : (p + 1) * slab]

    @pl.when(i == 2 * high - 1)
    def _():
        ex.finish(mom_out, weight)


def fourth_pass(n_clip, clips, a2, zp, base, mom2, mom3, sgain, sshift, fends, cot, fcot, fast_in, m, perm, wc,
                wfc, weight, so, fo, gs, gf, tot, so_keep, fo_keep, sums, big, z_line, f_line, *refs):
    i = pl.program_id(0)
    high = pl.num_programs(0) // 2
    cols, slab, _ = a2.shape
    ex = Exchange(n_clip, False, refs)

    @pl.when(i == 0)
    def _():
        ex.signal()
        expand_matrix(wfc, big)
        sums[...] = jnp.zeros_like(sums)

    def tile_sum(v):
        return jnp.sum(v.reshape(slab // 8, 8, v.shape[-1]), axis=0)

    @pl.when(i < high)
    def _():
        mid, far = 2 * C_MID, 2 * C_MID + C_IN
        mean_c = mom3[0:1, :C_IN]
        scale_c = lax.rsqrt(mom3[1:2, :C_IN] + eps_norm)
        mean_p = mom2[0:1, MIX:] - base[...]
        scale_p = lax.rsqrt(mom2[1:2, MIX:] + eps_norm)
        mean_f = jnp.tile(mom3[0:1, C_IN:], (1, ALPHA))
        scale_f = jnp.tile(lax.rsqrt(mom3[1:2, C_IN:] + eps_norm), (1, ALPHA))
        mult_c = 0.5 * sgain[:, mid:far] * scale_c
        mult_p = 0.5 * sgain[:, far:] * scale_p
        shift_cp = 0.5 * (sshift[:, mid:far] + sshift[:, far:])
        mult_f = 0.5 * jnp.tile(fends[0], (1, ALPHA)) * scale_f
        shift_f = 0.5 * jnp.tile(fends[1], (1, ALPHA))

        def gate(v, g):
            u = 1.0 + jnp.tanh(v)
            o = v * u
            return o, g * (u + o * (2.0 - u))

        totals = [jnp.zeros((8, C_IN), f32)] * 3 + [jnp.zeros((8, WIDE_FAST), f32)] * 2
        rows = a2[...].reshape(cols * slab, MIX)
        z_line[...] = dot(rows[:, :C_MID], wc[...]).reshape(cols, slab, C_IN)
        f_line[...] = dot(rows[:, C_MID:], big[...]).reshape(cols, slab, WIDE_FAST)
        for w in range(cols):
            zc = z_line[w] - mean_c
            zq = zp[w].astype(f32) - mean_p
            res, back = gate(mult_c * zc + mult_p * zq + shift_cp, cot[w].astype(f32))
            so_keep[i, w] = res.astype(bf16)
            gs[w] = back
            totals[0] += tile_sum(back)
            totals[1] += tile_sum(back * zc)
            totals[2] += tile_sum(back * zq)
            fc = f_line[w] - mean_f
            res, fback = gate(mult_f * fc + shift_f + 0.5 * fast_in[w].astype(f32), fcot[w].astype(f32))
            fo_keep[i, w] = res.astype(bf16)
            gf[w] = fback
            totals[3] += tile_sum(fback)
            totals[4] += tile_sum(fback * fc)
        scales = (None, scale_c, scale_p)
        for k in range(3):
            total = jnp.sum(totals[k], axis=0, keepdims=True)
            sums[:, k * C_IN : (k + 1) * C_IN] += total if k == 0 else total * scales[k]
        for k in range(2):
            at = 3 * C_IN + k * C_FAST
            total = jnp.sum(totals[3 + k], axis=0, keepdims=True)
            sums[:, at : at + C_FAST] += block_sum(total if k == 0 else total * scale_f)

    @pl.when(i == high)
    def _():
        ex.part[...] = sums[...]
        ex.meet()
        ex.send_near()

    @pl.when(i == high + 2)
    def _():
        ex.send_far()

    @pl.when(i >= high)
    def _():
        mask = spread(m[...], C_IN).astype(bf16)
        for w in range(cols):
            so[:, w] = (so_keep[i - high, w] * mask).reshape(slab // clips, clips, C_IN)
            wide = fo_keep[i - high, w]
            stacked = jnp.concatenate([wide[:, p * C_FAST : (p + 1) * C_FAST] for p in range(ALPHA)], axis=0)
            fo[:, w] = dot_tn(perm[...], stacked).astype(bf16).reshape(clips, slab, C_FAST)

    @pl.when(i == 2 * high - 1)
    def _():
        ex.finish(tot, weight)


def fifth_pass(n_clip, gs, gf, a2, zp, base, z2, mom2, mom3, tot4, inv, sgain, fends, mids, m, wc, wfc, x, weight,
               dzp_out, q_out, tot, row, col, corner, w_out, wfc_out,
               dzc_keep, dzp_keep, dfc_keep, a_keep, sums, big, z_line, f_line, line, side, *refs):
    i = pl.program_id(0)
    high, cols, slab, _ = dzc_keep.shape
    n = high * cols
    rows = cols * slab
    ex = Exchange(n_clip, False, refs[:8], refs[8:])

    @pl.when(i == 0)
    def _():
        ex.signal()
        expand_matrix(wfc, big)
        sums[...] = jnp.zeros_like(sums)

    @pl.when(i < high)
    def _():
        mask = spread(m[...], C_IN)
        inv_s = spread(inv[...], C_IN)
        inv_f = 0.25 * inv[...]
        mean_c = mom3[0:1, :C_IN]
        scale_c = lax.rsqrt(mom3[1:2, :C_IN] + eps_norm)
        mean_p = mom2[0:1, MIX:] - base[...]
        scale_p = lax.rsqrt(mom2[1:2, MIX:] + eps_norm)
        mean_f = jnp.tile(mom3[0:1, C_IN:], (1, ALPHA))
        scale_f = jnp.tile(lax.rsqrt(mom3[1:2, C_IN:] + eps_norm), (1, ALPHA))
        mult_c = sgain[:, 2 * C_MID : 2 * C_MID + C_IN] * scale_c
        mult_p = sgain[:, 2 * C_MID + C_IN :] * scale_p
        mult_f = jnp.tile(fends[0], (1, ALPHA)) * scale_f
        first_s = tot4[:, :C_IN] * inv_s
        second_c = mult_c * scale_c * tot4[:, C_IN : 2 * C_IN] * inv_s
        second_p = mult_p * scale_p * tot4[:, 2 * C_IN : 3 * C_IN] * inv_s
        first_f = mult_f * jnp.tile(tot4[:, 3 * C_IN : 3 * C_IN + C_FAST] * inv_f, (1, ALPHA))
        second_f = mult_f * scale_f * jnp.tile(tot4[:, 3 * C_IN + C_FAST :] * inv_f, (1, ALPHA))
        first_c = mult_c * first_s - mean_c * second_c
        first_p = mult_p * first_s - mean_p * second_p
        first_f = first_f - mean_f * second_f
        mask_f = spread(m[...], WIDE_FAST)
        a_keep[i] = a2[...]
        flat = a2[...].reshape(rows, MIX)
        z_line[...] = dot(flat[:, :C_MID], wc[...]).reshape(cols, slab, C_IN)
        f_line[...] = dot(flat[:, C_MID:], big[...]).reshape(cols, slab, WIDE_FAST)
        for w in range(cols):
            zc = z_line[w]
            g = gs[w]
            dzc_keep[i, w] = (mult_c * g - mask * (first_c + zc * second_c)).astype(bf16)
            dzp = (mult_p * g - mask * (first_p + zp[w].astype(f32) * second_p)).astype(bf16)
            dzp_keep[i, w] = dzp
            dzp_out[w] = dzp
            fc = f_line[w]
            dfc_keep[i, w] = (mult_f * gf[w] - mask_f * (first_f + fc * second_f)).astype(bf16)
        da = dot_nt(dzc_keep[i].reshape(rows, C_IN), wc[...]).reshape(cols, slab, C_MID)
        df = dot_nt(dfc_keep[i].reshape(rows, WIDE_FAST), big[...]).reshape(cols, slab, 128)
        grads = jnp.concatenate([da, df], axis=2)
        slope_back(grads, z2[...], mom2, mids[2], mids[3], m, q_out, sums)
        keep_rims(ex, i, high, q_out, line, side)

    @pl.when(i == high)
    def _():
        ex.part[...] = sums[...]
        ex.meet()
        ex.send_near()
        ex.send_rims(line, side)

    @pl.when(i == high + 2)
    def _():
        ex.send_far()

    @pl.when(i >= high)
    def _():
        c = i - high
        got = dot_tn(x[...].reshape(n * slab, C_MID), dzp_keep[...].reshape(n * slab, C_IN)).astype(bf16)
        for b in range(C_IN // 256):
            at = pl.multiple_of(b * C_JOIN + c * C_MID, C_MID)
            w_out[pl.ds(at, C_MID), :] = got[:, b * 256 : (b + 1) * 256]

    @pl.when(i == pl.num_programs(0) - 1)
    def _():
        a = a_keep[...].reshape(n * slab, MIX)
        got = dot_tn(a[:, :C_MID], dzc_keep[...].reshape(n * slab, C_IN)).astype(bf16)
        for b in range(C_IN // 256):
            at = 4 * C_JOIN + b * C_MID
            w_out[at : at + C_MID, :] = got[:, b * 256 : (b + 1) * 256]
        wide = dot_tn(a[:, C_MID:], dfc_keep[...].reshape(n * slab, WIDE_FAST))
        wfc_out[...] = sum(
            wide[p * C_FMID : (p + 1) * C_FMID, p * C_FAST : (p + 1) * C_FAST] for p in range(ALPHA)
        )
        ex.finish(tot, weight)
        ex.finish_rims((row, col, corner))


def slope_back(grads, z, mom, gain, shift, m, q_out, sums):
    mean, scale, g, b = affine(mom, gain, shift, 0, MIX)
    zhat = (z - mean) * scale
    v = g * zhat + b
    sig = sigmoid(v)
    q = grads * (sig * (1.0 + v * (1.0 - sig)) * spread(m[...], MIX))
    q_out[...] = q
    for k, s in enumerate((rows_sum(q), rows_sum(q * zhat))):
        at = k * MIX
        sums[:, at : at + C_MID] += s[:, :C_MID]
        sums[:, at + C_MID : at + MIX] += phase_sum(s[:, C_MID:])


def norm_terms(mom, gain, tot, inv):
    mean = mom[0:1, :MIX]
    scale = lax.rsqrt(mom[1:2, :MIX] + eps_norm)
    share = jnp.concatenate([spread(inv[...], C_MID), 0.25 * inv[...]], axis=1)
    return mean, scale, gain * scale, tot[:, :MIX] * share, tot[:, MIX:] * share


def sixth_pass(n_clip, early_sizes, q2_hbm, z2_hbm, z1_hbm, a1_hbm, qrow, qcol, qcorner, zrow, zcol, zcorner, mom1, mom2, tot5, inv,
               mids, m, wb, wfb, weight, dwfc, w_hbm, q_hbm, tot, wb_out, kept_out,
               q_out, fast_sums, wide, q2, z2, z1, a1, q2_sem, z2_sem, z1_sem, a1_sem, sums, mine, land, *refs):
    i = pl.program_id(0)
    high, cols, slab, _ = z1.shape
    rows = cols * slab
    ex = Exchange(n_clip, False, refs[:8])
    early = Reducer(n_clip, early_sizes, mine, land, None, refs[8:10] + (None, None))
    end = early.stages - 1

    def fetch_w():
        return pltpu.make_async_copy(w_hbm, mine, a1_sem.at[1])

    def save_q():
        return pltpu.make_async_copy(q_out, q_hbm, a1_sem.at[2])

    moved = ((q2_hbm, q2, q2_sem), (z2_hbm, z2, z2_sem), (z1_hbm, z1, z1_sem))

    def fetch(k, h):
        a, b, s = moved[k]
        return pltpu.make_async_copy(a.at[h], b.at[h], s.at[h])

    def fetch_a1():
        return pltpu.make_async_copy(a1_hbm, a1, a1_sem.at[0])

    @pl.when(i == 0)
    def _():
        fetch_w().start()
        wb_out[9 * C_MID :, :] = jnp.zeros((wb_out.shape[0] - 9 * C_MID, 256), bf16)
        for h in range(high):
            fetch(0, h).start()
            fetch(1, h).start()
        for h in range(high):
            fetch(2, h).start()
        fetch_a1().start()
        ex.signal()
        mean, scale, mult, first, second = norm_terms(mom2, mids[2], tot5, inv)
        mask = spread(m[...], MIX)

        def grad(q, z):
            return (mult * (q - mask * (first + (z - mean) * scale * second))).astype(bf16)

        far = high + 1
        wide[far * ex.ha] = jnp.zeros((cols + 2, slab, MIX), bf16)
        wide[:, far * ex.wa] = jnp.zeros((high + 2, slab, MIX), bf16)
        wide[far * (1 - ex.ha), 1 : 1 + cols] = grad(qrow[...], zrow[...])
        wide[1 : 1 + high, far * (1 - ex.wa)] = grad(qcol[...], zcol[...])
        wide[far * (1 - ex.ha), far * (1 - ex.wa)] = grad(qcorner[...], zcorner[...])
        fetch_w().wait()
        ex.meet()
        early.send(0)

        def fill(h, carry):
            fetch(0, h).wait()
            fetch(1, h).wait()
            wide[h + 1, 1 : 1 + cols] = grad(q2[h], z2[h])
            return carry

        lax.fori_loop(0, high, fill, 0)
        sums[...] = jnp.zeros_like(sums)

        def space(h, carry):
            fetch(2, h).wait()
            slow = jnp.zeros((rows, C_MID), f32)
            fast = jnp.zeros((rows, 128), f32)
            for a in range(3):
                v = [wide[h + 2 - a, 2 - c : 2 - c + cols].reshape(rows, MIX) for c in range(3)]
                slow = slow + dot_nt(
                    jnp.concatenate([u[:, :C_MID] for u in v], axis=1),
                    jnp.concatenate([wb[a, c] for c in range(3)], axis=1),
                )
                fast = fast + dot_nt(
                    jnp.concatenate([u[:, C_MID:] for u in v], axis=1),
                    jnp.concatenate([wfb[3 * a + c] for c in range(3)], axis=1),
                )
            grads = jnp.concatenate([slow, fast], axis=1).reshape(cols, slab, MIX)
            slope_back(grads, z1[h], mom1, mids[0], mids[1], m, q_out.at[h], sums)
            return carry

        lax.fori_loop(0, 3, space, 0)
        early.gather(0)
        lax.fori_loop(3, high, space, 0)
        ex.part[...] = sums[...]
        ex.send_near()
        save_q().start()
        fetch_a1().wait()

    @pl.when(i == 3)
    def _():
        ex.send_far()

    @pl.when(i > 0)
    def _():
        tap = i - 1
        v = a1[pl.ds(tap // 3, high), pl.ds(lax.rem(tap, 3), cols)].reshape(high * rows, MIX)
        d = wide[1 : 1 + high, 1 : 1 + cols].reshape(high * rows, MIX)
        wb_out[pl.ds(pl.multiple_of(tap * C_MID, C_MID), C_MID), :] = dot_tn(v[:, :C_MID], d[:, :C_MID]).astype(bf16)
        both = dot_tn(v[:, C_MID:], d[:, C_MID:])
        fast_sums[tap] = sum(
            both[p * C_FMID : (p + 1) * C_FMID, p * C_FMID : (p + 1) * C_FMID] for p in range(ALPHA)
        )

    for k, step in ((1, 1), (2, 5), (3, 7)):

        @pl.when(i == step)
        def _():
            early.gather(k)

    @pl.when(i == 9)
    def _():
        ex.finish(tot, weight)
        for k in range(4, end + 1):
            early.gather(k)
        early.export(kept_out)
        save_q().wait()
        for q in range(10):
            r, c, width = small_place(q)
            wb_out[r : r + C_FMID, c : c + width] = (fast_sums[q] if q < 9 else dwfc[...]).astype(bf16)


def bit_of(axis, power):
    return lax.rem(lax.axis_index(axis) // (1 << power), 2)


def partner_of(axis, power):
    where = {name: lax.axis_index(name) for name in ("clip", "ha", "wa")}
    where[axis] = where[axis] + (1 - 2 * bit_of(axis, power)) * (1 << power)
    return (where["clip"], where["ha"], where["wa"])


def stage_orders(n_clip, sets):
    rest = [("wa", 0)] + [("clip", b) for b in range(n_clip.bit_length() - 1)]
    turn, last = rest[:3], rest[3:]
    return [[("ha", 0)] + turn[s % len(turn) :] + turn[: s % len(turn)] + last for s in range(sets)]


def chunk_of(rows):
    return max(k for k in range(16, min(rows, 256) + 1, 16) if rows % k == 0)


class Reducer:
    def __init__(self, n_clip, sizes, mine, land, done, sems):
        self.mine, self.land, self.done = mine, land, done
        self.rs_sent, self.rs_came, self.ag_sent, self.ag_came = sems
        self.sets = range(len(sizes))
        self.orders = stage_orders(n_clip, len(sizes))
        self.stages = len(self.orders[0])
        self.plan, self.starts, self.kept = Reducer.layout(n_clip, sizes)

    @staticmethod
    def layout(n_clip, sizes):
        stages = len(stage_orders(n_clip, 1)[0])
        plan, starts, kept = [], [], []
        start = land = 0
        for size in sizes:
            starts.append(start)
            start += size
            row = []
            for _ in range(stages):
                halve = size % 32 == 0
                size = size // 2 if halve else size
                row.append((halve, size, land))
                land += size
            plan.append(row)
            kept.append(size)
        return plan, starts, kept

    @staticmethod
    def scratch(n_clip, sizes):
        plan = Reducer.layout(n_clip, sizes)[0]
        last = plan[-1][-1]
        return pltpu.VMEM((last[1] + last[2], 256), bf16)

    @staticmethod
    def sems(n_clip, sizes, count=4):
        stages = len(stage_orders(n_clip, 1)[0])
        return [pltpu.SemaphoreType.DMA((len(sizes), stages)) for _ in range(count)]

    def low(self, s, k):
        low = jnp.int32(self.starts[s])
        for j in range(k):
            halve, count, _ = self.plan[s][j]
            if halve:
                low = low + bit_of(*self.orders[s][j]) * count
        return low

    @staticmethod
    def rows(ref, begin, count):
        return ref.at[pl.ds(pl.multiple_of(begin, 16), count)]

    def scatter_copy(self, s, k):
        halve, count, land = self.plan[s][k]
        axis, power = self.orders[s][k]
        begin = self.low(s, k)
        if halve:
            begin = begin + (1 - bit_of(axis, power)) * count
        return pltpu.make_async_remote_copy(
            src_ref=self.rows(self.mine, begin, count), dst_ref=self.rows(self.land, land, count),
            send_sem=self.rs_sent.at[s, k], recv_sem=self.rs_came.at[s, k],
            device_id=partner_of(axis, power), device_id_type=MESH,
        )

    def send(self, k):
        for s in self.sets:
            self.scatter_copy(s, k).start()

    def gather(self, k):
        for s in self.sets:
            halve, count, land = self.plan[s][k]
            copy = self.scatter_copy(s, k)
            copy.wait_recv()
            copy.wait_send()
            begin = self.low(s, k + 1)
            step = chunk_of(count)

            def add(i, carry):
                own = pl.ds(pl.multiple_of(begin + i * step, 16), step)
                came = pl.ds(pl.multiple_of(land + i * step, 16), step)
                self.mine[own, :] = (self.mine[own, :].astype(f32) + self.land[came, :].astype(f32)).astype(bf16)
                return carry

            lax.fori_loop(0, count // step, add, 0)
            if k + 1 < self.stages:
                self.scatter_copy(s, k + 1).start()

    def export(self, out):
        at = 0
        for s in self.sets:
            count = self.kept[s]
            out[at : at + count] = self.mine[pl.ds(pl.multiple_of(self.low(s, self.stages), 16), count), :]
            at += count

    def load(self, kept):
        at = 0
        for s in self.sets:
            count = self.kept[s]
            self.done[pl.ds(pl.multiple_of(self.low(s, self.stages), 16), count), :] = kept[at : at + count]
            at += count

    def keep(self):
        for s in self.sets:
            own = pl.ds(pl.multiple_of(self.low(s, self.stages), 16), self.kept[s])
            self.done[own, :] = self.mine[own, :]

    def regain(self):
        self.keep()
        self.spread(self.stages - 1)

    def gather_copy(self, s, k, other):
        halve, count, _ = self.plan[s][k]
        axis, power = self.orders[s][k]
        bit = bit_of(axis, power)
        begin = self.low(s, k) + ((1 - bit) if other else bit) * count
        return pltpu.make_async_remote_copy(
            src_ref=self.rows(self.done, begin, count), dst_ref=self.rows(self.done, begin, count),
            send_sem=self.ag_sent.at[s, k], recv_sem=self.ag_came.at[s, k],
            device_id=partner_of(axis, power), device_id_type=MESH,
        )

    def spread(self, k):
        for s in self.sets:
            if self.plan[s][k][0]:
                self.gather_copy(s, k, False).start()

    def take(self, k):
        for s in self.sets:
            if self.plan[s][k][0]:
                self.gather_copy(s, k, True).wait_recv()
                self.gather_copy(s, k, False).wait_send()
            if k > 0 and self.plan[s][k - 1][0]:
                self.gather_copy(s, k - 1, False).start()


SPACE_STEPS = (5, 9, 12, 15, 18, 18, 18, 18, 18, 18, 18)
FIRST_STEPS = (5, 9, 12, 15, 18)
HALF_STEPS = (12, 15, 17, 18, 18, 18, 18, 18, 18, 18, 18)
LATE_STEPS = (15, 17, 18, 18, 18, 18, 18, 18, 18, 18, 18)


def seventh_pass(clips, n_clip, early_sizes, space_sizes, half_sizes, late_sizes, q1, z1, dzp, gf, x, f_hbm, kept, space_hbm, mom1, tot6, inv,
                 mids, m, perm, wl, wa_hbm, wp_hbm, wfa, sx, fx, out1, out_b, out_h, out_a,
                 wa, wp, f, done1, done_b, done_h, done_a, da, dl, df, taps, ends, mine_b, land_b, mine_h, land_h, mine_a, land_a, load_sem, *sems):
    i = pl.program_id(0)
    cols, slab, _ = q1.shape
    high = da.shape[0]
    rows = cols * slab
    every = high * rows
    steps = C_JOIN // C_MID
    late = high + steps
    sems = iter(sems)
    first = Reducer(n_clip, early_sizes, None, None, done1, (None, None, next(sems), next(sems)))
    space = Reducer(n_clip, space_sizes, mine_b, land_b, done_b, [next(sems) for _ in range(4)])
    half = Reducer(n_clip, half_sizes, mine_h, land_h, done_h, [next(sems) for _ in range(4)])
    last = Reducer(n_clip, late_sizes, mine_a, land_a, done_a, [next(sems) for _ in range(4)])
    end = last.stages - 1

    def fetch_f():
        return pltpu.make_async_copy(f_hbm, f, load_sem.at[4])

    def fetch_weight(k):
        source, target = ((wp_hbm, wp), (wa_hbm, wa))[k]
        return pltpu.make_async_copy(source, target, load_sem.at[5 + k])

    @pl.when(i == 0)
    def _():
        load = pltpu.make_async_copy(space_hbm, mine_b, load_sem.at[0])
        load.start()
        fetch_weight(0).start()
        fetch_weight(1).start()
        fetch_f().start()
        greet_signal(n_clip)
        frames_matrix(wfa, taps, ends)
        first.load(kept)
        greet_wait(n_clip)
        first.spread(end)
        load.wait()
        space.send(0)
        fetch_weight(0).wait()
        fetch_weight(1).wait()

    plan, rest = {}, []
    final = pl.num_programs(0) - 1

    def book(ops, steps):
        left = []
        for j, op in enumerate(ops):
            step = steps[j * len(steps) // len(ops)]
            if step >= 2 * high + C_JOIN // C_MID - 1:
                left.append(op)
            else:
                plan.setdefault(step, []).append(op)
        rest.append(left)

    down, up = range(end + 1), range(end, -1, -1)
    book(
        [functools.partial(space.gather, k) for k in down] + [space.regain]
        + [functools.partial(space.take, k) for k in up], SPACE_STEPS,
    )
    book([functools.partial(first.take, k) for k in up], FIRST_STEPS)
    book(
        [functools.partial(half.gather, k) for k in down] + [half.regain]
        + [functools.partial(half.take, k) for k in up], HALF_STEPS,
    )
    book(
        [functools.partial(last.gather, k) for k in down] + [last.regain]
        + [functools.partial(last.take, k) for k in up], LATE_STEPS,
    )
    for step, ops in sorted(plan.items()):

        @pl.when(i == step)
        def _():
            for op in ops:
                op()

    @pl.when(i < high)
    def _():
        mean, scale, mult, one, two = norm_terms(mom1, mids[0], tot6, inv)
        zhat = (z1[...] - mean) * scale
        dz = mult * (q1[...] - spread(m[...], MIX) * (one + zhat * two))
        up, down = sooner(dz, clips), later(dz, clips)
        for k, v in enumerate((up, dz, down)):
            da[i, :, :, k * C_MID : (k + 1) * C_MID] = v[:, :, :C_MID].astype(bf16)
            df[i, :, :, k * 128 : (k + 1) * 128] = v[:, :, C_MID:].astype(bf16)
        dlat = dot_nt(
            jnp.concatenate([dzp[...].reshape(rows, C_IN), da[i].reshape(rows, 3 * C_MID)], axis=1),
            jnp.concatenate([wp[C_IN:]] + [wa[k, C_IN:] for k in range(3)], axis=1),
        )
        dlat = dlat.astype(bf16).astype(f32).reshape(cols, slab, C_LAT)
        dl[i, :, :, :C_LAT] = dlat.astype(bf16)
        dl[i, :, :, C_LAT:] = sooner(dlat, clips).astype(bf16)

    @pl.when((i >= high) & (i < late))
    def _():
        c = i - high
        got = dot_tn(x[...].reshape(every, C_MID), da[...].reshape(every, 3 * C_MID)).astype(bf16)

        @pl.when(c < 2)
        def _():
            for k in range(3):
                mine_h[pl.ds(pl.multiple_of((2 * k + c) * C_MID, C_MID), C_MID), :] = got[:, k * C_MID : (k + 1) * C_MID]

        @pl.when(c >= 2)
        def _():
            for k in range(3):
                at = pl.multiple_of((3 * k + c - 2) * C_MID, C_MID)
                mine_a[pl.ds(at, C_MID), :] = got[:, k * C_MID : (k + 1) * C_MID]

        @pl.when(c == 1)
        def _():
            half.send(0)

    @pl.when(i == late - 1)
    def _():
        fetch_f().wait()
        fast = f[...].reshape(every, WIDE_FAST)
        d = dl[...].reshape(every, 2 * C_LAT)
        at = 9 * C_MID
        mine_a[at + 2 * C_FAST : at + 5 * C_FAST, :] = dot_tn(fast[:, : 3 * C_FAST], d[:, :C_LAT]).astype(bf16)
        mine_a[at : at + 2 * C_FAST, :] = dot_tn(fast[:, 2 * C_FAST :], d[:, C_LAT:]).astype(bf16)
        at += 5 * C_FAST
        g = df[...].reshape(every, 3 * 128)
        mid = dot_tn(g[:, 128:256], fast)
        sums = [jnp.zeros((C_FMID, C_FAST), f32) for _ in range(3)]
        for p in range(ALPHA):
            for s in range(max(p - 1, 0), min(p + 2, ALPHA)):
                sums[s - p + 1] += mid[p * C_FMID : (p + 1) * C_FMID, s * C_FAST : (s + 1) * C_FAST]
        sums[0] += dot_tn(g[:, :128], fast[:, 3 * C_FAST :])[:C_FMID]
        sums[2] += dot_tn(g[:, 256:], fast[:, :C_FAST])[3 * C_FMID :]
        mine_a[at:, :] = jnp.zeros((mine_a.shape[0] - at, 256), bf16)
        for q in range(3):
            mine_a[at + q * C_FMID : at + (q + 1) * C_FMID, :C_FAST] = sums[q].astype(bf16)
        last.send(0)

    @pl.when(i >= late)
    def _():
        h = i - late
        dj = dot_nt(
            jnp.concatenate([dzp[...].reshape(rows, C_IN), da[h].reshape(rows, 3 * C_MID)], axis=1),
            jnp.concatenate([wp[:C_IN]] + [wa[k, :C_IN] for k in range(3)], axis=1),
        )
        mask = spread(m[...], C_IN)
        dj = dj.reshape(cols, slab, C_IN)
        for w in range(cols):
            sx[:, w] = (dj[w] * mask).astype(bf16).reshape(slab // clips, clips, C_IN)
        g = df[h].reshape(rows, 3 * 128)
        d = dl[h].reshape(rows, 2 * C_LAT)
        total = gf[...].reshape(rows, WIDE_FAST) + dot(g[:, 128:256], taps[...])
        head = dot_nt(d[:, :C_LAT], wl[2:5].reshape(3 * C_FAST, C_LAT))
        tail = dot_nt(d[:, C_LAT:], wl[0:2].reshape(2 * C_FAST, C_LAT))
        blocks = [total[:, p * C_FAST : (p + 1) * C_FAST] for p in range(ALPHA)]
        for p in range(3):
            blocks[p] = blocks[p] + head[:, p * C_FAST : (p + 1) * C_FAST]
        for p in range(2):
            blocks[2 + p] = blocks[2 + p] + tail[:, p * C_FAST : (p + 1) * C_FAST]
        blocks[3] = blocks[3] + dot(g[:, :128], ends[0])
        blocks[0] = blocks[0] + dot(g[:, 256:], ends[1])
        blocks = [v.astype(bf16) for v in blocks]
        for w in range(cols):
            stacked = jnp.concatenate([v[w * slab : (w + 1) * slab] for v in blocks], axis=0)
            fx[:, w] = dot_tn(perm[...], stacked).astype(bf16).reshape(clips, slab, C_FAST)

    @pl.when(i == final)
    def _():
        for k in range(max(len(left) for left in rest)):
            for left in rest:
                if k < len(left):
                    left[k]()
        saves = [
            pltpu.make_async_copy(a, b, load_sem.at[k])
            for k, (a, b) in enumerate(((done1, out1), (done_b, out_b), (done_h, out_h), (done_a, out_a)))
        ]
        for save in saves:
            save.start()
        for save in saves:
            save.wait()


def small_place(q):
    return 9 * C_MID + (q % 5) * C_FMID, (q // 5) * 128, C_FMID if q < 9 else C_FAST


def greet_signal(n_clip):
    barrier = pltpu.get_barrier_semaphore()
    for axis, power in stage_orders(n_clip, 1)[0]:
        pl.semaphore_signal(barrier, inc=1, device_id=partner_of(axis, power), device_id_type=MESH)


def greet_wait(n_clip):
    pl.semaphore_wait(pltpu.get_barrier_semaphore(), len(stage_orders(n_clip, 1)[0]))


def finish_outputs(so, fo, sx, fx, in1, in_b, in_h, in_a, tot4, tot5, tot6, so_out, fo_out, sx_out, fx_out,
                   wp_hbm, wc_hbm, wb_hbm, wa_hbm, wl_hbm, wfa_out, wfc_out, wfb_out, sgain_out, sshift_out, fgain_out,
                   fshift_out, wp, wc, wb, wa, wl, done1, done_b, done_h, done_a, sem, in_sem):
    i = pl.program_id(0)
    moves = ((wp, wp_hbm), (wc, wc_hbm), (wb, wb_hbm), (wa, wa_hbm), (wl, wl_hbm))

    loads = ((in1, done1), (in_b, done_b), (in_h, done_h), (in_a, done_a))

    def move(k):
        return pltpu.make_async_copy(moves[k][0], moves[k][1], sem.at[k])

    def load(k):
        return pltpu.make_async_copy(loads[k][0], loads[k][1], in_sem.at[k])

    @pl.when(i == 0)
    def _():
        for k in range(4):
            load(k).start()

    @pl.when(i == 1)
    def _():
        load(0).wait()
        for b in range(C_IN // 256):
            wp[:, b * 256 : (b + 1) * 256] = done1[b * C_JOIN : (b + 1) * C_JOIN, :].astype(f32)
        move(0).start()
        for b in range(C_IN // 256):
            at = 4 * C_JOIN + b * C_MID
            wc[:, b * 256 : (b + 1) * 256] = done1[at : at + C_MID, :].astype(f32)
        move(1).start()

    @pl.when(i == 2)
    def _():
        load(1).wait()
        for t in range(9):
            wb[t // 3, t % 3] = done_b[t * C_MID : (t + 1) * C_MID, :].astype(f32)
        move(2).start()

    @pl.when(i == 3)
    def _():
        load(2).wait()
        load(3).wait()
        for k in range(3):
            wa[k, : 2 * C_MID] = done_h[2 * k * C_MID : 2 * (k + 1) * C_MID, :].astype(f32)
            wa[k, 2 * C_MID :] = done_a[3 * k * C_MID : 3 * (k + 1) * C_MID, :].astype(f32)
        move(3).start()
        at = 9 * C_MID
        for k in range(5):
            wl[k] = done_a[at + k * C_FAST : at + (k + 1) * C_FAST, :].astype(f32)
        move(4).start()

    @pl.when(i == 4)
    def _():
        at = 9 * C_MID + 5 * C_FAST
        for q in range(3):
            wfa_out[q] = done_a[at + q * C_FMID : at + (q + 1) * C_FMID, :C_FAST].astype(f32)
        for q in range(10):
            r, c, width = small_place(q)
            piece = done_b[r : r + C_FMID, c : c + width].astype(f32)
            if q < 9:
                wfb_out[q] = piece
            else:
                wfc_out[...] = piece
        lane = lax.broadcasted_iota(jnp.int32, (1, 128), 1)
        for k, slow, fast in ((0, sshift_out, fshift_out), (1, sgain_out, fgain_out)):
            at = k * MIX
            row = 0
            for source, begin, width in (
                (tot6, at, C_MID), (tot5, at, C_MID), (tot4, k * C_IN, C_IN), (tot4, 2 * k * C_IN, C_IN)
            ):
                for c in range(begin, begin + width, 128):
                    slow[row : row + 1] = source[:, c : c + 128]
                    row += 1
            c = pltpu.roll(tot4[:, 3 * C_IN + k * C_FAST : 3 * C_IN + (k + 1) * C_FAST], 2 * C_FMID, 1)
            a, b = tot6[:, at + C_MID : at + MIX], tot5[:, at + C_MID : at + MIX]
            fast[:, :128] = jnp.where(lane < C_FMID, a, jnp.where(lane < 2 * C_FMID, b, c))
            fast[:, 128:] = c[:, : 2 * C_FMID]

    so_out[...] = so[...]
    fo_out[...] = fo[...]
    sx_out[...] = sx[...]
    fx_out[...] = fx[...]

    @pl.when(i == pl.num_programs(0) - 1)
    def _():
        for k in range(5):
            move(k).wait()


def prepare(clips, n_clip, counts, sgain_rows, sshift_rows, fgain, fshift, wb, m, perm, weight, inv, mids, last, wide,
            sgain, sshift):
    for k in range(sgain_rows.shape[0]):
        sgain[:, k * 128 : (k + 1) * 128] = sgain_rows[k : k + 1]
        sshift[:, k * 128 : (k + 1) * 128] = sshift_rows[k : k + 1]
    slab = m.shape[0]
    frames = slab // clips
    me = lax.axis_index("clip") * clips
    shift = clips.bit_length() - 1

    def real(shape):
        r = lax.broadcasted_iota(jnp.int32, shape, 0)
        own = jnp.zeros(shape, jnp.int32)
        for c in range(clips):
            own = jnp.where((r & (clips - 1)) == c, counts[me + c], own)
        return r, (r >> shift) < own

    m[...] = real(m.shape)[1].astype(f32)
    width = perm.shape[1]
    r, there = real((slab, width))
    col = lax.broadcasted_iota(jnp.int32, (slab, width), 1)
    for p in range(ALPHA):
        want = (r & (clips - 1)) * (ALPHA * frames) + ALPHA * (r >> shift) + p
        perm[p * slab : (p + 1) * slab] = ((want == col) & there).astype(f32).astype(bf16)
    groups = []
    for g in range(n_clip):
        part = counts[g * clips]
        for c in range(1, clips):
            part = part + counts[g * clips + c]
        groups.append(part)
    total = groups[0]
    for part in groups[1:]:
        total = total + part
    whole_count = jnp.full((1, 128), total, jnp.int32).astype(f32)
    inv[...] = 1.0 / (whole_count * (H * W))
    for g in range(n_clip):
        weight[g] = jnp.full((1, 128), groups[g], jnp.int32).astype(f32) / whole_count
    lane = lax.broadcasted_iota(jnp.int32, (1, 128), 1)
    for k in range(2):
        for j, (slow, fast) in enumerate(((sgain, fgain), (sshift, fshift))):
            mine = (lane >= k * C_FMID) & (lane < (k + 1) * C_FMID)
            mids[2 * k + j, :, :C_MID] = slow[:, k * C_MID : (k + 1) * C_MID]
            mids[2 * k + j, :, C_MID:] = phase_sum(jnp.where(mine, fast[:, :128], 0.0))
    for j, fast in enumerate((fgain, fshift)):
        last[j] = fast[:, 2 * C_FMID :]
    for t in range(9):
        w = wb[t]
        for p in range(ALPHA):
            parts = [jnp.zeros((C_FMID, C_FMID), bf16)] * ALPHA
            parts[p] = w
            wide[t, p * C_FMID : (p + 1) * C_FMID] = jnp.concatenate(parts, axis=1)


def vmem_spec():
    return pl.BlockSpec(memory_space=pltpu.VMEM)


def shaped(shape, kind):
    return jax.ShapeDtypeStruct(shape, kind)


def whole(shape):
    return pl.BlockSpec(shape, lambda h: (0,) * len(shape))


def per_line(shape):
    return pl.BlockSpec((None,) + tuple(shape), lambda h: (h,) + (0,) * len(shape))


def params(limit):
    return pltpu.CompilerParams(vmem_limit_bytes=60 * MIB)


def on_device(
    slow_input,
    fast_input,
    frame_counts,
    lateral_weight,
    slow_a_weight,
    slow_b_weight,
    slow_c_weight,
    slow_proj_weight,
    fast_a_weight,
    fast_b_weight,
    fast_c_weight,
    slow_gain,
    slow_shift,
    fast_gain,
    fast_shift,
    slow_cotangent,
    fast_cotangent,
):
    n_clip = lax.axis_size("clip")
    clips, frames, high, cols, _ = slow_input.shape
    slab = clips * frames
    lanes = slow_gain.reshape(-1, 128), slow_shift.reshape(-1, 128)
    slow_row = shaped((1, slow_gain.shape[0]), f32)
    vm = vmem_spec()
    m, perm, weight, inv, mids, ends, wfb, sgain, sshift = pl.pallas_call(
        functools.partial(prepare, clips, n_clip),
        in_specs=[pl.BlockSpec(memory_space=pltpu.SMEM)] + [vm] * 5,
        out_specs=(vm,) * 9,
        out_shape=(
            shaped((slab, 128), f32), shaped((ALPHA * slab, ALPHA * slab), bf16), shaped((n_clip, 1, 128), f32),
            shaped((1, 128), f32), shaped((4, 1, MIX), f32), shaped((2, 1, C_FAST), f32), shaped((9, 128, 128), bf16),
            slow_row, slow_row,
        ),
        compiler_params=params(60),
        name="prepare",
    )(frame_counts, *lanes, fast_gain[None], fast_shift[None], fast_b_weight.reshape(9, C_FMID, C_FMID))
    wfa = fast_a_weight.transpose(0, 2, 1)
    xs = slow_input.transpose(1, 2, 3, 0, 4)
    xf = fast_input.transpose(0, 2, 3, 1, 4)
    cot = slow_cotangent.transpose(1, 2, 3, 0, 4)
    fcot = fast_cotangent.transpose(0, 2, 3, 1, 4)
    def lines(c, kind):
        return shaped((high, cols, slab, c), kind)

    m_spec = whole((slab, 128))
    vm = vmem_spec()
    hbm = pl.BlockSpec(memory_space=pl.ANY)

    def early_line(shape):
        return pl.BlockSpec((None,) + tuple(shape), lambda i: (jnp.minimum(i, high - 1),) + (0,) * len(shape))

    def late_line(shape, begin):
        return pl.BlockSpec((None,) + tuple(shape), lambda i: (jnp.maximum(i - begin, 0),) + (0,) * len(shape))

    def slow_block(index):
        return pl.BlockSpec((frames, None, cols, clips, C_IN), lambda i: (0, index(i), 0, 0, 0))

    def fast_block(index):
        return pl.BlockSpec((clips, None, cols, ALPHA * frames, C_FAST), lambda i: (0, index(i), 0, 0, 0))

    def early(i):
        return jnp.minimum(i, high - 1)

    def after(begin):
        return lambda i: jnp.maximum(i - begin, 0)

    def remote(ident):
        return pltpu.CompilerParams(collective_id=ident, has_side_effects=True, vmem_limit_bytes=60 * MIB)

    rim_shapes = (shaped((cols, slab, MIX), f32), shaped((high, slab, MIX), f32), shaped((slab, MIX), f32))
    edge_scratch = [pltpu.VMEM((cols, slab, MIX), f32), pltpu.VMEM((high, slab, MIX), f32)]
    rims = rim_scratch(cols, slab)
    L1 = MIX + C_IN
    x, f, z1, zp, stp, base, mom1, row1, col1, corner1 = pl.pallas_call(
        functools.partial(first_pass, clips, n_clip),
        grid=(2 * high,),
        in_specs=[slow_block(early), fast_block(early)] + [vm] * 4 + [hbm] + [vm] * 2,
        out_specs=(
            early_line((cols, slab, C_JOIN)), early_line((cols, slab, WIDE_FAST)), early_line((cols, slab, MIX)),
            late_line((cols, slab, C_IN), high), vm, vm, vm, vm, vm, vm,
        ),
        out_shape=(
            lines(C_JOIN, bf16), lines(WIDE_FAST, bf16), lines(MIX, f32), lines(C_IN, bf16), shaped((2, C_IN), f32),
            shaped((1, C_IN), f32), shaped((2, MIX), f32),
        ) + rim_shapes,
        scratch_shapes=[
            pltpu.VMEM((C_JOIN, C_IN), bf16), pltpu.SemaphoreType.DMA((1,)),
            pltpu.VMEM((high, cols, slab, C_JOIN), bf16), pltpu.VMEM((128, WIDE_FAST), bf16),
            pltpu.VMEM((2, 128, C_FAST), bf16), pltpu.VMEM((1, L1), f32), pltpu.VMEM((1, L1), f32),
            pltpu.VMEM((1, L1), f32),
        ] + edge_scratch + exchange_scratch(n_clip, 2, MIX) + rims,
        compiler_params=remote(1),
        name="first_pass",
    )(xs, xf, m, perm, lateral_weight, slow_a_weight, slow_proj_weight, wfa, weight)

    a1, z2, mom2, zrow, zcol, zcorner, cot = pl.pallas_call(
        functools.partial(second_pass, n_clip),
        grid=(high + 1,),
        in_specs=[hbm] + [vm] * 10 + [slow_block(after(1))],
        out_specs=(hbm, hbm, vm, vm, vm, vm, late_line((cols, slab, C_IN), 1)),
        out_shape=(
            shaped((high + 2, cols + 2, slab, MIX), bf16), lines(MIX, f32), shaped((2, L1), f32),
        ) + rim_shapes + (lines(C_IN, bf16),),
        scratch_shapes=[
            pltpu.VMEM((high + 2, cols + 2, slab, MIX), bf16), pltpu.VMEM((high, cols, slab, MIX), f32),
            pltpu.SemaphoreType.DMA((2,)),
            pltpu.VMEM((high, cols, slab, MIX), f32), pltpu.SemaphoreType.DMA((high,)), pltpu.VMEM((1, MIX), f32),
            pltpu.VMEM((1, MIX), f32),
        ] + exchange_scratch(n_clip, 2, L1) + rims,
        compiler_params=remote(2),
        name="second_pass",
    )(z1, row1, col1, corner1, mom1, mids, m, slow_b_weight, wfb, stp, weight, cot)

    L3 = C_IN + C_FAST
    a2, mom3, fcot = pl.pallas_call(
        functools.partial(third_pass, n_clip),
        grid=(2 * high,),
        in_specs=[early_line((cols, slab, MIX))] + [vm] * 6 + [fast_block(after(high)), vm],
        out_specs=(early_line((cols, slab, MIX)), vm, late_line((cols, slab, WIDE_FAST), high)),
        out_shape=(lines(MIX, bf16), shaped((2, L3), f32), lines(WIDE_FAST, bf16)),
        scratch_shapes=[pltpu.VMEM((128, WIDE_FAST), bf16)] + [pltpu.VMEM((1, L3), f32)] * 3
        + exchange_scratch(n_clip, 2, L3),
        compiler_params=remote(3),
        name="third_pass",
    )(z2, mom2, mids, m, slow_c_weight, fast_c_weight, weight, fcot, perm)

    L4 = 3 * C_IN + 2 * C_FAST
    so, fo, gs, gf, tot4 = pl.pallas_call(
        functools.partial(fourth_pass, n_clip, clips),
        grid=(2 * high,),
        in_specs=[early_line((cols, slab, MIX)), early_line((cols, slab, C_IN))] + [vm] * 6 + [
            early_line((cols, slab, C_IN)), early_line((cols, slab, WIDE_FAST)), early_line((cols, slab, WIDE_FAST)),
        ] + [vm] * 5,
        out_specs=(
            slow_block(after(high)), fast_block(after(high)), early_line((cols, slab, C_IN)),
            early_line((cols, slab, WIDE_FAST)), vm,
        ),
        out_shape=(
            shaped(xs.shape, bf16), shaped(xf.shape, bf16), lines(C_IN, f32), lines(WIDE_FAST, f32),
            shaped((1, L4), f32),
        ),
        scratch_shapes=[
            pltpu.VMEM((high, cols, slab, C_IN), bf16), pltpu.VMEM((high, cols, slab, WIDE_FAST), bf16),
            pltpu.VMEM((1, L4), f32), pltpu.VMEM((128, WIDE_FAST), bf16), pltpu.VMEM((cols, slab, C_IN), f32),
            pltpu.VMEM((cols, slab, WIDE_FAST), f32),
        ] + exchange_scratch(n_clip, 1, L4),
        compiler_params=remote(4),
        name="fourth_pass",
    )(
        a2, zp, base, mom2, mom3, sgain, sshift, ends, cot, fcot, f, m, perm, slow_c_weight, fast_c_weight, weight,
    )

    n = high * cols
    early_sizes = (2048, 2048, 2048)
    space_sizes = (1024, 1024, 512)
    half_sizes = (512, 512, 512)
    late_sizes = (1024, 1024, 1024)

    def flat(v):
        return v.reshape((n,) + v.shape[2:])

    steps = C_JOIN // C_MID
    dzp, q2, tot5, qrow, qcol, qcorner, dw1, dwfc = pl.pallas_call(
        functools.partial(fifth_pass, n_clip),
        grid=(high + steps,),
        in_specs=[
            early_line((cols, slab, C_IN)), early_line((cols, slab, WIDE_FAST)), early_line((cols, slab, MIX)),
            early_line((cols, slab, C_IN)), vm, early_line((cols, slab, MIX)),
        ] + [vm] * 10 + [pl.BlockSpec((n, slab, C_MID), lambda i: (0, 0, jnp.clip(i - high, 0, steps - 1))), vm],
        out_specs=(
            early_line((cols, slab, C_IN)), early_line((cols, slab, MIX)), vm, vm, vm, vm, vm, vm,
        ),
        out_shape=(lines(C_IN, bf16), lines(MIX, f32), shaped((1, 2 * MIX), f32)) + rim_shapes + (
            shaped((sum(early_sizes), 256), bf16), shaped((C_FMID, C_FAST), f32),
        ),
        scratch_shapes=[
            pltpu.VMEM((high, cols, slab, C_IN), bf16), pltpu.VMEM((high, cols, slab, C_IN), bf16),
            pltpu.VMEM((high, cols, slab, WIDE_FAST), bf16), pltpu.VMEM((high, cols, slab, MIX), bf16),
            pltpu.VMEM((1, 2 * MIX), f32), pltpu.VMEM((128, WIDE_FAST), bf16), pltpu.VMEM((cols, slab, C_IN), f32),
            pltpu.VMEM((cols, slab, WIDE_FAST), f32),
        ] + edge_scratch + exchange_scratch(n_clip, 1, 2 * MIX) + rims,
        compiler_params=remote(5),
        name="fifth_pass",
    )(
        gs, gf, a2, zp, base, z2, mom2, mom3, tot4, inv, sgain, ends, mids, m, slow_c_weight, fast_c_weight,
        flat(x), weight,
    )

    q1, tot6, dwb, kept = pl.pallas_call(
        functools.partial(sixth_pass, n_clip, early_sizes),
        grid=(10,),
        in_specs=[hbm] * 4 + [vm] * 16 + [hbm],
        out_specs=(hbm,) + (vm,) * 3,
        out_shape=(
            lines(MIX, f32), shaped((1, 2 * MIX), f32), shaped((sum(space_sizes), 256), bf16),
            shaped((sum(Reducer.layout(n_clip, early_sizes)[2]), 256), bf16),
        ),
        scratch_shapes=[
            pltpu.VMEM((high, cols, slab, MIX), f32), pltpu.VMEM((9, C_FMID, C_FMID), f32),
            pltpu.VMEM((high + 2, cols + 2, slab, MIX), bf16),
        ]
        + [pltpu.VMEM((high, cols, slab, MIX), f32)] * 3
        + [pltpu.VMEM((high + 2, cols + 2, slab, MIX), bf16)]
        + [pltpu.SemaphoreType.DMA((high,))] * 3
        + [pltpu.SemaphoreType.DMA((3,)), pltpu.VMEM((1, 2 * MIX), f32)]
        + [pltpu.VMEM((sum(early_sizes), 256), bf16), Reducer.scratch(n_clip, early_sizes)]
        + exchange_scratch(n_clip, 1, 2 * MIX) + Reducer.sems(n_clip, early_sizes, 2),
        compiler_params=remote(6),
        name="sixth_pass",
    )(
        q2, z2, z1, a1, qrow, qcol, qcorner, zrow, zcol, zcorner, mom1, mom2, tot5, inv, mids, m,
        slow_b_weight, wfb, weight, dwfc, dw1,
    )

    def twice_line(shape):
        begin = high + steps
        return pl.BlockSpec(
            (None,) + tuple(shape),
            lambda i: (jnp.where(i < begin, jnp.minimum(i, high - 1), i - begin),) + (0,) * len(shape),
        )

    sx, fx, done1, done_b, done_h, done_a = pl.pallas_call(
        functools.partial(seventh_pass, clips, n_clip, early_sizes, space_sizes, half_sizes, late_sizes),
        grid=(2 * high + steps,),
        in_specs=[
            early_line((cols, slab, MIX)), early_line((cols, slab, MIX)), twice_line((cols, slab, C_IN)),
            late_line((cols, slab, WIDE_FAST), high + steps),
            pl.BlockSpec((n, slab, C_MID), lambda i: (0, 0, jnp.clip(i - high, 0, steps - 1))), hbm, vm, hbm,
        ] + [vm] * 7 + [hbm, hbm, vm],
        out_specs=(slow_block(after(high + steps)), fast_block(after(high + steps)), hbm, hbm, hbm, hbm),
        out_shape=(
            shaped(xs.shape, bf16), shaped(xf.shape, bf16), shaped((sum(early_sizes), 256), bf16),
            shaped((sum(space_sizes), 256), bf16), shaped((sum(half_sizes), 256), bf16), shaped((sum(late_sizes), 256), bf16),
        ),
        scratch_shapes=[
            pltpu.VMEM((3, C_JOIN, C_MID), bf16), pltpu.VMEM((C_JOIN, C_IN), bf16), pltpu.VMEM((n, slab, WIDE_FAST), bf16),
        ] + [
            pltpu.VMEM((sum(v), 256), bf16) for v in (early_sizes, space_sizes, half_sizes, late_sizes)
        ] + [
            pltpu.VMEM((high, cols, slab, 3 * C_MID), bf16), pltpu.VMEM((high, cols, slab, 2 * C_LAT), bf16),
            pltpu.VMEM((high, cols, slab, 3 * 128), bf16), pltpu.VMEM((128, WIDE_FAST), bf16),
            pltpu.VMEM((2, 128, C_FAST), bf16), pltpu.VMEM((sum(space_sizes), 256), bf16),
            Reducer.scratch(n_clip, space_sizes), pltpu.VMEM((sum(half_sizes), 256), bf16),
            Reducer.scratch(n_clip, half_sizes), pltpu.VMEM((sum(late_sizes), 256), bf16),
            Reducer.scratch(n_clip, late_sizes), pltpu.SemaphoreType.DMA((7,)),
        ] + Reducer.sems(n_clip, early_sizes, 2) + Reducer.sems(n_clip, space_sizes) + Reducer.sems(n_clip, half_sizes)
        + Reducer.sems(n_clip, late_sizes),
        compiler_params=remote(7),
        name="seventh_pass",
    )(
        q1, z1, dzp, gf, flat(x), flat(f), kept, dwb, mom1, tot6, inv, mids, m, perm, lateral_weight, slow_a_weight,
        slow_proj_weight, wfa,
    )

    slow_rows, fast_row = shaped(lanes[0].shape, f32), shaped((1, fast_gain.shape[0]), f32)
    def here(i):
        return i

    weights = (
        shaped((C_JOIN, C_IN), f32), shaped((C_MID, C_IN), f32), shaped((3, 3, C_MID, C_MID), f32),
        shaped((3, C_JOIN, C_MID), f32), shaped((5, C_FAST, C_LAT), f32),
    )
    maps = [slow_block(here), fast_block(here)] * 2
    so, fo, sx, fx, dwp, dwc, dwb, dwa, dwl, dwfa, dwfc, dwfb, dsg, dss, dfg, dfs = pl.pallas_call(
        finish_outputs,
        grid=(high,),
        in_specs=maps + [hbm] * 4 + [vm] * 3,
        out_specs=tuple(maps) + (hbm,) * 5 + (vm,) * 7,
        out_shape=(shaped(xs.shape, bf16), shaped(xf.shape, bf16)) * 2 + weights + (
            shaped((3, C_FMID, C_FAST), f32), shaped((C_FMID, C_FAST), f32), shaped((9, C_FMID, C_FMID), f32),
            slow_rows, slow_rows, fast_row, fast_row,
        ),
        scratch_shapes=[pltpu.VMEM(v.shape, f32) for v in weights]
        + [pltpu.VMEM((sum(v), 256), bf16) for v in (early_sizes, space_sizes, half_sizes, late_sizes)]
        + [pltpu.SemaphoreType.DMA((5,)), pltpu.SemaphoreType.DMA((4,))],
        compiler_params=params(60),
        name="finish_outputs",
    )(so, fo, sx, fx, done1, done_b, done_h, done_a, tot4, tot5, tot6)
    return (
        so.transpose(3, 0, 1, 2, 4),
        fo.transpose(0, 3, 1, 2, 4),
        sx.transpose(3, 0, 1, 2, 4),
        fx.transpose(0, 3, 1, 2, 4),
        dwl,
        dwa,
        dwb,
        dwc,
        dwp,
        dwfa.transpose(0, 2, 1),
        dwfb.reshape(3, 3, C_FMID, C_FMID),
        dwfc,
        dsg.reshape(-1),
        dss.reshape(-1),
        dfg[0],
        dfs[0],
    )


def solution(mesh):
    tiles = P("clip", None, "ha", "wa", None)
    return jax.shard_map(
        on_device,
        mesh=mesh,
        in_specs=(tiles, tiles) + (P(),) * 13 + (tiles, tiles),
        out_specs=(tiles,) * 4 + (P(),) * 12,
        check_vma=False,
    )
```
